32 devices in a mesh: expert: 8 (over z, core), cuts: 4 (over y, x).
Axes of the slice: x: 2, y: 2, z: 4, core: 2. Of those that a mesh axis runs over, the one named last changes fastest.
Arguments:
- block_input: bfloat16 [8192, 1024], P(('expert', 'cuts')), may hold values from -6 to 6
- routes: int32 [8192], P(('expert', 'cuts')), may hold values from 0 to 31, as said below
- kept_mask: int32 [8192], P(('expert', 'cuts')), may hold values from 0 to 1, as said below
- w_qkv: bfloat16 [1024, 3072], P('cuts'), may hold values from -0.1875 to 0.1875
- w_attn_out: bfloat16 [1024, 1024], P('cuts'), may hold values from -1 to 1
- w_in: bfloat16 [1024, 4096], P('cuts'), may hold values from -0.1875 to 0.1875
- w_out: bfloat16 [4096, 1024], P('cuts'), may hold values from -0.1875 to 0.1875
- w_router: bfloat16 [1024, 32], P('cuts'), may hold values from -0.09375 to 0.09375
- w_mix: bfloat16 [1024, 2], P('cuts'), may hold values from -0.1875 to 0.1875
- gain_attn: bfloat16 [1024], P('cuts'), may hold values from 0.5 to 1.5
- gain_ffn: bfloat16 [1024], P('cuts'), may hold values from 0.5 to 1.5
- expert_in: bfloat16 [32, 1024, 4096], P('expert', None, 'cuts'), may hold values from -0.1875 to 0.1875
- expert_out: bfloat16 [32, 4096, 1024], P('expert', 'cuts'), may hold values from -6 to 6
- cotangent: bfloat16 [8192, 1024], P(('expert', 'cuts')), may hold values from -6 to 6
Outputs:
- block_out: bfloat16 [8192, 1024], P(('expert', 'cuts'))
- d_block_input: float32 [8192, 1024], P(('expert', 'cuts'))
- d_w_qkv: float32 [1024, 3072], P(('expert', 'cuts'))
- d_w_attn_out: float32 [1024, 1024], P(('expert', 'cuts'))
- d_w_in: float32 [1024, 4096], P(('expert', 'cuts'))
- d_w_out: float32 [4096, 1024], P(('expert', 'cuts'))
- d_w_router: float32 [1024, 32], P(('expert', 'cuts'))
- d_w_mix: float32 [1024, 2], P(('expert', 'cuts'))
- d_gain_attn: float32 [1024], P(('expert', 'cuts'))
- d_gain_ffn: float32 [1024], P(('expert', 'cuts'))
- d_expert_in: float32 [32, 1024, 4096], P('expert', None, 'cuts')
- d_expert_out: float32 [32, 4096, 1024], P('expert', 'cuts')
The draws below stay inside these ranges and needn't reach their ends.
Inputs may be any that keep to these rules, and one draw needn't show every extreme that they name: `routes`: the expert of each token; a few experts are far more common than the rest. kept_mask is 1 exactly for the first 12 tokens of each expert within the rows of one device, in token order; on every device some expert fills all 12 of its slots.
All inputs are finite; a program needn't handle non-finite values.
Results may differ from the reference program's by a relative error of at most 0.017.
Values may be sent and summed in bfloat16 or wider, within the bound.
A program may use at most 320 MiB of HBM per device.

```python
import jax
import jax.numpy as jnp
import numpy as np
from jax import lax

D = 1024
H = 16
HD = 64
FF = 4096
EH = 4096
TOK_DEV = 256
EXPERTS = 32
CAP = 12
SEQ = 1024
TOKENS = 8192
N_EXPERT = 8
N_CUTS = 4


def route_plan(key):
    base = jax.random.fold_in(key, 11)
    order_key, pick_key = jax.random.split(base)
    weights = np.floor(65536.0 / np.sqrt(np.arange(1, EXPERTS + 1))).astype(np.int32)
    bounds = jnp.asarray(np.cumsum(weights).astype(np.int32))
    weight_sum = int(np.sum(weights))
    picks = jax.random.randint(pick_key, (TOKENS,), 0, weight_sum, dtype=jnp.int32)
    ranked = jnp.sum((picks[:, None] >= bounds[None, :]).astype(jnp.int32), axis=1)
    ranking = jax.random.permutation(order_key, EXPERTS).astype(jnp.int32)
    chosen = ranking[ranked]
    onehot = (chosen.reshape(-1, TOK_DEV)[:, :, None] == jnp.arange(EXPERTS, dtype=jnp.int32)[None, None, :]).astype(jnp.int32)
    running = jnp.cumsum(onehot, axis=1)
    place = jnp.sum(onehot * running, axis=2) - 1
    keeping = (place < CAP).astype(jnp.int32).reshape(TOKENS)
    return (chosen.astype(jnp.int32), keeping)


def draw_routes(key, part):
    chosen, keeping = route_plan(key)
    return chosen


def draw_kept_mask(key, part):
    chosen, keeping = route_plan(key)
    return keeping


def levels(rng, shape, cuts, low, top_value):
    level, own = 1.0, jax.random.fold_in(rng, 6)
    for dim, parts in cuts:
        heights = jnp.exp(jax.random.uniform(jax.random.fold_in(own, dim), (parts,), jnp.float32, low / len(cuts), top_value / len(cuts)))
        level = level * jnp.repeat(heights, shape[dim] // parts).reshape([-1 if axis == dim else 1 for axis in range(len(shape))])
    return level


def scatter_about(key, shape, deviation, most, cuts=(), kind=jnp.bfloat16):
    values = deviation * jax.random.normal(key, shape, jnp.float32)
    if cuts:
        values = values * levels(key, shape, cuts, -0.22, 0.18)
    return jnp.clip(values, -most, most).astype(kind)


def setup_inputs(seed: int = 0) -> dict:
    arg_keys = jax.random.split(jax.random.key(seed), 15)
    block_input = scatter_about(arg_keys[0], (TOKENS, D), 1.0, 6.0, ((0, 32),))
    routes = draw_routes(jax.random.fold_in(arg_keys[14], 71), 0)
    kept_mask = draw_kept_mask(jax.random.fold_in(arg_keys[14], 71), 0)
    w_qkv = scatter_about(arg_keys[3], (D, 3 * D), D ** -0.5, 0.1875, ((0, 4),))
    w_attn_out = scatter_about(arg_keys[4], (D, D), (D // 32) ** -0.5, 1.0, ((0, 4),))
    w_in = scatter_about(arg_keys[5], (D, FF), D ** -0.5, 0.1875, ((0, 4),))
    w_out = scatter_about(arg_keys[6], (FF, D), (FF // 4) ** -0.5, 0.1875, ((0, 4),))
    w_router = scatter_about(arg_keys[7], (D, EXPERTS), (4 * D) ** -0.5, 0.09375, ((0, 4),))
    w_mix = scatter_about(arg_keys[8], (D, 2), D ** -0.5, 0.1875, ((0, 4),))
    gain_attn = jnp.clip(1.0 + 0.1 * jax.random.normal(arg_keys[9], (D,), jnp.float32), 0.5, 1.5).astype(jnp.bfloat16)
    gain_ffn = jnp.clip(1.0 + 0.1 * jax.random.normal(arg_keys[10], (D,), jnp.float32), 0.5, 1.5).astype(jnp.bfloat16)
    expert_in = scatter_about(arg_keys[11], (EXPERTS, D, EH), D ** -0.5, 0.1875, ((0, 8), (2, 4)))
    expert_out = scatter_about(arg_keys[12], (EXPERTS, EH, D), (EXPERTS // 32), 6.0, ((0, 8), (1, 4)))
    cotangent = scatter_about(arg_keys[13], (TOKENS, D), 1.0, 6.0, ((0, 32),))
    return {"block_input": block_input, "routes": routes, "kept_mask": kept_mask, "w_qkv": w_qkv, "w_attn_out": w_attn_out, "w_in": w_in, "w_out": w_out, "w_router": w_router, "w_mix": w_mix, "gain_attn": gain_attn, "gain_ffn": gain_ffn, "expert_in": expert_in, "expert_out": expert_out, "cotangent": cotangent}


@jax.custom_vjp
def low(v):
    return lax.optimization_barrier(v.astype(jnp.bfloat16)).astype(jnp.float32)

@jax.custom_vjp
def low_back(v):
    return v

def low_keep(v):
    return (low(v), None)

def low_pass(kept, grad):
    return (grad,)

def back_keep(v):
    return (v, None)

def back_low(kept, grad):
    return (low(grad),)
low.defvjp(low_keep, low_pass)
low_back.defvjp(back_keep, back_low)
highest = lax.Precision.HIGHEST

def layer_norm(values, gain):
    center = values - lax.optimization_barrier(jnp.mean(values, axis=-1, keepdims=True))
    spread = lax.optimization_barrier(jnp.mean(center * center, axis=-1, keepdims=True))
    return center * lax.rsqrt(spread + 1e-05) * gain

def matmul(left, right):
    return jnp.dot(left, right, precision=highest, preferred_element_type=jnp.float32)

def softmax_rows(logits):
    shifted = logits - lax.optimization_barrier(jnp.max(logits, axis=-1, keepdims=True))
    row_exp = jnp.exp(shifted)
    return row_exp / lax.optimization_barrier(jnp.sum(row_exp, axis=-1, keepdims=True))

def attend(seq_block):
    queries = seq_block[:, :D].reshape(SEQ, H, HD)
    key_rows = seq_block[:, D:2 * D].reshape(SEQ, H, HD)
    value_rows = seq_block[:, 2 * D:].reshape(SEQ, H, HD)
    scores = jnp.einsum('qhd,khd->hqk', queries, key_rows, precision=highest) * HD ** (-0.5)
    scores = low_back(scores)
    places = jnp.arange(SEQ, dtype=jnp.int32)
    visible = places[None, :] <= places[:, None]
    scores = jnp.where(visible[None], scores, -1e+30)
    weights_p = softmax_rows(scores)
    head_out = jnp.einsum('hqk,khd->qhd', low(weights_p), value_rows, precision=highest)
    return head_out.reshape(SEQ, D)

def expert_apply(pieces):
    weight_in, weight_out, rows_in = pieces
    first = low_back(matmul(rows_in, weight_in))
    active = low(jax.nn.gelu(first))
    return low(low_back(matmul(active, weight_out)))

def slot_index(routes, kept_mask):
    device_count = N_EXPERT * N_CUTS
    route_grid = routes.reshape(device_count, TOK_DEV)
    keep_grid = kept_mask.reshape(device_count, TOK_DEV)
    onehot = (route_grid[:, :, None] == jnp.arange(EXPERTS, dtype=jnp.int32)[None, None, :]).astype(jnp.int32)
    onehot = onehot * keep_grid[:, :, None]
    running = jnp.cumsum(onehot, axis=1)
    place = lax.optimization_barrier(jnp.sum(onehot * running, axis=2)) - 1
    device = jnp.arange(device_count, dtype=jnp.int32)[:, None]
    flat = route_grid * (device_count * CAP) + device * CAP + place
    flat = jnp.where(keep_grid > 0, flat, EXPERTS * device_count * CAP)
    return flat.reshape(TOKENS).astype(jnp.int32)

def forward(inputs, w_qkv, w_attn_out, w_in, w_out, w_router, w_mix, gain_attn, gain_ffn, expert_in, expert_out, flat, onehot, keep_col):
    normed = low(layer_norm(inputs, gain_attn))
    joined = low(low_back(matmul(normed, w_qkv)))
    head_out = lax.map(jax.checkpoint(attend), joined.reshape(N_EXPERT, SEQ, 3 * D)).reshape(TOKENS, D)
    head_out = low(low_back(head_out))
    hidden = inputs + low_back(matmul(head_out, w_attn_out))
    second = low(layer_norm(hidden, gain_ffn))
    up_proj = low_back(matmul(second, w_in))
    dense = low_back(matmul(low(jax.nn.gelu(up_proj)), w_out))
    router_p = softmax_rows(low_back(matmul(second, w_router)))
    gate = lax.optimization_barrier(jnp.sum(router_p * onehot, axis=1, keepdims=True))
    mixing = softmax_rows(low_back(matmul(second, w_mix)))
    slot_total = EXPERTS * N_EXPERT * N_CUTS * CAP
    buffer_in = jnp.zeros((slot_total, D), jnp.float32).at[flat].add(low_back(second), mode='drop')
    expert_vals = lax.map(jax.checkpoint(expert_apply), (expert_in, expert_out, buffer_in.reshape(EXPERTS, slot_total // EXPERTS, D)))
    picked = expert_vals.reshape(slot_total, D)[jnp.minimum(flat, slot_total - 1)] * keep_col
    return hidden + mixing[:, 0:1] * dense + mixing[:, 1:2] * (gate * picked)

def reference(block_input, routes, kept_mask, w_qkv, w_attn_out, w_in, w_out, w_router, w_mix, gain_attn, gain_ffn, expert_in, expert_out, cotangent):
    flat = slot_index(routes, kept_mask)
    onehot = (routes[:, None] == jnp.arange(EXPERTS, dtype=jnp.int32)[None, :]).astype(jnp.float32)
    keep_col = kept_mask.astype(jnp.float32)[:, None]
    floats = [array.astype(jnp.float32) for array in (block_input, w_qkv, w_attn_out, w_in, w_out, w_router, w_mix, gain_attn, gain_ffn, expert_in, expert_out)]

    def closed(*params):
        return forward(*params, flat, onehot, keep_col)
    result, pull = jax.vjp(closed, *floats)
    grads = pull(cotangent.astype(jnp.float32))
    return (result.astype(jnp.bfloat16), grads[0], grads[1], grads[2], grads[3], grads[4], grads[5], grads[6], grads[7], grads[8], grads[9], grads[10])
```

```python
import jax
import jax.numpy as jnp
from jax import lax
from jax.sharding import PartitionSpec as P

HD = 64
BF = jnp.bfloat16
F32 = jnp.float32


def norm_parts(values):
    center = values - jnp.mean(values, axis=-1, keepdims=True)
    spread = jnp.mean(center * center, axis=-1, keepdims=True)
    inv = lax.rsqrt(spread + 1e-05)
    return center * inv, inv


def norm_back(grad, xhat, inv, gain):
    q = grad * gain
    mean_q = jnp.mean(q, axis=-1, keepdims=True)
    mean_qx = jnp.mean(q * xhat, axis=-1, keepdims=True)
    return (q - mean_q - xhat * mean_qx) * inv, jnp.sum(grad * xhat, axis=0)


def mm(left, right):
    return jnp.dot(left, right, preferred_element_type=F32)


def mm_nt(left, right):
    return lax.dot_general(left, right, (((1,), (1,)), ((), ())), preferred_element_type=F32)


def mm_tn(left, right):
    return lax.dot_general(left, right, (((0,), (0,)), ((), ())), preferred_element_type=F32)


def softmax_rows(logits):
    shifted = logits - jnp.max(logits, axis=-1, keepdims=True)
    row_exp = jnp.exp(shifted)
    return row_exp / jnp.sum(row_exp, axis=-1, keepdims=True)


def gather_cuts(rows):
    return lax.all_gather(rows, "cuts", axis=0, tiled=True)


def scatter_cuts(rows):
    return lax.psum_scatter(rows.astype(BF), "cuts", scatter_dimension=0, tiled=True)


def columns_to_cuts(rows):
    return lax.all_to_all(rows, "cuts", split_axis=1, concat_axis=0, tiled=True)


def rows_to_cuts(rows):
    return lax.all_to_all(rows, "cuts", split_axis=0, concat_axis=1, tiled=True)


def shards(
    block_input,
    routes,
    kept_mask,
    w_qkv,
    w_attn_out,
    w_in,
    w_out,
    w_router,
    w_mix,
    gain_attn,
    gain_ffn,
    expert_in,
    expert_out,
    cotangent,
):
    tokens, features = block_input.shape
    n_cuts = lax.axis_size("cuts")
    n_expert = lax.axis_size("expert")
    seq_len = tokens * n_cuts
    scaling = HD ** (-0.5)
    own = features // n_cuts
    heads = own // HD
    experts_all = w_router.shape[1]
    experts_here = expert_in.shape[0]
    capacity = 3 * tokens // (2 * experts_all)

    gains = gather_cuts(jnp.stack([gain_attn, gain_ffn], axis=1)).astype(F32)
    gain_one, gain_two = gains[:, 0], gains[:, 1]
    inputs = block_input.astype(F32)
    xhat_one, inv_one = norm_parts(inputs)
    normed = gather_cuts((xhat_one * gain_one).astype(BF))
    qkv_here = lax.all_to_all(
        w_qkv.reshape(own, 3, n_cuts, own), "cuts", split_axis=2, concat_axis=0, tiled=True
    ).reshape(features, 3 * own)
    joined = mm(normed, qkv_here).astype(BF)
    split = joined.reshape(seq_len, 3, heads, HD)
    q_heads, k_heads, v_heads = split[:, 0], split[:, 1], split[:, 2]
    spots = jnp.arange(seq_len, dtype=jnp.int32)
    visible = (spots[None, :] <= spots[:, None])[None]

    def masked_scores():
        scores = jnp.einsum("qhd,khd->hqk", q_heads, k_heads, preferred_element_type=F32) * scaling
        return jnp.where(visible, scores, -1e30)

    scores = masked_scores()
    peak = jnp.max(scores, axis=-1, keepdims=True)
    row_exp = jnp.exp(scores - peak)
    total = jnp.sum(row_exp, axis=-1, keepdims=True)
    weights_p = (row_exp / total).astype(BF)
    heads_here = jnp.einsum("hqk,khd->qhd", weights_p, v_heads, preferred_element_type=F32)
    log_norm = peak + jnp.log(total)
    head_out = rows_to_cuts(heads_here.reshape(seq_len, own).astype(BF))
    attn_full = gather_cuts(w_attn_out)
    small_full = gather_cuts(jnp.concatenate([w_router, w_mix], axis=1))
    hidden = inputs + mm(head_out, attn_full)
    xhat_two, inv_two = norm_parts(hidden)
    second = (xhat_two * gain_two).astype(BF)

    logits = mm(second, small_full)
    onehot = (routes[:, None] == jnp.arange(experts_all, dtype=jnp.int32)[None, :]).astype(F32)
    router_p = softmax_rows(logits[:, :experts_all])
    mixing = softmax_rows(logits[:, experts_all:])
    gate = jnp.sum(router_p * onehot, axis=1)
    grad = cotangent.astype(F32)
    d_dense = (grad * mixing[:, 0:1]).astype(BF)
    d_moe = grad * mixing[:, 1:2]
    d_picked = (d_moe * gate[:, None]).astype(BF)

    onehot_kept = onehot * kept_mask.astype(F32)[:, None]
    lower_tri = (jnp.arange(tokens)[:, None] >= jnp.arange(tokens)[None, :]).astype(BF)
    running = mm(lower_tri, onehot_kept.astype(BF))
    slot_num = jnp.sum(onehot_kept * running, axis=1) - 1.0
    target = routes.astype(F32) * capacity + slot_num
    columns = jnp.arange(experts_all * capacity, dtype=jnp.int32).astype(F32)
    placer = ((columns[None, :] == target[:, None]) & (kept_mask[:, None] > 0)).astype(BF)
    both = jnp.concatenate([second, d_picked], axis=1)
    slots = mm_tn(placer, both).astype(BF)
    grid = slots.reshape(n_expert, experts_here, capacity, 2 * features)
    moved = lax.all_to_all(grid, "expert", split_axis=0, concat_axis=2, tiled=True)
    rows_both = lax.all_gather(moved, "cuts", axis=2, tiled=True)[0]
    rows_in, d_rows = rows_both[:, :, :features], rows_both[:, :, features:]

    ffn_both = gather_cuts(jnp.concatenate([second, d_dense], axis=1))
    second_all, d_dense_all = ffn_both[:, :features], ffn_both[:, features:]
    in_here = columns_to_cuts(w_in)
    up_proj = mm(second_all, in_here)
    activ, gelu_pull = jax.vjp(jax.nn.gelu, up_proj)
    activ_low = activ.astype(BF)
    dense_part = mm(activ_low, w_out)
    d_activ = mm_nt(d_dense_all, w_out)
    g_out = mm_tn(activ_low, d_dense_all)
    d_up = gelu_pull(d_activ)[0].astype(BF)
    g_in = mm_tn(second_all, d_up)
    d_second_part = mm_nt(d_up, in_here)
    ffn_sums = scatter_cuts(jnp.concatenate([dense_part, d_second_part], axis=1))
    dense, d_second_ffn = ffn_sums[:, :features].astype(F32), ffn_sums[:, features:].astype(F32)

    first = jnp.einsum("erd,edh->erh", rows_in, expert_in, preferred_element_type=F32)
    expert_act, expert_pull = jax.vjp(jax.nn.gelu, first)
    expert_low = expert_act.astype(BF)
    partial_out = jnp.einsum("erh,ehd->erd", expert_low, expert_out, preferred_element_type=F32)
    d_expert_act = jnp.einsum("erd,ehd->erh", d_rows, expert_out, preferred_element_type=F32)
    d_first = expert_pull(d_expert_act)[0].astype(BF)
    d_rows_in = jnp.einsum("erh,edh->erd", d_first, expert_in, preferred_element_type=F32)
    g_expert_out = jnp.einsum("erh,erd->ehd", expert_low, d_rows, preferred_element_type=F32)
    g_expert_in = jnp.einsum("erd,erh->edh", rows_in, d_first, preferred_element_type=F32)
    back = jnp.concatenate([partial_out, d_rows_in], axis=2).astype(BF)
    summed = lax.psum_scatter(back[None], "cuts", scatter_dimension=2, tiled=True)
    returned = lax.all_to_all(summed, "expert", split_axis=2, concat_axis=0, tiled=True)
    picked_both = mm(placer, returned.reshape(-1, 2 * features))
    picked, d_picked_in = picked_both[:, :features], picked_both[:, features:]

    moe_val = gate[:, None] * picked
    block_out = (hidden + mixing[:, 0:1] * dense + mixing[:, 1:2] * moe_val).astype(BF)
    d_mixing = jnp.stack([jnp.sum(grad * dense, axis=1), jnp.sum(grad * moe_val, axis=1)], axis=1)
    d_gate = jnp.sum(d_moe * picked, axis=1)
    d_router = router_p * (onehot - gate[:, None]) * d_gate[:, None]
    d_mix = mixing * (d_mixing - jnp.sum(mixing * d_mixing, axis=1, keepdims=True))
    d_small = jnp.concatenate([d_router, d_mix], axis=1).astype(BF)
    g_small = mm_tn(second, d_small)
    d_second = d_second_ffn + mm_nt(d_small, small_full) + d_picked_in
    d_hidden_norm, g_gain_two = norm_back(d_second, xhat_two, inv_two, gain_two)
    d_hidden = grad + d_hidden_norm
    d_attn = d_hidden.astype(BF)
    g_attn_out = mm_tn(head_out, d_attn)
    d_heads = columns_to_cuts(mm_nt(d_attn, attn_full).astype(BF)).reshape(seq_len, heads, HD)

    soft_p = jnp.exp(masked_scores() - log_norm)
    d_soft = jnp.einsum("qhd,khd->hqk", d_heads, v_heads, preferred_element_type=F32)
    delta = jnp.sum(soft_p * d_soft, axis=-1, keepdims=True)
    d_scores = (soft_p * (d_soft - delta)).astype(BF)
    d_query = jnp.einsum("hqk,khd->qhd", d_scores, k_heads, preferred_element_type=F32) * scaling
    d_keys = jnp.einsum("hqk,qhd->khd", d_scores, q_heads, preferred_element_type=F32) * scaling
    d_values = jnp.einsum("hqk,qhd->khd", soft_p.astype(BF), d_heads, preferred_element_type=F32)
    d_joined = jnp.stack([d_query, d_keys, d_values], axis=1).reshape(seq_len, 3 * own).astype(BF)
    g_qkv = mm_tn(normed, d_joined)
    d_normed = scatter_cuts(mm_nt(d_joined, qkv_here)).astype(F32)
    d_input_norm, g_gain_one = norm_back(d_normed, xhat_one, inv_one, gain_one)
    d_block_input = d_hidden + d_input_norm

    def over_experts(part):
        return lax.psum_scatter(part.astype(BF), "expert", scatter_dimension=0, tiled=True)

    s_in = rows_to_cuts(over_experts(g_in)).astype(F32)
    s_out = over_experts(g_out)
    swap = [
        ((flat % n_expert) * n_cuts + flat // n_expert, flat) for flat in range(n_expert * n_cuts)
    ]
    s_out = lax.ppermute(s_out, ("expert", "cuts"), swap).astype(F32)
    s_qkv = over_experts(g_qkv)
    deep = s_qkv.shape[0]
    s_qkv = lax.all_to_all(
        s_qkv.reshape(deep, 3, 1, own), "cuts", split_axis=0, concat_axis=2, tiled=True
    )
    s_qkv = s_qkv.reshape(-1, 3 * features).astype(F32)
    s_attn_out = lax.psum_scatter(
        g_attn_out.astype(BF), ("expert", "cuts"), scatter_dimension=0, tiled=True
    ).astype(F32)
    tiny = jnp.concatenate([g_small, g_gain_one[:, None], g_gain_two[:, None]], axis=1)
    s_tiny = lax.psum_scatter(tiny, ("expert", "cuts"), scatter_dimension=0, tiled=True)
    return (
        block_out,
        d_block_input,
        s_qkv,
        s_attn_out,
        s_in,
        s_out,
        s_tiny[:, :experts_all],
        s_tiny[:, experts_all : experts_all + 2],
        s_tiny[:, experts_all + 2],
        s_tiny[:, experts_all + 3],
        g_expert_in,
        g_expert_out,
    )


def solution(mesh):
    both = ("expert", "cuts")
    placed = (
        P(both, None),
        P(both),
        P(both),
        P("cuts", None),
        P("cuts", None),
        P("cuts", None),
        P("cuts", None),
        P("cuts", None),
        P("cuts", None),
        P("cuts"),
        P("cuts"),
        P("expert", None, "cuts"),
        P("expert", "cuts", None),
        P(both, None),
    )
    results = (
        P(both, None),
        P(both, None),
        P(both, None),
        P(both, None),
        P(both, None),
        P(both, None),
        P(both, None),
        P(both, None),
        P(both),
        P(both),
        P("expert", None, "cuts"),
        P("expert", "cuts", None),
    )
    return jax.shard_map(
        shards, mesh=mesh, in_specs=placed, out_specs=results, check_vma=False
    )
```

```python
import functools
import math

import jax
import jax.numpy as jnp
from jax import lax
from jax.experimental import pallas as pl
from jax.experimental.pallas import tpu as pltpu
from jax.sharding import PartitionSpec as P

HD = 64
BF = jnp.bfloat16
F32 = jnp.float32
MESH = pl.DeviceIdType.MESH


def norm_parts(values):
    center = values - jnp.mean(values, axis=-1, keepdims=True)
    spread = jnp.mean(center * center, axis=-1, keepdims=True)
    inv = lax.rsqrt(spread + 1e-05)
    return center * inv, inv


def norm_back(grad, xhat, inv, gain):
    q = grad * gain
    mean_q = jnp.mean(q, axis=-1, keepdims=True)
    mean_qx = jnp.mean(q * xhat, axis=-1, keepdims=True)
    return (q - mean_q - xhat * mean_qx) * inv, jnp.sum(grad * xhat, axis=0)


def mm(left, right):
    return jnp.dot(left, right, preferred_element_type=F32)


def mm_nt(left, right):
    return lax.dot_general(left, right, (((1,), (1,)), ((), ())), preferred_element_type=F32)


def mm_tn(left, right):
    return lax.dot_general(left, right, (((0,), (0,)), ((), ())), preferred_element_type=F32)


def softmax_rows(logits):
    shifted = logits - jnp.max(logits, axis=-1, keepdims=True)
    row_exp = jnp.exp(shifted)
    return row_exp / jnp.sum(row_exp, axis=-1, keepdims=True)


def gather_cuts(rows):
    return lax.all_gather(rows, "cuts", axis=0, tiled=True)


def scatter_cuts(rows):
    return lax.psum_scatter(rows.astype(BF), "cuts", scatter_dimension=0, tiled=True)


def columns_to_cuts(rows):
    return lax.all_to_all(rows, "cuts", split_axis=1, concat_axis=0, tiled=True)


def rows_to_cuts(rows):
    return lax.all_to_all(rows, "cuts", split_axis=0, concat_axis=1, tiled=True)


def ring_mod(index, count):
    return lax.rem(index, count)


def small_kernel(n_expert, n_cuts, src, out, by_expert, mine, by_cuts, send_a, recv_a, send_b, recv_b):
    me, cut = lax.axis_index("expert"), lax.axis_index("cuts")
    width = out.shape[1]
    barrier = pltpu.get_barrier_semaphore()
    for step in range(1, n_expert):
        peer = ring_mod(me + step, n_expert)
        pl.semaphore_signal(barrier, inc=1, device_id=(peer, cut), device_id_type=MESH)
    for step in range(1, n_cuts):
        peer = ring_mod(cut + step, n_cuts)
        pl.semaphore_signal(barrier, inc=1, device_id=(me, peer), device_id_type=MESH)
    pl.semaphore_wait(barrier, n_expert + n_cuts - 2)

    def part(owner):
        return src.at[:, pl.ds(pl.multiple_of(owner * width, 128), width)]

    copies = []
    for step in range(1, n_expert):
        peer = ring_mod(me + step, n_expert)
        copies.append(
            pltpu.make_async_remote_copy(
                src_ref=part(peer),
                dst_ref=by_expert.at[step],
                send_sem=send_a.at[step],
                recv_sem=recv_a.at[step],
                device_id=(peer, cut),
                device_id_type=MESH,
            )
        )
        copies[-1].start()
    total = src[:, pl.ds(pl.multiple_of(me * width, 128), width)]
    for step in range(1, n_expert):
        copies[step - 1].wait()
        total = total + by_expert[step]
    mine[...] = total
    copies = []
    for step in range(1, n_cuts):
        peer = ring_mod(cut + step, n_cuts)
        copies.append(
            pltpu.make_async_remote_copy(
                src_ref=mine,
                dst_ref=by_cuts.at[step],
                send_sem=send_b.at[step],
                recv_sem=recv_b.at[step],
                device_id=(me, peer),
                device_id_type=MESH,
            )
        )
        copies[-1].start()
    for step in range(1, n_cuts):
        copies[step - 1].wait()
        total = total + by_cuts[step]
    out[...] = total


def sum_small(values, n_expert, n_cuts):
    rows, features = values.shape
    width = features // n_expert
    pad = -width % 128
    if pad:
        values = jnp.pad(values.reshape(rows, n_expert, width), ((0, 0), (0, 0), (0, pad)))
        values = values.reshape(rows, n_expert * (width + pad))
    wide = width + pad
    summed = pl.pallas_call(
        functools.partial(small_kernel, n_expert, n_cuts),
        name="sum_small",
        out_shape=jax.ShapeDtypeStruct((rows, wide), F32),
        in_specs=[pl.BlockSpec(memory_space=pltpu.VMEM)],
        out_specs=pl.BlockSpec(memory_space=pltpu.VMEM),
        scratch_shapes=[
            pltpu.VMEM((n_expert, rows, wide), F32),
            pltpu.VMEM((rows, wide), F32),
            pltpu.VMEM((n_cuts, rows, wide), F32),
            pltpu.SemaphoreType.DMA((n_expert,)),
            pltpu.SemaphoreType.DMA((n_expert,)),
            pltpu.SemaphoreType.DMA((n_cuts,)),
            pltpu.SemaphoreType.DMA((n_cuts,)),
        ],
        compiler_params=pltpu.CompilerParams(collective_id=0, has_side_effects=True),
    )(values)
    return summed[:, :width]


def dot_nt(left, right):
    return lax.dot_general(left, right, (((1,), (1,)), ((), ())), preferred_element_type=F32)


def tile_of(step, size):
    return pl.ds(pl.multiple_of(step * size, size), size)


def lane_softmax(logits, low, high):
    lane = lax.broadcasted_iota(jnp.int32, logits.shape, 1)
    inside = (lane >= low) & (lane < high)
    kept = jnp.where(inside, logits, -1e30)
    powers = jnp.exp(kept - jnp.max(kept, axis=1, keepdims=True))
    powers = jnp.where(inside, powers, 0.0)
    return powers / jnp.sum(powers, axis=1, keepdims=True), lane


def mlp_both(rows, d_rows, w_up, w_down, act, d_up, write):
    root, cubic = math.sqrt(2.0 / math.pi), 0.044715

    @pl.loop(0, act.shape[1] // 256)
    def _(step):
        span = tile_of(step, 256)
        up = mm(rows[...], w_up[:, span])
        d_act = dot_nt(d_rows[...], w_down[span, :])
        square = up * up
        bent = jnp.tanh(root * up * (1.0 + cubic * square))
        half = 0.5 * (1.0 + bent)
        act[:, span] = (up * half).astype(BF)
        slope = half + 0.5 * up * (1.0 - bent * bent) * (root + 3.0 * root * cubic * square)
        d_up[:, span] = (d_act * slope).astype(BF)

    @pl.loop(0, w_up.shape[0] // 256)
    def _(step):
        span = tile_of(step, 256)
        write(span, mm(act[...], w_down[:, span]), dot_nt(d_up[...], w_up[span, :]))


def middle_kernel(
    sizes, slots, second, grad_all, grad_rows, w_in, w_out, small, sort, unsort, e_in, e_out,
    sums, returned, second_all, act_all, d_up_all, d_dense_all, rows_in, d_rows_all, act_e_all, d_first_all,
    sec, grd, win, wout, act, d_up, d_dense, part_a, part_b, ffn_x, ffn_y, ffn_qa, ffn_qb,
    zbuf, rows, g_rows, d_rows, act_e, d_first, wi_e, wo_e, out_a, out_b, row_x, row_y, row_qa, row_qb, sorted_back, send_back,
    load_sem, weight_sem, store_sem, store_e_sem, z_sem, ag_sem, eag_sem, frs_sem, ers_sem, zr_sem,
):
    n_expert, groups, here, slab = sizes
    me, cut = lax.axis_index("expert"), lax.axis_index("cuts")
    at_x, at_y, at_d = (jnp.bitwise_xor(cut, k) for k in (1, 2, 3))
    block = zbuf.shape[2]
    per_group = here // groups
    experts_all = n_expert * here

    def load(src, dst, index):
        copy = pltpu.make_async_copy(src, dst, load_sem.at[index])
        copy.start()
        return copy

    def send(src, dst, sems, index, peer):
        copy = pltpu.make_async_remote_copy(
            src_ref=src, dst_ref=dst, send_sem=sems.at[0, index], recv_sem=sems.at[1, index],
            device_id=peer, device_id_type=MESH,
        )
        copy.start()
        return copy

    loads = [
        load(second, sec.at[cut], 0), load(w_in, win, 1), load(w_out, wout, 2), load(grad_all, grd, 3),
    ]

    def fetch_expert(i):
        slot = i % 2
        copies = [
            pltpu.make_async_copy(e_in.at[i], wi_e.at[slot], weight_sem.at[0, slot]),
            pltpu.make_async_copy(e_out.at[i], wo_e.at[slot], weight_sem.at[1, slot]),
            pltpu.make_async_copy(grad_rows.at[i], g_rows.at[slot], weight_sem.at[2, slot]),
        ]
        for copy in copies:
            copy.start()
        return copies

    fetched = [fetch_expert(0), fetch_expert(1)]
    barrier = pltpu.get_barrier_semaphore()
    for k in range(1, n_expert):
        pl.semaphore_signal(barrier, inc=1, device_id=(jnp.bitwise_xor(me, k), cut), device_id_type=MESH)
    for peer in (at_x, at_y):
        pl.semaphore_signal(barrier, inc=1, device_id=(me, peer), device_id_type=MESH)
    pl.semaphore_wait(barrier, n_expert + 1)

    z_copies = []
    for g in range(groups):
        for k in range(1, n_expert):
            peer = jnp.bitwise_xor(me, k)
            z_copies.append(send(slots.at[g, peer], zbuf.at[g, me], z_sem, g * n_expert + k, (peer, cut)))
    loads[0].wait()
    ag = [
        send(sec.at[cut], sec.at[cut], ag_sem, 0, (me, at_x)),
        send(sec.at[cut], sec.at[cut], ag_sem, 1, (me, at_y)),
    ]
    for g in range(groups):
        zbuf[g, me] = slots[g, me]
    stores = []

    def store(src, dst, index):
        copy = pltpu.make_async_copy(src, dst, store_sem.at[index])
        copy.start()
        return copy

    ffn_stores = {}

    def ffn_block(which, owner):
        slot = which % 2
        if which >= 2:
            for copy in ffn_stores[which - 2]:
                copy.wait()
        mixing, lane = lane_softmax(mm(sec[owner], small[...]), experts_all, experts_all + 2)
        first_mix = jnp.sum(jnp.where(lane == experts_all, mixing, 0.0), axis=1, keepdims=True)
        d_dense[slot] = (grd[owner].astype(F32) * first_mix).astype(BF)

        def write(span, out, d_row):
            if which == 0:
                sums[0, :, span] = out
                sums[1, :, span] = d_row
            else:
                part_a[which, :, span] = out.astype(BF)
                part_b[which, :, span] = d_row.astype(BF)

        mlp_both(sec.at[owner], d_dense.at[slot], win, wout, act.at[slot], d_up.at[slot], write)
        ffn_stores[which] = [
            store(act.at[slot], act_all.at[owner], 3 * which),
            store(d_up.at[slot], d_up_all.at[owner], 3 * which + 1),
            store(d_dense.at[slot], d_dense_all.at[owner], 3 * which + 2),
        ]

    for copy in loads[1:]:
        copy.wait()
    ffn_block(0, cut)
    half = sec.shape[1] // 2
    ag[0].wait_recv()
    ag.append(send(sec.at[at_x, pl.ds(0, half)], sec.at[at_x, pl.ds(0, half)], ag_sem, 2, (me, at_y)))
    ag[1].wait_recv()
    ag.append(send(sec.at[at_y, pl.ds(half, half)], sec.at[at_y, pl.ds(half, half)], ag_sem, 3, (me, at_x)))
    ffn_block(1, at_x)

    def slab_of(owner):
        return pl.ds(pl.multiple_of(owner * slab, slab), slab)

    eag = {}
    for g in range(groups):
        for k in range(1, n_expert):
            z_copies[g * (n_expert - 1) + k - 1].wait_recv()
        flat = zbuf[g].reshape(n_expert * block, zbuf.shape[3])
        for j in range(per_group):
            i = g * per_group + j
            rows[i, slab_of(cut)] = mm(sort[pl.ds(j * slab, slab), :], flat).astype(BF)
            mine = rows.at[i, slab_of(cut)]
            eag[i] = [
                send(mine, mine, eag_sem, 4 * i, (me, at_x)),
                send(mine, mine, eag_sem, 4 * i + 1, (me, at_y)),
            ]
    ffn_block(2, at_y)
    ag[2].wait_recv()
    ag[3].wait_recv()

    def relay(i):
        cut_half = slab // 2
        eag[i][0].wait_recv()
        piece = rows.at[i, pl.ds(pl.multiple_of(at_x * slab, slab), cut_half)]
        eag[i].append(send(piece, piece, eag_sem, 4 * i + 2, (me, at_y)))
        eag[i][1].wait_recv()
        piece = rows.at[i, pl.ds(pl.multiple_of(at_y * slab + cut_half, cut_half), cut_half)]
        eag[i].append(send(piece, piece, eag_sem, 4 * i + 3, (me, at_x)))

    relay(0)
    ffn_block(3, at_d)
    frs = [
        send(part_a.at[1], ffn_x.at[0], frs_sem, 0, (me, at_x)),
        send(part_a.at[3], ffn_x.at[1], frs_sem, 1, (me, at_x)),
        send(part_b.at[2], ffn_y.at[0], frs_sem, 2, (me, at_y)),
        send(part_b.at[3], ffn_y.at[1], frs_sem, 3, (me, at_y)),
    ]
    second_store = store(sec, second_all, 12)
    expert_stores = {}
    ers = {}

    def expert(i):
        slot = i % 2
        if i >= 2:
            for copy in expert_stores[i - 2]:
                copy.wait()
        for copy in fetched[i]:
            copy.wait()
        logits = mm(rows[i], small[...])
        router, lane = lane_softmax(logits, 0, experts_all)
        gate = jnp.sum(jnp.where(lane == me * here + i, router, 0.0), axis=1, keepdims=True)
        mixing, lane = lane_softmax(logits, experts_all, experts_all + 2)
        mixing = jnp.sum(jnp.where(lane == experts_all + 1, mixing, 0.0), axis=1, keepdims=True)
        d_rows[slot] = (g_rows[slot].astype(F32) * mixing * gate).astype(BF)

        def write(span, out, d_row):
            out_a[i, :, span] = out.astype(BF)
            out_b[i, :, span] = d_row.astype(BF)

        mlp_both(rows.at[i], d_rows.at[slot], wi_e.at[slot], wo_e.at[slot], act_e.at[slot], d_first.at[slot], write)
        expert_stores[i] = []
        for n, (src, dst) in enumerate(((d_rows, d_rows_all), (act_e, act_e_all), (d_first, d_first_all))):
            copy = pltpu.make_async_copy(src.at[slot], dst.at[i], store_e_sem.at[n, slot])
            copy.start()
            expert_stores[i].append(copy)
        ers[i] = [
            send(out_a.at[i, slab_of(at_x)], row_x.at[i, 0], ers_sem, 6 * i, (me, at_x)),
            send(out_a.at[i, slab_of(at_d)], row_x.at[i, 1], ers_sem, 6 * i + 1, (me, at_x)),
            send(out_b.at[i, slab_of(at_y)], row_y.at[i, 0], ers_sem, 6 * i + 2, (me, at_y)),
            send(out_b.at[i, slab_of(at_d)], row_y.at[i, 1], ers_sem, 6 * i + 3, (me, at_y)),
        ]

    def add_into(ref, *others):
        total = ref[...].astype(F32)
        for other in others:
            total = total + other[...].astype(F32)
        ref[...] = total.astype(BF)

    def pass_on(i):
        for copy in ers[i][:4]:
            copy.wait_recv()
        add_into(out_a.at[i, slab_of(at_y)], row_x.at[i, 1])
        add_into(out_b.at[i, slab_of(at_x)], row_y.at[i, 1])
        ers[i] += [
            send(out_a.at[i, slab_of(at_y)], row_qa.at[i], ers_sem, 6 * i + 4, (me, at_y)),
            send(out_b.at[i, slab_of(at_x)], row_qb.at[i], ers_sem, 6 * i + 5, (me, at_x)),
        ]

    back_copies = []

    def finish(i):
        ers[i][4].wait_recv()
        ers[i][5].wait_recv()
        for n, (out, near, far) in enumerate(((out_a, row_x, row_qa), (out_b, row_y, row_qb))):
            total = out[i, slab_of(cut)].astype(F32) + near[i, 0].astype(F32) + far[i].astype(F32)
            sorted_back[n, i] = total.astype(BF)
        if (i + 1) % per_group == 0:
            g = i // per_group
            for n in range(2):
                flat = sorted_back[n, pl.ds(g * per_group, per_group)].reshape(per_group * slab, -1)
                placed = mm(unsort[...], flat).astype(BF)
                send_back[n, g] = placed.reshape(n_expert, block, -1)
                returned[n, g, me] = send_back[n, g, me]
                for k in range(1, n_expert):
                    peer = jnp.bitwise_xor(me, k)
                    back_copies.append(
                        send(
                            send_back.at[n, g, peer], returned.at[n, g, me], zr_sem,
                            (n * groups + g) * n_expert + k, (peer, cut),
                        )
                    )

    for i in range(here):
        if i + 1 < here:
            relay(i + 1)
        eag[i][2].wait_recv()
        eag[i][3].wait_recv()
        expert(i)
        if i + 2 < here:
            fetched.append(fetch_expert(i + 2))
        if i == 0:
            for copy in frs[:4]:
                copy.wait_recv()
            add_into(part_a.at[2], ffn_x.at[1])
            add_into(part_b.at[1], ffn_y.at[1])
            frs += [
                send(part_a.at[2], ffn_qa, frs_sem, 4, (me, at_y)),
                send(part_b.at[1], ffn_qb, frs_sem, 5, (me, at_x)),
            ]
        if i >= 1:
            pass_on(i - 1)
        if i >= 2:
            finish(i - 2)
    rows_store = store(rows, rows_in, 13)
    pass_on(here - 1)
    finish(here - 2)
    frs[4].wait_recv()
    frs[5].wait_recv()
    sums[0] = sums[0] + ffn_x[0].astype(F32) + ffn_qa[...].astype(F32)
    sums[1] = sums[1] + ffn_y[0].astype(F32) + ffn_qb[...].astype(F32)
    finish(here - 1)
    for copy in back_copies:
        copy.wait_recv()
    for copy in z_copies + ag + frs + back_copies:
        copy.wait_send()
    for i in range(here):
        for copy in eag[i] + ers[i]:
            copy.wait_send()
    for which in (2, 3):
        for copy in ffn_stores[which]:
            copy.wait()
    for i in (here - 2, here - 1):
        for copy in expert_stores[i]:
            copy.wait()
    second_store.wait()
    rows_store.wait()


def middle(slots, second, grad_all, grad_rows, w_in, w_out, small, sort, unsort, e_in, e_out, n_expert, n_cuts):
    groups, _, block, width = slots.shape
    tokens = second.shape[0]
    here, _, hidden = e_in.shape
    ffn = w_in.shape[1]
    slab = n_expert * block * groups // here
    rows = n_cuts * slab
    any_spec, vmem_spec = pl.BlockSpec(memory_space=pl.ANY), pl.BlockSpec(memory_space=pltpu.VMEM)
    shape = jax.ShapeDtypeStruct
    dma = pltpu.SemaphoreType.DMA
    flops = 8 * (n_cuts * tokens * ffn + here * rows * hidden) * width
    return pl.pallas_call(
        functools.partial(middle_kernel, (n_expert, groups, here, slab)),
        name="middle",
        out_shape=(
            shape((2, tokens, width), F32), shape((2, groups, n_expert, block, width), BF),
            shape((n_cuts, tokens, width), BF), shape((n_cuts, tokens, ffn), BF),
            shape((n_cuts, tokens, ffn), BF), shape((n_cuts, tokens, width), BF),
            shape((here, rows, width), BF), shape((here, rows, width), BF),
            shape((here, rows, hidden), BF), shape((here, rows, hidden), BF),
        ),
        in_specs=[vmem_spec] + [any_spec] * 5 + [vmem_spec] * 3 + [any_spec] * 2,
        out_specs=(vmem_spec,) * 2 + (any_spec,) * 8,
        scratch_shapes=[
            pltpu.VMEM((n_cuts, tokens, width), BF), pltpu.VMEM((n_cuts, tokens, width), BF),
            pltpu.VMEM((width, ffn), BF), pltpu.VMEM((ffn, width), BF),
            pltpu.VMEM((2, tokens, ffn), BF), pltpu.VMEM((2, tokens, ffn), BF), pltpu.VMEM((2, tokens, width), BF),
            pltpu.VMEM((n_cuts, tokens, width), BF), pltpu.VMEM((n_cuts, tokens, width), BF),
            pltpu.VMEM((2, tokens, width), BF), pltpu.VMEM((2, tokens, width), BF),
            pltpu.VMEM((tokens, width), BF), pltpu.VMEM((tokens, width), BF),
            pltpu.VMEM((groups, n_expert, block, width), BF), pltpu.VMEM((here, rows, width), BF),
            pltpu.VMEM((2, rows, width), BF), pltpu.VMEM((2, rows, width), BF),
            pltpu.VMEM((2, rows, hidden), BF), pltpu.VMEM((2, rows, hidden), BF),
            pltpu.VMEM((2, width, hidden), BF), pltpu.VMEM((2, hidden, width), BF),
            pltpu.VMEM((here, rows, width), BF), pltpu.VMEM((here, rows, width), BF),
            pltpu.VMEM((here, 2, slab, width), BF), pltpu.VMEM((here, 2, slab, width), BF),
            pltpu.VMEM((here, slab, width), BF), pltpu.VMEM((here, slab, width), BF),
            pltpu.VMEM((2, here, slab, width), BF), pltpu.VMEM((2, groups, n_expert, block, width), BF),
            dma((4,)), dma((3, 2)), dma((14,)), dma((3, 2)),
            dma((2, groups * n_expert)), dma((2, 4)), dma((2, 4 * here)), dma((2, 6)), dma((2, 6 * here)),
            dma((2, 2 * groups * n_expert)),
        ],
        compiler_params=pltpu.CompilerParams(
            collective_id=1, has_side_effects=True, vmem_limit_bytes=67_000_000
        ),
        cost_estimate=pl.CostEstimate(flops=flops, bytes_accessed=48 << 20, transcendentals=0),
    )(slots, second, grad_all, grad_rows, w_in, w_out, small, sort, unsort, e_in, e_out)


def shards(
    block_input,
    routes,
    kept_mask,
    w_qkv,
    w_attn_out,
    w_in,
    w_out,
    w_router,
    w_mix,
    gain_attn,
    gain_ffn,
    expert_in,
    expert_out,
    cotangent,
):
    tokens, features = block_input.shape
    n_cuts = lax.axis_size("cuts")
    n_expert = lax.axis_size("expert")
    seq_len = tokens * n_cuts
    scaling = HD ** (-0.5)
    own = features // n_cuts
    heads = own // HD
    experts_all = w_router.shape[1]
    experts_here = expert_in.shape[0]
    capacity = 3 * tokens // (2 * experts_all)

    onehot = (routes[:, None] == jnp.arange(experts_all, dtype=jnp.int32)[None, :]).astype(F32)
    onehot_kept = onehot * kept_mask.astype(F32)[:, None]
    lower_tri = (jnp.arange(tokens)[:, None] >= jnp.arange(tokens)[None, :]).astype(BF)
    running = mm(lower_tri, onehot_kept.astype(BF))
    slot_num = jnp.sum(onehot_kept * running, axis=1) - 1.0
    fused = n_cuts == 4
    groups = 2 if fused else 1
    per_group = experts_here // groups
    block = per_group * capacity
    owner, local = routes // experts_here, routes % experts_here
    start = (local // per_group) * (n_expert * block) + owner * block + local % per_group * capacity
    target = start.astype(F32) + slot_num
    columns = jnp.arange(experts_all * capacity, dtype=jnp.int32).astype(F32)
    placer = ((columns[None, :] == target[:, None]) & (kept_mask[:, None] > 0)).astype(BF)

    def to_owners(rows):
        grid = mm_tn(placer, rows).astype(BF).reshape(groups, n_expert, block, features)
        grid = grid.swapaxes(0, 1).reshape(n_expert, experts_here, capacity, features)
        moved = lax.all_to_all(grid, "expert", split_axis=0, concat_axis=2, tiled=True)
        return lax.all_gather(moved, "cuts", axis=2, tiled=True)[0]

    def to_sources(rows):
        summed = lax.psum_scatter(rows[None].astype(BF), "cuts", scatter_dimension=2, tiled=True)
        moved = lax.all_to_all(summed, "expert", split_axis=2, concat_axis=0, tiled=True)
        return mm(placer, moved.reshape(-1, features))

    gains = gather_cuts(jnp.stack([gain_attn, gain_ffn], axis=1)).astype(F32)
    gain_one, gain_two = gains[:, 0], gains[:, 1]
    inputs = block_input.astype(F32)
    xhat_one, inv_one = norm_parts(inputs)
    normed = gather_cuts((xhat_one * gain_one).astype(BF))
    qkv_here = lax.all_to_all(
        w_qkv.reshape(own, 3, n_cuts, own), "cuts", split_axis=2, concat_axis=0, tiled=True
    ).reshape(features, 3 * own)
    joined = mm(normed, qkv_here).astype(BF)
    split = joined.reshape(seq_len, 3, heads, HD)
    q_heads, k_heads, v_heads = split[:, 0], split[:, 1], split[:, 2]
    spots = jnp.arange(seq_len, dtype=jnp.int32)
    visible = (spots[None, :] <= spots[:, None])[None]

    def masked_scores():
        scores = jnp.einsum("qhd,khd->hqk", q_heads, k_heads, preferred_element_type=F32) * scaling
        return jnp.where(visible, scores, -1e30)

    scores = masked_scores()
    peak = jnp.max(scores, axis=-1, keepdims=True)
    row_exp = jnp.exp(scores - peak)
    total = jnp.sum(row_exp, axis=-1, keepdims=True)
    weights_p = (row_exp / total).astype(BF)
    heads_here = jnp.einsum("hqk,khd->qhd", weights_p, v_heads, preferred_element_type=F32)
    log_norm = peak + jnp.log(total)
    head_out = rows_to_cuts(heads_here.reshape(seq_len, own).astype(BF))
    attn_full = gather_cuts(w_attn_out)
    small_full = gather_cuts(jnp.concatenate([w_router, w_mix], axis=1))
    grad_all = gather_cuts(cotangent)
    grad_rows = to_owners(cotangent)
    in_here = columns_to_cuts(w_in)
    hidden = inputs + mm(head_out, attn_full)
    xhat_two, inv_two = norm_parts(hidden)
    second = (xhat_two * gain_two).astype(BF)

    logits = mm(second, small_full)
    router_p = softmax_rows(logits[:, :experts_all])
    mixing = softmax_rows(logits[:, experts_all:])
    gate = jnp.sum(router_p * onehot, axis=1)
    grad = cotangent.astype(F32)
    d_moe = grad * mixing[:, 1:2]

    if fused:
        slots = mm_tn(placer, second).astype(BF).reshape(groups, n_expert, block, features)
        width = n_expert * block
        at = jnp.arange(width, dtype=jnp.int32)
        slab = n_expert * capacity
        goal = at % slab // capacity * block + at // slab * capacity + at % capacity
        sort = (goal[:, None] == at[None, :]).astype(BF)
        small_wide = jnp.pad(small_full, ((0, 0), (0, -small_full.shape[1] % 128)))
        sums, returned, second_all, activ_low, d_up, d_dense_all, rows_in, d_rows, expert_low, d_first = middle(
            slots, second, grad_all.reshape(n_cuts, tokens, features), grad_rows, in_here, w_out, small_wide,
            sort, sort.T, expert_in, expert_out, n_expert, n_cuts,
        )
        dense, d_second_ffn = sums[0], sums[1]
        second_all, activ_low, d_up, d_dense_all = (
            v.reshape(seq_len, -1) for v in (second_all, activ_low, d_up, d_dense_all)
        )
        g_out = mm_tn(activ_low, d_dense_all)
        g_in = mm_tn(second_all, d_up)
        g_expert_out = jnp.einsum("erh,erd->ehd", expert_low, d_rows, preferred_element_type=F32)
        g_expert_in = jnp.einsum("erd,erh->edh", rows_in, d_first, preferred_element_type=F32)
        picked = mm(placer, returned[0].reshape(-1, features))
        d_picked_in = mm(placer, returned[1].reshape(-1, features))
    else:
        rows_in = to_owners(second)
        row_logits = jnp.einsum("erd,dk->erk", rows_in, small_full, preferred_element_type=F32)
        ids = lax.axis_index("expert") * experts_here + jnp.arange(experts_here, dtype=jnp.int32)
        is_here = (jnp.arange(experts_all, dtype=jnp.int32)[None, :] == ids[:, None]).astype(F32)
        row_gate = jnp.sum(
            softmax_rows(row_logits[:, :, :experts_all]) * is_here[:, None, :], axis=2, keepdims=True
        )
        row_mixing = softmax_rows(row_logits[:, :, experts_all:])[:, :, 1:2]
        d_rows = (grad_rows.astype(F32) * row_mixing * row_gate).astype(BF)

        first = jnp.einsum("erd,edh->erh", rows_in, expert_in, preferred_element_type=F32)
        expert_act, expert_pull = jax.vjp(jax.nn.gelu, first)
        expert_low = expert_act.astype(BF)
        partial_out = jnp.einsum("erh,ehd->erd", expert_low, expert_out, preferred_element_type=F32)
        picked = to_sources(partial_out)

        second_all = gather_cuts(second)
        mixing_all = softmax_rows(mm(second_all, small_full[:, experts_all:]))
        d_dense_all = (grad_all.astype(F32) * mixing_all[:, 0:1]).astype(BF)
        up_proj = mm(second_all, in_here)
        activ, gelu_pull = jax.vjp(jax.nn.gelu, up_proj)
        activ_low = activ.astype(BF)
        dense = scatter_cuts(mm(activ_low, w_out)).astype(F32)
        d_activ = mm_nt(d_dense_all, w_out)
        g_out = mm_tn(activ_low, d_dense_all)
        d_up = gelu_pull(d_activ)[0].astype(BF)
        g_in = mm_tn(second_all, d_up)
        d_second_ffn = scatter_cuts(mm_nt(d_up, in_here)).astype(F32)

        d_expert_act = jnp.einsum("erd,ehd->erh", d_rows, expert_out, preferred_element_type=F32)
        d_first = expert_pull(d_expert_act)[0].astype(BF)
        d_rows_in = jnp.einsum("erh,edh->erd", d_first, expert_in, preferred_element_type=F32)
        g_expert_out = jnp.einsum("erh,erd->ehd", expert_low, d_rows, preferred_element_type=F32)
        g_expert_in = jnp.einsum("erd,erh->edh", rows_in, d_first, preferred_element_type=F32)
        d_picked_in = to_sources(d_rows_in)

    moe_val = gate[:, None] * picked
    block_out = (hidden + mixing[:, 0:1] * dense + mixing[:, 1:2] * moe_val).astype(BF)
    d_mixing = jnp.stack([jnp.sum(grad * dense, axis=1), jnp.sum(grad * moe_val, axis=1)], axis=1)
    d_gate = jnp.sum(d_moe * picked, axis=1)
    d_router = router_p * (onehot - gate[:, None]) * d_gate[:, None]
    d_mix = mixing * (d_mixing - jnp.sum(mixing * d_mixing, axis=1, keepdims=True))
    d_small = jnp.concatenate([d_router, d_mix], axis=1).astype(BF)
    g_small = mm_tn(d_small, second)
    d_second = d_second_ffn + mm_nt(d_small, small_full) + d_picked_in
    d_hidden_norm, g_gain_two = norm_back(d_second, xhat_two, inv_two, gain_two)
    d_hidden = grad + d_hidden_norm
    d_attn = d_hidden.astype(BF)
    g_attn_out = mm_tn(head_out, d_attn)
    d_heads = columns_to_cuts(mm_nt(d_attn, attn_full).astype(BF)).reshape(seq_len, heads, HD)

    soft_p = jnp.exp(masked_scores() - log_norm)
    d_soft = jnp.einsum("qhd,khd->hqk", d_heads, v_heads, preferred_element_type=F32)
    delta = jnp.sum(soft_p * d_soft, axis=-1, keepdims=True)
    d_scores = (soft_p * (d_soft - delta)).astype(BF)
    d_query = jnp.einsum("hqk,khd->qhd", d_scores, k_heads, preferred_element_type=F32) * scaling
    d_keys = jnp.einsum("hqk,qhd->khd", d_scores, q_heads, preferred_element_type=F32) * scaling
    d_values = jnp.einsum("hqk,qhd->khd", soft_p.astype(BF), d_heads, preferred_element_type=F32)
    d_joined = jnp.stack([d_query, d_keys, d_values], axis=1).reshape(seq_len, 3 * own).astype(BF)
    g_qkv = mm_tn(normed, d_joined)
    d_normed = scatter_cuts(mm_nt(d_joined, qkv_here)).astype(F32)
    d_input_norm, g_gain_one = norm_back(d_normed, xhat_one, inv_one, gain_one)
    d_block_input = d_hidden + d_input_norm

    def over_experts(part):
        return lax.psum_scatter(part.astype(BF), "expert", scatter_dimension=0, tiled=True)

    s_in = rows_to_cuts(over_experts(g_in)).astype(F32)
    s_out = over_experts(g_out)
    swap = [
        ((flat % n_expert) * n_cuts + flat // n_expert, flat) for flat in range(n_expert * n_cuts)
    ]
    s_out = lax.ppermute(s_out, ("expert", "cuts"), swap).astype(F32)
    s_qkv = over_experts(g_qkv)
    deep = s_qkv.shape[0]
    s_qkv = lax.all_to_all(
        s_qkv.reshape(deep, 3, 1, own), "cuts", split_axis=0, concat_axis=2, tiled=True
    )
    s_qkv = s_qkv.reshape(-1, 3 * features).astype(F32)
    s_attn_out = scatter_cuts(over_experts(g_attn_out)).astype(F32)
    tiny = jnp.concatenate([g_small, g_gain_one[None, :], g_gain_two[None, :]], axis=0)
    tiny = jnp.pad(tiny, ((0, -tiny.shape[0] % 8), (0, 0)))
    tiny = sum_small(tiny, n_expert, n_cuts)
    width = features // (n_expert * n_cuts)
    s_tiny = lax.dynamic_slice_in_dim(tiny, lax.axis_index("cuts") * width, width, axis=1)
    return (
        block_out,
        d_block_input,
        s_qkv,
        s_attn_out,
        s_in,
        s_out,
        s_tiny[:experts_all].T,
        s_tiny[experts_all : experts_all + 2].T,
        s_tiny[experts_all + 2],
        s_tiny[experts_all + 3],
        g_expert_in,
        g_expert_out,
    )


def solution(mesh):
    both = ("expert", "cuts")
    placed = (
        P(both, None),
        P(both),
        P(both),
        P("cuts", None),
        P("cuts", None),
        P("cuts", None),
        P("cuts", None),
        P("cuts", None),
        P("cuts", None),
        P("cuts"),
        P("cuts"),
        P("expert", None, "cuts"),
        P("expert", "cuts", None),
        P(both, None),
    )
    results = (
        P(both, None),
        P(both, None),
        P(both, None),
        P(both, None),
        P(both, None),
        P(both, None),
        P(both, None),
        P(both, None),
        P(both),
        P(both),
        P("expert", None, "cuts"),
        P("expert", "cuts", None),
    )
    return jax.shard_map(
        shards, mesh=mesh, in_specs=placed, out_specs=results, check_vma=False
    )
```

```python
import functools
import math

import jax
import jax.numpy as jnp
from jax import lax
from jax.experimental import pallas as pl
from jax.experimental.pallas import tpu as pltpu
from jax.sharding import PartitionSpec as P

HD = 64
BF = jnp.bfloat16
F32 = jnp.float32
MESH = pl.DeviceIdType.MESH


def norm_parts(values):
    center = values - jnp.mean(values, axis=-1, keepdims=True)
    spread = jnp.mean(center * center, axis=-1, keepdims=True)
    inv = lax.rsqrt(spread + 1e-05)
    return center * inv, inv


def norm_back(grad, xhat, inv, gain):
    q = grad * gain
    mean_q = jnp.mean(q, axis=-1, keepdims=True)
    mean_qx = jnp.mean(q * xhat, axis=-1, keepdims=True)
    return (q - mean_q - xhat * mean_qx) * inv, jnp.sum(grad * xhat, axis=0)


def mm(left, right):
    return jnp.dot(left, right, preferred_element_type=F32)


def mm_nt(left, right):
    return lax.dot_general(left, right, (((1,), (1,)), ((), ())), preferred_element_type=F32)


def mm_tn(left, right):
    return lax.dot_general(left, right, (((0,), (0,)), ((), ())), preferred_element_type=F32)


def softmax_rows(logits):
    shifted = logits - jnp.max(logits, axis=-1, keepdims=True)
    row_exp = jnp.exp(shifted)
    return row_exp / jnp.sum(row_exp, axis=-1, keepdims=True)


def gather_cuts(rows):
    return lax.all_gather(rows, "cuts", axis=0, tiled=True)


def scatter_cuts(rows):
    return lax.psum_scatter(rows.astype(BF), "cuts", scatter_dimension=0, tiled=True)


def columns_to_cuts(rows):
    return lax.all_to_all(rows, "cuts", split_axis=1, concat_axis=0, tiled=True)


def rows_to_cuts(rows):
    return lax.all_to_all(rows, "cuts", split_axis=0, concat_axis=1, tiled=True)


def ring_mod(index, count):
    return lax.rem(index, count)


def small_kernel(n_expert, n_cuts, src, out, by_expert, mine, by_cuts, send_a, recv_a, send_b, recv_b):
    me, cut = lax.axis_index("expert"), lax.axis_index("cuts")
    width = out.shape[1]
    barrier = pltpu.get_barrier_semaphore()
    for step in range(1, n_expert):
        peer = ring_mod(me + step, n_expert)
        pl.semaphore_signal(barrier, inc=1, device_id=(peer, cut), device_id_type=MESH)
    for step in range(1, n_cuts):
        peer = ring_mod(cut + step, n_cuts)
        pl.semaphore_signal(barrier, inc=1, device_id=(me, peer), device_id_type=MESH)
    pl.semaphore_wait(barrier, n_expert + n_cuts - 2)

    def part(owner):
        return src.at[:, pl.ds(pl.multiple_of(owner * width, 128), width)]

    copies = []
    for step in range(1, n_expert):
        peer = ring_mod(me + step, n_expert)
        copies.append(
            pltpu.make_async_remote_copy(
                src_ref=part(peer),
                dst_ref=by_expert.at[step],
                send_sem=send_a.at[step],
                recv_sem=recv_a.at[step],
                device_id=(peer, cut),
                device_id_type=MESH,
            )
        )
        copies[-1].start()
    total = src[:, pl.ds(pl.multiple_of(me * width, 128), width)]
    for step in range(1, n_expert):
        copies[step - 1].wait()
        total = total + by_expert[step]
    mine[...] = total
    copies = []
    for step in range(1, n_cuts):
        peer = ring_mod(cut + step, n_cuts)
        copies.append(
            pltpu.make_async_remote_copy(
                src_ref=mine,
                dst_ref=by_cuts.at[step],
                send_sem=send_b.at[step],
                recv_sem=recv_b.at[step],
                device_id=(me, peer),
                device_id_type=MESH,
            )
        )
        copies[-1].start()
    for step in range(1, n_cuts):
        copies[step - 1].wait()
        total = total + by_cuts[step]
    out[...] = total


def sum_small(values, n_expert, n_cuts):
    rows, features = values.shape
    width = features // n_expert
    pad = -width % 128
    if pad:
        values = jnp.pad(values.reshape(rows, n_expert, width), ((0, 0), (0, 0), (0, pad)))
        values = values.reshape(rows, n_expert * (width + pad))
    wide = width + pad
    summed = pl.pallas_call(
        functools.partial(small_kernel, n_expert, n_cuts),
        name="sum_small",
        out_shape=jax.ShapeDtypeStruct((rows, wide), F32),
        in_specs=[pl.BlockSpec(memory_space=pltpu.VMEM)],
        out_specs=pl.BlockSpec(memory_space=pltpu.VMEM),
        scratch_shapes=[
            pltpu.VMEM((n_expert, rows, wide), F32),
            pltpu.VMEM((rows, wide), F32),
            pltpu.VMEM((n_cuts, rows, wide), F32),
            pltpu.SemaphoreType.DMA((n_expert,)),
            pltpu.SemaphoreType.DMA((n_expert,)),
            pltpu.SemaphoreType.DMA((n_cuts,)),
            pltpu.SemaphoreType.DMA((n_cuts,)),
        ],
        compiler_params=pltpu.CompilerParams(collective_id=0, has_side_effects=True),
    )(values)
    return summed[:, :width]


def dot_nt(left, right):
    return lax.dot_general(left, right, (((1,), (1,)), ((), ())), preferred_element_type=F32)


def tile_of(step, size):
    return pl.ds(pl.multiple_of(step * size, size), size)


def lane_softmax(logits, low, high):
    lane = lax.broadcasted_iota(jnp.int32, logits.shape, 1)
    inside = (lane >= low) & (lane < high)
    kept = jnp.where(inside, logits, -1e30)
    powers = jnp.exp(kept - jnp.max(kept, axis=1, keepdims=True))
    powers = jnp.where(inside, powers, 0.0)
    return powers / jnp.sum(powers, axis=1, keepdims=True), lane


def mlp_both(rows, d_rows, w_up, w_down, act, d_up, write):
    root, cubic = math.sqrt(2.0 / math.pi), 0.044715

    @pl.loop(0, act.shape[1] // 256)
    def _(step):
        span = tile_of(step, 256)
        up = mm(rows[...], w_up[:, span])
        d_act = dot_nt(d_rows[...], w_down[span, :])
        square = up * up
        bent = jnp.tanh(root * up * (1.0 + cubic * square))
        half = 0.5 * (1.0 + bent)
        act[:, span] = (up * half).astype(BF)
        slope = half + 0.5 * up * (1.0 - bent * bent) * (root + 3.0 * root * cubic * square)
        d_up[:, span] = (d_act * slope).astype(BF)

    @pl.loop(0, w_up.shape[0] // 256)
    def _(step):
        span = tile_of(step, 256)
        write(span, mm(act[...], w_down[:, span]), dot_nt(d_up[...], w_up[span, :]))


def middle_kernel(
    sizes, slots, second, grad_all, grad_rows, w_in, w_out, small, sort, unsort, e_in, e_out,
    sums, returned, second_all, act_all, d_up_all, d_dense_all, rows_in, d_rows_all, act_e_all, d_first_all,
    sec, grd, win, wout, act, d_up, d_dense, part_a, part_b, ffn_x, ffn_y, ffn_qa, ffn_qb,
    zbuf, rows, g_rows, d_rows, act_e, d_first, wi_e, wo_e, out_a, out_b, row_x, row_y, row_qa, row_qb, sorted_back, send_back,
    load_sem, weight_sem, store_sem, store_e_sem, z_sem, ag_sem, eag_sem, frs_sem, ers_sem, zr_sem,
):
    n_expert, groups, here, slab = sizes
    me, cut = lax.axis_index("expert"), lax.axis_index("cuts")
    at_x, at_y, at_d = (jnp.bitwise_xor(cut, k) for k in (1, 2, 3))
    block = zbuf.shape[2]
    per_group = here // groups
    experts_all = n_expert * here

    def load(src, dst, index):
        copy = pltpu.make_async_copy(src, dst, load_sem.at[index])
        copy.start()
        return copy

    def send(src, dst, sems, index, peer):
        copy = pltpu.make_async_remote_copy(
            src_ref=src, dst_ref=dst, send_sem=sems.at[0, index], recv_sem=sems.at[1, index],
            device_id=peer, device_id_type=MESH,
        )
        copy.start()
        return copy

    loads = [
        load(second, sec.at[cut], 0), load(w_in, win, 1), load(w_out, wout, 2), load(grad_all, grd, 3),
    ]

    def fetch_expert(i):
        slot = i % 2
        copies = [
            pltpu.make_async_copy(e_in.at[i], wi_e.at[slot], weight_sem.at[0, slot]),
            pltpu.make_async_copy(e_out.at[i], wo_e.at[slot], weight_sem.at[1, slot]),
            pltpu.make_async_copy(grad_rows.at[i], g_rows.at[slot], weight_sem.at[2, slot]),
        ]
        for copy in copies:
            copy.start()
        return copies

    fetched = [fetch_expert(0), fetch_expert(1)]
    barrier = pltpu.get_barrier_semaphore()
    for k in range(1, n_expert):
        pl.semaphore_signal(barrier, inc=1, device_id=(jnp.bitwise_xor(me, k), cut), device_id_type=MESH)
    for peer in (at_x, at_y):
        pl.semaphore_signal(barrier, inc=1, device_id=(me, peer), device_id_type=MESH)
    pl.semaphore_wait(barrier, n_expert + 1)

    z_copies = []
    for g in range(groups):
        for k in range(1, n_expert):
            peer = jnp.bitwise_xor(me, k)
            z_copies.append(send(slots.at[g, peer], zbuf.at[g, me], z_sem, g * n_expert + k, (peer, cut)))
    loads[0].wait()
    ag = [
        send(sec.at[cut], sec.at[cut], ag_sem, 0, (me, at_x)),
        send(sec.at[cut], sec.at[cut], ag_sem, 1, (me, at_y)),
    ]
    for g in range(groups):
        zbuf[g, me] = slots[g, me]
    stores = []

    def store(src, dst, index):
        copy = pltpu.make_async_copy(src, dst, store_sem.at[index])
        copy.start()
        return copy

    ffn_stores = {}

    def ffn_block(which, owner):
        slot = which % 2
        if which >= 2:
            for copy in ffn_stores[which - 2]:
                copy.wait()
        mixing, lane = lane_softmax(mm(sec[owner], small[...]), experts_all, experts_all + 2)
        first_mix = jnp.sum(jnp.where(lane == experts_all, mixing, 0.0), axis=1, keepdims=True)
        d_dense[slot] = (grd[owner].astype(F32) * first_mix).astype(BF)

        def write(span, out, d_row):
            if which == 0:
                sums[0, :, span] = out
                sums[1, :, span] = d_row
            else:
                part_a[which, :, span] = out.astype(BF)
                part_b[which, :, span] = d_row.astype(BF)

        mlp_both(sec.at[owner], d_dense.at[slot], win, wout, act.at[slot], d_up.at[slot], write)
        ffn_stores[which] = [
            store(act.at[slot], act_all.at[owner], 3 * which),
            store(d_up.at[slot], d_up_all.at[owner], 3 * which + 1),
            store(d_dense.at[slot], d_dense_all.at[owner], 3 * which + 2),
        ]

    for copy in loads[1:]:
        copy.wait()
    ffn_block(0, cut)
    half = sec.shape[1] // 2
    ag[0].wait_recv()
    ag.append(send(sec.at[at_x, pl.ds(0, half)], sec.at[at_x, pl.ds(0, half)], ag_sem, 2, (me, at_y)))
    ag[1].wait_recv()
    ag.append(send(sec.at[at_y, pl.ds(half, half)], sec.at[at_y, pl.ds(half, half)], ag_sem, 3, (me, at_x)))
    ffn_block(1, at_x)

    def slab_of(owner):
        return pl.ds(pl.multiple_of(owner * slab, slab), slab)

    eag = {}
    for g in range(groups):
        for k in range(1, n_expert):
            z_copies[g * (n_expert - 1) + k - 1].wait_recv()
        flat = zbuf[g].reshape(n_expert * block, zbuf.shape[3])
        for j in range(per_group):
            i = g * per_group + j
            rows[i, slab_of(cut)] = mm(sort[pl.ds(j * slab, slab), :], flat).astype(BF)
            mine = rows.at[i, slab_of(cut)]
            eag[i] = [
                send(mine, mine, eag_sem, 4 * i, (me, at_x)),
                send(mine, mine, eag_sem, 4 * i + 1, (me, at_y)),
            ]
    ffn_block(2, at_y)
    ag[2].wait_recv()
    ag[3].wait_recv()

    def relay(i):
        cut_half = slab // 2
        eag[i][0].wait_recv()
        piece = rows.at[i, pl.ds(pl.multiple_of(at_x * slab, slab), cut_half)]
        eag[i].append(send(piece, piece, eag_sem, 4 * i + 2, (me, at_y)))
        eag[i][1].wait_recv()
        piece = rows.at[i, pl.ds(pl.multiple_of(at_y * slab + cut_half, cut_half), cut_half)]
        eag[i].append(send(piece, piece, eag_sem, 4 * i + 3, (me, at_x)))

    relay(0)
    ffn_block(3, at_d)
    frs = [
        send(part_a.at[1], ffn_x.at[0], frs_sem, 0, (me, at_x)),
        send(part_a.at[3], ffn_x.at[1], frs_sem, 1, (me, at_x)),
        send(part_b.at[2], ffn_y.at[0], frs_sem, 2, (me, at_y)),
        send(part_b.at[3], ffn_y.at[1], frs_sem, 3, (me, at_y)),
    ]
    second_store = store(sec, second_all, 12)
    expert_stores = {}
    ers = {}

    def expert(i):
        slot = i % 2
        if i >= 2:
            for copy in expert_stores[i - 2]:
                copy.wait()
        for copy in fetched[i]:
            copy.wait()
        logits = mm(rows[i], small[...])
        router, lane = lane_softmax(logits, 0, experts_all)
        gate = jnp.sum(jnp.where(lane == me * here + i, router, 0.0), axis=1, keepdims=True)
        mixing, lane = lane_softmax(logits, experts_all, experts_all + 2)
        mixing = jnp.sum(jnp.where(lane == experts_all + 1, mixing, 0.0), axis=1, keepdims=True)
        d_rows[slot] = (g_rows[slot].astype(F32) * mixing * gate).astype(BF)

        def write(span, out, d_row):
            out_a[i, :, span] = out.astype(BF)
            out_b[i, :, span] = d_row.astype(BF)

        mlp_both(rows.at[i], d_rows.at[slot], wi_e.at[slot], wo_e.at[slot], act_e.at[slot], d_first.at[slot], write)
        expert_stores[i] = []
        for n, (src, dst) in enumerate(((d_rows, d_rows_all), (act_e, act_e_all), (d_first, d_first_all))):
            copy = pltpu.make_async_copy(src.at[slot], dst.at[i], store_e_sem.at[n, slot])
            copy.start()
            expert_stores[i].append(copy)
        ers[i] = [
            send(out_a.at[i, slab_of(at_x)], row_x.at[i, 0], ers_sem, 6 * i, (me, at_x)),
            send(out_a.at[i, slab_of(at_d)], row_x.at[i, 1], ers_sem, 6 * i + 1, (me, at_x)),
            send(out_b.at[i, slab_of(at_y)], row_y.at[i, 0], ers_sem, 6 * i + 2, (me, at_y)),
            send(out_b.at[i, slab_of(at_d)], row_y.at[i, 1], ers_sem, 6 * i + 3, (me, at_y)),
        ]

    def add_into(ref, *others):
        total = ref[...].astype(F32)
        for other in others:
            total = total + other[...].astype(F32)
        ref[...] = total.astype(BF)

    def pass_on(i):
        for copy in ers[i][:4]:
            copy.wait_recv()
        add_into(out_a.at[i, slab_of(at_y)], row_x.at[i, 1])
        add_into(out_b.at[i, slab_of(at_x)], row_y.at[i, 1])
        ers[i] += [
            send(out_a.at[i, slab_of(at_y)], row_qa.at[i], ers_sem, 6 * i + 4, (me, at_y)),
            send(out_b.at[i, slab_of(at_x)], row_qb.at[i], ers_sem, 6 * i + 5, (me, at_x)),
        ]

    back_copies = []

    def finish(i):
        ers[i][4].wait_recv()
        ers[i][5].wait_recv()
        for n, (out, near, far) in enumerate(((out_a, row_x, row_qa), (out_b, row_y, row_qb))):
            total = out[i, slab_of(cut)].astype(F32) + near[i, 0].astype(F32) + far[i].astype(F32)
            sorted_back[n, i] = total.astype(BF)
        if (i + 1) % per_group == 0:
            g = i // per_group
            for n in range(2):
                flat = sorted_back[n, pl.ds(g * per_group, per_group)].reshape(per_group * slab, -1)
                placed = mm(unsort[...], flat).astype(BF)
                send_back[n, g] = placed.reshape(n_expert, block, -1)
                returned[n, g, me] = send_back[n, g, me]
                for k in range(1, n_expert):
                    peer = jnp.bitwise_xor(me, k)
                    back_copies.append(
                        send(
                            send_back.at[n, g, peer], returned.at[n, g, me], zr_sem,
                            (n * groups + g) * n_expert + k, (peer, cut),
                        )
                    )

    for i in range(here):
        if i + 1 < here:
            relay(i + 1)
        eag[i][2].wait_recv()
        eag[i][3].wait_recv()
        expert(i)
        if i + 2 < here:
            fetched.append(fetch_expert(i + 2))
        if i == 0:
            for copy in frs[:4]:
                copy.wait_recv()
            add_into(part_a.at[2], ffn_x.at[1])
            add_into(part_b.at[1], ffn_y.at[1])
            frs += [
                send(part_a.at[2], ffn_qa, frs_sem, 4, (me, at_y)),
                send(part_b.at[1], ffn_qb, frs_sem, 5, (me, at_x)),
            ]
        if i >= 1:
            pass_on(i - 1)
        if i >= 2:
            finish(i - 2)
    rows_store = store(rows, rows_in, 13)
    pass_on(here - 1)
    finish(here - 2)
    frs[4].wait_recv()
    frs[5].wait_recv()
    sums[0] = sums[0] + ffn_x[0].astype(F32) + ffn_qa[...].astype(F32)
    sums[1] = sums[1] + ffn_y[0].astype(F32) + ffn_qb[...].astype(F32)
    finish(here - 1)
    for copy in back_copies:
        copy.wait_recv()
    for copy in z_copies + ag + frs + back_copies:
        copy.wait_send()
    for i in range(here):
        for copy in eag[i] + ers[i]:
            copy.wait_send()
    for which in (2, 3):
        for copy in ffn_stores[which]:
            copy.wait()
    for i in (here - 2, here - 1):
        for copy in expert_stores[i]:
            copy.wait()
    second_store.wait()
    rows_store.wait()


def middle(slots, second, grad_all, grad_rows, w_in, w_out, small, sort, unsort, e_in, e_out, n_expert, n_cuts):
    groups, _, block, width = slots.shape
    tokens = second.shape[0]
    here, _, hidden = e_in.shape
    ffn = w_in.shape[1]
    slab = n_expert * block * groups // here
    rows = n_cuts * slab
    any_spec, vmem_spec = pl.BlockSpec(memory_space=pl.ANY), pl.BlockSpec(memory_space=pltpu.VMEM)
    shape = jax.ShapeDtypeStruct
    dma = pltpu.SemaphoreType.DMA
    flops = 8 * (n_cuts * tokens * ffn + here * rows * hidden) * width
    return pl.pallas_call(
        functools.partial(middle_kernel, (n_expert, groups, here, slab)),
        name="middle",
        out_shape=(
            shape((2, tokens, width), F32), shape((2, groups, n_expert, block, width), BF),
            shape((n_cuts, tokens, width), BF), shape((n_cuts, tokens, ffn), BF),
            shape((n_cuts, tokens, ffn), BF), shape((n_cuts, tokens, width), BF),
            shape((here, rows, width), BF), shape((here, rows, width), BF),
            shape((here, rows, hidden), BF), shape((here, rows, hidden), BF),
        ),
        in_specs=[vmem_spec] + [any_spec] * 5 + [vmem_spec] * 3 + [any_spec] * 2,
        out_specs=(vmem_spec,) * 2 + (any_spec,) * 8,
        scratch_shapes=[
            pltpu.VMEM((n_cuts, tokens, width), BF), pltpu.VMEM((n_cuts, tokens, width), BF),
            pltpu.VMEM((width, ffn), BF), pltpu.VMEM((ffn, width), BF),
            pltpu.VMEM((2, tokens, ffn), BF), pltpu.VMEM((2, tokens, ffn), BF), pltpu.VMEM((2, tokens, width), BF),
            pltpu.VMEM((n_cuts, tokens, width), BF), pltpu.VMEM((n_cuts, tokens, width), BF),
            pltpu.VMEM((2, tokens, width), BF), pltpu.VMEM((2, tokens, width), BF),
            pltpu.VMEM((tokens, width), BF), pltpu.VMEM((tokens, width), BF),
            pltpu.VMEM((groups, n_expert, block, width), BF), pltpu.VMEM((here, rows, width), BF),
            pltpu.VMEM((2, rows, width), BF), pltpu.VMEM((2, rows, width), BF),
            pltpu.VMEM((2, rows, hidden), BF), pltpu.VMEM((2, rows, hidden), BF),
            pltpu.VMEM((2, width, hidden), BF), pltpu.VMEM((2, hidden, width), BF),
            pltpu.VMEM((here, rows, width), BF), pltpu.VMEM((here, rows, width), BF),
            pltpu.VMEM((here, 2, slab, width), BF), pltpu.VMEM((here, 2, slab, width), BF),
            pltpu.VMEM((here, slab, width), BF), pltpu.VMEM((here, slab, width), BF),
            pltpu.VMEM((2, here, slab, width), BF), pltpu.VMEM((2, groups, n_expert, block, width), BF),
            dma((4,)), dma((3, 2)), dma((14,)), dma((3, 2)),
            dma((2, groups * n_expert)), dma((2, 4)), dma((2, 4 * here)), dma((2, 6)), dma((2, 6 * here)),
            dma((2, 2 * groups * n_expert)),
        ],
        compiler_params=pltpu.CompilerParams(
            collective_id=1, has_side_effects=True, vmem_limit_bytes=67_000_000
        ),
        cost_estimate=pl.CostEstimate(flops=flops, bytes_accessed=48 << 20, transcendentals=0),
    )(slots, second, grad_all, grad_rows, w_in, w_out, small, sort, unsort, e_in, e_out)


def tail_kernel(
    heads, scaling, g_in, g_out, g_attn, d_heads, joined, lse, normed, qkv, source, gain, d_hidden, tiny,
    d_source, o_in, o_out, o_qkv, o_attn, o_tiny, o_gain,
    core_in, own, z_in, a_in, a_z, a_mine, gq, core_q, own_q, z_q, fin_in, fin_q,
    dh, dj, acc_q, acc_k, acc_v, dn, dn_in, norm_v, qkv_v, tiny_e, tiny_m, tiny_c, late, late_e, late_m, late_c,
    load_sem, core_sem, z_sem, cut_sem, te_sem, tc_sem,
):
    me, cut = lax.axis_index("expert"), lax.axis_index("cuts")
    core, level = lax.rem(me, 2), lax.div(me, 2)
    other = 1 - core
    n_cuts, tokens, width = dh.shape
    n_expert = tiny_e.shape[0]
    levels = n_expert // 2
    twin = (jnp.bitwise_xor(me, 1), cut)

    def send(src, dst, sems, index, peer):
        copy = pltpu.make_async_remote_copy(
            src_ref=src, dst_ref=dst, send_sem=sems.at[0, index], recv_sem=sems.at[1, index],
            device_id=peer, device_id_type=MESH,
        )
        copy.start()
        return copy

    def load(src, dst, index):
        copy = pltpu.make_async_copy(src, dst, load_sem.at[index])
        copy.start()
        return copy

    grads = (g_in, g_out, g_attn)
    mine = [load(grads[m].at[:, core], own.at[m], m) for m in range(3)]
    later = [load(normed, norm_v, 3), load(qkv, qkv_v, 4)]
    barrier = pltpu.get_barrier_semaphore()
    for k in range(1, n_expert):
        pl.semaphore_signal(barrier, inc=1, device_id=(jnp.bitwise_xor(me, k), cut), device_id_type=MESH)
    for k in range(1, n_cuts):
        pl.semaphore_signal(barrier, inc=1, device_id=(me, jnp.bitwise_xor(cut, k)), device_id_type=MESH)
    pl.semaphore_wait(barrier, n_expert + n_cuts - 2)

    def columns(index, size):
        return pl.ds(pl.multiple_of(index * size, size), size)

    sent = []

    def to_cuts(src_of, dst_of, base):
        copies = []
        for k in range(1, n_cuts):
            peer = jnp.bitwise_xor(cut, k)
            copies.append(send(src_of(peer), dst_of(k), cut_sem, base + k - 1, (me, peer)))
        sent.extend(copies)
        return copies

    def to_levels(src_of, dst_of, base):
        copies = []
        for k in range(1, levels):
            peer = jnp.bitwise_xor(level, k)
            copies.append(send(src_of(peer), dst_of(k), z_sem, base + k - 1, (2 * peer + core, cut)))
        sent.extend(copies)
        return copies

    def to_experts(src, dst, base):
        copies = []
        for k in range(1, n_expert):
            peer = jnp.bitwise_xor(me, k)
            copies.append(send(src.at[:, columns(peer, 128)], dst.at[k], te_sem, base + k - 1, (peer, cut)))
        sent.extend(copies)
        return copies

    heads_moved = to_cuts(lambda peer: d_heads.at[:, columns(peer, width)], lambda k: dh.at[cut], 0)
    twins = [send(grads[m].at[:, other], core_in.at[m], core_sem, m, twin) for m in range(3)]
    tiny_moved = to_experts(tiny, tiny_e, 0)
    dh[cut] = d_heads[:, columns(cut, width)]
    z_moved = []
    attn_moved = None
    for m in range(3):
        mine[m].wait()
        twins[m].wait_recv()

        @pl.loop(0, levels)
        def _(step):
            own[m, step] = (own[m, step].astype(F32) + core_in[m, step].astype(F32)).astype(BF)

        if m < 2:
            z_moved.append(to_levels(lambda peer: own.at[m, peer], lambda k: z_in.at[m, k - 1], 3 * m))
        else:
            piece = own.shape[2] // n_cuts
            attn_moved = to_cuts(
                lambda peer: own.at[2, :, columns(peer, piece)], lambda k: a_in.at[k - 1], 3
            )

    acc_q[...] = jnp.zeros_like(acc_q)
    acc_k[...] = jnp.zeros_like(acc_k)
    acc_v[...] = jnp.zeros_like(acc_v)
    for copy in heads_moved:
        copy.wait_recv()

    @pl.loop(0, heads)
    def _(head):
        pair, half = lax.div(head, 2), lax.rem(head, 2)
        lane = lax.broadcasted_iota(jnp.int32, (1, 128), 1)
        keep = (lax.div(lane, HD) == half).astype(F32)
        keep_low = keep.astype(BF)
        cols = columns(pair, 128)
        k_cols = pl.ds(pl.multiple_of(width + pair * 128, 128), 128)
        v_cols = pl.ds(pl.multiple_of(2 * width + pair * 128, 128), 128)
        for i in range(n_cuts):
            reach = (i + 1) * tokens
            here = pl.ds(i * tokens, tokens)
            query = joined[here, cols] * keep_low
            d_out = dh[i, :, cols] * keep_low
            keys = joined[pl.ds(0, reach), k_cols]
            scores = mm_nt(keys, query) * scaling - lse[head, :, here]
            key_at = lax.broadcasted_iota(jnp.int32, scores.shape, 0)
            query_at = lax.broadcasted_iota(jnp.int32, scores.shape, 1) + i * tokens
            soft = jnp.exp(jnp.where(key_at <= query_at, scores, -1e30))
            d_soft = mm_nt(joined[pl.ds(0, reach), v_cols], d_out)
            delta = jnp.sum(soft * d_soft, axis=0, keepdims=True)
            d_scores = (soft * (d_soft - delta)).astype(BF)
            acc_v[pl.ds(0, reach), cols] += mm(soft.astype(BF), d_out)
            acc_k[pl.ds(0, reach), cols] += mm(d_scores, query)
            acc_q[here, cols] += mm_tn(d_scores, keys) * keep

    dj[:, pl.ds(0, width)] = (acc_q[...] * scaling).astype(BF)
    dj[:, pl.ds(width, width)] = (acc_k[...] * scaling).astype(BF)
    dj[:, pl.ds(2 * width, width)] = acc_v[...].astype(BF)
    for copy in later:
        copy.wait()
    dn_moved = []
    for k in (3, 1, 2):
        peer = jnp.bitwise_xor(cut, k)
        dn[k] = mm_nt(dj[columns(peer, tokens), :], qkv_v[...]).astype(BF)
        dn_moved.append(send(dn.at[k], dn_in.at[k - 1], cut_sem, 6 + k - 1, (me, peer)))
    sent.extend(dn_moved)

    @pl.loop(0, levels)
    def _(step):
        part = mm_tn(norm_v[:, columns(step, 256)], dj[...]).astype(BF)
        gq[step] = part.reshape(2, 128, part.shape[1])

    twins.append(send(gq.at[:, other], core_q, core_sem, 3, twin))
    d_normed = mm_nt(dj[columns(cut, tokens), :], qkv_v[...])

    for copy in attn_moved:
        copy.wait_recv()
    total = own[2, :, columns(cut, piece)].astype(F32)
    for k in range(1, n_cuts):
        total = total + a_in[k - 1].astype(F32)
    a_mine[...] = total.astype(BF)
    attn_z = to_levels(lambda peer: a_mine.at[peer], lambda k: a_z.at[k - 1], 9)

    twins[3].wait_recv()

    @pl.loop(0, levels)
    def _(step):
        own_q[step] = (gq[step, core].astype(F32) + core_q[step].astype(F32)).astype(BF)

    qkv_z = to_levels(lambda peer: own_q.at[peer], lambda k: z_q.at[k - 1], 6)

    for copy in tiny_moved:
        copy.wait_recv()
    small = tiny[:, columns(me, 128)]
    for k in range(1, n_expert):
        small = small + tiny_e[k]
    tiny_m[...] = small

    def tiny_cuts(src, dst, base):
        copies = []
        for k in range(1, n_cuts):
            copies.append(send(src, dst.at[k], tc_sem, base + k - 1, (me, jnp.bitwise_xor(cut, k))))
        sent.extend(copies)
        return copies

    tiny_last = tiny_cuts(tiny_m, tiny_c, 0)

    for copy in z_moved[0]:
        copy.wait_recv()
    total = own[0, level].astype(F32)
    for k in range(1, levels):
        total = total + z_in[0, k - 1].astype(F32)
    fin_in[...] = total.astype(BF).reshape(fin_in.shape)
    in_last = to_cuts(lambda peer: fin_in.at[peer], lambda k: o_in.at[cut], 9)
    o_in[cut] = fin_in[cut]

    for copy in dn_moved:
        copy.wait_recv()
    for k in range(1, n_cuts):
        d_normed = d_normed + dn_in[k - 1].astype(F32)
    xhat, inv = norm_parts(source[...].astype(F32))
    q = d_normed * gain[...]
    mean_q = jnp.mean(q, axis=-1, keepdims=True)
    mean_qx = jnp.mean(q * xhat, axis=-1, keepdims=True)
    d_source[...] = d_hidden[...] + (q - mean_q - xhat * mean_qx) * inv
    late[...] = jnp.broadcast_to(jnp.sum(d_normed * xhat, axis=0, keepdims=True), late.shape)
    late_moved = to_experts(late, late_e, n_expert - 1)

    for copy in tiny_last:
        copy.wait_recv()
    for k in range(1, n_cuts):
        small = small + tiny_c[k]
    o_tiny[...] = small

    for copy in z_moved[1]:
        copy.wait_recv()
    total = own[1, level].astype(F32)
    for k in range(1, levels):
        total = total + z_in[1, k - 1].astype(F32)
    o_out[...] = total.astype(BF)

    for copy in late_moved:
        copy.wait_recv()
    small = late[:, columns(me, 128)]
    for k in range(1, n_expert):
        small = small + late_e[k]
    late_m[...] = small
    late_last = tiny_cuts(late_m, late_c, n_cuts - 1)

    for copy in attn_z:
        copy.wait_recv()
    total = a_mine[level].astype(F32)
    for k in range(1, levels):
        total = total + a_z[k - 1].astype(F32)
    o_attn[...] = total

    for copy in qkv_z:
        copy.wait_recv()
    total = own_q[level].astype(F32)
    for k in range(1, levels):
        total = total + z_q[k - 1].astype(F32)
    fin_q[...] = total.astype(BF).reshape(fin_q.shape)
    qkv_last = to_cuts(lambda peer: fin_q.at[peer], lambda k: o_qkv.at[cut], 12)
    o_qkv[cut] = fin_q[cut]

    for copy in late_last:
        copy.wait_recv()
    for k in range(1, n_cuts):
        small = small + late_c[k]
    o_gain[...] = small
    for copy in in_last + qkv_last:
        copy.wait_recv()
    for copy in sent + twins:
        copy.wait_send()


def tail(g_in, g_out, g_attn, d_heads, joined, lse, normed, qkv, source, gain, d_hidden, tiny, n_expert, n_cuts):
    tokens, features = d_heads.shape
    heads, seq_len = lse.shape
    levels, own = n_expert // 2, features // n_cuts
    deep = features // n_expert
    piece, wide = deep // n_cuts, 3 * own
    any_spec, vmem_spec = pl.BlockSpec(memory_space=pl.ANY), pl.BlockSpec(memory_space=pltpu.VMEM)
    shape, vmem, dma = jax.ShapeDtypeStruct, pltpu.VMEM, pltpu.SemaphoreType.DMA
    rows = tiny.shape[0]
    grid = (levels, 2, deep, features)
    return pl.pallas_call(
        functools.partial(tail_kernel, heads, HD ** (-0.5)),
        name="tail",
        out_shape=(
            shape((tokens, features), F32), shape((n_cuts, piece, features), BF), shape((deep, features), BF),
            shape((n_cuts, piece, wide), BF), shape((piece, features), F32), shape((rows, 128), F32), shape((8, 128), F32),
        ),
        in_specs=[any_spec] * 3 + [vmem_spec] * 3 + [any_spec] * 2 + [vmem_spec] * 4,
        out_specs=(vmem_spec,) * 7,
        scratch_shapes=[
            vmem((3, levels, deep, features), BF), vmem((3, levels, deep, features), BF),
            vmem((2, levels - 1, deep, features), BF), vmem((n_cuts - 1, levels, piece, features), BF),
            vmem((levels - 1, piece, features), BF), vmem((levels, piece, features), BF),
            vmem((levels, 2, deep, wide), BF), vmem((levels, deep, wide), BF), vmem((levels, deep, wide), BF),
            vmem((levels - 1, deep, wide), BF), vmem((n_cuts, piece, features), BF), vmem((n_cuts, piece, wide), BF),
            vmem((n_cuts, tokens, own), BF), vmem((seq_len, wide), BF),
            vmem((seq_len, own), F32), vmem((seq_len, own), F32), vmem((seq_len, own), F32),
            vmem((n_cuts, tokens, features), BF), vmem((n_cuts - 1, tokens, features), BF),
            vmem((seq_len, features), BF), vmem((features, wide), BF),
            vmem((n_expert, rows, 128), F32), vmem((rows, 128), F32), vmem((n_cuts, rows, 128), F32),
            vmem((8, features), F32), vmem((n_expert, 8, 128), F32), vmem((8, 128), F32), vmem((n_cuts, 8, 128), F32),
            dma((5,)), dma((2, 4)), dma((2, 4 * (levels - 1))), dma((2, 5 * (n_cuts - 1))),
            dma((2, 2 * (n_expert - 1))), dma((2, 2 * (n_cuts - 1))),
        ],
        compiler_params=pltpu.CompilerParams(
            collective_id=2, has_side_effects=True, vmem_limit_bytes=48 << 20
        ),
        cost_estimate=pl.CostEstimate(flops=20_000_000_000, bytes_accessed=24 << 20, transcendentals=0),
    )(
        g_in.reshape(grid), g_out.reshape(grid), g_attn.reshape(grid), d_heads, joined, lse.reshape(heads, 1, seq_len),
        normed, qkv, source, gain, d_hidden, tiny,
    )


def shards(
    block_input,
    routes,
    kept_mask,
    w_qkv,
    w_attn_out,
    w_in,
    w_out,
    w_router,
    w_mix,
    gain_attn,
    gain_ffn,
    expert_in,
    expert_out,
    cotangent,
):
    tokens, features = block_input.shape
    n_cuts = lax.axis_size("cuts")
    n_expert = lax.axis_size("expert")
    seq_len = tokens * n_cuts
    scaling = HD ** (-0.5)
    own = features // n_cuts
    heads = own // HD
    experts_all = w_router.shape[1]
    experts_here = expert_in.shape[0]
    capacity = 3 * tokens // (2 * experts_all)

    onehot = (routes[:, None] == jnp.arange(experts_all, dtype=jnp.int32)[None, :]).astype(F32)
    onehot_kept = onehot * kept_mask.astype(F32)[:, None]
    lower_tri = (jnp.arange(tokens)[:, None] >= jnp.arange(tokens)[None, :]).astype(BF)
    running = mm(lower_tri, onehot_kept.astype(BF))
    slot_num = jnp.sum(onehot_kept * running, axis=1) - 1.0
    fused = n_cuts == 4
    groups = 2 if fused else 1
    per_group = experts_here // groups
    block = per_group * capacity
    owner, local = routes // experts_here, routes % experts_here
    start = (local // per_group) * (n_expert * block) + owner * block + local % per_group * capacity
    target = start.astype(F32) + slot_num
    columns = jnp.arange(experts_all * capacity, dtype=jnp.int32).astype(F32)
    placer = ((columns[None, :] == target[:, None]) & (kept_mask[:, None] > 0)).astype(BF)

    def to_owners(rows):
        grid = mm_tn(placer, rows).astype(BF).reshape(groups, n_expert, block, features)
        grid = grid.swapaxes(0, 1).reshape(n_expert, experts_here, capacity, features)
        moved = lax.all_to_all(grid, "expert", split_axis=0, concat_axis=2, tiled=True)
        return lax.all_gather(moved, "cuts", axis=2, tiled=True)[0]

    def to_sources(rows):
        summed = lax.psum_scatter(rows[None].astype(BF), "cuts", scatter_dimension=2, tiled=True)
        moved = lax.all_to_all(summed, "expert", split_axis=2, concat_axis=0, tiled=True)
        return mm(placer, moved.reshape(-1, features))

    gains = gather_cuts(jnp.stack([gain_attn, gain_ffn], axis=1)).astype(F32)
    gain_one, gain_two = gains[:, 0], gains[:, 1]
    inputs = block_input.astype(F32)
    xhat_one, inv_one = norm_parts(inputs)
    normed = gather_cuts((xhat_one * gain_one).astype(BF))
    qkv_here = lax.all_to_all(
        w_qkv.reshape(own, 3, n_cuts, own), "cuts", split_axis=2, concat_axis=0, tiled=True
    ).reshape(features, 3 * own)
    joined = mm(normed, qkv_here).astype(BF)
    split = joined.reshape(seq_len, 3, heads, HD)
    q_heads, k_heads, v_heads = split[:, 0], split[:, 1], split[:, 2]
    spots = jnp.arange(seq_len, dtype=jnp.int32)
    visible = (spots[None, :] <= spots[:, None])[None]

    def masked_scores():
        scores = jnp.einsum("qhd,khd->hqk", q_heads, k_heads, preferred_element_type=F32) * scaling
        return jnp.where(visible, scores, -1e30)

    scores = masked_scores()
    peak = jnp.max(scores, axis=-1, keepdims=True)
    row_exp = jnp.exp(scores - peak)
    total = jnp.sum(row_exp, axis=-1, keepdims=True)
    weights_p = (row_exp / total).astype(BF)
    heads_here = jnp.einsum("hqk,khd->qhd", weights_p, v_heads, preferred_element_type=F32)
    log_norm = peak + jnp.log(total)
    head_out = rows_to_cuts(heads_here.reshape(seq_len, own).astype(BF))
    attn_full = gather_cuts(w_attn_out)
    small_full = gather_cuts(jnp.concatenate([w_router, w_mix], axis=1))
    grad_all = gather_cuts(cotangent)
    grad_rows = to_owners(cotangent)
    in_here = columns_to_cuts(w_in)
    hidden = inputs + mm(head_out, attn_full)
    xhat_two, inv_two = norm_parts(hidden)
    second = (xhat_two * gain_two).astype(BF)

    logits = mm(second, small_full)
    router_p = softmax_rows(logits[:, :experts_all])
    mixing = softmax_rows(logits[:, experts_all:])
    gate = jnp.sum(router_p * onehot, axis=1)
    grad = cotangent.astype(F32)
    d_moe = grad * mixing[:, 1:2]

    if fused:
        slots = mm_tn(placer, second).astype(BF).reshape(groups, n_expert, block, features)
        width = n_expert * block
        at = jnp.arange(width, dtype=jnp.int32)
        slab = n_expert * capacity
        goal = at % slab // capacity * block + at // slab * capacity + at % capacity
        sort = (goal[:, None] == at[None, :]).astype(BF)
        small_wide = jnp.pad(small_full, ((0, 0), (0, -small_full.shape[1] % 128)))
        sums, returned, second_all, activ_low, d_up, d_dense_all, rows_in, d_rows, expert_low, d_first = middle(
            slots, second, grad_all.reshape(n_cuts, tokens, features), grad_rows, in_here, w_out, small_wide,
            sort, sort.T, expert_in, expert_out, n_expert, n_cuts,
        )
        dense, d_second_ffn = sums[0], sums[1]
        second_all, activ_low, d_up, d_dense_all = (
            v.reshape(seq_len, -1) for v in (second_all, activ_low, d_up, d_dense_all)
        )
        g_out = mm_tn(activ_low, d_dense_all)
        g_in = mm_tn(second_all, d_up)
        g_expert_out = jnp.einsum("erh,erd->ehd", expert_low, d_rows, preferred_element_type=F32)
        g_expert_in = jnp.einsum("erd,erh->edh", rows_in, d_first, preferred_element_type=F32)
        picked = mm(placer, returned[0].reshape(-1, features))
        d_picked_in = mm(placer, returned[1].reshape(-1, features))
    else:
        rows_in = to_owners(second)
        row_logits = jnp.einsum("erd,dk->erk", rows_in, small_full, preferred_element_type=F32)
        ids = lax.axis_index("expert") * experts_here + jnp.arange(experts_here, dtype=jnp.int32)
        is_here = (jnp.arange(experts_all, dtype=jnp.int32)[None, :] == ids[:, None]).astype(F32)
        row_gate = jnp.sum(
            softmax_rows(row_logits[:, :, :experts_all]) * is_here[:, None, :], axis=2, keepdims=True
        )
        row_mixing = softmax_rows(row_logits[:, :, experts_all:])[:, :, 1:2]
        d_rows = (grad_rows.astype(F32) * row_mixing * row_gate).astype(BF)

        first = jnp.einsum("erd,edh->erh", rows_in, expert_in, preferred_element_type=F32)
        expert_act, expert_pull = jax.vjp(jax.nn.gelu, first)
        expert_low = expert_act.astype(BF)
        partial_out = jnp.einsum("erh,ehd->erd", expert_low, expert_out, preferred_element_type=F32)
        picked = to_sources(partial_out)

        second_all = gather_cuts(second)
        mixing_all = softmax_rows(mm(second_all, small_full[:, experts_all:]))
        d_dense_all = (grad_all.astype(F32) * mixing_all[:, 0:1]).astype(BF)
        up_proj = mm(second_all, in_here)
        activ, gelu_pull = jax.vjp(jax.nn.gelu, up_proj)
        activ_low = activ.astype(BF)
        dense = scatter_cuts(mm(activ_low, w_out)).astype(F32)
        d_activ = mm_nt(d_dense_all, w_out)
        g_out = mm_tn(activ_low, d_dense_all)
        d_up = gelu_pull(d_activ)[0].astype(BF)
        g_in = mm_tn(second_all, d_up)
        d_second_ffn = scatter_cuts(mm_nt(d_up, in_here)).astype(F32)

        d_expert_act = jnp.einsum("erd,ehd->erh", d_rows, expert_out, preferred_element_type=F32)
        d_first = expert_pull(d_expert_act)[0].astype(BF)
        d_rows_in = jnp.einsum("erh,edh->erd", d_first, expert_in, preferred_element_type=F32)
        g_expert_out = jnp.einsum("erh,erd->ehd", expert_low, d_rows, preferred_element_type=F32)
        g_expert_in = jnp.einsum("erd,erh->edh", rows_in, d_first, preferred_element_type=F32)
        d_picked_in = to_sources(d_rows_in)

    moe_val = gate[:, None] * picked
    block_out = (hidden + mixing[:, 0:1] * dense + mixing[:, 1:2] * moe_val).astype(BF)
    d_mixing = jnp.stack([jnp.sum(grad * dense, axis=1), jnp.sum(grad * moe_val, axis=1)], axis=1)
    d_gate = jnp.sum(d_moe * picked, axis=1)
    d_router = router_p * (onehot - gate[:, None]) * d_gate[:, None]
    d_mix = mixing * (d_mixing - jnp.sum(mixing * d_mixing, axis=1, keepdims=True))
    d_small = jnp.concatenate([d_router, d_mix], axis=1).astype(BF)
    g_small = mm_tn(d_small, second)
    d_second = d_second_ffn + mm_nt(d_small, small_full) + d_picked_in
    d_hidden_norm, g_gain_two = norm_back(d_second, xhat_two, inv_two, gain_two)
    d_hidden = grad + d_hidden_norm
    d_attn = d_hidden.astype(BF)
    g_attn_out = mm_tn(head_out, d_attn)
    d_head_rows = mm_nt(d_attn, attn_full).astype(BF)
    if fused:
        tiny = jnp.concatenate([g_small, g_gain_two[None, :]], axis=0)
        tiny = jnp.pad(tiny, ((0, -tiny.shape[0] % 8), (0, 0)))
        d_block_input, s_in, s_out, s_qkv, s_attn_out, tiny, late = tail(
            g_in.astype(BF), g_out.astype(BF), g_attn_out.astype(BF), d_head_rows, joined, log_norm[:, :, 0], normed,
            qkv_here, block_input, gain_one[None, :], d_hidden, tiny, n_expert, n_cuts,
        )
        swap = [
            ((flat % n_expert) * n_cuts + flat // n_expert, flat) for flat in range(n_expert * n_cuts)
        ]
        s_out = lax.ppermute(s_out, ("expert", "cuts"), swap).astype(F32)
        s_in = s_in.swapaxes(0, 1).reshape(-1, w_in.shape[1]).astype(F32)
        s_qkv = s_qkv.reshape(n_cuts, -1, 3, own).transpose(1, 2, 0, 3).reshape(-1, 3 * features).astype(F32)
        width = features // (n_expert * n_cuts)
        spot = lax.axis_index("cuts") * width
        s_tiny = lax.dynamic_slice_in_dim(tiny, spot, width, axis=1)
        s_late = lax.dynamic_slice_in_dim(late, spot, width, axis=1)
        return (
            block_out,
            d_block_input,
            s_qkv,
            s_attn_out,
            s_in,
            s_out,
            s_tiny[:experts_all].T,
            s_tiny[experts_all : experts_all + 2].T,
            s_late[0],
            s_tiny[experts_all + 2],
            g_expert_in,
            g_expert_out,
        )
    d_heads = columns_to_cuts(d_head_rows).reshape(seq_len, heads, HD)

    soft_p = jnp.exp(masked_scores() - log_norm)
    d_soft = jnp.einsum("qhd,khd->hqk", d_heads, v_heads, preferred_element_type=F32)
    delta = jnp.sum(soft_p * d_soft, axis=-1, keepdims=True)
    d_scores = (soft_p * (d_soft - delta)).astype(BF)
    d_query = jnp.einsum("hqk,khd->qhd", d_scores, k_heads, preferred_element_type=F32) * scaling
    d_keys = jnp.einsum("hqk,qhd->khd", d_scores, q_heads, preferred_element_type=F32) * scaling
    d_values = jnp.einsum("hqk,qhd->khd", soft_p.astype(BF), d_heads, preferred_element_type=F32)
    d_joined = jnp.stack([d_query, d_keys, d_values], axis=1).reshape(seq_len, 3 * own).astype(BF)
    g_qkv = mm_tn(normed, d_joined)
    d_normed = scatter_cuts(mm_nt(d_joined, qkv_here)).astype(F32)
    d_input_norm, g_gain_one = norm_back(d_normed, xhat_one, inv_one, gain_one)
    d_block_input = d_hidden + d_input_norm

    def over_experts(part):
        return lax.psum_scatter(part.astype(BF), "expert", scatter_dimension=0, tiled=True)

    s_in = rows_to_cuts(over_experts(g_in)).astype(F32)
    s_out = over_experts(g_out)
    swap = [
        ((flat % n_expert) * n_cuts + flat // n_expert, flat) for flat in range(n_expert * n_cuts)
    ]
    s_out = lax.ppermute(s_out, ("expert", "cuts"), swap).astype(F32)
    s_qkv = over_experts(g_qkv)
    deep = s_qkv.shape[0]
    s_qkv = lax.all_to_all(
        s_qkv.reshape(deep, 3, 1, own), "cuts", split_axis=0, concat_axis=2, tiled=True
    )
    s_qkv = s_qkv.reshape(-1, 3 * features).astype(F32)
    s_attn_out = scatter_cuts(over_experts(g_attn_out)).astype(F32)
    tiny = jnp.concatenate([g_small, g_gain_one[None, :], g_gain_two[None, :]], axis=0)
    tiny = jnp.pad(tiny, ((0, -tiny.shape[0] % 8), (0, 0)))
    tiny = sum_small(tiny, n_expert, n_cuts)
    width = features // (n_expert * n_cuts)
    s_tiny = lax.dynamic_slice_in_dim(tiny, lax.axis_index("cuts") * width, width, axis=1)
    return (
        block_out,
        d_block_input,
        s_qkv,
        s_attn_out,
        s_in,
        s_out,
        s_tiny[:experts_all].T,
        s_tiny[experts_all : experts_all + 2].T,
        s_tiny[experts_all + 2],
        s_tiny[experts_all + 3],
        g_expert_in,
        g_expert_out,
    )


def solution(mesh):
    both = ("expert", "cuts")
    placed = (
        P(both, None),
        P(both),
        P(both),
        P("cuts", None),
        P("cuts", None),
        P("cuts", None),
        P("cuts", None),
        P("cuts", None),
        P("cuts", None),
        P("cuts"),
        P("cuts"),
        P("expert", None, "cuts"),
        P("expert", "cuts", None),
        P(both, None),
    )
    results = (
        P(both, None),
        P(both, None),
        P(both, None),
        P(both, None),
        P(both, None),
        P(both, None),
        P(both, None),
        P(both, None),
        P(both),
        P(both),
        P("expert", None, "cuts"),
        P("expert", "cuts", None),
    )
    return jax.shard_map(
        shards, mesh=mesh, in_specs=placed, out_specs=results, check_vma=False
    )
```

```python
import functools
import math

import jax
import jax.numpy as jnp
import numpy as np
from jax import lax
from jax.experimental import pallas as pl
from jax.experimental.pallas import tpu as pltpu
from jax.sharding import PartitionSpec as P

HD = 64
BF = jnp.bfloat16
F32 = jnp.float32
MESH = pl.DeviceIdType.MESH


def norm_parts(values):
    center = values - jnp.mean(values, axis=-1, keepdims=True)
    spread = jnp.mean(center * center, axis=-1, keepdims=True)
    inv = lax.rsqrt(spread + 1e-05)
    return center * inv, inv


def norm_back(grad, xhat, inv, gain):
    q = grad * gain
    mean_q = jnp.mean(q, axis=-1, keepdims=True)
    mean_qx = jnp.mean(q * xhat, axis=-1, keepdims=True)
    return (q - mean_q - xhat * mean_qx) * inv, jnp.sum(grad * xhat, axis=0)


def mm(left, right):
    return jnp.dot(left, right, preferred_element_type=F32)


def mm_nt(left, right):
    return lax.dot_general(left, right, (((1,), (1,)), ((), ())), preferred_element_type=F32)


def mm_tn(left, right):
    return lax.dot_general(left, right, (((0,), (0,)), ((), ())), preferred_element_type=F32)


def softmax_rows(logits):
    shifted = logits - jnp.max(logits, axis=-1, keepdims=True)
    row_exp = jnp.exp(shifted)
    return row_exp / jnp.sum(row_exp, axis=-1, keepdims=True)


def gather_cuts(rows):
    return lax.all_gather(rows, "cuts", axis=0, tiled=True)


def scatter_cuts(rows):
    return lax.psum_scatter(rows.astype(BF), "cuts", scatter_dimension=0, tiled=True)


def columns_to_cuts(rows):
    return lax.all_to_all(rows, "cuts", split_axis=1, concat_axis=0, tiled=True)


def rows_to_cuts(rows):
    return lax.all_to_all(rows, "cuts", split_axis=0, concat_axis=1, tiled=True)


def ring_mod(index, count):
    return lax.rem(index, count)


def small_kernel(n_expert, n_cuts, src, out, by_expert, mine, by_cuts, send_a, recv_a, send_b, recv_b):
    me, cut = lax.axis_index("expert"), lax.axis_index("cuts")
    width = out.shape[1]
    barrier = pltpu.get_barrier_semaphore()
    for step in range(1, n_expert):
        peer = ring_mod(me + step, n_expert)
        pl.semaphore_signal(barrier, inc=1, device_id=(peer, cut), device_id_type=MESH)
    for step in range(1, n_cuts):
        peer = ring_mod(cut + step, n_cuts)
        pl.semaphore_signal(barrier, inc=1, device_id=(me, peer), device_id_type=MESH)
    pl.semaphore_wait(barrier, n_expert + n_cuts - 2)

    def part(owner):
        return src.at[:, pl.ds(pl.multiple_of(owner * width, 128), width)]

    copies = []
    for step in range(1, n_expert):
        peer = ring_mod(me + step, n_expert)
        copies.append(
            pltpu.make_async_remote_copy(
                src_ref=part(peer),
                dst_ref=by_expert.at[step],
                send_sem=send_a.at[step],
                recv_sem=recv_a.at[step],
                device_id=(peer, cut),
                device_id_type=MESH,
            )
        )
        copies[-1].start()
    total = src[:, pl.ds(pl.multiple_of(me * width, 128), width)]
    for step in range(1, n_expert):
        copies[step - 1].wait()
        total = total + by_expert[step]
    mine[...] = total
    copies = []
    for step in range(1, n_cuts):
        peer = ring_mod(cut + step, n_cuts)
        copies.append(
            pltpu.make_async_remote_copy(
                src_ref=mine,
                dst_ref=by_cuts.at[step],
                send_sem=send_b.at[step],
                recv_sem=recv_b.at[step],
                device_id=(me, peer),
                device_id_type=MESH,
            )
        )
        copies[-1].start()
    for step in range(1, n_cuts):
        copies[step - 1].wait()
        total = total + by_cuts[step]
    out[...] = total


def sum_small(values, n_expert, n_cuts):
    rows, features = values.shape
    width = features // n_expert
    pad = -width % 128
    if pad:
        values = jnp.pad(values.reshape(rows, n_expert, width), ((0, 0), (0, 0), (0, pad)))
        values = values.reshape(rows, n_expert * (width + pad))
    wide = width + pad
    summed = pl.pallas_call(
        functools.partial(small_kernel, n_expert, n_cuts),
        name="sum_small",
        out_shape=jax.ShapeDtypeStruct((rows, wide), F32),
        in_specs=[pl.BlockSpec(memory_space=pltpu.VMEM)],
        out_specs=pl.BlockSpec(memory_space=pltpu.VMEM),
        scratch_shapes=[
            pltpu.VMEM((n_expert, rows, wide), F32),
            pltpu.VMEM((rows, wide), F32),
            pltpu.VMEM((n_cuts, rows, wide), F32),
            pltpu.SemaphoreType.DMA((n_expert,)),
            pltpu.SemaphoreType.DMA((n_expert,)),
            pltpu.SemaphoreType.DMA((n_cuts,)),
            pltpu.SemaphoreType.DMA((n_cuts,)),
        ],
        compiler_params=pltpu.CompilerParams(collective_id=0, has_side_effects=True),
    )(values)
    return summed[:, :width]


def dot_nt(left, right):
    return lax.dot_general(left, right, (((1,), (1,)), ((), ())), preferred_element_type=F32)


def tile_of(step, size):
    return pl.ds(pl.multiple_of(step * size, size), size)


def lane_softmax(logits, low, high):
    lane = lax.broadcasted_iota(jnp.int32, logits.shape, 1)
    inside = (lane >= low) & (lane < high)
    kept = jnp.where(inside, logits, -1e30)
    powers = jnp.exp(kept - jnp.max(kept, axis=1, keepdims=True))
    powers = jnp.where(inside, powers, 0.0)
    return powers / jnp.sum(powers, axis=1, keepdims=True), lane


def mlp_both(rows, d_rows, w_up, w_down, act, d_up, write):
    root, cubic = math.sqrt(2.0 / math.pi), 0.044715

    @pl.loop(0, act.shape[1] // 256)
    def _(step):
        span = tile_of(step, 256)
        up = mm(rows[...], w_up[:, span])
        d_act = dot_nt(d_rows[...], w_down[span, :])
        square = up * up
        bent = jnp.tanh(root * up * (1.0 + cubic * square))
        half = 0.5 * (1.0 + bent)
        act[:, span] = (up * half).astype(BF)
        slope = half + 0.5 * up * (1.0 - bent * bent) * (root + 3.0 * root * cubic * square)
        d_up[:, span] = (d_act * slope).astype(BF)

    @pl.loop(0, w_up.shape[0] // 256)
    def _(step):
        span = tile_of(step, 256)
        write(span, mm(act[...], w_down[:, span]), dot_nt(d_up[...], w_up[span, :]))


def middle_kernel(
    sizes, slots, second, grad_all, grad_rows, w_in, w_out, small, sort, unsort, e_in, e_out,
    sums, returned, second_all, act_all, d_up_all, d_dense_all, rows_in, d_rows_all, act_e_all, d_first_all,
    sec, grd, win, wout, act, d_up, d_dense, part_a, part_b, ffn_x, ffn_y, ffn_qa, ffn_qb,
    zbuf, rows, g_rows, d_rows, act_e, d_first, wi_e, wo_e, out_a, out_b, row_x, row_y, row_qa, row_qb, sorted_back, send_back,
    load_sem, weight_sem, store_sem, store_e_sem, z_sem, ag_sem, eag_sem, frs_sem, ers_sem, zr_sem,
):
    n_expert, groups, here, slab = sizes
    me, cut = lax.axis_index("expert"), lax.axis_index("cuts")
    at_x, at_y, at_d = (jnp.bitwise_xor(cut, k) for k in (1, 2, 3))
    block = zbuf.shape[2]
    per_group = here // groups
    experts_all = n_expert * here

    def load(src, dst, index):
        copy = pltpu.make_async_copy(src, dst, load_sem.at[index])
        copy.start()
        return copy

    def send(src, dst, sems, index, peer):
        copy = pltpu.make_async_remote_copy(
            src_ref=src, dst_ref=dst, send_sem=sems.at[0, index], recv_sem=sems.at[1, index],
            device_id=peer, device_id_type=MESH,
        )
        copy.start()
        return copy

    loads = [
        load(second, sec.at[cut], 0), load(w_in, win, 1), load(w_out, wout, 2), load(grad_all, grd, 3),
    ]

    def fetch_expert(i):
        slot = i % 2
        copies = [
            pltpu.make_async_copy(e_in.at[i], wi_e.at[slot], weight_sem.at[0, slot]),
            pltpu.make_async_copy(e_out.at[i], wo_e.at[slot], weight_sem.at[1, slot]),
            pltpu.make_async_copy(grad_rows.at[i], g_rows.at[slot], weight_sem.at[2, slot]),
        ]
        for copy in copies:
            copy.start()
        return copies

    fetched = [fetch_expert(0), fetch_expert(1)]
    barrier = pltpu.get_barrier_semaphore()
    for k in range(1, n_expert):
        pl.semaphore_signal(barrier, inc=1, device_id=(jnp.bitwise_xor(me, k), cut), device_id_type=MESH)
    for peer in (at_x, at_y):
        pl.semaphore_signal(barrier, inc=1, device_id=(me, peer), device_id_type=MESH)
    pl.semaphore_wait(barrier, n_expert + 1)

    z_copies = []
    for g in range(groups):
        for k in range(1, n_expert):
            peer = jnp.bitwise_xor(me, k)
            z_copies.append(send(slots.at[g, peer], zbuf.at[g, me], z_sem, g * n_expert + k, (peer, cut)))
    loads[0].wait()
    ag = [
        send(sec.at[cut], sec.at[cut], ag_sem, 0, (me, at_x)),
        send(sec.at[cut], sec.at[cut], ag_sem, 1, (me, at_y)),
    ]
    for g in range(groups):
        zbuf[g, me] = slots[g, me]
    stores = []

    def store(src, dst, index):
        copy = pltpu.make_async_copy(src, dst, store_sem.at[index])
        copy.start()
        return copy

    ffn_stores = {}

    def ffn_block(which, owner):
        slot = which % 2
        if which >= 2:
            for copy in ffn_stores[which - 2]:
                copy.wait()
        mixing, lane = lane_softmax(mm(sec[owner], small[...]), experts_all, experts_all + 2)
        first_mix = jnp.sum(jnp.where(lane == experts_all, mixing, 0.0), axis=1, keepdims=True)
        d_dense[slot] = (grd[owner].astype(F32) * first_mix).astype(BF)

        def write(span, out, d_row):
            if which == 0:
                sums[0, :, span] = out
                sums[1, :, span] = d_row
            else:
                part_a[which, :, span] = out.astype(BF)
                part_b[which, :, span] = d_row.astype(BF)

        mlp_both(sec.at[owner], d_dense.at[slot], win, wout, act.at[slot], d_up.at[slot], write)
        ffn_stores[which] = [
            store(act.at[slot], act_all.at[owner], 3 * which),
            store(d_up.at[slot], d_up_all.at[owner], 3 * which + 1),
            store(d_dense.at[slot], d_dense_all.at[owner], 3 * which + 2),
        ]

    for copy in loads[1:]:
        copy.wait()
    ffn_block(0, cut)
    half = sec.shape[1] // 2
    ag[0].wait_recv()
    ag.append(send(sec.at[at_x, pl.ds(0, half)], sec.at[at_x, pl.ds(0, half)], ag_sem, 2, (me, at_y)))
    ag[1].wait_recv()
    ag.append(send(sec.at[at_y, pl.ds(half, half)], sec.at[at_y, pl.ds(half, half)], ag_sem, 3, (me, at_x)))
    ffn_block(1, at_x)

    def slab_of(owner):
        return pl.ds(pl.multiple_of(owner * slab, slab), slab)

    eag = {}
    for g in range(groups):
        for k in range(1, n_expert):
            z_copies[g * (n_expert - 1) + k - 1].wait_recv()
        flat = zbuf[g].reshape(n_expert * block, zbuf.shape[3])
        for j in range(per_group):
            i = g * per_group + j
            rows[i, slab_of(cut)] = mm(sort[pl.ds(j * slab, slab), :], flat).astype(BF)
            mine = rows.at[i, slab_of(cut)]
            eag[i] = [
                send(mine, mine, eag_sem, 4 * i, (me, at_x)),
                send(mine, mine, eag_sem, 4 * i + 1, (me, at_y)),
            ]
    ffn_block(2, at_y)
    ag[2].wait_recv()
    ag[3].wait_recv()

    def relay(i):
        cut_half = slab // 2
        eag[i][0].wait_recv()
        piece = rows.at[i, pl.ds(pl.multiple_of(at_x * slab, slab), cut_half)]
        eag[i].append(send(piece, piece, eag_sem, 4 * i + 2, (me, at_y)))
        eag[i][1].wait_recv()
        piece = rows.at[i, pl.ds(pl.multiple_of(at_y * slab + cut_half, cut_half), cut_half)]
        eag[i].append(send(piece, piece, eag_sem, 4 * i + 3, (me, at_x)))

    relay(0)
    ffn_block(3, at_d)
    frs = [
        send(part_a.at[1], ffn_x.at[0], frs_sem, 0, (me, at_x)),
        send(part_a.at[3], ffn_x.at[1], frs_sem, 1, (me, at_x)),
        send(part_b.at[2], ffn_y.at[0], frs_sem, 2, (me, at_y)),
        send(part_b.at[3], ffn_y.at[1], frs_sem, 3, (me, at_y)),
    ]
    second_store = store(sec, second_all, 12)
    expert_stores = {}
    ers = {}

    def expert(i):
        slot = i % 2
        if i >= 2:
            for copy in expert_stores[i - 2]:
                copy.wait()
        for copy in fetched[i]:
            copy.wait()
        logits = mm(rows[i], small[...])
        router, lane = lane_softmax(logits, 0, experts_all)
        gate = jnp.sum(jnp.where(lane == me * here + i, router, 0.0), axis=1, keepdims=True)
        mixing, lane = lane_softmax(logits, experts_all, experts_all + 2)
        mixing = jnp.sum(jnp.where(lane == experts_all + 1, mixing, 0.0), axis=1, keepdims=True)
        d_rows[slot] = (g_rows[slot].astype(F32) * mixing * gate).astype(BF)

        def write(span, out, d_row):
            out_a[i, :, span] = out.astype(BF)
            out_b[i, :, span] = d_row.astype(BF)

        mlp_both(rows.at[i], d_rows.at[slot], wi_e.at[slot], wo_e.at[slot], act_e.at[slot], d_first.at[slot], write)
        expert_stores[i] = []
        for n, (src, dst) in enumerate(((d_rows, d_rows_all), (act_e, act_e_all), (d_first, d_first_all))):
            copy = pltpu.make_async_copy(src.at[slot], dst.at[i], store_e_sem.at[n, slot])
            copy.start()
            expert_stores[i].append(copy)
        ers[i] = [
            send(out_a.at[i, slab_of(at_x)], row_x.at[i, 0], ers_sem, 6 * i, (me, at_x)),
            send(out_a.at[i, slab_of(at_d)], row_x.at[i, 1], ers_sem, 6 * i + 1, (me, at_x)),
            send(out_b.at[i, slab_of(at_y)], row_y.at[i, 0], ers_sem, 6 * i + 2, (me, at_y)),
            send(out_b.at[i, slab_of(at_d)], row_y.at[i, 1], ers_sem, 6 * i + 3, (me, at_y)),
        ]

    def add_into(ref, *others):
        total = ref[...].astype(F32)
        for other in others:
            total = total + other[...].astype(F32)
        ref[...] = total.astype(BF)

    def pass_on(i):
        for copy in ers[i][:4]:
            copy.wait_recv()
        add_into(out_a.at[i, slab_of(at_y)], row_x.at[i, 1])
        add_into(out_b.at[i, slab_of(at_x)], row_y.at[i, 1])
        ers[i] += [
            send(out_a.at[i, slab_of(at_y)], row_qa.at[i], ers_sem, 6 * i + 4, (me, at_y)),
            send(out_b.at[i, slab_of(at_x)], row_qb.at[i], ers_sem, 6 * i + 5, (me, at_x)),
        ]

    back_copies = []

    def finish(i):
        ers[i][4].wait_recv()
        ers[i][5].wait_recv()
        for n, (out, near, far) in enumerate(((out_a, row_x, row_qa), (out_b, row_y, row_qb))):
            total = out[i, slab_of(cut)].astype(F32) + near[i, 0].astype(F32) + far[i].astype(F32)
            sorted_back[n, i] = total.astype(BF)
        if (i + 1) % per_group == 0:
            g = i // per_group
            for n in range(2):
                flat = sorted_back[n, pl.ds(g * per_group, per_group)].reshape(per_group * slab, -1)
                placed = mm(unsort[...], flat).astype(BF)
                send_back[n, g] = placed.reshape(n_expert, block, -1)
                returned[n, g, me] = send_back[n, g, me]
                for k in range(1, n_expert):
                    peer = jnp.bitwise_xor(me, k)
                    back_copies.append(
                        send(
                            send_back.at[n, g, peer], returned.at[n, g, me], zr_sem,
                            (n * groups + g) * n_expert + k, (peer, cut),
                        )
                    )

    for i in range(here):
        if i + 1 < here:
            relay(i + 1)
        eag[i][2].wait_recv()
        eag[i][3].wait_recv()
        expert(i)
        if i + 2 < here:
            fetched.append(fetch_expert(i + 2))
        if i == 0:
            for copy in frs[:4]:
                copy.wait_recv()
            add_into(part_a.at[2], ffn_x.at[1])
            add_into(part_b.at[1], ffn_y.at[1])
            frs += [
                send(part_a.at[2], ffn_qa, frs_sem, 4, (me, at_y)),
                send(part_b.at[1], ffn_qb, frs_sem, 5, (me, at_x)),
            ]
        if i >= 1:
            pass_on(i - 1)
        if i >= 2:
            finish(i - 2)
    rows_store = store(rows, rows_in, 13)
    pass_on(here - 1)
    finish(here - 2)
    frs[4].wait_recv()
    frs[5].wait_recv()
    sums[0] = sums[0] + ffn_x[0].astype(F32) + ffn_qa[...].astype(F32)
    sums[1] = sums[1] + ffn_y[0].astype(F32) + ffn_qb[...].astype(F32)
    finish(here - 1)
    for copy in back_copies:
        copy.wait_recv()
    for copy in z_copies + ag + frs + back_copies:
        copy.wait_send()
    for i in range(here):
        for copy in eag[i] + ers[i]:
            copy.wait_send()
    for which in (2, 3):
        for copy in ffn_stores[which]:
            copy.wait()
    for i in (here - 2, here - 1):
        for copy in expert_stores[i]:
            copy.wait()
    second_store.wait()
    rows_store.wait()


def middle(slots, second, grad_all, grad_rows, w_in, w_out, small, sort, unsort, e_in, e_out, n_expert, n_cuts):
    groups, _, block, width = slots.shape
    tokens = second.shape[0]
    here, _, hidden = e_in.shape
    ffn = w_in.shape[1]
    slab = n_expert * block * groups // here
    rows = n_cuts * slab
    any_spec, vmem_spec = pl.BlockSpec(memory_space=pl.ANY), pl.BlockSpec(memory_space=pltpu.VMEM)
    shape = jax.ShapeDtypeStruct
    dma = pltpu.SemaphoreType.DMA
    flops = 8 * (n_cuts * tokens * ffn + here * rows * hidden) * width
    return pl.pallas_call(
        functools.partial(middle_kernel, (n_expert, groups, here, slab)),
        name="middle",
        out_shape=(
            shape((2, tokens, width), F32), shape((2, groups, n_expert, block, width), BF),
            shape((n_cuts, tokens, width), BF), shape((n_cuts, tokens, ffn), BF),
            shape((n_cuts, tokens, ffn), BF), shape((n_cuts, tokens, width), BF),
            shape((here, rows, width), BF), shape((here, rows, width), BF),
            shape((here, rows, hidden), BF), shape((here, rows, hidden), BF),
        ),
        in_specs=[vmem_spec] + [any_spec] * 5 + [vmem_spec] * 3 + [any_spec] * 2,
        out_specs=(vmem_spec,) * 2 + (any_spec,) * 8,
        scratch_shapes=[
            pltpu.VMEM((n_cuts, tokens, width), BF), pltpu.VMEM((n_cuts, tokens, width), BF),
            pltpu.VMEM((width, ffn), BF), pltpu.VMEM((ffn, width), BF),
            pltpu.VMEM((2, tokens, ffn), BF), pltpu.VMEM((2, tokens, ffn), BF), pltpu.VMEM((2, tokens, width), BF),
            pltpu.VMEM((n_cuts, tokens, width), BF), pltpu.VMEM((n_cuts, tokens, width), BF),
            pltpu.VMEM((2, tokens, width), BF), pltpu.VMEM((2, tokens, width), BF),
            pltpu.VMEM((tokens, width), BF), pltpu.VMEM((tokens, width), BF),
            pltpu.VMEM((groups, n_expert, block, width), BF), pltpu.VMEM((here, rows, width), BF),
            pltpu.VMEM((2, rows, width), BF), pltpu.VMEM((2, rows, width), BF),
            pltpu.VMEM((2, rows, hidden), BF), pltpu.VMEM((2, rows, hidden), BF),
            pltpu.VMEM((2, width, hidden), BF), pltpu.VMEM((2, hidden, width), BF),
            pltpu.VMEM((here, rows, width), BF), pltpu.VMEM((here, rows, width), BF),
            pltpu.VMEM((here, 2, slab, width), BF), pltpu.VMEM((here, 2, slab, width), BF),
            pltpu.VMEM((here, slab, width), BF), pltpu.VMEM((here, slab, width), BF),
            pltpu.VMEM((2, here, slab, width), BF), pltpu.VMEM((2, groups, n_expert, block, width), BF),
            dma((4,)), dma((3, 2)), dma((14,)), dma((3, 2)),
            dma((2, groups * n_expert)), dma((2, 4)), dma((2, 4 * here)), dma((2, 6)), dma((2, 6 * here)),
            dma((2, 2 * groups * n_expert)),
        ],
        compiler_params=pltpu.CompilerParams(
            collective_id=1, has_side_effects=True, vmem_limit_bytes=67_000_000
        ),
        cost_estimate=pl.CostEstimate(flops=flops, bytes_accessed=48 << 20, transcendentals=0),
    )(slots, second, grad_all, grad_rows, w_in, w_out, small, sort, unsort, e_in, e_out)


def tail_kernel(
    heads, scaling, g_in, g_out, g_attn, d_heads, joined, lse, normed, qkv, source, gain, d_hidden, tiny,
    d_source, o_in, o_out, o_qkv, o_attn, o_tiny, o_gain,
    core_in, own, z_in, a_in, a_z, a_mine, gq, core_q, own_q, z_q, fin_in, fin_q,
    dh, dj, acc_q, acc_k, acc_v, dn, dn_in, norm_v, qkv_v, tiny_e, tiny_m, tiny_c, late, late_e, late_m, late_c,
    load_sem, core_sem, z_sem, cut_sem, te_sem, tc_sem,
):
    me, cut = lax.axis_index("expert"), lax.axis_index("cuts")
    core, level = lax.rem(me, 2), lax.div(me, 2)
    other = 1 - core
    n_cuts, tokens, width = dh.shape
    n_expert = tiny_e.shape[0]
    levels = n_expert // 2
    twin = (jnp.bitwise_xor(me, 1), cut)

    def send(src, dst, sems, index, peer):
        copy = pltpu.make_async_remote_copy(
            src_ref=src, dst_ref=dst, send_sem=sems.at[0, index], recv_sem=sems.at[1, index],
            device_id=peer, device_id_type=MESH,
        )
        copy.start()
        return copy

    def load(src, dst, index):
        copy = pltpu.make_async_copy(src, dst, load_sem.at[index])
        copy.start()
        return copy

    grads = (g_in, g_out, g_attn)
    mine = [load(grads[m].at[:, core], own.at[m], m) for m in range(3)]
    later = [load(normed, norm_v, 3), load(qkv, qkv_v, 4)]
    barrier = pltpu.get_barrier_semaphore()
    for k in range(1, n_expert):
        pl.semaphore_signal(barrier, inc=1, device_id=(jnp.bitwise_xor(me, k), cut), device_id_type=MESH)
    for k in range(1, n_cuts):
        pl.semaphore_signal(barrier, inc=1, device_id=(me, jnp.bitwise_xor(cut, k)), device_id_type=MESH)
    pl.semaphore_wait(barrier, n_expert + n_cuts - 2)

    def columns(index, size):
        return pl.ds(pl.multiple_of(index * size, size), size)

    sent = []

    def to_cuts(src_of, dst_of, base):
        copies = []
        for k in range(1, n_cuts):
            peer = jnp.bitwise_xor(cut, k)
            copies.append(send(src_of(peer), dst_of(k), cut_sem, base + k - 1, (me, peer)))
        sent.extend(copies)
        return copies

    def to_levels(src_of, dst_of, base):
        copies = []
        for k in range(1, levels):
            peer = jnp.bitwise_xor(level, k)
            copies.append(send(src_of(peer), dst_of(k), z_sem, base + k - 1, (2 * peer + core, cut)))
        sent.extend(copies)
        return copies

    def to_experts(src, dst, base):
        copies = []
        for k in range(1, n_expert):
            peer = jnp.bitwise_xor(me, k)
            copies.append(send(src.at[:, columns(peer, 128)], dst.at[k], te_sem, base + k - 1, (peer, cut)))
        sent.extend(copies)
        return copies

    heads_moved = to_cuts(lambda peer: d_heads.at[:, columns(peer, width)], lambda k: dh.at[cut], 0)
    twins = [send(grads[m].at[:, other], core_in.at[m], core_sem, m, twin) for m in range(3)]
    tiny_moved = to_experts(tiny, tiny_e, 0)
    dh[cut] = d_heads[:, columns(cut, width)]
    z_moved = []
    attn_moved = None
    for m in range(3):
        mine[m].wait()
        twins[m].wait_recv()

        @pl.loop(0, levels)
        def _(step):
            own[m, step] = (own[m, step].astype(F32) + core_in[m, step].astype(F32)).astype(BF)

        if m < 2:
            z_moved.append(to_levels(lambda peer: own.at[m, peer], lambda k: z_in.at[m, k - 1], 3 * m))
        else:
            piece = own.shape[2] // n_cuts
            attn_moved = to_cuts(
                lambda peer: own.at[2, :, columns(peer, piece)], lambda k: a_in.at[k - 1], 3
            )

    acc_q[...] = jnp.zeros_like(acc_q)
    acc_k[...] = jnp.zeros_like(acc_k)
    acc_v[...] = jnp.zeros_like(acc_v)
    for copy in heads_moved:
        copy.wait_recv()

    @pl.loop(0, heads)
    def _(head):
        pair, half = lax.div(head, 2), lax.rem(head, 2)
        lane = lax.broadcasted_iota(jnp.int32, (1, 128), 1)
        keep = (lax.div(lane, HD) == half).astype(F32)
        keep_low = keep.astype(BF)
        cols = columns(pair, 128)
        k_cols = pl.ds(pl.multiple_of(width + pair * 128, 128), 128)
        v_cols = pl.ds(pl.multiple_of(2 * width + pair * 128, 128), 128)
        for i in range(n_cuts):
            reach = (i + 1) * tokens
            here = pl.ds(i * tokens, tokens)
            query = joined[here, cols] * keep_low
            d_out = dh[i, :, cols] * keep_low
            keys = joined[pl.ds(0, reach), k_cols]
            scores = mm_nt(keys, query) * scaling - lse[head, :, here]
            key_at = lax.broadcasted_iota(jnp.int32, scores.shape, 0)
            query_at = lax.broadcasted_iota(jnp.int32, scores.shape, 1) + i * tokens
            soft = jnp.exp(jnp.where(key_at <= query_at, scores, -1e30))
            d_soft = mm_nt(joined[pl.ds(0, reach), v_cols], d_out)
            delta = jnp.sum(soft * d_soft, axis=0, keepdims=True)
            d_scores = (soft * (d_soft - delta)).astype(BF)
            acc_v[pl.ds(0, reach), cols] += mm(soft.astype(BF), d_out)
            acc_k[pl.ds(0, reach), cols] += mm(d_scores, query)
            acc_q[here, cols] += mm_tn(d_scores, keys) * keep

    dj[:, pl.ds(0, width)] = (acc_q[...] * scaling).astype(BF)
    dj[:, pl.ds(width, width)] = (acc_k[...] * scaling).astype(BF)
    dj[:, pl.ds(2 * width, width)] = acc_v[...].astype(BF)
    for copy in later:
        copy.wait()
    dn_moved = []
    for k in (3, 1, 2):
        peer = jnp.bitwise_xor(cut, k)
        dn[k] = mm_nt(dj[columns(peer, tokens), :], qkv_v[...]).astype(BF)
        dn_moved.append(send(dn.at[k], dn_in.at[k - 1], cut_sem, 6 + k - 1, (me, peer)))
    sent.extend(dn_moved)

    @pl.loop(0, levels)
    def _(step):
        part = mm_tn(norm_v[:, columns(step, 256)], dj[...]).astype(BF)
        gq[step] = part.reshape(2, 128, part.shape[1])

    twins.append(send(gq.at[:, other], core_q, core_sem, 3, twin))
    d_normed = mm_nt(dj[columns(cut, tokens), :], qkv_v[...])

    for copy in attn_moved:
        copy.wait_recv()
    total = own[2, :, columns(cut, piece)].astype(F32)
    for k in range(1, n_cuts):
        total = total + a_in[k - 1].astype(F32)
    a_mine[...] = total.astype(BF)
    attn_z = to_levels(lambda peer: a_mine.at[peer], lambda k: a_z.at[k - 1], 9)

    twins[3].wait_recv()

    @pl.loop(0, levels)
    def _(step):
        own_q[step] = (gq[step, core].astype(F32) + core_q[step].astype(F32)).astype(BF)

    qkv_z = to_levels(lambda peer: own_q.at[peer], lambda k: z_q.at[k - 1], 6)

    for copy in tiny_moved:
        copy.wait_recv()
    small = tiny[:, columns(me, 128)]
    for k in range(1, n_expert):
        small = small + tiny_e[k]
    tiny_m[...] = small

    def tiny_cuts(src, dst, base):
        copies = []
        for k in range(1, n_cuts):
            copies.append(send(src, dst.at[k], tc_sem, base + k - 1, (me, jnp.bitwise_xor(cut, k))))
        sent.extend(copies)
        return copies

    tiny_last = tiny_cuts(tiny_m, tiny_c, 0)

    for copy in z_moved[0]:
        copy.wait_recv()
    total = own[0, level].astype(F32)
    for k in range(1, levels):
        total = total + z_in[0, k - 1].astype(F32)
    fin_in[...] = total.astype(BF).reshape(fin_in.shape)
    in_last = to_cuts(lambda peer: fin_in.at[peer], lambda k: o_in.at[cut], 9)
    o_in[cut] = fin_in[cut]

    for copy in dn_moved:
        copy.wait_recv()
    for k in range(1, n_cuts):
        d_normed = d_normed + dn_in[k - 1].astype(F32)
    xhat, inv = norm_parts(source[...].astype(F32))
    q = d_normed * gain[...]
    mean_q = jnp.mean(q, axis=-1, keepdims=True)
    mean_qx = jnp.mean(q * xhat, axis=-1, keepdims=True)
    d_source[...] = d_hidden[...] + (q - mean_q - xhat * mean_qx) * inv
    late[...] = jnp.broadcast_to(jnp.sum(d_normed * xhat, axis=0, keepdims=True), late.shape)
    late_moved = to_experts(late, late_e, n_expert - 1)

    for copy in tiny_last:
        copy.wait_recv()
    for k in range(1, n_cuts):
        small = small + tiny_c[k]
    o_tiny[...] = small

    for copy in z_moved[1]:
        copy.wait_recv()
    total = own[1, level].astype(F32)
    for k in range(1, levels):
        total = total + z_in[1, k - 1].astype(F32)
    o_out[...] = total.astype(BF)

    for copy in late_moved:
        copy.wait_recv()
    small = late[:, columns(me, 128)]
    for k in range(1, n_expert):
        small = small + late_e[k]
    late_m[...] = small
    late_last = tiny_cuts(late_m, late_c, n_cuts - 1)

    for copy in attn_z:
        copy.wait_recv()
    total = a_mine[level].astype(F32)
    for k in range(1, levels):
        total = total + a_z[k - 1].astype(F32)
    o_attn[...] = total

    for copy in qkv_z:
        copy.wait_recv()
    total = own_q[level].astype(F32)
    for k in range(1, levels):
        total = total + z_q[k - 1].astype(F32)
    fin_q[...] = total.astype(BF).reshape(fin_q.shape)
    qkv_last = to_cuts(lambda peer: fin_q.at[peer], lambda k: o_qkv.at[cut], 12)
    o_qkv[cut] = fin_q[cut]

    for copy in late_last:
        copy.wait_recv()
    for k in range(1, n_cuts):
        small = small + late_c[k]
    o_gain[...] = small
    for copy in in_last + qkv_last:
        copy.wait_recv()
    for copy in sent + twins:
        copy.wait_send()


def tail(g_in, g_out, g_attn, d_heads, joined, lse, normed, qkv, source, gain, d_hidden, tiny, n_expert, n_cuts):
    tokens, features = d_heads.shape
    heads, seq_len = lse.shape
    levels, own = n_expert // 2, features // n_cuts
    deep = features // n_expert
    piece, wide = deep // n_cuts, 3 * own
    any_spec, vmem_spec = pl.BlockSpec(memory_space=pl.ANY), pl.BlockSpec(memory_space=pltpu.VMEM)
    shape, vmem, dma = jax.ShapeDtypeStruct, pltpu.VMEM, pltpu.SemaphoreType.DMA
    rows = tiny.shape[0]
    grid = (levels, 2, deep, features)
    return pl.pallas_call(
        functools.partial(tail_kernel, heads, HD ** (-0.5)),
        name="tail",
        out_shape=(
            shape((tokens, features), F32), shape((n_cuts, piece, features), BF), shape((deep, features), BF),
            shape((n_cuts, piece, wide), BF), shape((piece, features), F32), shape((rows, 128), F32), shape((8, 128), F32),
        ),
        in_specs=[any_spec] * 3 + [vmem_spec] * 3 + [any_spec] * 2 + [vmem_spec] * 4,
        out_specs=(vmem_spec,) * 7,
        scratch_shapes=[
            vmem((3, levels, deep, features), BF), vmem((3, levels, deep, features), BF),
            vmem((2, levels - 1, deep, features), BF), vmem((n_cuts - 1, levels, piece, features), BF),
            vmem((levels - 1, piece, features), BF), vmem((levels, piece, features), BF),
            vmem((levels, 2, deep, wide), BF), vmem((levels, deep, wide), BF), vmem((levels, deep, wide), BF),
            vmem((levels - 1, deep, wide), BF), vmem((n_cuts, piece, features), BF), vmem((n_cuts, piece, wide), BF),
            vmem((n_cuts, tokens, own), BF), vmem((seq_len, wide), BF),
            vmem((seq_len, own), F32), vmem((seq_len, own), F32), vmem((seq_len, own), F32),
            vmem((n_cuts, tokens, features), BF), vmem((n_cuts - 1, tokens, features), BF),
            vmem((seq_len, features), BF), vmem((features, wide), BF),
            vmem((n_expert, rows, 128), F32), vmem((rows, 128), F32), vmem((n_cuts, rows, 128), F32),
            vmem((8, features), F32), vmem((n_expert, 8, 128), F32), vmem((8, 128), F32), vmem((n_cuts, 8, 128), F32),
            dma((5,)), dma((2, 4)), dma((2, 4 * (levels - 1))), dma((2, 5 * (n_cuts - 1))),
            dma((2, 2 * (n_expert - 1))), dma((2, 2 * (n_cuts - 1))),
        ],
        compiler_params=pltpu.CompilerParams(
            collective_id=2, has_side_effects=True, vmem_limit_bytes=48 << 20
        ),
        cost_estimate=pl.CostEstimate(flops=20_000_000_000, bytes_accessed=24 << 20, transcendentals=0),
    )(
        g_in.reshape(grid), g_out.reshape(grid), g_attn.reshape(grid), d_heads, joined, lse.reshape(heads, 1, seq_len),
        normed, qkv, source, gain, d_hidden, tiny,
    )


def head_kernel(
    sizes, source, gains, small, info, sort, w_qkv, w_attn, w_in, cotangent,
    normed, qkv, joined, lse, head_out, attn_full, in_here, small_full, grad_all, grad_rows, placer, gains_all,
    src_v, qkv_v, norm_v, join_v, acc, heads_low, attn_v, in_v, cot_v, slots, zbuf, row_v,
    load_sem, store_sem, cut_sem, twin_sem, z_sem,
):
    heads, scaling, groups, here, slab = sizes
    me, cut = lax.axis_index("expert"), lax.axis_index("cuts")
    core = lax.rem(me, 2)
    twin = (jnp.bitwise_xor(me, 1), cut)
    at = [jnp.bitwise_xor(cut, k) for k in range(4)]
    n_cuts, tokens, width = src_v.shape
    n_expert, block = zbuf.shape[1], zbuf.shape[2]
    own, half, part = width // n_cuts, tokens // 2, tokens // 4

    def span(start, size, step):
        return pl.ds(pl.multiple_of(start, step), size)

    def remote(src, dst, sems, index, peer):
        return pltpu.make_async_remote_copy(
            src_ref=src, dst_ref=dst, send_sem=sems.at[0, index], recv_sem=sems.at[1, index],
            device_id=peer, device_id_type=MESH,
        )

    def local(src, dst, sems, index):
        copy = pltpu.make_async_copy(src, dst, sems.at[index])
        copy.start()
        return copy

    loads = [
        local(cotangent, cot_v, load_sem, 0),
        local(w_attn, attn_v, load_sem, 1),
        local(w_in.at[:, span(cut * width, width, width)], in_v, load_sem, 2),
    ]
    own_qkv = [
        local(
            w_qkv.at[:, span(n * width + cut * own, own, own)],
            qkv_v.at[span(cut * tokens, tokens, tokens), pl.ds(n * own, own)], load_sem, 3 + n,
        )
        for n in range(3)
    ]
    barrier = pltpu.get_barrier_semaphore()
    for k in range(1, n_expert):
        pl.semaphore_signal(barrier, inc=1, device_id=(jnp.bitwise_xor(me, k), cut), device_id_type=MESH)
    for k in range(1, n_cuts):
        pl.semaphore_signal(barrier, inc=1, device_id=(me, at[k]), device_id_type=MESH)
    pl.semaphore_wait(barrier, n_expert + n_cuts - 2)

    def gather(view, first, base):
        return [
            remote(first, view(cut), cut_sem, base, (me, at[1])),
            remote(first, view(cut), cut_sem, base + 1, (me, at[2])),
            remote(view(at[1], 0), view(at[1], 0), cut_sem, base + 2, (me, at[2])),
            remote(view(at[2], 1), view(at[2], 1), cut_sem, base + 3, (me, at[1])),
        ]

    def relay(copies):
        copies[0].wait_recv()
        copies[2].start()
        copies[1].wait_recv()
        copies[3].start()

    def whole(ref):
        def view(owner, piece=None):
            return ref.at[owner] if piece is None else ref.at[owner, pl.ds(piece * half, half)]

        return view

    def attn_view(owner, piece=None):
        start = owner * tokens + core * half
        if piece is None:
            return attn_full.at[span(start, half, half)]
        return attn_full.at[span(start + piece * part, part, part)]

    def slab_view(owner, piece=None):
        if piece is None:
            return grad_rows.at[:, span(owner * slab, slab, slab // 2)]
        return grad_rows.at[:, span(owner * slab + piece * (slab // 2), slab // 2, slab // 2)]

    def to_cuts(src_of, dst_of, base):
        return [remote(src_of(at[k]), dst_of(k), cut_sem, base + k - 1, (me, at[k])) for k in (3, 1, 2)]

    tokens_moved = gather(whole(src_v), source, 0)
    gains_moved = to_cuts(lambda peer: gains, lambda k: gains_all.at[cut], 16)
    small_moved = to_cuts(lambda peer: small, lambda k: small_full.at[cut], 19)
    qkv_moved = []
    for n in range(3):
        qkv_moved += to_cuts(
            lambda peer: w_qkv.at[span(core * half, half, half), span(n * width + peer * own, own, own)],
            lambda k: qkv_v.at[span(cut * tokens + core * half, half, half), pl.ds(n * own, own)],
            22 + 3 * n,
        )
    for copy in gains_moved + tokens_moved[:2] + qkv_moved + small_moved:
        copy.start()
    grad_moved = gather(whole(grad_all), cot_v, 4)
    attn_moved = gather(attn_view, attn_v.at[span(core * half, half, half)], 8)
    slab_moved = gather(slab_view, row_v, 12)
    in_moved = to_cuts(
        lambda peer: w_in.at[span(core * half, half, half), span(peer * width, width, width)],
        lambda k: in_here.at[span(cut * tokens + core * half, half, half)], 31,
    )
    head_moved = to_cuts(
        lambda peer: heads_low.at[span(peer * tokens, tokens, tokens)],
        lambda k: head_out.at[:, span(cut * own, own, own)], 34,
    )

    loads[0].wait()
    lane = lax.broadcasted_iota(jnp.int32, (tokens, 128), 1).astype(F32)
    picked = jnp.where(lane == info[:, 0:1], info[:, 1:2], 0.0)
    down = lax.broadcasted_iota(jnp.int32, (tokens, tokens), 0)
    right = lax.broadcasted_iota(jnp.int32, (tokens, tokens), 1)
    running = mm((down >= right).astype(F32).astype(BF), picked.astype(BF))
    target = info[:, 2:3] + jnp.sum(picked * running, axis=1, keepdims=True) - 1.0
    column = lax.broadcasted_iota(jnp.int32, placer.shape, 1).astype(F32)
    placer[...] = jnp.where(column == target, info[:, 1:2], 0.0).astype(BF)
    slots[...] = mm_tn(placer[...], cot_v[...]).astype(BF).reshape(slots.shape)
    z_moved = []
    for g in range(groups):
        for k in range(1, n_expert):
            peer = jnp.bitwise_xor(me, k)
            z_moved.append(remote(slots.at[g, peer], zbuf.at[g, me], z_sem, g * n_expert + k, (peer, cut)))
            z_moved[-1].start()
        zbuf[g, me] = slots[g, me]
    src_v[cut] = source[...]
    gains_all[cut] = gains[...]
    small_full[cut] = small[...]
    relay(tokens_moved)
    for copy in loads[1:] + own_qkv:
        copy.wait()
    stores = [
        local(cot_v, grad_all.at[cut], store_sem, 0),
        local(attn_v, attn_full.at[span(cut * tokens, tokens, tokens)], store_sem, 1),
        local(in_v, in_here.at[span(cut * tokens, tokens, tokens)], store_sem, 2),
    ]
    for copy in gains_moved:
        copy.wait_recv()

    def normalize(index):
        xhat, _ = norm_parts(src_v[index].astype(F32))
        for n in range(n_cuts):
            cols = slice(n * own, (n + 1) * own)
            norm_v[index, :, cols] = (xhat[:, cols] * gains_all[n, 0:1, :]).astype(BF)

    normalize(cut)
    normalize(at[1])
    normalize(at[2])
    for copy in qkv_moved:
        copy.wait_recv()

    def share(ref, base):
        copies = []
        for k in range(1, n_cuts):
            view = ref.at[span(at[k] * tokens + core * half, half, half)]
            copies.append(remote(view, view, twin_sem, base + k - 1, twin))
            copies[-1].start()
        return copies

    shared = share(qkv_v, 0)
    for copy in tokens_moved[2:]:
        copy.wait_recv()
    for copy in grad_moved[:2] + attn_moved[:2] + in_moved:
        copy.start()
    normalize(at[3])
    for copy in shared:
        copy.wait_recv()

    @pl.loop(0, n_cuts)
    def _(step):
        join_v[step] = mm(norm_v[step], qkv_v[...]).astype(BF)

    stores += [
        local(norm_v, normed, store_sem, 3), local(qkv_v, qkv, store_sem, 4), local(join_v, joined, store_sem, 5),
    ]
    acc[...] = jnp.zeros_like(acc)
    per_group = here // groups
    for copy in z_moved:
        copy.wait_recv()
    for g in range(groups):
        flat = zbuf[g].reshape(n_expert * block, width)
        for j in range(per_group):
            row_v[g * per_group + j] = mm(sort[pl.ds(j * slab, slab), :], flat).astype(BF)
    stores.append(local(row_v, slab_view(cut), store_sem, 6))

    @pl.loop(0, heads)
    def _(head):
        @pl.when(head == 2)
        def _():
            relay(grad_moved)
            relay(attn_moved)
            for copy in slab_moved[:2]:
                copy.start()

        pair = lax.div(head, 2)
        lane = lax.broadcasted_iota(jnp.int32, (1, 128), 1)
        keep = (lax.div(lane, HD) == lax.rem(head, 2)).astype(F32)
        keep_low = keep.astype(BF)
        cols = span(pair * 128, 128, 128)
        k_cols = span(own + pair * 128, 128, 128)
        v_cols = span(2 * own + pair * 128, 128, 128)
        for i in range(n_cuts):
            reach = (i + 1) * tokens
            query = join_v[i, :, cols] * keep_low
            keys = join_v[pl.ds(0, i + 1), :, k_cols].reshape(reach, 128)
            values = join_v[pl.ds(0, i + 1), :, v_cols].reshape(reach, 128)
            scores = mm_nt(keys, query) * scaling
            key_at = lax.broadcasted_iota(jnp.int32, scores.shape, 0)
            query_at = lax.broadcasted_iota(jnp.int32, scores.shape, 1) + i * tokens
            scores = jnp.where(key_at <= query_at, scores, -1e30)
            peak = jnp.max(scores, axis=0, keepdims=True)
            powers = jnp.exp(scores - peak)
            total = jnp.sum(powers, axis=0, keepdims=True)
            lse[head, :, pl.ds(i * tokens, tokens)] = peak + jnp.log(total)
            soft = (powers / total).astype(BF)
            acc[pl.ds(i * tokens, tokens), cols] += mm_tn(soft, values) * keep

    heads_low[...] = acc[...].astype(BF)
    for copy in head_moved:
        copy.start()
    head_out[:, span(cut * own, own, own)] = heads_low[span(cut * tokens, tokens, tokens), :]
    for copy in in_moved:
        copy.wait_recv()
    shared += share(in_here, 3)
    for copy in attn_moved[2:]:
        copy.wait_recv()
    shared += share(attn_full, 6)
    relay(slab_moved)
    for copy in shared[3:] + grad_moved[2:] + slab_moved[2:] + head_moved + small_moved:
        copy.wait_recv()
    for copy in stores:
        copy.wait()
    everything = tokens_moved + gains_moved + small_moved + qkv_moved + grad_moved + attn_moved + slab_moved
    for copy in everything + in_moved + head_moved + z_moved + shared:
        copy.wait_send()


def head(source, gains, small, info, sort, w_qkv, w_attn, w_in, cotangent, here, groups, capacity, n_expert, n_cuts):
    tokens, features = source.shape
    seq_len, own = tokens * n_cuts, features // n_cuts
    heads, slab = own // HD, n_expert * capacity
    block = here // groups * capacity
    any_spec, vmem_spec = pl.BlockSpec(memory_space=pl.ANY), pl.BlockSpec(memory_space=pltpu.VMEM)
    shape, vmem, dma = jax.ShapeDtypeStruct, pltpu.VMEM, pltpu.SemaphoreType.DMA
    slots = n_expert * groups * block
    return pl.pallas_call(
        functools.partial(head_kernel, (heads, HD ** (-0.5), groups, here, slab)),
        name="head",
        out_shape=(
            shape((n_cuts, tokens, features), BF), shape((features, 3 * own), BF), shape((n_cuts, tokens, 3 * own), BF),
            shape((heads, 1, seq_len), F32), shape((tokens, features), BF), shape((features, features), BF),
            shape((features, w_in.shape[1] // n_cuts), BF), shape((n_cuts,) + small.shape, BF),
            shape((n_cuts, tokens, features), BF), shape((here, n_cuts * slab, features), BF),
            shape((tokens, slots), BF), shape((n_cuts,) + gains.shape, F32),
        ),
        in_specs=[vmem_spec] * 5 + [any_spec] * 4,
        out_specs=(any_spec,) * 3 + (vmem_spec,) * 2 + (any_spec,) * 2 + (vmem_spec,) + (any_spec,) * 2 + (vmem_spec,) * 2,
        scratch_shapes=[
            vmem((n_cuts, tokens, features), BF), vmem((features, 3 * own), BF), vmem((n_cuts, tokens, features), BF),
            vmem((n_cuts, tokens, 3 * own), BF), vmem((seq_len, own), F32), vmem((seq_len, own), BF),
            vmem((tokens, features), BF), vmem((tokens, features), BF), vmem((tokens, features), BF),
            vmem((groups, n_expert, block, features), BF), vmem((groups, n_expert, block, features), BF),
            vmem((here, slab, features), BF),
            dma((6,)), dma((7,)), dma((2, 37)), dma((2, 9)), dma((2, groups * n_expert)),
        ],
        compiler_params=pltpu.CompilerParams(
            collective_id=3, has_side_effects=True, vmem_limit_bytes=48 << 20
        ),
        cost_estimate=pl.CostEstimate(flops=8_000_000_000, bytes_accessed=24 << 20, transcendentals=0),
    )(source, gains, small, info, sort, w_qkv, w_attn, w_in, cotangent)


def shards(
    block_input,
    routes,
    kept_mask,
    w_qkv,
    w_attn_out,
    w_in,
    w_out,
    w_router,
    w_mix,
    gain_attn,
    gain_ffn,
    expert_in,
    expert_out,
    cotangent,
):
    tokens, features = block_input.shape
    n_cuts = lax.axis_size("cuts")
    n_expert = lax.axis_size("expert")
    seq_len = tokens * n_cuts
    scaling = HD ** (-0.5)
    own = features // n_cuts
    heads = own // HD
    experts_all = w_router.shape[1]
    experts_here = expert_in.shape[0]
    capacity = 3 * tokens // (2 * experts_all)

    onehot = (routes[:, None] == jnp.arange(experts_all, dtype=jnp.int32)[None, :]).astype(F32)
    fused = n_cuts == 4
    groups = 2 if fused else 1
    per_group = experts_here // groups
    block = per_group * capacity
    owner, local = routes // experts_here, routes % experts_here
    start = (local // per_group) * (n_expert * block) + owner * block + local % per_group * capacity
    if not fused:
        onehot_kept = onehot * kept_mask.astype(F32)[:, None]
        lower_tri = (jnp.arange(tokens)[:, None] >= jnp.arange(tokens)[None, :]).astype(BF)
        running = mm(lower_tri, onehot_kept.astype(BF))
        slot_num = jnp.sum(onehot_kept * running, axis=1) - 1.0
        target = start.astype(F32) + slot_num
        columns = jnp.arange(experts_all * capacity, dtype=jnp.int32).astype(F32)
        placer = ((columns[None, :] == target[:, None]) & (kept_mask[:, None] > 0)).astype(BF)

    def to_owners(rows):
        grid = mm_tn(placer, rows).astype(BF).reshape(groups, n_expert, block, features)
        grid = grid.swapaxes(0, 1).reshape(n_expert, experts_here, capacity, features)
        moved = lax.all_to_all(grid, "expert", split_axis=0, concat_axis=2, tiled=True)
        return lax.all_gather(moved, "cuts", axis=2, tiled=True)[0]

    def to_sources(rows):
        summed = lax.psum_scatter(rows[None].astype(BF), "cuts", scatter_dimension=2, tiled=True)
        moved = lax.all_to_all(summed, "expert", split_axis=2, concat_axis=0, tiled=True)
        return mm(placer, moved.reshape(-1, features))

    inputs = block_input.astype(F32)
    if fused:
        pair = jnp.stack([gain_attn, gain_ffn], axis=0).astype(F32)
        small_here = jnp.concatenate([w_router, w_mix], axis=1)
        small_cols = small_here.shape[1]
        at = np.arange(n_expert * block)
        slab = n_expert * capacity
        goal = at % slab // capacity * block + at // slab * capacity + at % capacity
        sort = np.asarray(goal[:, None] == at[None, :], dtype=BF)
        info = jnp.stack([routes, kept_mask, start], axis=1).astype(F32)
        normed, qkv_here, joined, log_norm, head_out, attn_full, in_here, small_wide, grad_all, grad_rows, placer, gains = head(
            block_input, jnp.pad(pair, ((0, 6), (0, 0))), jnp.pad(small_here, ((0, 0), (0, -small_cols % 128))),
            info, jnp.asarray(sort), w_qkv, w_attn_out, w_in, cotangent,
            experts_here, groups, capacity, n_expert, n_cuts,
        )
        normed, joined = normed.reshape(seq_len, features), joined.reshape(seq_len, 3 * own)
        small_wide = small_wide.reshape(features, -1)
        small_full = small_wide[:, :small_cols]
        gain_one, gain_two = gains[:, 0].reshape(features), gains[:, 1].reshape(features)
    else:
        gains = gather_cuts(jnp.stack([gain_attn, gain_ffn], axis=1)).astype(F32)
        gain_one, gain_two = gains[:, 0], gains[:, 1]
        xhat_one, inv_one = norm_parts(inputs)
        normed = gather_cuts((xhat_one * gain_one).astype(BF))
        qkv_here = lax.all_to_all(
            w_qkv.reshape(own, 3, n_cuts, own), "cuts", split_axis=2, concat_axis=0, tiled=True
        ).reshape(features, 3 * own)
        joined = mm(normed, qkv_here).astype(BF)
        split = joined.reshape(seq_len, 3, heads, HD)
        q_heads, k_heads, v_heads = split[:, 0], split[:, 1], split[:, 2]
        spots = jnp.arange(seq_len, dtype=jnp.int32)
        visible = (spots[None, :] <= spots[:, None])[None]

        def masked_scores():
            scores = jnp.einsum("qhd,khd->hqk", q_heads, k_heads, preferred_element_type=F32) * scaling
            return jnp.where(visible, scores, -1e30)

        scores = masked_scores()
        peak = jnp.max(scores, axis=-1, keepdims=True)
        row_exp = jnp.exp(scores - peak)
        total = jnp.sum(row_exp, axis=-1, keepdims=True)
        weights_p = (row_exp / total).astype(BF)
        heads_here = jnp.einsum("hqk,khd->qhd", weights_p, v_heads, preferred_element_type=F32)
        log_norm = peak + jnp.log(total)
        head_out = rows_to_cuts(heads_here.reshape(seq_len, own).astype(BF))
        attn_full = gather_cuts(w_attn_out)
        small_full = gather_cuts(jnp.concatenate([w_router, w_mix], axis=1))
        grad_all = gather_cuts(cotangent)
        grad_rows = to_owners(cotangent)
        in_here = columns_to_cuts(w_in)
    hidden = inputs + mm(head_out, attn_full)
    xhat_two, inv_two = norm_parts(hidden)
    second = (xhat_two * gain_two).astype(BF)

    logits = mm(second, small_full)
    router_p = softmax_rows(logits[:, :experts_all])
    mixing = softmax_rows(logits[:, experts_all:])
    gate = jnp.sum(router_p * onehot, axis=1)
    grad = cotangent.astype(F32)
    d_moe = grad * mixing[:, 1:2]

    if fused:
        slots = mm_tn(placer, second).astype(BF).reshape(groups, n_expert, block, features)
        sums, returned, second_all, activ_low, d_up, d_dense_all, rows_in, d_rows, expert_low, d_first = middle(
            slots, second, grad_all, grad_rows, in_here, w_out, small_wide,
            jnp.asarray(sort), jnp.asarray(sort.T), expert_in, expert_out, n_expert, n_cuts,
        )
        dense, d_second_ffn = sums[0], sums[1]
        second_all, activ_low, d_up, d_dense_all = (
            v.reshape(seq_len, -1) for v in (second_all, activ_low, d_up, d_dense_all)
        )
        g_out = mm_tn(activ_low, d_dense_all)
        g_in = mm_tn(second_all, d_up)
        g_expert_out = jnp.einsum("erh,erd->ehd", expert_low, d_rows, preferred_element_type=F32)
        g_expert_in = jnp.einsum("erd,erh->edh", rows_in, d_first, preferred_element_type=F32)
        picked = mm(placer, returned[0].reshape(-1, features))
        d_picked_in = mm(placer, returned[1].reshape(-1, features))
    else:
        rows_in = to_owners(second)
        row_logits = jnp.einsum("erd,dk->erk", rows_in, small_full, preferred_element_type=F32)
        ids = lax.axis_index("expert") * experts_here + jnp.arange(experts_here, dtype=jnp.int32)
        is_here = (jnp.arange(experts_all, dtype=jnp.int32)[None, :] == ids[:, None]).astype(F32)
        row_gate = jnp.sum(
            softmax_rows(row_logits[:, :, :experts_all]) * is_here[:, None, :], axis=2, keepdims=True
        )
        row_mixing = softmax_rows(row_logits[:, :, experts_all:])[:, :, 1:2]
        d_rows = (grad_rows.astype(F32) * row_mixing * row_gate).astype(BF)

        first = jnp.einsum("erd,edh->erh", rows_in, expert_in, preferred_element_type=F32)
        expert_act, expert_pull = jax.vjp(jax.nn.gelu, first)
        expert_low = expert_act.astype(BF)
        partial_out = jnp.einsum("erh,ehd->erd", expert_low, expert_out, preferred_element_type=F32)
        picked = to_sources(partial_out)

        second_all = gather_cuts(second)
        mixing_all = softmax_rows(mm(second_all, small_full[:, experts_all:]))
        d_dense_all = (grad_all.astype(F32) * mixing_all[:, 0:1]).astype(BF)
        up_proj = mm(second_all, in_here)
        activ, gelu_pull = jax.vjp(jax.nn.gelu, up_proj)
        activ_low = activ.astype(BF)
        dense = scatter_cuts(mm(activ_low, w_out)).astype(F32)
        d_activ = mm_nt(d_dense_all, w_out)
        g_out = mm_tn(activ_low, d_dense_all)
        d_up = gelu_pull(d_activ)[0].astype(BF)
        g_in = mm_tn(second_all, d_up)
        d_second_ffn = scatter_cuts(mm_nt(d_up, in_here)).astype(F32)

        d_expert_act = jnp.einsum("erd,ehd->erh", d_rows, expert_out, preferred_element_type=F32)
        d_first = expert_pull(d_expert_act)[0].astype(BF)
        d_rows_in = jnp.einsum("erh,edh->erd", d_first, expert_in, preferred_element_type=F32)
        g_expert_out = jnp.einsum("erh,erd->ehd", expert_low, d_rows, preferred_element_type=F32)
        g_expert_in = jnp.einsum("erd,erh->edh", rows_in, d_first, preferred_element_type=F32)
        d_picked_in = to_sources(d_rows_in)

    moe_val = gate[:, None] * picked
    block_out = (hidden + mixing[:, 0:1] * dense + mixing[:, 1:2] * moe_val).astype(BF)
    d_mixing = jnp.stack([jnp.sum(grad * dense, axis=1), jnp.sum(grad * moe_val, axis=1)], axis=1)
    d_gate = jnp.sum(d_moe * picked, axis=1)
    d_router = router_p * (onehot - gate[:, None]) * d_gate[:, None]
    d_mix = mixing * (d_mixing - jnp.sum(mixing * d_mixing, axis=1, keepdims=True))
    d_small = jnp.concatenate([d_router, d_mix], axis=1).astype(BF)
    g_small = mm_tn(d_small, second)
    d_second = d_second_ffn + mm_nt(d_small, small_full) + d_picked_in
    d_hidden_norm, g_gain_two = norm_back(d_second, xhat_two, inv_two, gain_two)
    d_hidden = grad + d_hidden_norm
    d_attn = d_hidden.astype(BF)
    g_attn_out = mm_tn(head_out, d_attn)
    d_head_rows = mm_nt(d_attn, attn_full).astype(BF)
    if fused:
        tiny = jnp.concatenate([g_small, g_gain_two[None, :]], axis=0)
        tiny = jnp.pad(tiny, ((0, -tiny.shape[0] % 8), (0, 0)))
        d_block_input, s_in, s_out, s_qkv, s_attn_out, tiny, late = tail(
            g_in.astype(BF), g_out.astype(BF), g_attn_out.astype(BF), d_head_rows, joined, log_norm[:, 0], normed,
            qkv_here, block_input, gain_one[None, :], d_hidden, tiny, n_expert, n_cuts,
        )
        swap = [
            ((flat % n_expert) * n_cuts + flat // n_expert, flat) for flat in range(n_expert * n_cuts)
        ]
        s_out = lax.ppermute(s_out, ("expert", "cuts"), swap).astype(F32)
        s_in = s_in.swapaxes(0, 1).reshape(-1, w_in.shape[1]).astype(F32)
        s_qkv = s_qkv.reshape(n_cuts, -1, 3, own).transpose(1, 2, 0, 3).reshape(-1, 3 * features).astype(F32)
        width = features // (n_expert * n_cuts)
        spot = lax.axis_index("cuts") * width
        s_tiny = lax.dynamic_slice_in_dim(tiny, spot, width, axis=1)
        s_late = lax.dynamic_slice_in_dim(late, spot, width, axis=1)
        return (
            block_out,
            d_block_input,
            s_qkv,
            s_attn_out,
            s_in,
            s_out,
            s_tiny[:experts_all].T,
            s_tiny[experts_all : experts_all + 2].T,
            s_late[0],
            s_tiny[experts_all + 2],
            g_expert_in,
            g_expert_out,
        )
    d_heads = columns_to_cuts(d_head_rows).reshape(seq_len, heads, HD)

    soft_p = jnp.exp(masked_scores() - log_norm)
    d_soft = jnp.einsum("qhd,khd->hqk", d_heads, v_heads, preferred_element_type=F32)
    delta = jnp.sum(soft_p * d_soft, axis=-1, keepdims=True)
    d_scores = (soft_p * (d_soft - delta)).astype(BF)
    d_query = jnp.einsum("hqk,khd->qhd", d_scores, k_heads, preferred_element_type=F32) * scaling
    d_keys = jnp.einsum("hqk,qhd->khd", d_scores, q_heads, preferred_element_type=F32) * scaling
    d_values = jnp.einsum("hqk,qhd->khd", soft_p.astype(BF), d_heads, preferred_element_type=F32)
    d_joined = jnp.stack([d_query, d_keys, d_values], axis=1).reshape(seq_len, 3 * own).astype(BF)
    g_qkv = mm_tn(normed, d_joined)
    d_normed = scatter_cuts(mm_nt(d_joined, qkv_here)).astype(F32)
    d_input_norm, g_gain_one = norm_back(d_normed, xhat_one, inv_one, gain_one)
    d_block_input = d_hidden + d_input_norm

    def over_experts(part):
        return lax.psum_scatter(part.astype(BF), "expert", scatter_dimension=0, tiled=True)

    s_in = rows_to_cuts(over_experts(g_in)).astype(F32)
    s_out = over_experts(g_out)
    swap = [
        ((flat % n_expert) * n_cuts + flat // n_expert, flat) for flat in range(n_expert * n_cuts)
    ]
    s_out = lax.ppermute(s_out, ("expert", "cuts"), swap).astype(F32)
    s_qkv = over_experts(g_qkv)
    deep = s_qkv.shape[0]
    s_qkv = lax.all_to_all(
        s_qkv.reshape(deep, 3, 1, own), "cuts", split_axis=0, concat_axis=2, tiled=True
    )
    s_qkv = s_qkv.reshape(-1, 3 * features).astype(F32)
    s_attn_out = scatter_cuts(over_experts(g_attn_out)).astype(F32)
    tiny = jnp.concatenate([g_small, g_gain_one[None, :], g_gain_two[None, :]], axis=0)
    tiny = jnp.pad(tiny, ((0, -tiny.shape[0] % 8), (0, 0)))
    tiny = sum_small(tiny, n_expert, n_cuts)
    width = features // (n_expert * n_cuts)
    s_tiny = lax.dynamic_slice_in_dim(tiny, lax.axis_index("cuts") * width, width, axis=1)
    return (
        block_out,
        d_block_input,
        s_qkv,
        s_attn_out,
        s_in,
        s_out,
        s_tiny[:experts_all].T,
        s_tiny[experts_all : experts_all + 2].T,
        s_tiny[experts_all + 2],
        s_tiny[experts_all + 3],
        g_expert_in,
        g_expert_out,
    )


def solution(mesh):
    both = ("expert", "cuts")
    placed = (
        P(both, None),
        P(both),
        P(both),
        P("cuts", None),
        P("cuts", None),
        P("cuts", None),
        P("cuts", None),
        P("cuts", None),
        P("cuts", None),
        P("cuts"),
        P("cuts"),
        P("expert", None, "cuts"),
        P("expert", "cuts", None),
        P(both, None),
    )
    results = (
        P(both, None),
        P(both, None),
        P(both, None),
        P(both, None),
        P(both, None),
        P(both, None),
        P(both, None),
        P(both, None),
        P(both),
        P(both),
        P("expert", None, "cuts"),
        P("expert", "cuts", None),
    )
    return jax.shard_map(
        shards, mesh=mesh, in_specs=placed, out_specs=results, check_vma=False
    )
```

```python
import functools
import math

import jax
import jax.numpy as jnp
import numpy as np
from jax import lax
from jax.experimental import pallas as pl
from jax.experimental.pallas import tpu as pltpu
from jax.sharding import PartitionSpec as P

HD = 64
BF = jnp.bfloat16
F32 = jnp.float32
MESH = pl.DeviceIdType.MESH


def norm_parts(values):
    center = values - jnp.mean(values, axis=-1, keepdims=True)
    spread = jnp.mean(center * center, axis=-1, keepdims=True)
    inv = lax.rsqrt(spread + 1e-05)
    return center * inv, inv


def norm_back(grad, xhat, inv, gain):
    q = grad * gain
    mean_q = jnp.mean(q, axis=-1, keepdims=True)
    mean_qx = jnp.mean(q * xhat, axis=-1, keepdims=True)
    return (q - mean_q - xhat * mean_qx) * inv, jnp.sum(grad * xhat, axis=0)


def mm(left, right):
    return jnp.dot(left, right, preferred_element_type=F32)


def mm_nt(left, right):
    return lax.dot_general(left, right, (((1,), (1,)), ((), ())), preferred_element_type=F32)


def mm_tn(left, right):
    return lax.dot_general(left, right, (((0,), (0,)), ((), ())), preferred_element_type=F32)


def softmax_rows(logits):
    shifted = logits - jnp.max(logits, axis=-1, keepdims=True)
    row_exp = jnp.exp(shifted)
    return row_exp / jnp.sum(row_exp, axis=-1, keepdims=True)


def gather_cuts(rows):
    return lax.all_gather(rows, "cuts", axis=0, tiled=True)


def scatter_cuts(rows):
    return lax.psum_scatter(rows.astype(BF), "cuts", scatter_dimension=0, tiled=True)


def columns_to_cuts(rows):
    return lax.all_to_all(rows, "cuts", split_axis=1, concat_axis=0, tiled=True)


def rows_to_cuts(rows):
    return lax.all_to_all(rows, "cuts", split_axis=0, concat_axis=1, tiled=True)


def ring_mod(index, count):
    return lax.rem(index, count)


def small_kernel(n_expert, n_cuts, src, out, by_expert, mine, by_cuts, send_a, recv_a, send_b, recv_b):
    me, cut = lax.axis_index("expert"), lax.axis_index("cuts")
    width = out.shape[1]
    barrier = pltpu.get_barrier_semaphore()
    for step in range(1, n_expert):
        peer = ring_mod(me + step, n_expert)
        pl.semaphore_signal(barrier, inc=1, device_id=(peer, cut), device_id_type=MESH)
    for step in range(1, n_cuts):
        peer = ring_mod(cut + step, n_cuts)
        pl.semaphore_signal(barrier, inc=1, device_id=(me, peer), device_id_type=MESH)
    pl.semaphore_wait(barrier, n_expert + n_cuts - 2)

    def part(owner):
        return src.at[:, pl.ds(pl.multiple_of(owner * width, 128), width)]

    copies = []
    for step in range(1, n_expert):
        peer = ring_mod(me + step, n_expert)
        copies.append(
            pltpu.make_async_remote_copy(
                src_ref=part(peer),
                dst_ref=by_expert.at[step],
                send_sem=send_a.at[step],
                recv_sem=recv_a.at[step],
                device_id=(peer, cut),
                device_id_type=MESH,
            )
        )
        copies[-1].start()
    total = src[:, pl.ds(pl.multiple_of(me * width, 128), width)]
    for step in range(1, n_expert):
        copies[step - 1].wait()
        total = total + by_expert[step]
    mine[...] = total
    copies = []
    for step in range(1, n_cuts):
        peer = ring_mod(cut + step, n_cuts)
        copies.append(
            pltpu.make_async_remote_copy(
                src_ref=mine,
                dst_ref=by_cuts.at[step],
                send_sem=send_b.at[step],
                recv_sem=recv_b.at[step],
                device_id=(me, peer),
                device_id_type=MESH,
            )
        )
        copies[-1].start()
    for step in range(1, n_cuts):
        copies[step - 1].wait()
        total = total + by_cuts[step]
    out[...] = total


def sum_small(values, n_expert, n_cuts):
    rows, features = values.shape
    width = features // n_expert
    pad = -width % 128
    if pad:
        values = jnp.pad(values.reshape(rows, n_expert, width), ((0, 0), (0, 0), (0, pad)))
        values = values.reshape(rows, n_expert * (width + pad))
    wide = width + pad
    summed = pl.pallas_call(
        functools.partial(small_kernel, n_expert, n_cuts),
        name="sum_small",
        out_shape=jax.ShapeDtypeStruct((rows, wide), F32),
        in_specs=[pl.BlockSpec(memory_space=pltpu.VMEM)],
        out_specs=pl.BlockSpec(memory_space=pltpu.VMEM),
        scratch_shapes=[
            pltpu.VMEM((n_expert, rows, wide), F32),
            pltpu.VMEM((rows, wide), F32),
            pltpu.VMEM((n_cuts, rows, wide), F32),
            pltpu.SemaphoreType.DMA((n_expert,)),
            pltpu.SemaphoreType.DMA((n_expert,)),
            pltpu.SemaphoreType.DMA((n_cuts,)),
            pltpu.SemaphoreType.DMA((n_cuts,)),
        ],
        compiler_params=pltpu.CompilerParams(collective_id=0, has_side_effects=True),
    )(values)
    return summed[:, :width]


def dot_nt(left, right):
    return lax.dot_general(left, right, (((1,), (1,)), ((), ())), preferred_element_type=F32)


def tile_of(step, size):
    return pl.ds(pl.multiple_of(step * size, size), size)


def lane_softmax(logits, low, high):
    lane = lax.broadcasted_iota(jnp.int32, logits.shape, 1)
    inside = (lane >= low) & (lane < high)
    kept = jnp.where(inside, logits, -1e30)
    powers = jnp.exp(kept - jnp.max(kept, axis=1, keepdims=True))
    powers = jnp.where(inside, powers, 0.0)
    return powers / jnp.sum(powers, axis=1, keepdims=True), lane


def mlp_both(rows, d_rows, w_up, w_down, act, d_up, write):
    root, cubic = math.sqrt(2.0 / math.pi), 0.044715

    @pl.loop(0, act.shape[1] // 256)
    def _(step):
        span = tile_of(step, 256)
        up = mm(rows[...], w_up[:, span])
        d_act = dot_nt(d_rows[...], w_down[span, :])
        square = up * up
        bent = jnp.tanh(root * up * (1.0 + cubic * square))
        half = 0.5 * (1.0 + bent)
        act[:, span] = (up * half).astype(BF)
        slope = half + 0.5 * up * (1.0 - bent * bent) * (root + 3.0 * root * cubic * square)
        d_up[:, span] = (d_act * slope).astype(BF)

    @pl.loop(0, w_up.shape[0] // 256)
    def _(step):
        span = tile_of(step, 256)
        write(span, mm(act[...], w_down[:, span]), dot_nt(d_up[...], w_up[span, :]))


def middle_kernel(
    sizes, slots, second, grad_all, grad_rows, w_in, w_out, small, sort, e_in, e_out,
    sums, ret_a, ret_b, o_in, o_out, rows_in, d_rows_all, act_e_all, d_first_all,
    sec, grd, win, wout, act, d_up, part_a, part_b, ffn_x, ffn_y, ffn_qa, ffn_qb,
    zbuf, rows, g_rows, d_rows, act_e, d_first, wi_e, wo_e, out_a, out_b, row_x, row_y, row_qa, row_qb, sorted_back, send_back,
    twin_in, level_in, fin_in,
    load_sem, weight_sem, store_sem, store_e_sem, z_sem, ag_sem, eag_sem, frs_sem, ers_sem, zr_sem,
    twin_sem, level_sem, fin_sem,
):
    n_expert, groups, here, slab = sizes
    me, cut = lax.axis_index("expert"), lax.axis_index("cuts")
    at_x, at_y, at_d = (jnp.bitwise_xor(cut, k) for k in (1, 2, 3))
    block = zbuf.shape[2]
    per_group = here // groups
    experts_all = n_expert * here

    def load(src, dst, index):
        copy = pltpu.make_async_copy(src, dst, load_sem.at[index])
        copy.start()
        return copy

    def remote(src, dst, sems, index, peer):
        return pltpu.make_async_remote_copy(
            src_ref=src, dst_ref=dst, send_sem=sems.at[0, index], recv_sem=sems.at[1, index],
            device_id=peer, device_id_type=MESH,
        )

    def send(src, dst, sems, index, peer):
        copy = remote(src, dst, sems, index, peer)
        copy.start()
        return copy

    loads = [
        load(second, sec.at[cut], 0), load(w_in, win, 1), load(w_out, wout, 2), load(grad_all, grd, 3),
    ]

    def fetch_expert(i):
        slot = i % 2
        copies = [
            pltpu.make_async_copy(e_in.at[i], wi_e.at[slot], weight_sem.at[0, slot]),
            pltpu.make_async_copy(e_out.at[i], wo_e.at[slot], weight_sem.at[1, slot]),
            pltpu.make_async_copy(grad_rows.at[i], g_rows.at[slot], weight_sem.at[2, slot]),
        ]
        for copy in copies:
            copy.start()
        return copies

    fetched = [fetch_expert(0), fetch_expert(1)]
    barrier = pltpu.get_barrier_semaphore()
    for k in range(1, n_expert):
        pl.semaphore_signal(barrier, inc=1, device_id=(jnp.bitwise_xor(me, k), cut), device_id_type=MESH)
    for peer in (at_x, at_y):
        pl.semaphore_signal(barrier, inc=1, device_id=(me, peer), device_id_type=MESH)
    pl.semaphore_signal(barrier, inc=1, device_id=(me, at_d), device_id_type=MESH)
    pl.semaphore_wait(barrier, n_expert + 2)
    core, level = lax.rem(me, 2), lax.div(me, 2)
    levels = n_expert // 2

    z_copies = []
    for g in range(groups):
        for k in range(1, n_expert):
            peer = jnp.bitwise_xor(me, k)
            z_copies.append(send(slots.at[g, peer], zbuf.at[g, me], z_sem, g * n_expert + k, (peer, cut)))
    loads[0].wait()
    ag = [
        send(sec.at[cut], sec.at[cut], ag_sem, 0, (me, at_x)),
        send(sec.at[cut], sec.at[cut], ag_sem, 1, (me, at_y)),
    ]
    half = sec.shape[1] // 2
    ag += [
        remote(sec.at[at_x, pl.ds(0, half)], sec.at[at_x, pl.ds(0, half)], ag_sem, 2, (me, at_y)),
        remote(sec.at[at_y, pl.ds(half, half)], sec.at[at_y, pl.ds(half, half)], ag_sem, 3, (me, at_x)),
    ]
    for g in range(groups):
        zbuf[g, me] = slots[g, me]
    def ffn_block(which, owner):
        mixing, lane = lane_softmax(mm(sec[owner], small[...]), experts_all, experts_all + 2)
        first_mix = jnp.sum(jnp.where(lane == experts_all, mixing, 0.0), axis=1, keepdims=True)
        grd[owner] = (grd[owner].astype(F32) * first_mix).astype(BF)

        def write(span, out, d_row):
            @pl.when(which == 0)
            def _():
                sums[0, :, span] = out
                sums[1, :, span] = d_row

            part_a[which, :, span] = out.astype(BF)
            part_b[which, :, span] = d_row.astype(BF)

        mlp_both(sec.at[owner], grd.at[owner], win, wout, act.at[owner], d_up.at[owner], write)

    def level_rows(index, half):
        return pl.ds(pl.multiple_of(index * 256 + half * 128, 128), 128)

    def weight_grad(m, left, right, held):
        @pl.loop(0, levels)
        def _(step):
            span = tile_of(step, 256)
            lhs = left[:, :, span].reshape(-1, 256)
            held[span, :] = mm_tn(lhs, right[...].reshape(-1, right.shape[2])).astype(BF)

        return [
            send(held.at[level_rows(n, 1 - core)], twin_in.at[m, n], twin_sem, m * levels + n, (jnp.bitwise_xor(me, 1), cut))
            for n in range(levels)
        ]

    def weight_sum(m, held, twins):
        for copy in twins:
            copy.wait_recv()

        @pl.loop(0, levels)
        def _(step):
            here_rows = level_rows(step, core)
            held[here_rows, :] = (held[here_rows, :].astype(F32) + twin_in[m, step].astype(F32)).astype(BF)

        copies = []
        for k in range(1, levels):
            peer = jnp.bitwise_xor(level, k)
            copies.append(
                send(
                    held.at[level_rows(peer, core)], level_in.at[m, k - 1], level_sem, m * (levels - 1) + k - 1,
                    (2 * peer + core, cut),
                )
            )
        return copies

    def weight_total(m, held, copies):
        for copy in copies:
            copy.wait_recv()
        total = held[level_rows(level, core), :].astype(F32)
        for k in range(1, levels):
            total = total + level_in[m, k - 1].astype(F32)
        return total.astype(BF)

    for copy in loads[1:]:
        copy.wait()
    def slab_of(owner):
        return pl.ds(pl.multiple_of(owner * slab, slab), slab)

    eag = {}
    cut_half = slab // 2
    for i in range(here):
        mine = rows.at[i, slab_of(cut)]
        from_x = rows.at[i, pl.ds(pl.multiple_of(at_x * slab, slab), cut_half)]
        from_y = rows.at[i, pl.ds(pl.multiple_of(at_y * slab + cut_half, cut_half), cut_half)]
        eag[i] = [
            remote(mine, mine, eag_sem, 4 * i, (me, at_x)),
            remote(mine, mine, eag_sem, 4 * i + 1, (me, at_y)),
            remote(from_x, from_x, eag_sem, 4 * i + 2, (me, at_y)),
            remote(from_y, from_y, eag_sem, 4 * i + 3, (me, at_x)),
        ]

    def relay(copies):
        copies[0].wait_recv()
        copies[2].start()
        copies[1].wait_recv()
        copies[3].start()

    @pl.loop(0, sec.shape[0])
    def _(which):
        @pl.when(which == 1)
        def _():
            relay(ag)

        @pl.when(which == 2)
        def _():
            for g in range(groups):
                for k in range(1, n_expert):
                    z_copies[g * (n_expert - 1) + k - 1].wait_recv()
                flat = zbuf[g].reshape(n_expert * block, zbuf.shape[3])
                for j in range(per_group):
                    i = g * per_group + j
                    rows[i, slab_of(cut)] = mm(sort[pl.ds(j * slab, slab), :], flat).astype(BF)
                    eag[i][0].start()
                    eag[i][1].start()

        @pl.when(which == 3)
        def _():
            ag[2].wait_recv()
            ag[3].wait_recv()
            relay(eag[0])

        ffn_block(which, jnp.bitwise_xor(cut, which))

    twins_in = weight_grad(0, sec, d_up, win)
    expert_stores = {}
    ers = {}

    def expert(i):
        slot = i % 2
        if i >= 2:
            for copy in expert_stores[i - 2]:
                copy.wait()
        for copy in fetched[i]:
            copy.wait()
        logits = mm(rows[i], small[...])
        router, lane = lane_softmax(logits, 0, experts_all)
        gate = jnp.sum(jnp.where(lane == me * here + i, router, 0.0), axis=1, keepdims=True)
        mixing, lane = lane_softmax(logits, experts_all, experts_all + 2)
        mixing = jnp.sum(jnp.where(lane == experts_all + 1, mixing, 0.0), axis=1, keepdims=True)
        d_rows[slot] = (g_rows[slot].astype(F32) * mixing * gate).astype(BF)

        def write(span, out, d_row):
            out_a[i, :, span] = out.astype(BF)
            out_b[i, :, span] = d_row.astype(BF)

        mlp_both(rows.at[i], d_rows.at[slot], wi_e.at[slot], wo_e.at[slot], act_e.at[slot], d_first.at[slot], write)
        expert_stores[i] = []
        for n, (src, dst) in enumerate(((d_rows, d_rows_all), (act_e, act_e_all), (d_first, d_first_all))):
            copy = pltpu.make_async_copy(src.at[slot], dst.at[i], store_e_sem.at[n, slot])
            copy.start()
            expert_stores[i].append(copy)
        ers[i] = [
            send(out_a.at[i, slab_of(at_x)], row_x.at[i, 0], ers_sem, 6 * i, (me, at_x)),
            send(out_a.at[i, slab_of(at_d)], row_x.at[i, 1], ers_sem, 6 * i + 1, (me, at_x)),
            send(out_b.at[i, slab_of(at_y)], row_y.at[i, 0], ers_sem, 6 * i + 2, (me, at_y)),
            send(out_b.at[i, slab_of(at_d)], row_y.at[i, 1], ers_sem, 6 * i + 3, (me, at_y)),
        ]

    def add_into(ref, *others):
        total = ref[...].astype(F32)
        for other in others:
            total = total + other[...].astype(F32)
        ref[...] = total.astype(BF)

    def pass_on(i):
        for copy in ers[i][:4]:
            copy.wait_recv()
        add_into(out_a.at[i, slab_of(at_y)], row_x.at[i, 1])
        add_into(out_b.at[i, slab_of(at_x)], row_y.at[i, 1])
        ers[i] += [
            send(out_a.at[i, slab_of(at_y)], row_qa.at[i], ers_sem, 6 * i + 4, (me, at_y)),
            send(out_b.at[i, slab_of(at_x)], row_qb.at[i], ers_sem, 6 * i + 5, (me, at_x)),
        ]

    back_copies = []

    def finish(i):
        ers[i][4].wait_recv()
        ers[i][5].wait_recv()
        for n, (out, near, far) in enumerate(((out_a, row_x, row_qa), (out_b, row_y, row_qb))):
            total = out[i, slab_of(cut)].astype(F32) + near[i, 0].astype(F32) + far[i].astype(F32)
            sorted_back[n, i] = total.astype(BF)
        if (i + 1) % per_group == 0:
            g = i // per_group
            for n in range(2):
                flat = sorted_back[n, pl.ds(g * per_group, per_group)].reshape(per_group * slab, -1)
                placed = mm_tn(sort[...], flat).astype(BF)
                send_back[n, g] = placed.reshape(n_expert, block, -1)
                (ret_a, ret_b)[n][g, me] = send_back[n, g, me]
                for k in range(1, n_expert):
                    peer = jnp.bitwise_xor(me, k)
                    back_copies.append(
                        send(
                            send_back.at[n, g, peer], (ret_a, ret_b)[n].at[g, me], zr_sem,
                            (n * groups + g) * n_expert + k, (peer, cut),
                        )
                    )

    for i in range(here):
        if i + 1 < here:
            relay(eag[i + 1])
        eag[i][2].wait_recv()
        eag[i][3].wait_recv()
        expert(i)
        if i + 2 < here:
            fetched.append(fetch_expert(i + 2))
        if i == 0:
            levels_in = weight_sum(0, win, twins_in)
            twins_out = weight_grad(1, act, grd, wout)
        if i == here - 1:
            frs = [
                send(part_a.at[1], ffn_x.at[0], frs_sem, 0, (me, at_x)),
                send(part_a.at[3], ffn_x.at[1], frs_sem, 1, (me, at_x)),
                send(part_b.at[2], ffn_y.at[0], frs_sem, 2, (me, at_y)),
                send(part_b.at[3], ffn_y.at[1], frs_sem, 3, (me, at_y)),
            ]
        if i == 1:
            levels_out = weight_sum(1, wout, twins_out)
        if i >= 1:
            pass_on(i - 1)
        if i >= 2:
            finish(i - 2)
    rows_store = pltpu.make_async_copy(rows, rows_in, store_sem.at[0])
    rows_store.start()
    pass_on(here - 1)
    finish(here - 2)
    finish(here - 1)
    for copy in frs[:4]:
        copy.wait_recv()
    add_into(part_a.at[2], ffn_x.at[1])
    add_into(part_b.at[1], ffn_y.at[1])
    frs += [
        send(part_a.at[2], ffn_qa, frs_sem, 4, (me, at_y)),
        send(part_b.at[1], ffn_qb, frs_sem, 5, (me, at_x)),
    ]
    fin_in[...] = weight_total(0, win, levels_in).reshape(fin_in.shape)
    fin_copies = []
    for k, peer in ((1, at_x), (2, at_y), (3, at_d)):
        fin_copies.append(send(fin_in.at[peer], o_in.at[cut], fin_sem, k - 1, (me, peer)))
    o_in[cut] = fin_in[cut]
    o_out[...] = weight_total(1, wout, levels_out)
    frs[4].wait_recv()
    frs[5].wait_recv()
    sums[0] = sums[0] + ffn_x[0].astype(F32) + ffn_qa[...].astype(F32)
    sums[1] = sums[1] + ffn_y[0].astype(F32) + ffn_qb[...].astype(F32)
    for copy in back_copies + fin_copies:
        copy.wait_recv()
    for copy in z_copies + ag + frs + back_copies + fin_copies + twins_in + twins_out + levels_in + levels_out:
        copy.wait_send()
    for i in range(here):
        for copy in eag[i] + ers[i]:
            copy.wait_send()
    for i in (here - 2, here - 1):
        for copy in expert_stores[i]:
            copy.wait()
    rows_store.wait()


def middle(slots, second, grad_all, grad_rows, w_in, w_out, small, sort, e_in, e_out, n_expert, n_cuts):
    groups, _, block, width = slots.shape
    tokens = second.shape[0]
    here, _, hidden = e_in.shape
    ffn = w_in.shape[1]
    slab = n_expert * block * groups // here
    rows = n_cuts * slab
    levels, deep = n_expert // 2, width // n_expert
    any_spec, vmem_spec = pl.BlockSpec(memory_space=pl.ANY), pl.BlockSpec(memory_space=pltpu.VMEM)
    shape = jax.ShapeDtypeStruct
    dma = pltpu.SemaphoreType.DMA
    flops = 8 * (n_cuts * tokens * ffn + here * rows * hidden) * width
    return pl.pallas_call(
        functools.partial(middle_kernel, (n_expert, groups, here, slab)),
        name="middle",
        out_shape=(
            shape((2, tokens, width), F32), shape((groups, n_expert, block, width), BF),
            shape((groups, n_expert, block, width), BF), shape((n_cuts, deep // n_cuts, ffn), BF), shape((deep, width), BF),
            shape((here, rows, width), BF), shape((here, rows, width), BF),
            shape((here, rows, hidden), BF), shape((here, rows, hidden), BF),
        ),
        in_specs=[vmem_spec] + [any_spec] * 5 + [vmem_spec] * 2 + [any_spec] * 2,
        out_specs=(vmem_spec,) * 5 + (any_spec,) * 4,
        scratch_shapes=[
            pltpu.VMEM((n_cuts, tokens, width), BF), pltpu.VMEM((n_cuts, tokens, width), BF),
            pltpu.VMEM((width, ffn), BF), pltpu.VMEM((ffn, width), BF),
            pltpu.VMEM((n_cuts, tokens, ffn), BF), pltpu.VMEM((n_cuts, tokens, ffn), BF),
            pltpu.VMEM((n_cuts, tokens, width), BF), pltpu.VMEM((n_cuts, tokens, width), BF),
            pltpu.VMEM((2, tokens, width), BF), pltpu.VMEM((2, tokens, width), BF),
            pltpu.VMEM((tokens, width), BF), pltpu.VMEM((tokens, width), BF),
            pltpu.VMEM((groups, n_expert, block, width), BF), pltpu.VMEM((here, rows, width), BF),
            pltpu.VMEM((2, rows, width), BF), pltpu.VMEM((2, rows, width), BF),
            pltpu.VMEM((2, rows, hidden), BF), pltpu.VMEM((2, rows, hidden), BF),
            pltpu.VMEM((2, width, hidden), BF), pltpu.VMEM((2, hidden, width), BF),
            pltpu.VMEM((here, rows, width), BF), pltpu.VMEM((here, rows, width), BF),
            pltpu.VMEM((here, 2, slab, width), BF), pltpu.VMEM((here, 2, slab, width), BF),
            pltpu.VMEM((here, slab, width), BF), pltpu.VMEM((here, slab, width), BF),
            pltpu.VMEM((2, here, slab, width), BF), pltpu.VMEM((2, groups, n_expert, block, width), BF),
            pltpu.VMEM((2, levels, deep, width), BF), pltpu.VMEM((2, levels - 1, deep, width), BF),
            pltpu.VMEM((n_cuts, deep // n_cuts, ffn), BF),
            dma((4,)), dma((3, 2)), dma((1,)), dma((3, 2)),
            dma((2, groups * n_expert)), dma((2, 4)), dma((2, 4 * here)), dma((2, 6)), dma((2, 6 * here)),
            dma((2, 2 * groups * n_expert)),
            dma((2, 2 * levels)), dma((2, 2 * (levels - 1))), dma((2, 3)),
        ],
        compiler_params=pltpu.CompilerParams(
            collective_id=1, has_side_effects=True, vmem_limit_bytes=67_000_000
        ),
        cost_estimate=pl.CostEstimate(flops=flops, bytes_accessed=48 << 20, transcendentals=0),
    )(slots, second, grad_all, grad_rows, w_in, w_out, small, sort, e_in, e_out)


def tail_kernel(
    heads, scaling, g_attn, d_heads, joined, lse, normed, qkv, source, gain, d_hidden, tiny,
    d_source, o_qkv, o_attn, o_tiny, o_gain,
    core_in, own, a_in, a_z, a_mine, gq, core_q, own_q, z_q, fin_q,
    dh, dj, acc_q, acc_k, acc_v, dn, dn_in, norm_v, qkv_v, tiny_e, tiny_m, tiny_c, late, late_e, late_m, late_c,
    load_sem, core_sem, z_sem, cut_sem, te_sem, tc_sem,
):
    me, cut = lax.axis_index("expert"), lax.axis_index("cuts")
    core, level = lax.rem(me, 2), lax.div(me, 2)
    other = 1 - core
    n_cuts, tokens, width = dh.shape
    n_expert = tiny_e.shape[0]
    levels = n_expert // 2
    twin = (jnp.bitwise_xor(me, 1), cut)

    def send(src, dst, sems, index, peer):
        copy = pltpu.make_async_remote_copy(
            src_ref=src, dst_ref=dst, send_sem=sems.at[0, index], recv_sem=sems.at[1, index],
            device_id=peer, device_id_type=MESH,
        )
        copy.start()
        return copy

    def load(src, dst, index):
        copy = pltpu.make_async_copy(src, dst, load_sem.at[index])
        copy.start()
        return copy

    mine = load(g_attn.at[:, core], own, 0)
    later = [load(normed, norm_v, 1), load(qkv, qkv_v, 2)]
    barrier = pltpu.get_barrier_semaphore()
    for k in range(1, n_expert):
        pl.semaphore_signal(barrier, inc=1, device_id=(jnp.bitwise_xor(me, k), cut), device_id_type=MESH)
    for k in range(1, n_cuts):
        pl.semaphore_signal(barrier, inc=1, device_id=(me, jnp.bitwise_xor(cut, k)), device_id_type=MESH)
    pl.semaphore_wait(barrier, n_expert + n_cuts - 2)

    def columns(index, size):
        return pl.ds(pl.multiple_of(index * size, size), size)

    sent = []

    def to_cuts(src_of, dst_of, base):
        copies = []
        for k in range(1, n_cuts):
            peer = jnp.bitwise_xor(cut, k)
            copies.append(send(src_of(peer), dst_of(k), cut_sem, base + k - 1, (me, peer)))
        sent.extend(copies)
        return copies

    def to_levels(src_of, dst_of, base):
        copies = []
        for k in range(1, levels):
            peer = jnp.bitwise_xor(level, k)
            copies.append(send(src_of(peer), dst_of(k), z_sem, base + k - 1, (2 * peer + core, cut)))
        sent.extend(copies)
        return copies

    def to_experts(src, dst, base):
        copies = []
        for k in range(1, n_expert):
            peer = jnp.bitwise_xor(me, k)
            copies.append(send(src.at[:, columns(peer, 128)], dst.at[k], te_sem, base + k - 1, (peer, cut)))
        sent.extend(copies)
        return copies

    heads_moved = to_cuts(lambda peer: d_heads.at[:, columns(peer, width)], lambda k: dh.at[cut], 0)
    twins = [send(g_attn.at[:, other], core_in, core_sem, 0, twin)]
    tiny_moved = to_experts(tiny, tiny_e, 0)
    dh[cut] = d_heads[:, columns(cut, width)]
    mine.wait()
    twins[0].wait_recv()

    @pl.loop(0, levels)
    def _(step):
        own[step] = (own[step].astype(F32) + core_in[step].astype(F32)).astype(BF)

    piece = own.shape[1] // n_cuts
    attn_moved = to_cuts(lambda peer: own.at[:, columns(peer, piece)], lambda k: a_in.at[k - 1], 3)

    acc_q[...] = jnp.zeros_like(acc_q)
    acc_k[...] = jnp.zeros_like(acc_k)
    acc_v[...] = jnp.zeros_like(acc_v)
    for copy in heads_moved:
        copy.wait_recv()

    @pl.loop(0, heads)
    def _(head):
        pair, half = lax.div(head, 2), lax.rem(head, 2)
        lane = lax.broadcasted_iota(jnp.int32, (1, 128), 1)
        keep = (lax.div(lane, HD) == half).astype(F32)
        keep_low = keep.astype(BF)
        cols = columns(pair, 128)
        k_cols = pl.ds(pl.multiple_of(width + pair * 128, 128), 128)
        v_cols = pl.ds(pl.multiple_of(2 * width + pair * 128, 128), 128)
        for i in range(n_cuts):
            reach = (i + 1) * tokens
            here = pl.ds(i * tokens, tokens)
            query = joined[here, cols] * keep_low
            d_out = dh[i, :, cols] * keep_low
            keys = joined[pl.ds(0, reach), k_cols]
            scores = mm_nt(keys, query) * scaling - lse[head, :, here]
            key_at = lax.broadcasted_iota(jnp.int32, scores.shape, 0)
            query_at = lax.broadcasted_iota(jnp.int32, scores.shape, 1) + i * tokens
            soft = jnp.exp(jnp.where(key_at <= query_at, scores, -1e30))
            d_soft = mm_nt(joined[pl.ds(0, reach), v_cols], d_out)
            delta = jnp.sum(soft * d_soft, axis=0, keepdims=True)
            d_scores = (soft * (d_soft - delta)).astype(BF)
            acc_v[pl.ds(0, reach), cols] += mm(soft.astype(BF), d_out)
            acc_k[pl.ds(0, reach), cols] += mm(d_scores, query)
            acc_q[here, cols] += mm_tn(d_scores, keys) * keep

    dj[:, pl.ds(0, width)] = (acc_q[...] * scaling).astype(BF)
    dj[:, pl.ds(width, width)] = (acc_k[...] * scaling).astype(BF)
    dj[:, pl.ds(2 * width, width)] = acc_v[...].astype(BF)
    for copy in later:
        copy.wait()
    dn_moved = []
    for k in (3, 1, 2):
        peer = jnp.bitwise_xor(cut, k)
        dn[k] = mm_nt(dj[columns(peer, tokens), :], qkv_v[...]).astype(BF)
        dn_moved.append(send(dn.at[k], dn_in.at[k - 1], cut_sem, 6 + k - 1, (me, peer)))
    sent.extend(dn_moved)

    @pl.loop(0, levels)
    def _(step):
        part = mm_tn(norm_v[:, columns(step, 256)], dj[...]).astype(BF)
        gq[step] = part.reshape(2, 128, part.shape[1])

    twins.append(send(gq.at[:, other], core_q, core_sem, 1, twin))
    d_normed = mm_nt(dj[columns(cut, tokens), :], qkv_v[...])

    for copy in attn_moved:
        copy.wait_recv()
    total = own[:, columns(cut, piece)].astype(F32)
    for k in range(1, n_cuts):
        total = total + a_in[k - 1].astype(F32)
    a_mine[...] = total.astype(BF)
    attn_z = to_levels(lambda peer: a_mine.at[peer], lambda k: a_z.at[k - 1], 0)

    twins[1].wait_recv()

    @pl.loop(0, levels)
    def _(step):
        own_q[step] = (gq[step, core].astype(F32) + core_q[step].astype(F32)).astype(BF)

    qkv_z = to_levels(lambda peer: own_q.at[peer], lambda k: z_q.at[k - 1], levels - 1)

    for copy in tiny_moved:
        copy.wait_recv()
    small = tiny[:, columns(me, 128)]
    for k in range(1, n_expert):
        small = small + tiny_e[k]
    tiny_m[...] = small

    def tiny_cuts(src, dst, base):
        copies = []
        for k in range(1, n_cuts):
            copies.append(send(src, dst.at[k], tc_sem, base + k - 1, (me, jnp.bitwise_xor(cut, k))))
        sent.extend(copies)
        return copies

    tiny_last = tiny_cuts(tiny_m, tiny_c, 0)

    for copy in dn_moved:
        copy.wait_recv()
    for k in range(1, n_cuts):
        d_normed = d_normed + dn_in[k - 1].astype(F32)
    xhat, inv = norm_parts(source[...].astype(F32))
    q = d_normed * gain[...]
    mean_q = jnp.mean(q, axis=-1, keepdims=True)
    mean_qx = jnp.mean(q * xhat, axis=-1, keepdims=True)
    d_source[...] = d_hidden[...] + (q - mean_q - xhat * mean_qx) * inv
    late[...] = jnp.broadcast_to(jnp.sum(d_normed * xhat, axis=0, keepdims=True), late.shape)
    late_moved = to_experts(late, late_e, n_expert - 1)

    for copy in tiny_last:
        copy.wait_recv()
    for k in range(1, n_cuts):
        small = small + tiny_c[k]
    o_tiny[...] = small

    for copy in late_moved:
        copy.wait_recv()
    small = late[:, columns(me, 128)]
    for k in range(1, n_expert):
        small = small + late_e[k]
    late_m[...] = small
    late_last = tiny_cuts(late_m, late_c, n_cuts - 1)

    for copy in attn_z:
        copy.wait_recv()
    total = a_mine[level].astype(F32)
    for k in range(1, levels):
        total = total + a_z[k - 1].astype(F32)
    o_attn[...] = total

    for copy in qkv_z:
        copy.wait_recv()
    total = own_q[level].astype(F32)
    for k in range(1, levels):
        total = total + z_q[k - 1].astype(F32)
    fin_q[...] = total.astype(BF).reshape(fin_q.shape)
    qkv_last = to_cuts(lambda peer: fin_q.at[peer], lambda k: o_qkv.at[cut], 9)
    o_qkv[cut] = fin_q[cut]

    for copy in late_last:
        copy.wait_recv()
    for k in range(1, n_cuts):
        small = small + late_c[k]
    o_gain[...] = small
    for copy in qkv_last:
        copy.wait_recv()
    for copy in sent + twins:
        copy.wait_send()


def tail(g_attn, d_heads, joined, lse, normed, qkv, source, gain, d_hidden, tiny, n_expert, n_cuts):
    tokens, features = d_heads.shape
    heads, seq_len = lse.shape
    levels, own = n_expert // 2, features // n_cuts
    deep = features // n_expert
    piece, wide = deep // n_cuts, 3 * own
    any_spec, vmem_spec = pl.BlockSpec(memory_space=pl.ANY), pl.BlockSpec(memory_space=pltpu.VMEM)
    shape, vmem, dma = jax.ShapeDtypeStruct, pltpu.VMEM, pltpu.SemaphoreType.DMA
    rows = tiny.shape[0]
    grid = (levels, 2, deep, features)
    return pl.pallas_call(
        functools.partial(tail_kernel, heads, HD ** (-0.5)),
        name="tail",
        out_shape=(
            shape((tokens, features), F32), shape((n_cuts, piece, wide), BF), shape((piece, features), F32), shape((rows, 128), F32), shape((8, 128), F32),
        ),
        in_specs=[any_spec] + [vmem_spec] * 3 + [any_spec] * 2 + [vmem_spec] * 4,
        out_specs=(vmem_spec,) * 5,
        scratch_shapes=[
            vmem((levels, deep, features), BF), vmem((levels, deep, features), BF),
            vmem((n_cuts - 1, levels, piece, features), BF),
            vmem((levels - 1, piece, features), BF), vmem((levels, piece, features), BF),
            vmem((levels, 2, deep, wide), BF), vmem((levels, deep, wide), BF), vmem((levels, deep, wide), BF),
            vmem((levels - 1, deep, wide), BF), vmem((n_cuts, piece, wide), BF),
            vmem((n_cuts, tokens, own), BF), vmem((seq_len, wide), BF),
            vmem((seq_len, own), F32), vmem((seq_len, own), F32), vmem((seq_len, own), F32),
            vmem((n_cuts, tokens, features), BF), vmem((n_cuts - 1, tokens, features), BF),
            vmem((seq_len, features), BF), vmem((features, wide), BF),
            vmem((n_expert, rows, 128), F32), vmem((rows, 128), F32), vmem((n_cuts, rows, 128), F32),
            vmem((8, features), F32), vmem((n_expert, 8, 128), F32), vmem((8, 128), F32), vmem((n_cuts, 8, 128), F32),
            dma((3,)), dma((2, 2)), dma((2, 2 * (levels - 1))), dma((2, 4 * (n_cuts - 1))),
            dma((2, 2 * (n_expert - 1))), dma((2, 2 * (n_cuts - 1))),
        ],
        compiler_params=pltpu.CompilerParams(
            collective_id=2, has_side_effects=True, vmem_limit_bytes=48 << 20
        ),
        cost_estimate=pl.CostEstimate(flops=20_000_000_000, bytes_accessed=24 << 20, transcendentals=0),
    )(
        g_attn.reshape(grid), d_heads, joined, lse.reshape(heads, 1, seq_len),
        normed, qkv, source, gain, d_hidden, tiny,
    )


def head_kernel(
    sizes, source, gains, small, info, sort, w_qkv, w_attn, w_in, cotangent,
    normed, qkv, joined, lse, head_out, attn_full, in_here, small_full, grad_all, grad_rows, placer, gains_all,
    src_v, qkv_v, norm_v, join_v, acc, heads_low, attn_v, in_v, cot_v, slots, zbuf, row_v,
    load_sem, store_sem, cut_sem, twin_sem, z_sem,
):
    heads, scaling, groups, here, slab = sizes
    me, cut = lax.axis_index("expert"), lax.axis_index("cuts")
    core = lax.rem(me, 2)
    twin = (jnp.bitwise_xor(me, 1), cut)
    at = [jnp.bitwise_xor(cut, k) for k in range(4)]
    n_cuts, tokens, width = src_v.shape
    n_expert, block = zbuf.shape[1], zbuf.shape[2]
    own, half, part = width // n_cuts, tokens // 2, tokens // 4

    def span(start, size, step):
        return pl.ds(pl.multiple_of(start, step), size)

    def remote(src, dst, sems, index, peer):
        return pltpu.make_async_remote_copy(
            src_ref=src, dst_ref=dst, send_sem=sems.at[0, index], recv_sem=sems.at[1, index],
            device_id=peer, device_id_type=MESH,
        )

    def local(src, dst, sems, index):
        copy = pltpu.make_async_copy(src, dst, sems.at[index])
        copy.start()
        return copy

    loads = [
        local(cotangent, cot_v, load_sem, 0),
        local(w_attn, attn_v, load_sem, 1),
        local(w_in.at[:, span(cut * width, width, width)], in_v, load_sem, 2),
    ]
    own_qkv = [
        local(
            w_qkv.at[:, span(n * width + cut * own, own, own)],
            qkv_v.at[span(cut * tokens, tokens, tokens), pl.ds(n * own, own)], load_sem, 3 + n,
        )
        for n in range(3)
    ]
    barrier = pltpu.get_barrier_semaphore()
    for k in range(1, n_expert):
        pl.semaphore_signal(barrier, inc=1, device_id=(jnp.bitwise_xor(me, k), cut), device_id_type=MESH)
    for k in range(1, n_cuts):
        pl.semaphore_signal(barrier, inc=1, device_id=(me, at[k]), device_id_type=MESH)
    pl.semaphore_wait(barrier, n_expert + n_cuts - 2)

    def gather(view, first, base):
        return [
            remote(first, view(cut), cut_sem, base, (me, at[1])),
            remote(first, view(cut), cut_sem, base + 1, (me, at[2])),
            remote(view(at[1], 0), view(at[1], 0), cut_sem, base + 2, (me, at[2])),
            remote(view(at[2], 1), view(at[2], 1), cut_sem, base + 3, (me, at[1])),
        ]

    def relay(copies):
        copies[0].wait_recv()
        copies[2].start()
        copies[1].wait_recv()
        copies[3].start()

    def whole(ref):
        def view(owner, piece=None):
            return ref.at[owner] if piece is None else ref.at[owner, pl.ds(piece * half, half)]

        return view

    def attn_view(owner, piece=None):
        start = owner * tokens + core * half
        if piece is None:
            return attn_full.at[span(start, half, half)]
        return attn_full.at[span(start + piece * part, part, part)]

    def slab_view(owner, piece=None):
        if piece is None:
            return grad_rows.at[:, span(owner * slab, slab, slab // 2)]
        return grad_rows.at[:, span(owner * slab + piece * (slab // 2), slab // 2, slab // 2)]

    def to_cuts(src_of, dst_of, base):
        return [remote(src_of(at[k]), dst_of(k), cut_sem, base + k - 1, (me, at[k])) for k in (3, 1, 2)]

    tokens_moved = gather(whole(src_v), source, 0)
    gains_moved = to_cuts(lambda peer: gains, lambda k: gains_all.at[cut], 16)
    small_moved = to_cuts(lambda peer: small, lambda k: small_full.at[cut], 19)
    qkv_moved = []
    for n in range(3):
        qkv_moved += to_cuts(
            lambda peer: w_qkv.at[span(core * half, half, half), span(n * width + peer * own, own, own)],
            lambda k: qkv_v.at[span(cut * tokens + core * half, half, half), pl.ds(n * own, own)],
            22 + 3 * n,
        )
    for copy in gains_moved + tokens_moved[:2] + qkv_moved + small_moved:
        copy.start()
    grad_moved = gather(whole(grad_all), cot_v, 4)
    attn_moved = gather(attn_view, attn_v.at[span(core * half, half, half)], 8)
    slab_moved = gather(slab_view, row_v, 12)
    in_moved = to_cuts(
        lambda peer: w_in.at[span(core * half, half, half), span(peer * width, width, width)],
        lambda k: in_here.at[span(cut * tokens + core * half, half, half)], 31,
    )
    head_moved = to_cuts(
        lambda peer: heads_low.at[span(peer * tokens, tokens, tokens)],
        lambda k: head_out.at[:, span(cut * own, own, own)], 34,
    )

    loads[0].wait()
    lane = lax.broadcasted_iota(jnp.int32, (tokens, 128), 1).astype(F32)
    picked = jnp.where(lane == info[:, 0:1], info[:, 1:2], 0.0)
    down = lax.broadcasted_iota(jnp.int32, (tokens, tokens), 0)
    right = lax.broadcasted_iota(jnp.int32, (tokens, tokens), 1)
    running = mm((down >= right).astype(F32).astype(BF), picked.astype(BF))
    target = info[:, 2:3] + jnp.sum(picked * running, axis=1, keepdims=True) - 1.0
    column = lax.broadcasted_iota(jnp.int32, placer.shape, 1).astype(F32)
    placer[...] = jnp.where(column == target, info[:, 1:2], 0.0).astype(BF)
    slots[...] = mm_tn(placer[...], cot_v[...]).astype(BF).reshape(slots.shape)
    z_moved = []
    for g in range(groups):
        for k in range(1, n_expert):
            peer = jnp.bitwise_xor(me, k)
            z_moved.append(remote(slots.at[g, peer], zbuf.at[g, me], z_sem, g * n_expert + k, (peer, cut)))
            z_moved[-1].start()
        zbuf[g, me] = slots[g, me]
    src_v[cut] = source[...]
    gains_all[cut] = gains[...]
    small_full[cut] = small[...]
    relay(tokens_moved)
    for copy in loads[1:] + own_qkv:
        copy.wait()
    stores = [
        local(cot_v, grad_all.at[cut], store_sem, 0),
        local(attn_v, attn_full.at[span(cut * tokens, tokens, tokens)], store_sem, 1),
        local(in_v, in_here.at[span(cut * tokens, tokens, tokens)], store_sem, 2),
    ]
    for copy in gains_moved:
        copy.wait_recv()

    def normalize(index):
        xhat, _ = norm_parts(src_v[index].astype(F32))
        for n in range(n_cuts):
            cols = slice(n * own, (n + 1) * own)
            norm_v[index, :, cols] = (xhat[:, cols] * gains_all[n, 0:1, :]).astype(BF)

    normalize(cut)
    normalize(at[1])
    normalize(at[2])
    for copy in qkv_moved:
        copy.wait_recv()

    def share(ref, base):
        copies = []
        for k in range(1, n_cuts):
            view = ref.at[span(at[k] * tokens + core * half, half, half)]
            copies.append(remote(view, view, twin_sem, base + k - 1, twin))
            copies[-1].start()
        return copies

    shared = share(qkv_v, 0)
    for copy in tokens_moved[2:]:
        copy.wait_recv()
    for copy in grad_moved[:2] + attn_moved[:2] + in_moved:
        copy.start()
    normalize(at[3])
    for copy in shared:
        copy.wait_recv()

    @pl.loop(0, n_cuts)
    def _(step):
        join_v[step] = mm(norm_v[step], qkv_v[...]).astype(BF)

    stores += [
        local(norm_v, normed, store_sem, 3), local(qkv_v, qkv, store_sem, 4), local(join_v, joined, store_sem, 5),
    ]
    acc[...] = jnp.zeros_like(acc)
    per_group = here // groups
    for copy in z_moved:
        copy.wait_recv()
    for g in range(groups):
        flat = zbuf[g].reshape(n_expert * block, width)
        for j in range(per_group):
            row_v[g * per_group + j] = mm(sort[pl.ds(j * slab, slab), :], flat).astype(BF)
    stores.append(local(row_v, slab_view(cut), store_sem, 6))

    @pl.loop(0, heads)
    def _(head):
        @pl.when(head == 2)
        def _():
            relay(grad_moved)
            relay(attn_moved)
            for copy in slab_moved[:2]:
                copy.start()

        pair = lax.div(head, 2)
        lane = lax.broadcasted_iota(jnp.int32, (1, 128), 1)
        keep = (lax.div(lane, HD) == lax.rem(head, 2)).astype(F32)
        keep_low = keep.astype(BF)
        cols = span(pair * 128, 128, 128)
        k_cols = span(own + pair * 128, 128, 128)
        v_cols = span(2 * own + pair * 128, 128, 128)
        for i in range(n_cuts):
            reach = (i + 1) * tokens
            query = join_v[i, :, cols] * keep_low
            keys = join_v[pl.ds(0, i + 1), :, k_cols].reshape(reach, 128)
            values = join_v[pl.ds(0, i + 1), :, v_cols].reshape(reach, 128)
            scores = mm_nt(keys, query) * scaling
            key_at = lax.broadcasted_iota(jnp.int32, scores.shape, 0)
            query_at = lax.broadcasted_iota(jnp.int32, scores.shape, 1) + i * tokens
            scores = jnp.where(key_at <= query_at, scores, -1e30)
            peak = jnp.max(scores, axis=0, keepdims=True)
            powers = jnp.exp(scores - peak)
            total = jnp.sum(powers, axis=0, keepdims=True)
            lse[head, :, pl.ds(i * tokens, tokens)] = peak + jnp.log(total)
            soft = (powers / total).astype(BF)
            acc[pl.ds(i * tokens, tokens), cols] += mm_tn(soft, values) * keep

    heads_low[...] = acc[...].astype(BF)
    for copy in head_moved:
        copy.start()
    head_out[:, span(cut * own, own, own)] = heads_low[span(cut * tokens, tokens, tokens), :]
    for copy in in_moved:
        copy.wait_recv()
    shared += share(in_here, 3)
    for copy in attn_moved[2:]:
        copy.wait_recv()
    shared += share(attn_full, 6)
    relay(slab_moved)
    for copy in shared[3:] + grad_moved[2:] + slab_moved[2:] + head_moved + small_moved:
        copy.wait_recv()
    for copy in stores:
        copy.wait()
    everything = tokens_moved + gains_moved + small_moved + qkv_moved + grad_moved + attn_moved + slab_moved
    for copy in everything + in_moved + head_moved + z_moved + shared:
        copy.wait_send()


def head(source, gains, small, info, sort, w_qkv, w_attn, w_in, cotangent, here, groups, capacity, n_expert, n_cuts):
    tokens, features = source.shape
    seq_len, own = tokens * n_cuts, features // n_cuts
    heads, slab = own // HD, n_expert * capacity
    block = here // groups * capacity
    any_spec, vmem_spec = pl.BlockSpec(memory_space=pl.ANY), pl.BlockSpec(memory_space=pltpu.VMEM)
    shape, vmem, dma = jax.ShapeDtypeStruct, pltpu.VMEM, pltpu.SemaphoreType.DMA
    slots = n_expert * groups * block
    return pl.pallas_call(
        functools.partial(head_kernel, (heads, HD ** (-0.5), groups, here, slab)),
        name="head",
        out_shape=(
            shape((n_cuts, tokens, features), BF), shape((features, 3 * own), BF), shape((n_cuts, tokens, 3 * own), BF),
            shape((heads, 1, seq_len), F32), shape((tokens, features), BF), shape((features, features), BF),
            shape((features, w_in.shape[1] // n_cuts), BF), shape((n_cuts,) + small.shape, BF),
            shape((n_cuts, tokens, features), BF), shape((here, n_cuts * slab, features), BF),
            shape((tokens, slots), BF), shape((n_cuts,) + gains.shape, F32),
        ),
        in_specs=[vmem_spec] * 5 + [any_spec] * 4,
        out_specs=(any_spec,) * 3 + (vmem_spec,) * 2 + (any_spec,) * 2 + (vmem_spec,) + (any_spec,) * 2 + (vmem_spec,) * 2,
        scratch_shapes=[
            vmem((n_cuts, tokens, features), BF), vmem((features, 3 * own), BF), vmem((n_cuts, tokens, features), BF),
            vmem((n_cuts, tokens, 3 * own), BF), vmem((seq_len, own), F32), vmem((seq_len, own), BF),
            vmem((tokens, features), BF), vmem((tokens, features), BF), vmem((tokens, features), BF),
            vmem((groups, n_expert, block, features), BF), vmem((groups, n_expert, block, features), BF),
            vmem((here, slab, features), BF),
            dma((6,)), dma((7,)), dma((2, 37)), dma((2, 9)), dma((2, groups * n_expert)),
        ],
        compiler_params=pltpu.CompilerParams(
            collective_id=3, has_side_effects=True, vmem_limit_bytes=48 << 20
        ),
        cost_estimate=pl.CostEstimate(flops=8_000_000_000, bytes_accessed=24 << 20, transcendentals=0),
    )(source, gains, small, info, sort, w_qkv, w_attn, w_in, cotangent)


def expert_grads_kernel(rows, d_first, act, d_rows, grad_in, grad_out):
    grad_in[0] = mm_tn(rows[0], d_first[0])
    grad_out[0] = mm_tn(act[0], d_rows[0])


def expert_grads(rows, d_first, act, d_rows):
    here, count, width = rows.shape
    hidden = act.shape[2]
    part = pl.BlockSpec((1, count, 256), lambda e, t: (e, 0, t))
    return pl.pallas_call(
        expert_grads_kernel,
        name="expert_grads",
        grid=(here, width // 256),
        out_shape=(jax.ShapeDtypeStruct((here, width, hidden), F32), jax.ShapeDtypeStruct((here, hidden, width), F32)),
        in_specs=[
            part, pl.BlockSpec((1, count, hidden), lambda e, t: (e, 0, 0)),
            part, pl.BlockSpec((1, count, width), lambda e, t: (e, 0, 0)),
        ],
        out_specs=(
            pl.BlockSpec((1, 256, hidden), lambda e, t: (e, t, 0)), pl.BlockSpec((1, 256, width), lambda e, t: (e, t, 0)),
        ),
        compiler_params=pltpu.CompilerParams(vmem_limit_bytes=32 << 20),
        cost_estimate=pl.CostEstimate(flops=4 * here * count * width * hidden, bytes_accessed=46 << 20, transcendentals=0),
    )(rows, d_first, act, d_rows)


def shards(
    block_input,
    routes,
    kept_mask,
    w_qkv,
    w_attn_out,
    w_in,
    w_out,
    w_router,
    w_mix,
    gain_attn,
    gain_ffn,
    expert_in,
    expert_out,
    cotangent,
):
    tokens, features = block_input.shape
    n_cuts = lax.axis_size("cuts")
    n_expert = lax.axis_size("expert")
    seq_len = tokens * n_cuts
    scaling = HD ** (-0.5)
    own = features // n_cuts
    heads = own // HD
    experts_all = w_router.shape[1]
    experts_here = expert_in.shape[0]
    capacity = 3 * tokens // (2 * experts_all)

    onehot = (routes[:, None] == jnp.arange(experts_all, dtype=jnp.int32)[None, :]).astype(F32)
    fused = n_cuts == 4
    groups = 2 if fused else 1
    per_group = experts_here // groups
    block = per_group * capacity
    owner, local = routes // experts_here, routes % experts_here
    start = (local // per_group) * (n_expert * block) + owner * block + local % per_group * capacity
    if not fused:
        onehot_kept = onehot * kept_mask.astype(F32)[:, None]
        lower_tri = (jnp.arange(tokens)[:, None] >= jnp.arange(tokens)[None, :]).astype(BF)
        running = mm(lower_tri, onehot_kept.astype(BF))
        slot_num = jnp.sum(onehot_kept * running, axis=1) - 1.0
        target = start.astype(F32) + slot_num
        columns = jnp.arange(experts_all * capacity, dtype=jnp.int32).astype(F32)
        placer = ((columns[None, :] == target[:, None]) & (kept_mask[:, None] > 0)).astype(BF)

    def to_owners(rows):
        grid = mm_tn(placer, rows).astype(BF).reshape(groups, n_expert, block, features)
        grid = grid.swapaxes(0, 1).reshape(n_expert, experts_here, capacity, features)
        moved = lax.all_to_all(grid, "expert", split_axis=0, concat_axis=2, tiled=True)
        return lax.all_gather(moved, "cuts", axis=2, tiled=True)[0]

    def to_sources(rows):
        summed = lax.psum_scatter(rows[None].astype(BF), "cuts", scatter_dimension=2, tiled=True)
        moved = lax.all_to_all(summed, "expert", split_axis=2, concat_axis=0, tiled=True)
        return mm(placer, moved.reshape(-1, features))

    inputs = block_input.astype(F32)
    if fused:
        pair = jnp.stack([gain_attn, gain_ffn], axis=0).astype(F32)
        small_here = jnp.concatenate([w_router, w_mix], axis=1)
        small_cols = small_here.shape[1]
        at = np.arange(n_expert * block)
        slab = n_expert * capacity
        goal = at % slab // capacity * block + at // slab * capacity + at % capacity
        sort = np.asarray(goal[:, None] == at[None, :], dtype=BF)
        info = jnp.stack([routes, kept_mask, start], axis=1).astype(F32)
        normed, qkv_here, joined, log_norm, head_out, attn_full, in_here, small_wide, grad_all, grad_rows, placer, gains = head(
            block_input, jnp.pad(pair, ((0, 6), (0, 0))), jnp.pad(small_here, ((0, 0), (0, -small_cols % 128))),
            info, jnp.asarray(sort), w_qkv, w_attn_out, w_in, cotangent,
            experts_here, groups, capacity, n_expert, n_cuts,
        )
        normed, joined = normed.reshape(seq_len, features), joined.reshape(seq_len, 3 * own)
        small_wide = small_wide.reshape(features, -1)
        small_full = small_wide[:, :small_cols]
        gain_one, gain_two = gains[:, 0].reshape(features), gains[:, 1].reshape(features)
    else:
        gains = gather_cuts(jnp.stack([gain_attn, gain_ffn], axis=1)).astype(F32)
        gain_one, gain_two = gains[:, 0], gains[:, 1]
        xhat_one, inv_one = norm_parts(inputs)
        normed = gather_cuts((xhat_one * gain_one).astype(BF))
        qkv_here = lax.all_to_all(
            w_qkv.reshape(own, 3, n_cuts, own), "cuts", split_axis=2, concat_axis=0, tiled=True
        ).reshape(features, 3 * own)
        joined = mm(normed, qkv_here).astype(BF)
        split = joined.reshape(seq_len, 3, heads, HD)
        q_heads, k_heads, v_heads = split[:, 0], split[:, 1], split[:, 2]
        spots = jnp.arange(seq_len, dtype=jnp.int32)
        visible = (spots[None, :] <= spots[:, None])[None]

        def masked_scores():
            scores = jnp.einsum("qhd,khd->hqk", q_heads, k_heads, preferred_element_type=F32) * scaling
            return jnp.where(visible, scores, -1e30)

        scores = masked_scores()
        peak = jnp.max(scores, axis=-1, keepdims=True)
        row_exp = jnp.exp(scores - peak)
        total = jnp.sum(row_exp, axis=-1, keepdims=True)
        weights_p = (row_exp / total).astype(BF)
        heads_here = jnp.einsum("hqk,khd->qhd", weights_p, v_heads, preferred_element_type=F32)
        log_norm = peak + jnp.log(total)
        head_out = rows_to_cuts(heads_here.reshape(seq_len, own).astype(BF))
        attn_full = gather_cuts(w_attn_out)
        small_full = gather_cuts(jnp.concatenate([w_router, w_mix], axis=1))
        grad_all = gather_cuts(cotangent)
        grad_rows = to_owners(cotangent)
        in_here = columns_to_cuts(w_in)
    hidden = inputs + mm(head_out, attn_full)
    xhat_two, inv_two = norm_parts(hidden)
    second = (xhat_two * gain_two).astype(BF)

    logits = mm(second, small_full)
    router_p = softmax_rows(logits[:, :experts_all])
    mixing = softmax_rows(logits[:, experts_all:])
    gate = jnp.sum(router_p * onehot, axis=1)
    grad = cotangent.astype(F32)
    d_moe = grad * mixing[:, 1:2]

    if fused:
        slots = mm_tn(placer, second).astype(BF).reshape(groups, n_expert, block, features)
        sums, ret_a, ret_b, s_in, s_out, rows_in, d_rows, expert_low, d_first = middle(
            slots, second, grad_all, grad_rows, in_here, w_out, small_wide, jnp.asarray(sort),
            expert_in, expert_out, n_expert, n_cuts,
        )
        dense, d_second_ffn = sums[0], sums[1]
        g_expert_in, g_expert_out = expert_grads(rows_in, d_first, expert_low, d_rows)
        picked = mm(placer, ret_a.reshape(-1, features))
        d_picked_in = mm(placer, ret_b.reshape(-1, features))
    else:
        rows_in = to_owners(second)
        row_logits = jnp.einsum("erd,dk->erk", rows_in, small_full, preferred_element_type=F32)
        ids = lax.axis_index("expert") * experts_here + jnp.arange(experts_here, dtype=jnp.int32)
        is_here = (jnp.arange(experts_all, dtype=jnp.int32)[None, :] == ids[:, None]).astype(F32)
        row_gate = jnp.sum(
            softmax_rows(row_logits[:, :, :experts_all]) * is_here[:, None, :], axis=2, keepdims=True
        )
        row_mixing = softmax_rows(row_logits[:, :, experts_all:])[:, :, 1:2]
        d_rows = (grad_rows.astype(F32) * row_mixing * row_gate).astype(BF)

        first = jnp.einsum("erd,edh->erh", rows_in, expert_in, preferred_element_type=F32)
        expert_act, expert_pull = jax.vjp(jax.nn.gelu, first)
        expert_low = expert_act.astype(BF)
        partial_out = jnp.einsum("erh,ehd->erd", expert_low, expert_out, preferred_element_type=F32)
        picked = to_sources(partial_out)

        second_all = gather_cuts(second)
        mixing_all = softmax_rows(mm(second_all, small_full[:, experts_all:]))
        d_dense_all = (grad_all.astype(F32) * mixing_all[:, 0:1]).astype(BF)
        up_proj = mm(second_all, in_here)
        activ, gelu_pull = jax.vjp(jax.nn.gelu, up_proj)
        activ_low = activ.astype(BF)
        dense = scatter_cuts(mm(activ_low, w_out)).astype(F32)
        d_activ = mm_nt(d_dense_all, w_out)
        g_out = mm_tn(activ_low, d_dense_all)
        d_up = gelu_pull(d_activ)[0].astype(BF)
        g_in = mm_tn(second_all, d_up)
        d_second_ffn = scatter_cuts(mm_nt(d_up, in_here)).astype(F32)

        d_expert_act = jnp.einsum("erd,ehd->erh", d_rows, expert_out, preferred_element_type=F32)
        d_first = expert_pull(d_expert_act)[0].astype(BF)
        d_rows_in = jnp.einsum("erh,edh->erd", d_first, expert_in, preferred_element_type=F32)
        g_expert_out = jnp.einsum("erh,erd->ehd", expert_low, d_rows, preferred_element_type=F32)
        g_expert_in = jnp.einsum("erd,erh->edh", rows_in, d_first, preferred_element_type=F32)
        d_picked_in = to_sources(d_rows_in)

    moe_val = gate[:, None] * picked
    block_out = (hidden + mixing[:, 0:1] * dense + mixing[:, 1:2] * moe_val).astype(BF)
    d_mixing = jnp.stack([jnp.sum(grad * dense, axis=1), jnp.sum(grad * moe_val, axis=1)], axis=1)
    d_gate = jnp.sum(d_moe * picked, axis=1)
    d_router = router_p * (onehot - gate[:, None]) * d_gate[:, None]
    d_mix = mixing * (d_mixing - jnp.sum(mixing * d_mixing, axis=1, keepdims=True))
    d_small = jnp.concatenate([d_router, d_mix], axis=1).astype(BF)
    g_small = mm_tn(d_small, second)
    d_second = d_second_ffn + mm_nt(d_small, small_full) + d_picked_in
    d_hidden_norm, g_gain_two = norm_back(d_second, xhat_two, inv_two, gain_two)
    d_hidden = grad + d_hidden_norm
    d_attn = d_hidden.astype(BF)
    g_attn_out = mm_tn(head_out, d_attn)
    d_head_rows = mm_nt(d_attn, attn_full).astype(BF)
    if fused:
        tiny = jnp.concatenate([g_small, g_gain_two[None, :]], axis=0)
        tiny = jnp.pad(tiny, ((0, -tiny.shape[0] % 8), (0, 0)))
        d_block_input, s_qkv, s_attn_out, tiny, late = tail(
            g_attn_out.astype(BF), d_head_rows, joined, log_norm[:, 0], normed,
            qkv_here, block_input, gain_one[None, :], d_hidden, tiny, n_expert, n_cuts,
        )
        swap = [
            ((flat % n_expert) * n_cuts + flat // n_expert, flat) for flat in range(n_expert * n_cuts)
        ]
        s_out = lax.ppermute(s_out, ("expert", "cuts"), swap).astype(F32)
        s_in = s_in.swapaxes(0, 1).reshape(-1, w_in.shape[1]).astype(F32)
        s_qkv = s_qkv.reshape(n_cuts, -1, 3, own).transpose(1, 2, 0, 3).reshape(-1, 3 * features).astype(F32)
        width = features // (n_expert * n_cuts)
        spot = lax.axis_index("cuts") * width
        s_tiny = lax.dynamic_slice_in_dim(tiny, spot, width, axis=1)
        s_late = lax.dynamic_slice_in_dim(late, spot, width, axis=1)
        return (
            block_out,
            d_block_input,
            s_qkv,
            s_attn_out,
            s_in,
            s_out,
            s_tiny[:experts_all].T,
            s_tiny[experts_all : experts_all + 2].T,
            s_late[0],
            s_tiny[experts_all + 2],
            g_expert_in,
            g_expert_out,
        )
    d_heads = columns_to_cuts(d_head_rows).reshape(seq_len, heads, HD)

    soft_p = jnp.exp(masked_scores() - log_norm)
    d_soft = jnp.einsum("qhd,khd->hqk", d_heads, v_heads, preferred_element_type=F32)
    delta = jnp.sum(soft_p * d_soft, axis=-1, keepdims=True)
    d_scores = (soft_p * (d_soft - delta)).astype(BF)
    d_query = jnp.einsum("hqk,khd->qhd", d_scores, k_heads, preferred_element_type=F32) * scaling
    d_keys = jnp.einsum("hqk,qhd->khd", d_scores, q_heads, preferred_element_type=F32) * scaling
    d_values = jnp.einsum("hqk,qhd->khd", soft_p.astype(BF), d_heads, preferred_element_type=F32)
    d_joined = jnp.stack([d_query, d_keys, d_values], axis=1).reshape(seq_len, 3 * own).astype(BF)
    g_qkv = mm_tn(normed, d_joined)
    d_normed = scatter_cuts(mm_nt(d_joined, qkv_here)).astype(F32)
    d_input_norm, g_gain_one = norm_back(d_normed, xhat_one, inv_one, gain_one)
    d_block_input = d_hidden + d_input_norm

    def over_experts(part):
        return lax.psum_scatter(part.astype(BF), "expert", scatter_dimension=0, tiled=True)

    s_in = rows_to_cuts(over_experts(g_in)).astype(F32)
    s_out = over_experts(g_out)
    swap = [
        ((flat % n_expert) * n_cuts + flat // n_expert, flat) for flat in range(n_expert * n_cuts)
    ]
    s_out = lax.ppermute(s_out, ("expert", "cuts"), swap).astype(F32)
    s_qkv = over_experts(g_qkv)
    deep = s_qkv.shape[0]
    s_qkv = lax.all_to_all(
        s_qkv.reshape(deep, 3, 1, own), "cuts", split_axis=0, concat_axis=2, tiled=True
    )
    s_qkv = s_qkv.reshape(-1, 3 * features).astype(F32)
    s_attn_out = scatter_cuts(over_experts(g_attn_out)).astype(F32)
    tiny = jnp.concatenate([g_small, g_gain_one[None, :], g_gain_two[None, :]], axis=0)
    tiny = jnp.pad(tiny, ((0, -tiny.shape[0] % 8), (0, 0)))
    tiny = sum_small(tiny, n_expert, n_cuts)
    width = features // (n_expert * n_cuts)
    s_tiny = lax.dynamic_slice_in_dim(tiny, lax.axis_index("cuts") * width, width, axis=1)
    return (
        block_out,
        d_block_input,
        s_qkv,
        s_attn_out,
        s_in,
        s_out,
        s_tiny[:experts_all].T,
        s_tiny[experts_all : experts_all + 2].T,
        s_tiny[experts_all + 2],
        s_tiny[experts_all + 3],
        g_expert_in,
        g_expert_out,
    )


def solution(mesh):
    both = ("expert", "cuts")
    placed = (
        P(both, None),
        P(both),
        P(both),
        P("cuts", None),
        P("cuts", None),
        P("cuts", None),
        P("cuts", None),
        P("cuts", None),
        P("cuts", None),
        P("cuts"),
        P("cuts"),
        P("expert", None, "cuts"),
        P("expert", "cuts", None),
        P(both, None),
    )
    results = (
        P(both, None),
        P(both, None),
        P(both, None),
        P(both, None),
        P(both, None),
        P(both, None),
        P(both, None),
        P(both, None),
        P(both),
        P(both),
        P("expert", None, "cuts"),
        P("expert", "cuts", None),
    )
    return jax.shard_map(
        shards, mesh=mesh, in_specs=placed, out_specs=results, check_vma=False
    )
```

```python
import functools
import math

import jax
import jax.numpy as jnp
import numpy as np
from jax import lax
from jax.experimental import pallas as pl
from jax.experimental.pallas import tpu as pltpu
from jax.sharding import PartitionSpec as P

HD = 64
BF = jnp.bfloat16
F32 = jnp.float32
MESH = pl.DeviceIdType.MESH


def norm_parts(values):
    center = values - jnp.mean(values, axis=-1, keepdims=True)
    spread = jnp.mean(center * center, axis=-1, keepdims=True)
    inv = lax.rsqrt(spread + 1e-05)
    return center * inv, inv


def norm_back(grad, xhat, inv, gain):
    q = grad * gain
    mean_q = jnp.mean(q, axis=-1, keepdims=True)
    mean_qx = jnp.mean(q * xhat, axis=-1, keepdims=True)
    return (q - mean_q - xhat * mean_qx) * inv, jnp.sum(grad * xhat, axis=0)


def mm(left, right):
    return jnp.dot(left, right, preferred_element_type=F32)


def mm_nt(left, right):
    return lax.dot_general(left, right, (((1,), (1,)), ((), ())), preferred_element_type=F32)


def mm_tn(left, right):
    return lax.dot_general(left, right, (((0,), (0,)), ((), ())), preferred_element_type=F32)


def softmax_rows(logits):
    shifted = logits - jnp.max(logits, axis=-1, keepdims=True)
    row_exp = jnp.exp(shifted)
    return row_exp / jnp.sum(row_exp, axis=-1, keepdims=True)


def gather_cuts(rows):
    return lax.all_gather(rows, "cuts", axis=0, tiled=True)


def scatter_cuts(rows):
    return lax.psum_scatter(rows.astype(BF), "cuts", scatter_dimension=0, tiled=True)


def columns_to_cuts(rows):
    return lax.all_to_all(rows, "cuts", split_axis=1, concat_axis=0, tiled=True)


def rows_to_cuts(rows):
    return lax.all_to_all(rows, "cuts", split_axis=0, concat_axis=1, tiled=True)


def ring_mod(index, count):
    return lax.rem(index, count)


def small_kernel(n_expert, n_cuts, src, out, by_expert, mine, by_cuts, send_a, recv_a, send_b, recv_b):
    me, cut = lax.axis_index("expert"), lax.axis_index("cuts")
    width = out.shape[1]
    barrier = pltpu.get_barrier_semaphore()
    for step in range(1, n_expert):
        peer = ring_mod(me + step, n_expert)
        pl.semaphore_signal(barrier, inc=1, device_id=(peer, cut), device_id_type=MESH)
    for step in range(1, n_cuts):
        peer = ring_mod(cut + step, n_cuts)
        pl.semaphore_signal(barrier, inc=1, device_id=(me, peer), device_id_type=MESH)
    pl.semaphore_wait(barrier, n_expert + n_cuts - 2)

    def part(owner):
        return src.at[:, pl.ds(pl.multiple_of(owner * width, 128), width)]

    copies = []
    for step in range(1, n_expert):
        peer = ring_mod(me + step, n_expert)
        copies.append(
            pltpu.make_async_remote_copy(
                src_ref=part(peer),
                dst_ref=by_expert.at[step],
                send_sem=send_a.at[step],
                recv_sem=recv_a.at[step],
                device_id=(peer, cut),
                device_id_type=MESH,
            )
        )
        copies[-1].start()
    total = src[:, pl.ds(pl.multiple_of(me * width, 128), width)]
    for step in range(1, n_expert):
        copies[step - 1].wait()
        total = total + by_expert[step]
    mine[...] = total
    copies = []
    for step in range(1, n_cuts):
        peer = ring_mod(cut + step, n_cuts)
        copies.append(
            pltpu.make_async_remote_copy(
                src_ref=mine,
                dst_ref=by_cuts.at[step],
                send_sem=send_b.at[step],
                recv_sem=recv_b.at[step],
                device_id=(me, peer),
                device_id_type=MESH,
            )
        )
        copies[-1].start()
    for step in range(1, n_cuts):
        copies[step - 1].wait()
        total = total + by_cuts[step]
    out[...] = total


def sum_small(values, n_expert, n_cuts):
    rows, features = values.shape
    width = features // n_expert
    pad = -width % 128
    if pad:
        values = jnp.pad(values.reshape(rows, n_expert, width), ((0, 0), (0, 0), (0, pad)))
        values = values.reshape(rows, n_expert * (width + pad))
    wide = width + pad
    summed = pl.pallas_call(
        functools.partial(small_kernel, n_expert, n_cuts),
        name="sum_small",
        out_shape=jax.ShapeDtypeStruct((rows, wide), F32),
        in_specs=[pl.BlockSpec(memory_space=pltpu.VMEM)],
        out_specs=pl.BlockSpec(memory_space=pltpu.VMEM),
        scratch_shapes=[
            pltpu.VMEM((n_expert, rows, wide), F32),
            pltpu.VMEM((rows, wide), F32),
            pltpu.VMEM((n_cuts, rows, wide), F32),
            pltpu.SemaphoreType.DMA((n_expert,)),
            pltpu.SemaphoreType.DMA((n_expert,)),
            pltpu.SemaphoreType.DMA((n_cuts,)),
            pltpu.SemaphoreType.DMA((n_cuts,)),
        ],
        compiler_params=pltpu.CompilerParams(collective_id=0, has_side_effects=True),
    )(values)
    return summed[:, :width]


def dot_nt(left, right):
    return lax.dot_general(left, right, (((1,), (1,)), ((), ())), preferred_element_type=F32)


def tile_of(step, size):
    return pl.ds(pl.multiple_of(step * size, size), size)


def lane_softmax(logits, low, high):
    lane = lax.broadcasted_iota(jnp.int32, logits.shape, 1)
    inside = (lane >= low) & (lane < high)
    kept = jnp.where(inside, logits, -1e30)
    powers = jnp.exp(kept - jnp.max(kept, axis=1, keepdims=True))
    powers = jnp.where(inside, powers, 0.0)
    return powers / jnp.sum(powers, axis=1, keepdims=True), lane


def mlp_both(rows, d_rows, w_up, w_down, act, d_up, write):
    root, cubic = math.sqrt(2.0 / math.pi), 0.044715

    @pl.loop(0, act.shape[1] // 256)
    def _(step):
        span = tile_of(step, 256)
        up = mm(rows[...], w_up[:, span])
        d_act = dot_nt(d_rows[...], w_down[span, :])
        square = up * up
        bent = jnp.tanh(root * up * (1.0 + cubic * square))
        half = 0.5 * (1.0 + bent)
        act[:, span] = (up * half).astype(BF)
        slope = half + 0.5 * up * (1.0 - bent * bent) * (root + 3.0 * root * cubic * square)
        d_up[:, span] = (d_act * slope).astype(BF)

    @pl.loop(0, w_up.shape[0] // 256)
    def _(step):
        span = tile_of(step, 256)
        write(span, mm(act[...], w_down[:, span]), dot_nt(d_up[...], w_up[span, :]))


def middle_kernel(
    sizes, slots, second, grad_all, grad_rows, w_in, w_out, small, sort, e_in, e_out,
    sums, ret_a, ret_b, o_in, o_out, rows_in, d_rows_all, act_e_all, d_first_all,
    sec, grd, win, wout, act, d_up, part_a, part_b, ffn_x, ffn_y, ffn_qa, ffn_qb,
    zbuf, rows, g_rows, d_rows, act_e, d_first, wi_e, wo_e, out_a, out_b, row_x, row_y, row_qa, row_qb, sorted_back, send_back,
    twin_in, level_in, fin_in,
    load_sem, weight_sem, store_sem, store_e_sem, z_sem, ag_sem, eag_sem, frs_sem, ers_sem, zr_sem,
    twin_sem, level_sem, fin_sem,
):
    n_expert, groups, here, slab = sizes
    me, cut = lax.axis_index("expert"), lax.axis_index("cuts")
    at_x, at_y, at_d = (jnp.bitwise_xor(cut, k) for k in (1, 2, 3))
    block = zbuf.shape[2]
    per_group = here // groups
    experts_all = n_expert * here

    def load(src, dst, index):
        copy = pltpu.make_async_copy(src, dst, load_sem.at[index])
        copy.start()
        return copy

    def remote(src, dst, sems, index, peer):
        return pltpu.make_async_remote_copy(
            src_ref=src, dst_ref=dst, send_sem=sems.at[0, index], recv_sem=sems.at[1, index],
            device_id=peer, device_id_type=MESH,
        )

    def send(src, dst, sems, index, peer):
        copy = remote(src, dst, sems, index, peer)
        copy.start()
        return copy

    loads = [
        load(second, sec.at[cut], 0), load(w_in, win, 1), load(w_out, wout, 2), load(grad_all, grd, 3),
    ]

    def fetch_expert(i):
        slot = i % 2
        copies = [
            pltpu.make_async_copy(e_in.at[i], wi_e.at[slot], weight_sem.at[0, slot]),
            pltpu.make_async_copy(e_out.at[i], wo_e.at[slot], weight_sem.at[1, slot]),
            pltpu.make_async_copy(grad_rows.at[i], g_rows.at[slot], weight_sem.at[2, slot]),
        ]
        for copy in copies:
            copy.start()
        return copies

    fetched = [fetch_expert(0), fetch_expert(1)]
    barrier = pltpu.get_barrier_semaphore()
    for k in range(1, n_expert):
        pl.semaphore_signal(barrier, inc=1, device_id=(jnp.bitwise_xor(me, k), cut), device_id_type=MESH)
    for peer in (at_x, at_y):
        pl.semaphore_signal(barrier, inc=1, device_id=(me, peer), device_id_type=MESH)
    pl.semaphore_signal(barrier, inc=1, device_id=(me, at_d), device_id_type=MESH)
    pl.semaphore_wait(barrier, n_expert + 2)
    core, level = lax.rem(me, 2), lax.div(me, 2)
    levels = n_expert // 2

    z_copies = []
    for g in range(groups):
        for k in range(1, n_expert):
            peer = jnp.bitwise_xor(me, k)
            z_copies.append(send(slots.at[g, peer], zbuf.at[g, me], z_sem, g * n_expert + k, (peer, cut)))
    loads[0].wait()
    ag = [
        send(sec.at[cut], sec.at[cut], ag_sem, 0, (me, at_x)),
        send(sec.at[cut], sec.at[cut], ag_sem, 1, (me, at_y)),
    ]
    half = sec.shape[1] // 2
    ag += [
        remote(sec.at[at_x, pl.ds(0, half)], sec.at[at_x, pl.ds(0, half)], ag_sem, 2, (me, at_y)),
        remote(sec.at[at_y, pl.ds(half, half)], sec.at[at_y, pl.ds(half, half)], ag_sem, 3, (me, at_x)),
    ]
    for g in range(groups):
        zbuf[g, me] = slots[g, me]
    def ffn_block(which, owner):
        mixing, lane = lane_softmax(mm(sec[owner], small[...]), experts_all, experts_all + 2)
        first_mix = jnp.sum(jnp.where(lane == experts_all, mixing, 0.0), axis=1, keepdims=True)
        grd[owner] = (grd[owner].astype(F32) * first_mix).astype(BF)

        def write(span, out, d_row):
            @pl.when(which == 0)
            def _():
                sums[0, :, span] = out
                sums[1, :, span] = d_row

            part_a[which, :, span] = out.astype(BF)
            part_b[which, :, span] = d_row.astype(BF)

        mlp_both(sec.at[owner], grd.at[owner], win, wout, act.at[owner], d_up.at[owner], write)

    def level_rows(index, half):
        return pl.ds(pl.multiple_of(index * 256 + half * 128, 128), 128)

    def weight_grad(m, left, right, held):
        @pl.loop(0, levels)
        def _(step):
            span = tile_of(step, 256)
            lhs = left[:, :, span].reshape(-1, 256)
            held[span, :] = mm_tn(lhs, right[...].reshape(-1, right.shape[2])).astype(BF)

        return [
            send(held.at[level_rows(n, 1 - core)], twin_in.at[m, n], twin_sem, m * levels + n, (jnp.bitwise_xor(me, 1), cut))
            for n in range(levels)
        ]

    def weight_sum(m, held, twins):
        for copy in twins:
            copy.wait_recv()

        @pl.loop(0, levels)
        def _(step):
            here_rows = level_rows(step, core)
            held[here_rows, :] = (held[here_rows, :].astype(F32) + twin_in[m, step].astype(F32)).astype(BF)

        copies = []
        for k in range(1, levels):
            peer = jnp.bitwise_xor(level, k)
            copies.append(
                send(
                    held.at[level_rows(peer, core)], level_in.at[m, k - 1], level_sem, m * (levels - 1) + k - 1,
                    (2 * peer + core, cut),
                )
            )
        return copies

    def weight_total(m, held, copies):
        for copy in copies:
            copy.wait_recv()
        total = held[level_rows(level, core), :].astype(F32)
        for k in range(1, levels):
            total = total + level_in[m, k - 1].astype(F32)
        return total.astype(BF)

    for copy in loads[1:]:
        copy.wait()
    def slab_of(owner):
        return pl.ds(pl.multiple_of(owner * slab, slab), slab)

    eag = {}
    cut_half = slab // 2
    for i in range(here):
        mine = rows.at[i, slab_of(cut)]
        from_x = rows.at[i, pl.ds(pl.multiple_of(at_x * slab, slab), cut_half)]
        from_y = rows.at[i, pl.ds(pl.multiple_of(at_y * slab + cut_half, cut_half), cut_half)]
        eag[i] = [
            remote(mine, mine, eag_sem, 4 * i, (me, at_x)),
            remote(mine, mine, eag_sem, 4 * i + 1, (me, at_y)),
            remote(from_x, from_x, eag_sem, 4 * i + 2, (me, at_y)),
            remote(from_y, from_y, eag_sem, 4 * i + 3, (me, at_x)),
        ]

    def relay(copies):
        copies[0].wait_recv()
        copies[2].start()
        copies[1].wait_recv()
        copies[3].start()

    @pl.loop(0, sec.shape[0])
    def _(which):
        @pl.when(which == 1)
        def _():
            relay(ag)

        @pl.when(which == 2)
        def _():
            for g in range(groups):
                for k in range(1, n_expert):
                    z_copies[g * (n_expert - 1) + k - 1].wait_recv()
                flat = zbuf[g].reshape(n_expert * block, zbuf.shape[3])
                for j in range(per_group):
                    i = g * per_group + j
                    rows[i, slab_of(cut)] = mm(sort[pl.ds(j * slab, slab), :], flat).astype(BF)
                    eag[i][0].start()
                    eag[i][1].start()

        @pl.when(which == 3)
        def _():
            ag[2].wait_recv()
            ag[3].wait_recv()
            relay(eag[0])

        ffn_block(which, jnp.bitwise_xor(cut, which))

    twins_in = weight_grad(0, sec, d_up, win)
    expert_stores = {}
    ers = {}

    def expert(i):
        slot = i % 2
        if i >= 2:
            for copy in expert_stores[i - 2]:
                copy.wait()
        for copy in fetched[i]:
            copy.wait()
        logits = mm(rows[i], small[...])
        router, lane = lane_softmax(logits, 0, experts_all)
        gate = jnp.sum(jnp.where(lane == me * here + i, router, 0.0), axis=1, keepdims=True)
        mixing, lane = lane_softmax(logits, experts_all, experts_all + 2)
        mixing = jnp.sum(jnp.where(lane == experts_all + 1, mixing, 0.0), axis=1, keepdims=True)
        d_rows[slot] = (g_rows[slot].astype(F32) * mixing * gate).astype(BF)

        def write(span, out, d_row):
            out_a[i, :, span] = out.astype(BF)
            out_b[i, :, span] = d_row.astype(BF)

        mlp_both(rows.at[i], d_rows.at[slot], wi_e.at[slot], wo_e.at[slot], act_e.at[slot], d_first.at[slot], write)
        expert_stores[i] = []
        for n, (src, dst) in enumerate(((d_rows, d_rows_all), (act_e, act_e_all), (d_first, d_first_all))):
            copy = pltpu.make_async_copy(src.at[slot], dst.at[i], store_e_sem.at[n, slot])
            copy.start()
            expert_stores[i].append(copy)
        ers[i] = [
            send(out_a.at[i, slab_of(at_x)], row_x.at[i, 0], ers_sem, 6 * i, (me, at_x)),
            send(out_a.at[i, slab_of(at_d)], row_x.at[i, 1], ers_sem, 6 * i + 1, (me, at_x)),
            send(out_b.at[i, slab_of(at_y)], row_y.at[i, 0], ers_sem, 6 * i + 2, (me, at_y)),
            send(out_b.at[i, slab_of(at_d)], row_y.at[i, 1], ers_sem, 6 * i + 3, (me, at_y)),
        ]

    def add_into(ref, *others):
        total = ref[...].astype(F32)
        for other in others:
            total = total + other[...].astype(F32)
        ref[...] = total.astype(BF)

    def pass_on(i):
        for copy in ers[i][:4]:
            copy.wait_recv()
        add_into(out_a.at[i, slab_of(at_y)], row_x.at[i, 1])
        add_into(out_b.at[i, slab_of(at_x)], row_y.at[i, 1])
        ers[i] += [
            send(out_a.at[i, slab_of(at_y)], row_qa.at[i], ers_sem, 6 * i + 4, (me, at_y)),
            send(out_b.at[i, slab_of(at_x)], row_qb.at[i], ers_sem, 6 * i + 5, (me, at_x)),
        ]

    back_copies = []

    def finish(i):
        ers[i][4].wait_recv()
        ers[i][5].wait_recv()
        for n, (out, near, far) in enumerate(((out_a, row_x, row_qa), (out_b, row_y, row_qb))):
            total = out[i, slab_of(cut)].astype(F32) + near[i, 0].astype(F32) + far[i].astype(F32)
            sorted_back[n, i] = total.astype(BF)
        if (i + 1) % per_group == 0:
            g = i // per_group
            for n in range(2):
                flat = sorted_back[n, pl.ds(g * per_group, per_group)].reshape(per_group * slab, -1)
                placed = mm_tn(sort[...], flat).astype(BF)
                send_back[n, g] = placed.reshape(n_expert, block, -1)
                (ret_a, ret_b)[n][g, me] = send_back[n, g, me]
                for k in range(1, n_expert):
                    peer = jnp.bitwise_xor(me, k)
                    back_copies.append(
                        send(
                            send_back.at[n, g, peer], (ret_a, ret_b)[n].at[g, me], zr_sem,
                            (n * groups + g) * n_expert + k, (peer, cut),
                        )
                    )

    for i in range(here):
        if i + 1 < here:
            relay(eag[i + 1])
        eag[i][2].wait_recv()
        eag[i][3].wait_recv()
        expert(i)
        if i + 2 < here:
            fetched.append(fetch_expert(i + 2))
        if i == 0:
            levels_in = weight_sum(0, win, twins_in)
            twins_out = weight_grad(1, act, grd, wout)
        if i == here - 1:
            frs = [
                send(part_a.at[1], ffn_x.at[0], frs_sem, 0, (me, at_x)),
                send(part_a.at[3], ffn_x.at[1], frs_sem, 1, (me, at_x)),
                send(part_b.at[2], ffn_y.at[0], frs_sem, 2, (me, at_y)),
                send(part_b.at[3], ffn_y.at[1], frs_sem, 3, (me, at_y)),
            ]
        if i == 1:
            levels_out = weight_sum(1, wout, twins_out)
        if i >= 1:
            pass_on(i - 1)
        if i >= 2:
            finish(i - 2)
    rows_store = pltpu.make_async_copy(rows, rows_in, store_sem.at[0])
    rows_store.start()
    pass_on(here - 1)
    finish(here - 2)
    finish(here - 1)
    for copy in frs[:4]:
        copy.wait_recv()
    add_into(part_a.at[2], ffn_x.at[1])
    add_into(part_b.at[1], ffn_y.at[1])
    frs += [
        send(part_a.at[2], ffn_qa, frs_sem, 4, (me, at_y)),
        send(part_b.at[1], ffn_qb, frs_sem, 5, (me, at_x)),
    ]
    fin_in[...] = weight_total(0, win, levels_in).reshape(fin_in.shape)
    fin_copies = []
    for k, peer in ((1, at_x), (2, at_y), (3, at_d)):
        fin_copies.append(send(fin_in.at[peer], o_in.at[cut], fin_sem, k - 1, (me, peer)))
    o_in[cut] = fin_in[cut]
    o_out[...] = weight_total(1, wout, levels_out)
    frs[4].wait_recv()
    frs[5].wait_recv()
    sums[0] = sums[0] + ffn_x[0].astype(F32) + ffn_qa[...].astype(F32)
    sums[1] = sums[1] + ffn_y[0].astype(F32) + ffn_qb[...].astype(F32)
    for copy in back_copies + fin_copies:
        copy.wait_recv()
    for copy in z_copies + ag + frs + back_copies + fin_copies + twins_in + twins_out + levels_in + levels_out:
        copy.wait_send()
    for i in range(here):
        for copy in eag[i] + ers[i]:
            copy.wait_send()
    for i in (here - 2, here - 1):
        for copy in expert_stores[i]:
            copy.wait()
    rows_store.wait()


def middle(slots, second, grad_all, grad_rows, w_in, w_out, small, sort, e_in, e_out, n_expert, n_cuts):
    groups, _, block, width = slots.shape
    tokens = second.shape[0]
    here, _, hidden = e_in.shape
    ffn = w_in.shape[1]
    slab = n_expert * block * groups // here
    rows = n_cuts * slab
    levels, deep = n_expert // 2, width // n_expert
    any_spec, vmem_spec = pl.BlockSpec(memory_space=pl.ANY), pl.BlockSpec(memory_space=pltpu.VMEM)
    shape = jax.ShapeDtypeStruct
    dma = pltpu.SemaphoreType.DMA
    flops = 8 * (n_cuts * tokens * ffn + here * rows * hidden) * width
    return pl.pallas_call(
        functools.partial(middle_kernel, (n_expert, groups, here, slab)),
        name="middle",
        out_shape=(
            shape((2, tokens, width), F32), shape((groups, n_expert, block, width), BF),
            shape((groups, n_expert, block, width), BF), shape((n_cuts, deep // n_cuts, ffn), BF), shape((deep, width), BF),
            shape((here, rows, width), BF), shape((here, rows, width), BF),
            shape((here, rows, hidden), BF), shape((here, rows, hidden), BF),
        ),
        in_specs=[vmem_spec] + [any_spec] * 5 + [vmem_spec] * 2 + [any_spec] * 2,
        out_specs=(vmem_spec,) * 5 + (any_spec,) * 4,
        scratch_shapes=[
            pltpu.VMEM((n_cuts, tokens, width), BF), pltpu.VMEM((n_cuts, tokens, width), BF),
            pltpu.VMEM((width, ffn), BF), pltpu.VMEM((ffn, width), BF),
            pltpu.VMEM((n_cuts, tokens, ffn), BF), pltpu.VMEM((n_cuts, tokens, ffn), BF),
            pltpu.VMEM((n_cuts, tokens, width), BF), pltpu.VMEM((n_cuts, tokens, width), BF),
            pltpu.VMEM((2, tokens, width), BF), pltpu.VMEM((2, tokens, width), BF),
            pltpu.VMEM((tokens, width), BF), pltpu.VMEM((tokens, width), BF),
            pltpu.VMEM((groups, n_expert, block, width), BF), pltpu.VMEM((here, rows, width), BF),
            pltpu.VMEM((2, rows, width), BF), pltpu.VMEM((2, rows, width), BF),
            pltpu.VMEM((2, rows, hidden), BF), pltpu.VMEM((2, rows, hidden), BF),
            pltpu.VMEM((2, width, hidden), BF), pltpu.VMEM((2, hidden, width), BF),
            pltpu.VMEM((here, rows, width), BF), pltpu.VMEM((here, rows, width), BF),
            pltpu.VMEM((here, 2, slab, width), BF), pltpu.VMEM((here, 2, slab, width), BF),
            pltpu.VMEM((here, slab, width), BF), pltpu.VMEM((here, slab, width), BF),
            pltpu.VMEM((2, here, slab, width), BF), pltpu.VMEM((2, groups, n_expert, block, width), BF),
            pltpu.VMEM((2, levels, deep, width), BF), pltpu.VMEM((2, levels - 1, deep, width), BF),
            pltpu.VMEM((n_cuts, deep // n_cuts, ffn), BF),
            dma((4,)), dma((3, 2)), dma((1,)), dma((3, 2)),
            dma((2, groups * n_expert)), dma((2, 4)), dma((2, 4 * here)), dma((2, 6)), dma((2, 6 * here)),
            dma((2, 2 * groups * n_expert)),
            dma((2, 2 * levels)), dma((2, 2 * (levels - 1))), dma((2, 3)),
        ],
        compiler_params=pltpu.CompilerParams(
            collective_id=1, has_side_effects=True, vmem_limit_bytes=67_000_000
        ),
        cost_estimate=pl.CostEstimate(flops=flops, bytes_accessed=48 << 20, transcendentals=0),
    )(slots, second, grad_all, grad_rows, w_in, w_out, small, sort, e_in, e_out)


def tail_kernel(
    heads, scaling, g_attn, d_heads, joined, lse, normed, qkv, source, gain, d_hidden, tiny,
    d_source, o_qkv, o_attn, o_tiny, o_gain,
    core_in, own, a_in, a_z, a_mine, gq, core_q, own_q, z_q, fin_q,
    dh, dj, acc_q, acc_k, acc_v, dn, dn_in, norm_v, qkv_v, tiny_e, tiny_m, tiny_c, late, late_e, late_m, late_c,
    load_sem, core_sem, z_sem, cut_sem, te_sem, tc_sem,
):
    me, cut = lax.axis_index("expert"), lax.axis_index("cuts")
    core, level = lax.rem(me, 2), lax.div(me, 2)
    other = 1 - core
    n_cuts, tokens, width = dh.shape
    n_expert = tiny_e.shape[0]
    levels = n_expert // 2
    twin = (jnp.bitwise_xor(me, 1), cut)

    def send(src, dst, sems, index, peer):
        copy = pltpu.make_async_remote_copy(
            src_ref=src, dst_ref=dst, send_sem=sems.at[0, index], recv_sem=sems.at[1, index],
            device_id=peer, device_id_type=MESH,
        )
        copy.start()
        return copy

    def load(src, dst, index):
        copy = pltpu.make_async_copy(src, dst, load_sem.at[index])
        copy.start()
        return copy

    mine = load(g_attn.at[:, core], own, 0)
    later = [load(normed, norm_v, 1), load(qkv, qkv_v, 2)]
    barrier = pltpu.get_barrier_semaphore()
    for k in range(1, n_expert):
        pl.semaphore_signal(barrier, inc=1, device_id=(jnp.bitwise_xor(me, k), cut), device_id_type=MESH)
    for k in range(1, n_cuts):
        pl.semaphore_signal(barrier, inc=1, device_id=(me, jnp.bitwise_xor(cut, k)), device_id_type=MESH)
    pl.semaphore_wait(barrier, n_expert + n_cuts - 2)

    def columns(index, size):
        return pl.ds(pl.multiple_of(index * size, size), size)

    sent = []

    def to_cuts(src_of, dst_of, base):
        copies = []
        for k in range(1, n_cuts):
            peer = jnp.bitwise_xor(cut, k)
            copies.append(send(src_of(peer), dst_of(k), cut_sem, base + k - 1, (me, peer)))
        sent.extend(copies)
        return copies

    def to_levels(src_of, dst_of, base):
        copies = []
        for k in range(1, levels):
            peer = jnp.bitwise_xor(level, k)
            copies.append(send(src_of(peer), dst_of(k), z_sem, base + k - 1, (2 * peer + core, cut)))
        sent.extend(copies)
        return copies

    def to_experts(src, dst, base):
        copies = []
        for k in range(1, n_expert):
            peer = jnp.bitwise_xor(me, k)
            copies.append(send(src.at[:, columns(peer, 128)], dst.at[k], te_sem, base + k - 1, (peer, cut)))
        sent.extend(copies)
        return copies

    heads_moved = to_cuts(lambda peer: d_heads.at[:, columns(peer, width)], lambda k: dh.at[cut], 0)
    twins = [send(g_attn.at[:, other], core_in, core_sem, 0, twin)]
    tiny_moved = to_experts(tiny, tiny_e, 0)
    dh[cut] = d_heads[:, columns(cut, width)]
    mine.wait()
    twins[0].wait_recv()

    @pl.loop(0, levels)
    def _(step):
        own[step] = (own[step].astype(F32) + core_in[step].astype(F32)).astype(BF)

    piece = own.shape[1] // n_cuts
    attn_moved = to_cuts(lambda peer: own.at[:, columns(peer, piece)], lambda k: a_in.at[k - 1], 3)

    acc_q[...] = jnp.zeros_like(acc_q)
    acc_k[...] = jnp.zeros_like(acc_k)
    acc_v[...] = jnp.zeros_like(acc_v)
    for copy in heads_moved:
        copy.wait_recv()

    @pl.loop(0, heads)
    def _(head):
        pair, half = lax.div(head, 2), lax.rem(head, 2)
        lane = lax.broadcasted_iota(jnp.int32, (1, 128), 1)
        keep = (lax.div(lane, HD) == half).astype(F32)
        keep_low = keep.astype(BF)
        cols = columns(pair, 128)
        k_cols = pl.ds(pl.multiple_of(width + pair * 128, 128), 128)
        v_cols = pl.ds(pl.multiple_of(2 * width + pair * 128, 128), 128)
        for i in range(n_cuts):
            reach = (i + 1) * tokens
            here = pl.ds(i * tokens, tokens)
            query = joined[here, cols] * keep_low
            d_out = dh[i, :, cols] * keep_low
            keys = joined[pl.ds(0, reach), k_cols]
            scores = mm_nt(keys, query) * scaling - lse[head, :, here]
            key_at = lax.broadcasted_iota(jnp.int32, scores.shape, 0)
            query_at = lax.broadcasted_iota(jnp.int32, scores.shape, 1) + i * tokens
            soft = jnp.exp(jnp.where(key_at <= query_at, scores, -1e30))
            d_soft = mm_nt(joined[pl.ds(0, reach), v_cols], d_out)
            delta = jnp.sum(soft * d_soft, axis=0, keepdims=True)
            d_scores = (soft * (d_soft - delta)).astype(BF)
            acc_v[pl.ds(0, reach), cols] += mm(soft.astype(BF), d_out)
            acc_k[pl.ds(0, reach), cols] += mm(d_scores, query)
            acc_q[here, cols] += mm_tn(d_scores, keys) * keep

    dj[:, pl.ds(0, width)] = (acc_q[...] * scaling).astype(BF)
    dj[:, pl.ds(width, width)] = (acc_k[...] * scaling).astype(BF)
    dj[:, pl.ds(2 * width, width)] = acc_v[...].astype(BF)
    for copy in later:
        copy.wait()
    dn_moved = []
    for k in (3, 1, 2):
        peer = jnp.bitwise_xor(cut, k)
        dn[k] = mm_nt(dj[columns(peer, tokens), :], qkv_v[...]).astype(BF)
        dn_moved.append(send(dn.at[k], dn_in.at[k - 1], cut_sem, 6 + k - 1, (me, peer)))
    sent.extend(dn_moved)

    @pl.loop(0, levels)
    def _(step):
        part = mm_tn(norm_v[:, columns(step, 256)], dj[...]).astype(BF)
        gq[step] = part.reshape(2, 128, part.shape[1])

    twins.append(send(gq.at[:, other], core_q, core_sem, 1, twin))
    d_normed = mm_nt(dj[columns(cut, tokens), :], qkv_v[...])

    for copy in attn_moved:
        copy.wait_recv()
    total = own[:, columns(cut, piece)].astype(F32)
    for k in range(1, n_cuts):
        total = total + a_in[k - 1].astype(F32)
    a_mine[...] = total.astype(BF)
    attn_z = to_levels(lambda peer: a_mine.at[peer], lambda k: a_z.at[k - 1], 0)

    twins[1].wait_recv()

    @pl.loop(0, levels)
    def _(step):
        own_q[step] = (gq[step, core].astype(F32) + core_q[step].astype(F32)).astype(BF)

    qkv_z = to_levels(lambda peer: own_q.at[peer], lambda k: z_q.at[k - 1], levels - 1)

    for copy in tiny_moved:
        copy.wait_recv()
    small = tiny[:, columns(me, 128)]
    for k in range(1, n_expert):
        small = small + tiny_e[k]
    tiny_m[...] = small

    def tiny_cuts(src, dst, base):
        copies = []
        for k in range(1, n_cuts):
            copies.append(send(src, dst.at[k], tc_sem, base + k - 1, (me, jnp.bitwise_xor(cut, k))))
        sent.extend(copies)
        return copies

    tiny_last = tiny_cuts(tiny_m, tiny_c, 0)

    for copy in dn_moved:
        copy.wait_recv()
    for k in range(1, n_cuts):
        d_normed = d_normed + dn_in[k - 1].astype(F32)
    xhat, inv = norm_parts(source[...].astype(F32))
    q = d_normed * gain[...]
    mean_q = jnp.mean(q, axis=-1, keepdims=True)
    mean_qx = jnp.mean(q * xhat, axis=-1, keepdims=True)
    d_source[...] = d_hidden[...] + (q - mean_q - xhat * mean_qx) * inv
    late[...] = jnp.broadcast_to(jnp.sum(d_normed * xhat, axis=0, keepdims=True), late.shape)
    late_moved = to_experts(late, late_e, n_expert - 1)

    for copy in tiny_last:
        copy.wait_recv()
    for k in range(1, n_cuts):
        small = small + tiny_c[k]
    o_tiny[...] = small

    for copy in late_moved:
        copy.wait_recv()
    small = late[:, columns(me, 128)]
    for k in range(1, n_expert):
        small = small + late_e[k]
    late_m[...] = small
    late_last = tiny_cuts(late_m, late_c, n_cuts - 1)

    for copy in attn_z:
        copy.wait_recv()
    total = a_mine[level].astype(F32)
    for k in range(1, levels):
        total = total + a_z[k - 1].astype(F32)
    o_attn[...] = total

    for copy in qkv_z:
        copy.wait_recv()
    total = own_q[level].astype(F32)
    for k in range(1, levels):
        total = total + z_q[k - 1].astype(F32)
    fin_q[...] = total.astype(BF).reshape(fin_q.shape)
    qkv_last = to_cuts(lambda peer: fin_q.at[peer], lambda k: o_qkv.at[cut], 9)
    o_qkv[cut] = fin_q[cut]

    for copy in late_last:
        copy.wait_recv()
    for k in range(1, n_cuts):
        small = small + late_c[k]
    o_gain[...] = small
    for copy in qkv_last:
        copy.wait_recv()
    for copy in sent + twins:
        copy.wait_send()


def tail(g_attn, d_heads, joined, lse, normed, qkv, source, gain, d_hidden, tiny, n_expert, n_cuts):
    tokens, features = d_heads.shape
    heads, seq_len = lse.shape
    levels, own = n_expert // 2, features // n_cuts
    deep = features // n_expert
    piece, wide = deep // n_cuts, 3 * own
    any_spec, vmem_spec = pl.BlockSpec(memory_space=pl.ANY), pl.BlockSpec(memory_space=pltpu.VMEM)
    shape, vmem, dma = jax.ShapeDtypeStruct, pltpu.VMEM, pltpu.SemaphoreType.DMA
    rows = tiny.shape[0]
    grid = (levels, 2, deep, features)
    return pl.pallas_call(
        functools.partial(tail_kernel, heads, HD ** (-0.5)),
        name="tail",
        out_shape=(
            shape((tokens, features), F32), shape((n_cuts, piece, wide), BF), shape((piece, features), F32), shape((rows, 128), F32), shape((8, 128), F32),
        ),
        in_specs=[any_spec] + [vmem_spec] * 3 + [any_spec] * 2 + [vmem_spec] * 4,
        out_specs=(vmem_spec,) * 5,
        scratch_shapes=[
            vmem((levels, deep, features), BF), vmem((levels, deep, features), BF),
            vmem((n_cuts - 1, levels, piece, features), BF),
            vmem((levels - 1, piece, features), BF), vmem((levels, piece, features), BF),
            vmem((levels, 2, deep, wide), BF), vmem((levels, deep, wide), BF), vmem((levels, deep, wide), BF),
            vmem((levels - 1, deep, wide), BF), vmem((n_cuts, piece, wide), BF),
            vmem((n_cuts, tokens, own), BF), vmem((seq_len, wide), BF),
            vmem((seq_len, own), F32), vmem((seq_len, own), F32), vmem((seq_len, own), F32),
            vmem((n_cuts, tokens, features), BF), vmem((n_cuts - 1, tokens, features), BF),
            vmem((seq_len, features), BF), vmem((features, wide), BF),
            vmem((n_expert, rows, 128), F32), vmem((rows, 128), F32), vmem((n_cuts, rows, 128), F32),
            vmem((8, features), F32), vmem((n_expert, 8, 128), F32), vmem((8, 128), F32), vmem((n_cuts, 8, 128), F32),
            dma((3,)), dma((2, 2)), dma((2, 2 * (levels - 1))), dma((2, 4 * (n_cuts - 1))),
            dma((2, 2 * (n_expert - 1))), dma((2, 2 * (n_cuts - 1))),
        ],
        compiler_params=pltpu.CompilerParams(
            collective_id=2, has_side_effects=True, vmem_limit_bytes=48 << 20
        ),
        cost_estimate=pl.CostEstimate(flops=20_000_000_000, bytes_accessed=24 << 20, transcendentals=0),
    )(
        g_attn.reshape(grid), d_heads, joined, lse.reshape(heads, 1, seq_len),
        normed, qkv, source, gain, d_hidden, tiny,
    )


def head_kernel(
    sizes, source, gains, small, info, sort, w_qkv, w_attn, w_in, cotangent,
    normed, qkv, joined, lse, head_out, attn_full, in_here, small_full, grad_all, grad_rows, placer, gains_all,
    src_v, qkv_v, norm_v, join_v, acc, heads_low, attn_v, in_v, cot_v, slots, zbuf, row_v,
    load_sem, store_sem, cut_sem, twin_sem, z_sem, level_sem,
):
    heads, scaling, groups, here, slab = sizes
    me, cut = lax.axis_index("expert"), lax.axis_index("cuts")
    core = lax.rem(me, 2)
    twin = (jnp.bitwise_xor(me, 1), cut)
    at = [jnp.bitwise_xor(cut, k) for k in range(4)]
    n_cuts, tokens, width = src_v.shape
    n_expert, block = zbuf.shape[1], zbuf.shape[2]
    own, half, levels = width // n_cuts, tokens // 2, n_expert // 2
    level, quarter = lax.div(me, 2), tokens // n_expert

    def span(start, size, step):
        return pl.ds(pl.multiple_of(start, step), size)

    def remote(src, dst, sems, index, peer):
        return pltpu.make_async_remote_copy(
            src_ref=src, dst_ref=dst, send_sem=sems.at[0, index], recv_sem=sems.at[1, index],
            device_id=peer, device_id_type=MESH,
        )

    def local(src, dst, sems, index):
        copy = pltpu.make_async_copy(src, dst, sems.at[index])
        copy.start()
        return copy

    loads = [
        local(cotangent, cot_v, load_sem, 0),
        local(w_attn, attn_v, load_sem, 1),
        local(w_in.at[:, span(cut * width, width, width)], in_v, load_sem, 2),
    ]
    own_qkv = [
        local(
            w_qkv.at[:, span(n * width + cut * own, own, own)],
            qkv_v.at[span(cut * tokens, tokens, tokens), pl.ds(n * own, own)], load_sem, 3 + n,
        )
        for n in range(3)
    ]
    barrier = pltpu.get_barrier_semaphore()
    for k in range(1, n_expert):
        pl.semaphore_signal(barrier, inc=1, device_id=(jnp.bitwise_xor(me, k), cut), device_id_type=MESH)
    for k in range(1, n_cuts):
        pl.semaphore_signal(barrier, inc=1, device_id=(me, at[k]), device_id_type=MESH)
    pl.semaphore_wait(barrier, n_expert + n_cuts - 2)

    def gather(view, first, base):
        return [
            remote(first, view(cut), cut_sem, base, (me, at[1])),
            remote(first, view(cut), cut_sem, base + 1, (me, at[2])),
            remote(view(at[1], 0), view(at[1], 0), cut_sem, base + 2, (me, at[2])),
            remote(view(at[2], 1), view(at[2], 1), cut_sem, base + 3, (me, at[1])),
        ]

    def relay(copies):
        copies[0].wait_recv()
        copies[2].start()
        copies[1].wait_recv()
        copies[3].start()

    def whole(ref):
        def view(owner, piece=None):
            return ref.at[owner] if piece is None else ref.at[owner, pl.ds(piece * half, half)]

        return view

    def weight_rows(owner):
        return span(owner * tokens + core * half + level * quarter, quarter, quarter)

    def pass_levels(ref, base):
        copies = []
        for k in range(1, n_cuts):
            view = ref.at[weight_rows(at[k])]
            for n in range(1, levels):
                peer = (2 * jnp.bitwise_xor(level, n) + core, cut)
                copies.append(remote(view, view, level_sem, base + (k - 1) * (levels - 1) + n - 1, peer))
                copies[-1].start()
        return copies

    def slab_view(owner, piece=None):
        if piece is None:
            return grad_rows.at[:, span(owner * slab, slab, slab // 2)]
        return grad_rows.at[:, span(owner * slab + piece * (slab // 2), slab // 2, slab // 2)]

    def to_cuts(src_of, dst_of, base):
        return [remote(src_of(at[k]), dst_of(k), cut_sem, base + k - 1, (me, at[k])) for k in (3, 1, 2)]

    tokens_moved = gather(whole(src_v), source, 0)
    gains_moved = to_cuts(lambda peer: gains, lambda k: gains_all.at[cut], 16)
    small_moved = to_cuts(lambda peer: small, lambda k: small_full.at[cut], 19)
    qkv_moved = []
    for n in range(3):
        qkv_moved += to_cuts(
            lambda peer: w_qkv.at[weight_rows(0), span(n * width + peer * own, own, own)],
            lambda k: qkv_v.at[weight_rows(cut), pl.ds(n * own, own)],
            22 + 3 * n,
        )
    grad_moved = gather(whole(grad_all), cot_v, 4)
    attn_moved = to_cuts(lambda peer: w_attn.at[weight_rows(0)], lambda k: attn_full.at[weight_rows(cut)], 8)
    slab_moved = gather(slab_view, row_v, 12)
    in_moved = to_cuts(
        lambda peer: w_in.at[weight_rows(0), span(peer * width, width, width)],
        lambda k: in_here.at[weight_rows(cut)], 31,
    )
    for copy in gains_moved + tokens_moved[:2] + qkv_moved + attn_moved + in_moved + small_moved:
        copy.start()
    head_moved = to_cuts(
        lambda peer: heads_low.at[span(peer * tokens, tokens, tokens)],
        lambda k: head_out.at[:, span(cut * own, own, own)], 34,
    )

    loads[0].wait()
    lane = lax.broadcasted_iota(jnp.int32, (tokens, 128), 1).astype(F32)
    picked = jnp.where(lane == info[:, 0:1], info[:, 1:2], 0.0)
    down = lax.broadcasted_iota(jnp.int32, (tokens, tokens), 0)
    right = lax.broadcasted_iota(jnp.int32, (tokens, tokens), 1)
    running = mm((down >= right).astype(F32).astype(BF), picked.astype(BF))
    target = info[:, 2:3] + jnp.sum(picked * running, axis=1, keepdims=True) - 1.0
    column = lax.broadcasted_iota(jnp.int32, placer.shape, 1).astype(F32)
    placer[...] = jnp.where(column == target, info[:, 1:2], 0.0).astype(BF)
    slots[...] = mm_tn(placer[...], cot_v[...]).astype(BF).reshape(slots.shape)
    z_moved = []
    for g in range(groups):
        for k in range(1, n_expert):
            peer = jnp.bitwise_xor(me, k)
            z_moved.append(remote(slots.at[g, peer], zbuf.at[g, me], z_sem, g * n_expert + k, (peer, cut)))
            z_moved[-1].start()
        zbuf[g, me] = slots[g, me]
    src_v[cut] = source[...]
    gains_all[cut] = gains[...]
    small_full[cut] = small[...]
    relay(tokens_moved)
    for copy in grad_moved[:2]:
        copy.start()
    for copy in qkv_moved:
        copy.wait_recv()
    qkv_levels = pass_levels(qkv_v, 0)
    for copy in loads[1:] + own_qkv:
        copy.wait()
    stores = [
        local(cot_v, grad_all.at[cut], store_sem, 0),
        local(attn_v, attn_full.at[span(cut * tokens, tokens, tokens)], store_sem, 1),
        local(in_v, in_here.at[span(cut * tokens, tokens, tokens)], store_sem, 2),
    ]
    for copy in gains_moved:
        copy.wait_recv()

    def normalize(index):
        xhat, _ = norm_parts(src_v[index].astype(F32))
        for n in range(n_cuts):
            cols = slice(n * own, (n + 1) * own)
            norm_v[index, :, cols] = (xhat[:, cols] * gains_all[n, 0:1, :]).astype(BF)

    normalize(cut)
    normalize(at[1])
    normalize(at[2])
    for copy in attn_moved + in_moved:
        copy.wait_recv()
    attn_levels = pass_levels(attn_full, 3 * (levels - 1))
    in_levels = pass_levels(in_here, 6 * (levels - 1))
    for copy in qkv_levels:
        copy.wait_recv()

    def share(ref, base):
        copies = []
        for k in range(1, n_cuts):
            view = ref.at[span(at[k] * tokens + core * half, half, half)]
            copies.append(remote(view, view, twin_sem, base + k - 1, twin))
            copies[-1].start()
        return copies

    shared = share(qkv_v, 0)
    for copy in tokens_moved[2:]:
        copy.wait_recv()
    normalize(at[3])
    for copy in shared:
        copy.wait_recv()

    @pl.loop(0, n_cuts)
    def _(step):
        join_v[step] = mm(norm_v[step], qkv_v[...]).astype(BF)

    stores += [
        local(norm_v, normed, store_sem, 3), local(qkv_v, qkv, store_sem, 4), local(join_v, joined, store_sem, 5),
    ]
    acc[...] = jnp.zeros_like(acc)
    per_group = here // groups
    for copy in z_moved:
        copy.wait_recv()
    for g in range(groups):
        flat = zbuf[g].reshape(n_expert * block, width)
        for j in range(per_group):
            row_v[g * per_group + j] = mm(sort[pl.ds(j * slab, slab), :], flat).astype(BF)
    for copy in slab_moved[:2]:
        copy.start()
    stores.append(local(row_v, slab_view(cut), store_sem, 6))

    @pl.loop(0, heads)
    def _(head):
        @pl.when(head == 2)
        def _():
            relay(grad_moved)

        pair = lax.div(head, 2)
        lane = lax.broadcasted_iota(jnp.int32, (1, 128), 1)
        keep = (lax.div(lane, HD) == lax.rem(head, 2)).astype(F32)
        keep_low = keep.astype(BF)
        cols = span(pair * 128, 128, 128)
        k_cols = span(own + pair * 128, 128, 128)
        v_cols = span(2 * own + pair * 128, 128, 128)
        for i in range(n_cuts):
            reach = (i + 1) * tokens
            query = join_v[i, :, cols] * keep_low
            keys = join_v[pl.ds(0, i + 1), :, k_cols].reshape(reach, 128)
            values = join_v[pl.ds(0, i + 1), :, v_cols].reshape(reach, 128)
            scores = mm_nt(keys, query) * scaling
            key_at = lax.broadcasted_iota(jnp.int32, scores.shape, 0)
            query_at = lax.broadcasted_iota(jnp.int32, scores.shape, 1) + i * tokens
            scores = jnp.where(key_at <= query_at, scores, -1e30)
            peak = jnp.max(scores, axis=0, keepdims=True)
            powers = jnp.exp(scores - peak)
            total = jnp.sum(powers, axis=0, keepdims=True)
            lse[head, :, pl.ds(i * tokens, tokens)] = peak + jnp.log(total)
            soft = (powers / total).astype(BF)
            acc[pl.ds(i * tokens, tokens), cols] += mm_tn(soft, values) * keep

    heads_low[...] = acc[...].astype(BF)
    for copy in head_moved:
        copy.start()
    head_out[:, span(cut * own, own, own)] = heads_low[span(cut * tokens, tokens, tokens), :]
    relay(slab_moved)
    for copy in attn_levels + in_levels:
        copy.wait_recv()
    shared += share(attn_full, 3)
    shared += share(in_here, 6)
    for copy in shared[3:] + grad_moved[2:] + slab_moved[2:] + head_moved + small_moved:
        copy.wait_recv()
    for copy in stores:
        copy.wait()
    everything = tokens_moved + gains_moved + small_moved + qkv_moved + grad_moved + attn_moved + slab_moved
    everything += qkv_levels + attn_levels + in_levels
    for copy in everything + in_moved + head_moved + z_moved + shared:
        copy.wait_send()


def head(source, gains, small, info, sort, w_qkv, w_attn, w_in, cotangent, here, groups, capacity, n_expert, n_cuts):
    tokens, features = source.shape
    seq_len, own = tokens * n_cuts, features // n_cuts
    heads, slab = own // HD, n_expert * capacity
    block = here // groups * capacity
    any_spec, vmem_spec = pl.BlockSpec(memory_space=pl.ANY), pl.BlockSpec(memory_space=pltpu.VMEM)
    shape, vmem, dma = jax.ShapeDtypeStruct, pltpu.VMEM, pltpu.SemaphoreType.DMA
    slots = n_expert * groups * block
    return pl.pallas_call(
        functools.partial(head_kernel, (heads, HD ** (-0.5), groups, here, slab)),
        name="head",
        out_shape=(
            shape((n_cuts, tokens, features), BF), shape((features, 3 * own), BF), shape((n_cuts, tokens, 3 * own), BF),
            shape((heads, 1, seq_len), F32), shape((tokens, features), BF), shape((features, features), BF),
            shape((features, w_in.shape[1] // n_cuts), BF), shape((n_cuts,) + small.shape, BF),
            shape((n_cuts, tokens, features), BF), shape((here, n_cuts * slab, features), BF),
            shape((tokens, slots), BF), shape((n_cuts,) + gains.shape, F32),
        ),
        in_specs=[vmem_spec] * 5 + [any_spec] * 4,
        out_specs=(any_spec,) * 3 + (vmem_spec,) * 2 + (any_spec,) * 2 + (vmem_spec,) + (any_spec,) * 2 + (vmem_spec,) * 2,
        scratch_shapes=[
            vmem((n_cuts, tokens, features), BF), vmem((features, 3 * own), BF), vmem((n_cuts, tokens, features), BF),
            vmem((n_cuts, tokens, 3 * own), BF), vmem((seq_len, own), F32), vmem((seq_len, own), BF),
            vmem((tokens, features), BF), vmem((tokens, features), BF), vmem((tokens, features), BF),
            vmem((groups, n_expert, block, features), BF), vmem((groups, n_expert, block, features), BF),
            vmem((here, slab, features), BF),
            dma((6,)), dma((7,)), dma((2, 37)), dma((2, 9)), dma((2, groups * n_expert)), dma((2, 9 * (n_expert // 2 - 1))),
        ],
        compiler_params=pltpu.CompilerParams(
            collective_id=3, has_side_effects=True, vmem_limit_bytes=48 << 20
        ),
        cost_estimate=pl.CostEstimate(flops=8_000_000_000, bytes_accessed=24 << 20, transcendentals=0),
    )(source, gains, small, info, sort, w_qkv, w_attn, w_in, cotangent)


def expert_grads_kernel(rows, d_first, act, d_rows, grad_in, grad_out):
    grad_in[0] = mm_tn(rows[0], d_first[0])
    grad_out[0] = mm_tn(act[0], d_rows[0])


def expert_grads(rows, d_first, act, d_rows):
    here, count, width = rows.shape
    hidden = act.shape[2]
    part = pl.BlockSpec((1, count, 256), lambda e, t: (e, 0, t))
    return pl.pallas_call(
        expert_grads_kernel,
        name="expert_grads",
        grid=(here, width // 256),
        out_shape=(jax.ShapeDtypeStruct((here, width, hidden), F32), jax.ShapeDtypeStruct((here, hidden, width), F32)),
        in_specs=[
            part, pl.BlockSpec((1, count, hidden), lambda e, t: (e, 0, 0)),
            part, pl.BlockSpec((1, count, width), lambda e, t: (e, 0, 0)),
        ],
        out_specs=(
            pl.BlockSpec((1, 256, hidden), lambda e, t: (e, t, 0)), pl.BlockSpec((1, 256, width), lambda e, t: (e, t, 0)),
        ),
        compiler_params=pltpu.CompilerParams(vmem_limit_bytes=32 << 20),
        cost_estimate=pl.CostEstimate(flops=4 * here * count * width * hidden, bytes_accessed=46 << 20, transcendentals=0),
    )(rows, d_first, act, d_rows)


def shards(
    block_input,
    routes,
    kept_mask,
    w_qkv,
    w_attn_out,
    w_in,
    w_out,
    w_router,
    w_mix,
    gain_attn,
    gain_ffn,
    expert_in,
    expert_out,
    cotangent,
):
    tokens, features = block_input.shape
    n_cuts = lax.axis_size("cuts")
    n_expert = lax.axis_size("expert")
    seq_len = tokens * n_cuts
    scaling = HD ** (-0.5)
    own = features // n_cuts
    heads = own // HD
    experts_all = w_router.shape[1]
    experts_here = expert_in.shape[0]
    capacity = 3 * tokens // (2 * experts_all)

    onehot = (routes[:, None] == jnp.arange(experts_all, dtype=jnp.int32)[None, :]).astype(F32)
    fused = n_cuts == 4
    groups = 2 if fused else 1
    per_group = experts_here // groups
    block = per_group * capacity
    owner, local = routes // experts_here, routes % experts_here
    start = (local // per_group) * (n_expert * block) + owner * block + local % per_group * capacity
    if not fused:
        onehot_kept = onehot * kept_mask.astype(F32)[:, None]
        lower_tri = (jnp.arange(tokens)[:, None] >= jnp.arange(tokens)[None, :]).astype(BF)
        running = mm(lower_tri, onehot_kept.astype(BF))
        slot_num = jnp.sum(onehot_kept * running, axis=1) - 1.0
        target = start.astype(F32) + slot_num
        columns = jnp.arange(experts_all * capacity, dtype=jnp.int32).astype(F32)
        placer = ((columns[None, :] == target[:, None]) & (kept_mask[:, None] > 0)).astype(BF)

    def to_owners(rows):
        grid = mm_tn(placer, rows).astype(BF).reshape(groups, n_expert, block, features)
        grid = grid.swapaxes(0, 1).reshape(n_expert, experts_here, capacity, features)
        moved = lax.all_to_all(grid, "expert", split_axis=0, concat_axis=2, tiled=True)
        return lax.all_gather(moved, "cuts", axis=2, tiled=True)[0]

    def to_sources(rows):
        summed = lax.psum_scatter(rows[None].astype(BF), "cuts", scatter_dimension=2, tiled=True)
        moved = lax.all_to_all(summed, "expert", split_axis=2, concat_axis=0, tiled=True)
        return mm(placer, moved.reshape(-1, features))

    inputs = block_input.astype(F32)
    if fused:
        pair = jnp.stack([gain_attn, gain_ffn], axis=0).astype(F32)
        small_here = jnp.concatenate([w_router, w_mix], axis=1)
        small_cols = small_here.shape[1]
        at = np.arange(n_expert * block)
        slab = n_expert * capacity
        goal = at % slab // capacity * block + at // slab * capacity + at % capacity
        sort = np.asarray(goal[:, None] == at[None, :], dtype=BF)
        info = jnp.stack([routes, kept_mask, start], axis=1).astype(F32)
        normed, qkv_here, joined, log_norm, head_out, attn_full, in_here, small_wide, grad_all, grad_rows, placer, gains = head(
            block_input, jnp.pad(pair, ((0, 6), (0, 0))), jnp.pad(small_here, ((0, 0), (0, -small_cols % 128))),
            info, jnp.asarray(sort), w_qkv, w_attn_out, w_in, cotangent,
            experts_here, groups, capacity, n_expert, n_cuts,
        )
        normed, joined = normed.reshape(seq_len, features), joined.reshape(seq_len, 3 * own)
        small_wide = small_wide.reshape(features, -1)
        small_full = small_wide[:, :small_cols]
        gain_one, gain_two = gains[:, 0].reshape(features), gains[:, 1].reshape(features)
    else:
        gains = gather_cuts(jnp.stack([gain_attn, gain_ffn], axis=1)).astype(F32)
        gain_one, gain_two = gains[:, 0], gains[:, 1]
        xhat_one, inv_one = norm_parts(inputs)
        normed = gather_cuts((xhat_one * gain_one).astype(BF))
        qkv_here = lax.all_to_all(
            w_qkv.reshape(own, 3, n_cuts, own), "cuts", split_axis=2, concat_axis=0, tiled=True
        ).reshape(features, 3 * own)
        joined = mm(normed, qkv_here).astype(BF)
        split = joined.reshape(seq_len, 3, heads, HD)
        q_heads, k_heads, v_heads = split[:, 0], split[:, 1], split[:, 2]
        spots = jnp.arange(seq_len, dtype=jnp.int32)
        visible = (spots[None, :] <= spots[:, None])[None]

        def masked_scores():
            scores = jnp.einsum("qhd,khd->hqk", q_heads, k_heads, preferred_element_type=F32) * scaling
            return jnp.where(visible, scores, -1e30)

        scores = masked_scores()
        peak = jnp.max(scores, axis=-1, keepdims=True)
        row_exp = jnp.exp(scores - peak)
        total = jnp.sum(row_exp, axis=-1, keepdims=True)
        weights_p = (row_exp / total).astype(BF)
        heads_here = jnp.einsum("hqk,khd->qhd", weights_p, v_heads, preferred_element_type=F32)
        log_norm = peak + jnp.log(total)
        head_out = rows_to_cuts(heads_here.reshape(seq_len, own).astype(BF))
        attn_full = gather_cuts(w_attn_out)
        small_full = gather_cuts(jnp.concatenate([w_router, w_mix], axis=1))
        grad_all = gather_cuts(cotangent)
        grad_rows = to_owners(cotangent)
        in_here = columns_to_cuts(w_in)
    hidden = inputs + mm(head_out, attn_full)
    xhat_two, inv_two = norm_parts(hidden)
    second = (xhat_two * gain_two).astype(BF)

    logits = mm(second, small_full)
    router_p = softmax_rows(logits[:, :experts_all])
    mixing = softmax_rows(logits[:, experts_all:])
    gate = jnp.sum(router_p * onehot, axis=1)
    grad = cotangent.astype(F32)
    d_moe = grad * mixing[:, 1:2]

    if fused:
        slots = mm_tn(placer, second).astype(BF).reshape(groups, n_expert, block, features)
        sums, ret_a, ret_b, s_in, s_out, rows_in, d_rows, expert_low, d_first = middle(
            slots, second, grad_all, grad_rows, in_here, w_out, small_wide, jnp.asarray(sort),
            expert_in, expert_out, n_expert, n_cuts,
        )
        dense, d_second_ffn = sums[0], sums[1]
        g_expert_in, g_expert_out = expert_grads(rows_in, d_first, expert_low, d_rows)
        picked = mm(placer, ret_a.reshape(-1, features))
        d_picked_in = mm(placer, ret_b.reshape(-1, features))
    else:
        rows_in = to_owners(second)
        row_logits = jnp.einsum("erd,dk->erk", rows_in, small_full, preferred_element_type=F32)
        ids = lax.axis_index("expert") * experts_here + jnp.arange(experts_here, dtype=jnp.int32)
        is_here = (jnp.arange(experts_all, dtype=jnp.int32)[None, :] == ids[:, None]).astype(F32)
        row_gate = jnp.sum(
            softmax_rows(row_logits[:, :, :experts_all]) * is_here[:, None, :], axis=2, keepdims=True
        )
        row_mixing = softmax_rows(row_logits[:, :, experts_all:])[:, :, 1:2]
        d_rows = (grad_rows.astype(F32) * row_mixing * row_gate).astype(BF)

        first = jnp.einsum("erd,edh->erh", rows_in, expert_in, preferred_element_type=F32)
        expert_act, expert_pull = jax.vjp(jax.nn.gelu, first)
        expert_low = expert_act.astype(BF)
        partial_out = jnp.einsum("erh,ehd->erd", expert_low, expert_out, preferred_element_type=F32)
        picked = to_sources(partial_out)

        second_all = gather_cuts(second)
        mixing_all = softmax_rows(mm(second_all, small_full[:, experts_all:]))
        d_dense_all = (grad_all.astype(F32) * mixing_all[:, 0:1]).astype(BF)
        up_proj = mm(second_all, in_here)
        activ, gelu_pull = jax.vjp(jax.nn.gelu, up_proj)
        activ_low = activ.astype(BF)
        dense = scatter_cuts(mm(activ_low, w_out)).astype(F32)
        d_activ = mm_nt(d_dense_all, w_out)
        g_out = mm_tn(activ_low, d_dense_all)
        d_up = gelu_pull(d_activ)[0].astype(BF)
        g_in = mm_tn(second_all, d_up)
        d_second_ffn = scatter_cuts(mm_nt(d_up, in_here)).astype(F32)

        d_expert_act = jnp.einsum("erd,ehd->erh", d_rows, expert_out, preferred_element_type=F32)
        d_first = expert_pull(d_expert_act)[0].astype(BF)
        d_rows_in = jnp.einsum("erh,edh->erd", d_first, expert_in, preferred_element_type=F32)
        g_expert_out = jnp.einsum("erh,erd->ehd", expert_low, d_rows, preferred_element_type=F32)
        g_expert_in = jnp.einsum("erd,erh->edh", rows_in, d_first, preferred_element_type=F32)
        d_picked_in = to_sources(d_rows_in)

    moe_val = gate[:, None] * picked
    block_out = (hidden + mixing[:, 0:1] * dense + mixing[:, 1:2] * moe_val).astype(BF)
    d_mixing = jnp.stack([jnp.sum(grad * dense, axis=1), jnp.sum(grad * moe_val, axis=1)], axis=1)
    d_gate = jnp.sum(d_moe * picked, axis=1)
    d_router = router_p * (onehot - gate[:, None]) * d_gate[:, None]
    d_mix = mixing * (d_mixing - jnp.sum(mixing * d_mixing, axis=1, keepdims=True))
    d_small = jnp.concatenate([d_router, d_mix], axis=1).astype(BF)
    g_small = mm_tn(d_small, second)
    d_second = d_second_ffn + mm_nt(d_small, small_full) + d_picked_in
    d_hidden_norm, g_gain_two = norm_back(d_second, xhat_two, inv_two, gain_two)
    d_hidden = grad + d_hidden_norm
    d_attn = d_hidden.astype(BF)
    g_attn_out = mm_tn(head_out, d_attn)
    d_head_rows = mm_nt(d_attn, attn_full).astype(BF)
    if fused:
        tiny = jnp.concatenate([g_small, g_gain_two[None, :]], axis=0)
        tiny = jnp.pad(tiny, ((0, -tiny.shape[0] % 8), (0, 0)))
        d_block_input, s_qkv, s_attn_out, tiny, late = tail(
            g_attn_out.astype(BF), d_head_rows, joined, log_norm[:, 0], normed,
            qkv_here, block_input, gain_one[None, :], d_hidden, tiny, n_expert, n_cuts,
        )
        swap = [
            ((flat % n_expert) * n_cuts + flat // n_expert, flat) for flat in range(n_expert * n_cuts)
        ]
        s_out = lax.ppermute(s_out, ("expert", "cuts"), swap).astype(F32)
        s_in = s_in.swapaxes(0, 1).reshape(-1, w_in.shape[1]).astype(F32)
        s_qkv = s_qkv.reshape(n_cuts, -1, 3, own).transpose(1, 2, 0, 3).reshape(-1, 3 * features).astype(F32)
        width = features // (n_expert * n_cuts)
        spot = lax.axis_index("cuts") * width
        s_tiny = lax.dynamic_slice_in_dim(tiny, spot, width, axis=1)
        s_late = lax.dynamic_slice_in_dim(late, spot, width, axis=1)
        return (
            block_out,
            d_block_input,
            s_qkv,
            s_attn_out,
            s_in,
            s_out,
            s_tiny[:experts_all].T,
            s_tiny[experts_all : experts_all + 2].T,
            s_late[0],
            s_tiny[experts_all + 2],
            g_expert_in,
            g_expert_out,
        )
    d_heads = columns_to_cuts(d_head_rows).reshape(seq_len, heads, HD)

    soft_p = jnp.exp(masked_scores() - log_norm)
    d_soft = jnp.einsum("qhd,khd->hqk", d_heads, v_heads, preferred_element_type=F32)
    delta = jnp.sum(soft_p * d_soft, axis=-1, keepdims=True)
    d_scores = (soft_p * (d_soft - delta)).astype(BF)
    d_query = jnp.einsum("hqk,khd->qhd", d_scores, k_heads, preferred_element_type=F32) * scaling
    d_keys = jnp.einsum("hqk,qhd->khd", d_scores, q_heads, preferred_element_type=F32) * scaling
    d_values = jnp.einsum("hqk,qhd->khd", soft_p.astype(BF), d_heads, preferred_element_type=F32)
    d_joined = jnp.stack([d_query, d_keys, d_values], axis=1).reshape(seq_len, 3 * own).astype(BF)
    g_qkv = mm_tn(normed, d_joined)
    d_normed = scatter_cuts(mm_nt(d_joined, qkv_here)).astype(F32)
    d_input_norm, g_gain_one = norm_back(d_normed, xhat_one, inv_one, gain_one)
    d_block_input = d_hidden + d_input_norm

    def over_experts(part):
        return lax.psum_scatter(part.astype(BF), "expert", scatter_dimension=0, tiled=True)

    s_in = rows_to_cuts(over_experts(g_in)).astype(F32)
    s_out = over_experts(g_out)
    swap = [
        ((flat % n_expert) * n_cuts + flat // n_expert, flat) for flat in range(n_expert * n_cuts)
    ]
    s_out = lax.ppermute(s_out, ("expert", "cuts"), swap).astype(F32)
    s_qkv = over_experts(g_qkv)
    deep = s_qkv.shape[0]
    s_qkv = lax.all_to_all(
        s_qkv.reshape(deep, 3, 1, own), "cuts", split_axis=0, concat_axis=2, tiled=True
    )
    s_qkv = s_qkv.reshape(-1, 3 * features).astype(F32)
    s_attn_out = scatter_cuts(over_experts(g_attn_out)).astype(F32)
    tiny = jnp.concatenate([g_small, g_gain_one[None, :], g_gain_two[None, :]], axis=0)
    tiny = jnp.pad(tiny, ((0, -tiny.shape[0] % 8), (0, 0)))
    tiny = sum_small(tiny, n_expert, n_cuts)
    width = features // (n_expert * n_cuts)
    s_tiny = lax.dynamic_slice_in_dim(tiny, lax.axis_index("cuts") * width, width, axis=1)
    return (
        block_out,
        d_block_input,
        s_qkv,
        s_attn_out,
        s_in,
        s_out,
        s_tiny[:experts_all].T,
        s_tiny[experts_all : experts_all + 2].T,
        s_tiny[experts_all + 2],
        s_tiny[experts_all + 3],
        g_expert_in,
        g_expert_out,
    )


def solution(mesh):
    both = ("expert", "cuts")
    placed = (
        P(both, None),
        P(both),
        P(both),
        P("cuts", None),
        P("cuts", None),
        P("cuts", None),
        P("cuts", None),
        P("cuts", None),
        P("cuts", None),
        P("cuts"),
        P("cuts"),
        P("expert", None, "cuts"),
        P("expert", "cuts", None),
        P(both, None),
    )
    results = (
        P(both, None),
        P(both, None),
        P(both, None),
        P(both, None),
        P(both, None),
        P(both, None),
        P(both, None),
        P(both, None),
        P(both),
        P(both),
        P("expert", None, "cuts"),
        P("expert", "cuts", None),
    )
    return jax.shard_map(
        shards, mesh=mesh, in_specs=placed, out_specs=results, check_vma=False
    )
```

```python
import functools
import math

import jax
import jax.numpy as jnp
import numpy as np
from jax import lax
from jax.experimental import pallas as pl
from jax.experimental.pallas import tpu as pltpu
from jax.sharding import PartitionSpec as P

HD = 64
BF = jnp.bfloat16
F32 = jnp.float32
MESH = pl.DeviceIdType.MESH


def norm_parts(values):
    center = values - jnp.mean(values, axis=-1, keepdims=True)
    spread = jnp.mean(center * center, axis=-1, keepdims=True)
    inv = lax.rsqrt(spread + 1e-05)
    return center * inv, inv


def norm_back(grad, xhat, inv, gain):
    q = grad * gain
    mean_q = jnp.mean(q, axis=-1, keepdims=True)
    mean_qx = jnp.mean(q * xhat, axis=-1, keepdims=True)
    return (q - mean_q - xhat * mean_qx) * inv, jnp.sum(grad * xhat, axis=0)


def mm(left, right):
    return jnp.dot(left, right, preferred_element_type=F32)


def mm_nt(left, right):
    return lax.dot_general(left, right, (((1,), (1,)), ((), ())), preferred_element_type=F32)


def mm_tn(left, right):
    return lax.dot_general(left, right, (((0,), (0,)), ((), ())), preferred_element_type=F32)


def softmax_rows(logits):
    shifted = logits - jnp.max(logits, axis=-1, keepdims=True)
    row_exp = jnp.exp(shifted)
    return row_exp / jnp.sum(row_exp, axis=-1, keepdims=True)


def gather_cuts(rows):
    return lax.all_gather(rows, "cuts", axis=0, tiled=True)


def scatter_cuts(rows):
    return lax.psum_scatter(rows.astype(BF), "cuts", scatter_dimension=0, tiled=True)


def columns_to_cuts(rows):
    return lax.all_to_all(rows, "cuts", split_axis=1, concat_axis=0, tiled=True)


def rows_to_cuts(rows):
    return lax.all_to_all(rows, "cuts", split_axis=0, concat_axis=1, tiled=True)


def ring_mod(index, count):
    return lax.rem(index, count)


def small_kernel(n_expert, n_cuts, src, out, by_expert, mine, by_cuts, send_a, recv_a, send_b, recv_b):
    me, cut = lax.axis_index("expert"), lax.axis_index("cuts")
    width = out.shape[1]
    barrier = pltpu.get_barrier_semaphore()
    for step in range(1, n_expert):
        peer = ring_mod(me + step, n_expert)
        pl.semaphore_signal(barrier, inc=1, device_id=(peer, cut), device_id_type=MESH)
    for step in range(1, n_cuts):
        peer = ring_mod(cut + step, n_cuts)
        pl.semaphore_signal(barrier, inc=1, device_id=(me, peer), device_id_type=MESH)
    pl.semaphore_wait(barrier, n_expert + n_cuts - 2)

    def part(owner):
        return src.at[:, pl.ds(pl.multiple_of(owner * width, 128), width)]

    copies = []
    for step in range(1, n_expert):
        peer = ring_mod(me + step, n_expert)
        copies.append(
            pltpu.make_async_remote_copy(
                src_ref=part(peer),
                dst_ref=by_expert.at[step],
                send_sem=send_a.at[step],
                recv_sem=recv_a.at[step],
                device_id=(peer, cut),
                device_id_type=MESH,
            )
        )
        copies[-1].start()
    total = src[:, pl.ds(pl.multiple_of(me * width, 128), width)]
    for step in range(1, n_expert):
        copies[step - 1].wait()
        total = total + by_expert[step]
    mine[...] = total
    copies = []
    for step in range(1, n_cuts):
        peer = ring_mod(cut + step, n_cuts)
        copies.append(
            pltpu.make_async_remote_copy(
                src_ref=mine,
                dst_ref=by_cuts.at[step],
                send_sem=send_b.at[step],
                recv_sem=recv_b.at[step],
                device_id=(me, peer),
                device_id_type=MESH,
            )
        )
        copies[-1].start()
    for step in range(1, n_cuts):
        copies[step - 1].wait()
        total = total + by_cuts[step]
    out[...] = total


def sum_small(values, n_expert, n_cuts):
    rows, features = values.shape
    width = features // n_expert
    pad = -width % 128
    if pad:
        values = jnp.pad(values.reshape(rows, n_expert, width), ((0, 0), (0, 0), (0, pad)))
        values = values.reshape(rows, n_expert * (width + pad))
    wide = width + pad
    summed = pl.pallas_call(
        functools.partial(small_kernel, n_expert, n_cuts),
        name="sum_small",
        out_shape=jax.ShapeDtypeStruct((rows, wide), F32),
        in_specs=[pl.BlockSpec(memory_space=pltpu.VMEM)],
        out_specs=pl.BlockSpec(memory_space=pltpu.VMEM),
        scratch_shapes=[
            pltpu.VMEM((n_expert, rows, wide), F32),
            pltpu.VMEM((rows, wide), F32),
            pltpu.VMEM((n_cuts, rows, wide), F32),
            pltpu.SemaphoreType.DMA((n_expert,)),
            pltpu.SemaphoreType.DMA((n_expert,)),
            pltpu.SemaphoreType.DMA((n_cuts,)),
            pltpu.SemaphoreType.DMA((n_cuts,)),
        ],
        compiler_params=pltpu.CompilerParams(collective_id=0, has_side_effects=True),
    )(values)
    return summed[:, :width]


def dot_nt(left, right):
    return lax.dot_general(left, right, (((1,), (1,)), ((), ())), preferred_element_type=F32)


def tile_of(step, size):
    return pl.ds(pl.multiple_of(step * size, size), size)


def lane_softmax(logits, low, high):
    lane = lax.broadcasted_iota(jnp.int32, logits.shape, 1)
    inside = (lane >= low) & (lane < high)
    kept = jnp.where(inside, logits, -1e30)
    powers = jnp.exp(kept - jnp.max(kept, axis=1, keepdims=True))
    powers = jnp.where(inside, powers, 0.0)
    return powers / jnp.sum(powers, axis=1, keepdims=True), lane


def mlp_both(rows, d_rows, w_up, w_down, act, d_up, write):
    root, cubic = math.sqrt(2.0 / math.pi), 0.044715

    @pl.loop(0, act.shape[1] // 256)
    def _(step):
        span = tile_of(step, 256)
        up = mm(rows[...], w_up[:, span])
        d_act = dot_nt(d_rows[...], w_down[span, :])
        square = up * up
        bent = jnp.tanh(root * up * (1.0 + cubic * square))
        half = 0.5 * (1.0 + bent)
        act[:, span] = (up * half).astype(BF)
        slope = half + 0.5 * up * (1.0 - bent * bent) * (root + 3.0 * root * cubic * square)
        d_up[:, span] = (d_act * slope).astype(BF)

    @pl.loop(0, w_up.shape[0] // 256)
    def _(step):
        span = tile_of(step, 256)
        write(span, mm(act[...], w_down[:, span]), dot_nt(d_up[...], w_up[span, :]))


def middle_kernel(
    sizes, slots, second, grad_all, grad_rows, w_in, w_out, small, sort, e_in, e_out,
    sums, ret_a, ret_b, o_in, o_out, rows_in, d_rows_all, act_e_all, d_first_all,
    sec, grd, win, wout, act, d_up, part_a, part_b, ffn_x, ffn_y, ffn_qa, ffn_qb,
    zbuf, rows, g_rows, d_rows, act_e, d_first, wi_e, wo_e, out_a, out_b, row_x, row_y, row_qa, row_qb, sorted_back, send_back,
    twin_in, level_in, fin_in,
    load_sem, weight_sem, store_sem, store_e_sem, z_sem, ag_sem, eag_sem, frs_sem, ers_sem, zr_sem,
    twin_sem, level_sem, fin_sem,
):
    n_expert, groups, here, slab = sizes
    me, cut = lax.axis_index("expert"), lax.axis_index("cuts")
    at_x, at_y, at_d = (jnp.bitwise_xor(cut, k) for k in (1, 2, 3))
    block = zbuf.shape[2]
    per_group = here // groups
    experts_all = n_expert * here

    def load(src, dst, index):
        copy = pltpu.make_async_copy(src, dst, load_sem.at[index])
        copy.start()
        return copy

    def remote(src, dst, sems, index, peer):
        return pltpu.make_async_remote_copy(
            src_ref=src, dst_ref=dst, send_sem=sems.at[0, index], recv_sem=sems.at[1, index],
            device_id=peer, device_id_type=MESH,
        )

    def send(src, dst, sems, index, peer):
        copy = remote(src, dst, sems, index, peer)
        copy.start()
        return copy

    loads = [
        load(second, sec.at[cut], 0), load(w_in, win, 1), load(w_out, wout, 2), load(grad_all, grd, 3),
    ]

    def fetch_expert(i):
        slot = i % 2
        copies = [
            pltpu.make_async_copy(e_in.at[i], wi_e.at[slot], weight_sem.at[0, slot]),
            pltpu.make_async_copy(e_out.at[i], wo_e.at[slot], weight_sem.at[1, slot]),
            pltpu.make_async_copy(grad_rows.at[i], g_rows.at[slot], weight_sem.at[2, slot]),
        ]
        for copy in copies:
            copy.start()
        return copies

    fetched = [fetch_expert(0), fetch_expert(1)]
    barrier = pltpu.get_barrier_semaphore()
    for k in range(1, n_expert):
        pl.semaphore_signal(barrier, inc=1, device_id=(jnp.bitwise_xor(me, k), cut), device_id_type=MESH)
    for peer in (at_x, at_y):
        pl.semaphore_signal(barrier, inc=1, device_id=(me, peer), device_id_type=MESH)
    pl.semaphore_signal(barrier, inc=1, device_id=(me, at_d), device_id_type=MESH)
    pl.semaphore_wait(barrier, n_expert + 2)
    core, level = lax.rem(me, 2), lax.div(me, 2)
    levels = n_expert // 2

    z_copies = []
    for g in range(groups):
        for k in range(1, n_expert):
            peer = jnp.bitwise_xor(me, k)
            z_copies.append(send(slots.at[g, peer], zbuf.at[g, me], z_sem, g * n_expert + k, (peer, cut)))
    loads[0].wait()
    ag = [
        send(sec.at[cut], sec.at[cut], ag_sem, 0, (me, at_x)),
        send(sec.at[cut], sec.at[cut], ag_sem, 1, (me, at_y)),
    ]
    half = sec.shape[1] // 2
    ag += [
        remote(sec.at[at_x, pl.ds(0, half)], sec.at[at_x, pl.ds(0, half)], ag_sem, 2, (me, at_y)),
        remote(sec.at[at_y, pl.ds(half, half)], sec.at[at_y, pl.ds(half, half)], ag_sem, 3, (me, at_x)),
    ]
    for g in range(groups):
        zbuf[g, me] = slots[g, me]
    def ffn_block(which, owner):
        mixing, lane = lane_softmax(mm(sec[owner], small[...]), experts_all, experts_all + 2)
        first_mix = jnp.sum(jnp.where(lane == experts_all, mixing, 0.0), axis=1, keepdims=True)
        grd[owner] = (grd[owner].astype(F32) * first_mix).astype(BF)

        def write(span, out, d_row):
            @pl.when(which == 0)
            def _():
                sums[0, :, span] = out
                sums[1, :, span] = d_row

            part_a[which, :, span] = out.astype(BF)
            part_b[which, :, span] = d_row.astype(BF)

        mlp_both(sec.at[owner], grd.at[owner], win, wout, act.at[owner], d_up.at[owner], write)

    def level_rows(index, half):
        return pl.ds(pl.multiple_of(index * 256 + half * 128, 128), 128)

    def weight_grad(m, left, right, held):
        @pl.loop(0, levels)
        def _(step):
            span = tile_of(step, 256)
            lhs = left[:, :, span].reshape(-1, 256)
            held[span, :] = mm_tn(lhs, right[...].reshape(-1, right.shape[2])).astype(BF)

        return [
            send(held.at[level_rows(n, 1 - core)], twin_in.at[m, n], twin_sem, m * levels + n, (jnp.bitwise_xor(me, 1), cut))
            for n in range(levels)
        ]

    def weight_sum(m, held, twins):
        for copy in twins:
            copy.wait_recv()

        @pl.loop(0, levels)
        def _(step):
            here_rows = level_rows(step, core)
            held[here_rows, :] = (held[here_rows, :].astype(F32) + twin_in[m, step].astype(F32)).astype(BF)

        copies = []
        for k in range(1, levels):
            peer = jnp.bitwise_xor(level, k)
            copies.append(
                send(
                    held.at[level_rows(peer, core)], level_in.at[m, k - 1], level_sem, m * (levels - 1) + k - 1,
                    (2 * peer + core, cut),
                )
            )
        return copies

    def weight_total(m, held, copies):
        for copy in copies:
            copy.wait_recv()
        total = held[level_rows(level, core), :].astype(F32)
        for k in range(1, levels):
            total = total + level_in[m, k - 1].astype(F32)
        return total.astype(BF)

    for copy in loads[1:]:
        copy.wait()
    def slab_of(owner):
        return pl.ds(pl.multiple_of(owner * slab, slab), slab)

    eag = {}
    cut_half = slab // 2
    for i in range(here):
        mine = rows.at[i, slab_of(cut)]
        from_x = rows.at[i, pl.ds(pl.multiple_of(at_x * slab, slab), cut_half)]
        from_y = rows.at[i, pl.ds(pl.multiple_of(at_y * slab + cut_half, cut_half), cut_half)]
        eag[i] = [
            remote(mine, mine, eag_sem, 4 * i, (me, at_x)),
            remote(mine, mine, eag_sem, 4 * i + 1, (me, at_y)),
            remote(from_x, from_x, eag_sem, 4 * i + 2, (me, at_y)),
            remote(from_y, from_y, eag_sem, 4 * i + 3, (me, at_x)),
        ]

    def relay(copies):
        copies[0].wait_recv()
        copies[2].start()
        copies[1].wait_recv()
        copies[3].start()

    @pl.loop(0, sec.shape[0])
    def _(which):
        @pl.when(which == 1)
        def _():
            relay(ag)

        @pl.when(which == 2)
        def _():
            for g in range(groups):
                for k in range(1, n_expert):
                    z_copies[g * (n_expert - 1) + k - 1].wait_recv()
                flat = zbuf[g].reshape(n_expert * block, zbuf.shape[3])
                for j in range(per_group):
                    i = g * per_group + j
                    rows[i, slab_of(cut)] = mm(sort[pl.ds(j * slab, slab), :], flat).astype(BF)
                    eag[i][0].start()
                    eag[i][1].start()

        @pl.when(which == 3)
        def _():
            ag[2].wait_recv()
            ag[3].wait_recv()
            relay(eag[0])

        ffn_block(which, jnp.bitwise_xor(cut, which))

    twins_in = weight_grad(0, sec, d_up, win)
    expert_stores = {}
    ers = {}

    def expert(i):
        slot = i % 2
        if i >= 2:
            for copy in expert_stores[i - 2]:
                copy.wait()
        for copy in fetched[i]:
            copy.wait()
        logits = mm(rows[i], small[...])
        router, lane = lane_softmax(logits, 0, experts_all)
        gate = jnp.sum(jnp.where(lane == me * here + i, router, 0.0), axis=1, keepdims=True)
        mixing, lane = lane_softmax(logits, experts_all, experts_all + 2)
        mixing = jnp.sum(jnp.where(lane == experts_all + 1, mixing, 0.0), axis=1, keepdims=True)
        d_rows[slot] = (g_rows[slot].astype(F32) * mixing * gate).astype(BF)

        def write(span, out, d_row):
            out_a[i, :, span] = out.astype(BF)
            out_b[i, :, span] = d_row.astype(BF)

        mlp_both(rows.at[i], d_rows.at[slot], wi_e.at[slot], wo_e.at[slot], act_e.at[slot], d_first.at[slot], write)
        expert_stores[i] = []
        for n, (src, dst) in enumerate(((d_rows, d_rows_all), (act_e, act_e_all), (d_first, d_first_all))):
            copy = pltpu.make_async_copy(src.at[slot], dst.at[i], store_e_sem.at[n, slot])
            copy.start()
            expert_stores[i].append(copy)
        ers[i] = [
            send(out_a.at[i, slab_of(at_x)], row_x.at[i, 0], ers_sem, 6 * i, (me, at_x)),
            send(out_a.at[i, slab_of(at_d)], row_x.at[i, 1], ers_sem, 6 * i + 1, (me, at_x)),
            send(out_b.at[i, slab_of(at_y)], row_y.at[i, 0], ers_sem, 6 * i + 2, (me, at_y)),
            send(out_b.at[i, slab_of(at_d)], row_y.at[i, 1], ers_sem, 6 * i + 3, (me, at_y)),
        ]

    def add_into(ref, *others):
        total = ref[...].astype(F32)
        for other in others:
            total = total + other[...].astype(F32)
        ref[...] = total.astype(BF)

    def pass_on(i):
        for copy in ers[i][:4]:
            copy.wait_recv()
        add_into(out_a.at[i, slab_of(at_y)], row_x.at[i, 1])
        add_into(out_b.at[i, slab_of(at_x)], row_y.at[i, 1])
        ers[i] += [
            send(out_a.at[i, slab_of(at_y)], row_qa.at[i], ers_sem, 6 * i + 4, (me, at_y)),
            send(out_b.at[i, slab_of(at_x)], row_qb.at[i], ers_sem, 6 * i + 5, (me, at_x)),
        ]

    back_copies = []

    def finish(i):
        ers[i][4].wait_recv()
        ers[i][5].wait_recv()
        for n, (out, near, far) in enumerate(((out_a, row_x, row_qa), (out_b, row_y, row_qb))):
            total = out[i, slab_of(cut)].astype(F32) + near[i, 0].astype(F32) + far[i].astype(F32)
            sorted_back[n, i] = total.astype(BF)
        if (i + 1) % per_group == 0:
            g = i // per_group
            for n in range(2):
                flat = sorted_back[n, pl.ds(g * per_group, per_group)].reshape(per_group * slab, -1)
                placed = mm_tn(sort[...], flat).astype(BF)
                send_back[n, g] = placed.reshape(n_expert, block, -1)
                (ret_a, ret_b)[n][g, me] = send_back[n, g, me]
                for k in range(1, n_expert):
                    peer = jnp.bitwise_xor(me, k)
                    back_copies.append(
                        send(
                            send_back.at[n, g, peer], (ret_a, ret_b)[n].at[g, me], zr_sem,
                            (n * groups + g) * n_expert + k, (peer, cut),
                        )
                    )

    for i in range(here):
        if i + 1 < here:
            relay(eag[i + 1])
        eag[i][2].wait_recv()
        eag[i][3].wait_recv()
        expert(i)
        if i + 2 < here:
            fetched.append(fetch_expert(i + 2))
        if i == 0:
            levels_in = weight_sum(0, win, twins_in)
            twins_out = weight_grad(1, act, grd, wout)
        if i == here - 1:
            frs = [
                send(part_a.at[1], ffn_x.at[0], frs_sem, 0, (me, at_x)),
                send(part_a.at[3], ffn_x.at[1], frs_sem, 1, (me, at_x)),
                send(part_b.at[2], ffn_y.at[0], frs_sem, 2, (me, at_y)),
                send(part_b.at[3], ffn_y.at[1], frs_sem, 3, (me, at_y)),
            ]
        if i == 1:
            levels_out = weight_sum(1, wout, twins_out)
        if i >= 1:
            pass_on(i - 1)
        if i >= 2:
            finish(i - 2)
    rows_store = pltpu.make_async_copy(rows, rows_in, store_sem.at[0])
    rows_store.start()
    pass_on(here - 1)
    finish(here - 2)
    finish(here - 1)
    for copy in frs[:4]:
        copy.wait_recv()
    add_into(part_a.at[2], ffn_x.at[1])
    add_into(part_b.at[1], ffn_y.at[1])
    frs += [
        send(part_a.at[2], ffn_qa, frs_sem, 4, (me, at_y)),
        send(part_b.at[1], ffn_qb, frs_sem, 5, (me, at_x)),
    ]
    fin_in[...] = weight_total(0, win, levels_in).reshape(fin_in.shape)
    fin_copies = []
    for k, peer in ((1, at_x), (2, at_y), (3, at_d)):
        fin_copies.append(send(fin_in.at[peer], o_in.at[cut], fin_sem, k - 1, (me, peer)))
    o_in[cut] = fin_in[cut]
    o_out[...] = weight_total(1, wout, levels_out)
    frs[4].wait_recv()
    frs[5].wait_recv()
    sums[0] = sums[0] + ffn_x[0].astype(F32) + ffn_qa[...].astype(F32)
    sums[1] = sums[1] + ffn_y[0].astype(F32) + ffn_qb[...].astype(F32)
    for copy in back_copies + fin_copies:
        copy.wait_recv()
    for copy in z_copies + ag + frs + back_copies + fin_copies + twins_in + twins_out + levels_in + levels_out:
        copy.wait_send()
    for i in range(here):
        for copy in eag[i] + ers[i]:
            copy.wait_send()
    for i in (here - 2, here - 1):
        for copy in expert_stores[i]:
            copy.wait()
    rows_store.wait()


def middle(slots, second, grad_all, grad_rows, w_in, w_out, small, sort, e_in, e_out, n_expert, n_cuts):
    groups, _, block, width = slots.shape
    tokens = second.shape[0]
    here, _, hidden = e_in.shape
    ffn = w_in.shape[1]
    slab = n_expert * block * groups // here
    rows = n_cuts * slab
    levels, deep = n_expert // 2, width // n_expert
    any_spec, vmem_spec = pl.BlockSpec(memory_space=pl.ANY), pl.BlockSpec(memory_space=pltpu.VMEM)
    shape = jax.ShapeDtypeStruct
    dma = pltpu.SemaphoreType.DMA
    flops = 8 * (n_cuts * tokens * ffn + here * rows * hidden) * width
    return pl.pallas_call(
        functools.partial(middle_kernel, (n_expert, groups, here, slab)),
        name="middle",
        out_shape=(
            shape((2, tokens, width), F32), shape((groups, n_expert, block, width), BF),
            shape((groups, n_expert, block, width), BF), shape((n_cuts, deep // n_cuts, ffn), BF), shape((deep, width), BF),
            shape((here, rows, width), BF), shape((here, rows, width), BF),
            shape((here, rows, hidden), BF), shape((here, rows, hidden), BF),
        ),
        in_specs=[vmem_spec] + [any_spec] * 5 + [vmem_spec] * 2 + [any_spec] * 2,
        out_specs=(vmem_spec,) * 5 + (any_spec,) * 4,
        scratch_shapes=[
            pltpu.VMEM((n_cuts, tokens, width), BF), pltpu.VMEM((n_cuts, tokens, width), BF),
            pltpu.VMEM((width, ffn), BF), pltpu.VMEM((ffn, width), BF),
            pltpu.VMEM((n_cuts, tokens, ffn), BF), pltpu.VMEM((n_cuts, tokens, ffn), BF),
            pltpu.VMEM((n_cuts, tokens, width), BF), pltpu.VMEM((n_cuts, tokens, width), BF),
            pltpu.VMEM((2, tokens, width), BF), pltpu.VMEM((2, tokens, width), BF),
            pltpu.VMEM((tokens, width), BF), pltpu.VMEM((tokens, width), BF),
            pltpu.VMEM((groups, n_expert, block, width), BF), pltpu.VMEM((here, rows, width), BF),
            pltpu.VMEM((2, rows, width), BF), pltpu.VMEM((2, rows, width), BF),
            pltpu.VMEM((2, rows, hidden), BF), pltpu.VMEM((2, rows, hidden), BF),
            pltpu.VMEM((2, width, hidden), BF), pltpu.VMEM((2, hidden, width), BF),
            pltpu.VMEM((here, rows, width), BF), pltpu.VMEM((here, rows, width), BF),
            pltpu.VMEM((here, 2, slab, width), BF), pltpu.VMEM((here, 2, slab, width), BF),
            pltpu.VMEM((here, slab, width), BF), pltpu.VMEM((here, slab, width), BF),
            pltpu.VMEM((2, here, slab, width), BF), pltpu.VMEM((2, groups, n_expert, block, width), BF),
            pltpu.VMEM((2, levels, deep, width), BF), pltpu.VMEM((2, levels - 1, deep, width), BF),
            pltpu.VMEM((n_cuts, deep // n_cuts, ffn), BF),
            dma((4,)), dma((3, 2)), dma((1,)), dma((3, 2)),
            dma((2, groups * n_expert)), dma((2, 4)), dma((2, 4 * here)), dma((2, 6)), dma((2, 6 * here)),
            dma((2, 2 * groups * n_expert)),
            dma((2, 2 * levels)), dma((2, 2 * (levels - 1))), dma((2, 3)),
        ],
        compiler_params=pltpu.CompilerParams(
            collective_id=1, has_side_effects=True, vmem_limit_bytes=67_000_000
        ),
        cost_estimate=pl.CostEstimate(flops=flops, bytes_accessed=48 << 20, transcendentals=0),
    )(slots, second, grad_all, grad_rows, w_in, w_out, small, sort, e_in, e_out)


def tail_kernel(
    heads, scaling, g_attn, d_heads, joined, lse, normed, qkv, source, gain, d_hidden, tiny,
    d_source, o_qkv, o_attn, o_tiny, o_gain,
    core_in, own, a_in, a_z, a_mine, gq, core_q, own_q, z_q, fin_q,
    dh, dj, acc_q, acc_k, acc_v, dn, dn_in, norm_v, qkv_v, tiny_e, tiny_m, tiny_c, late, late_e, late_m, late_c,
    load_sem, core_sem, z_sem, cut_sem, te_sem, tc_sem,
):
    me, cut = lax.axis_index("expert"), lax.axis_index("cuts")
    core, level = lax.rem(me, 2), lax.div(me, 2)
    other = 1 - core
    n_cuts, tokens, width = dh.shape
    n_expert = tiny_e.shape[0]
    levels = n_expert // 2
    twin = (jnp.bitwise_xor(me, 1), cut)

    def send(src, dst, sems, index, peer):
        copy = pltpu.make_async_remote_copy(
            src_ref=src, dst_ref=dst, send_sem=sems.at[0, index], recv_sem=sems.at[1, index],
            device_id=peer, device_id_type=MESH,
        )
        copy.start()
        return copy

    def load(src, dst, index):
        copy = pltpu.make_async_copy(src, dst, load_sem.at[index])
        copy.start()
        return copy

    mine = load(g_attn.at[:, core], own, 0)
    later = [load(normed, norm_v, 1), load(qkv, qkv_v, 2)]
    barrier = pltpu.get_barrier_semaphore()
    for k in range(1, n_expert):
        pl.semaphore_signal(barrier, inc=1, device_id=(jnp.bitwise_xor(me, k), cut), device_id_type=MESH)
    for k in range(1, n_cuts):
        pl.semaphore_signal(barrier, inc=1, device_id=(me, jnp.bitwise_xor(cut, k)), device_id_type=MESH)
    pl.semaphore_wait(barrier, n_expert + n_cuts - 2)

    def columns(index, size):
        return pl.ds(pl.multiple_of(index * size, size), size)

    sent = []

    def to_cuts(src_of, dst_of, base):
        copies = []
        for k in range(1, n_cuts):
            peer = jnp.bitwise_xor(cut, k)
            copies.append(send(src_of(peer), dst_of(k), cut_sem, base + k - 1, (me, peer)))
        sent.extend(copies)
        return copies

    def to_levels(src_of, dst_of, base):
        copies = []
        for k in range(1, levels):
            peer = jnp.bitwise_xor(level, k)
            copies.append(send(src_of(peer), dst_of(k), z_sem, base + k - 1, (2 * peer + core, cut)))
        sent.extend(copies)
        return copies

    def to_experts(src, dst, base):
        copies = []
        for k in range(1, n_expert):
            peer = jnp.bitwise_xor(me, k)
            copies.append(send(src.at[:, columns(peer, 128)], dst.at[k], te_sem, base + k - 1, (peer, cut)))
        sent.extend(copies)
        return copies

    heads_moved = to_cuts(lambda peer: d_heads.at[:, columns(peer, width)], lambda k: dh.at[cut], 0)
    twins = [send(g_attn.at[:, other], core_in, core_sem, 0, twin)]
    tiny_moved = to_experts(tiny, tiny_e, 0)
    dh[cut] = d_heads[:, columns(cut, width)]
    mine.wait()
    twins[0].wait_recv()

    @pl.loop(0, levels)
    def _(step):
        own[step] = (own[step].astype(F32) + core_in[step].astype(F32)).astype(BF)

    piece = own.shape[1] // n_cuts
    attn_moved = to_cuts(lambda peer: own.at[:, columns(peer, piece)], lambda k: a_in.at[k - 1], 3)

    acc_q[...] = jnp.zeros_like(acc_q)
    acc_k[...] = jnp.zeros_like(acc_k)
    acc_v[...] = jnp.zeros_like(acc_v)
    for copy in heads_moved:
        copy.wait_recv()

    @pl.loop(0, heads)
    def _(head):
        pair, half = lax.div(head, 2), lax.rem(head, 2)
        lane = lax.broadcasted_iota(jnp.int32, (1, 128), 1)
        keep = (lax.div(lane, HD) == half).astype(F32)
        keep_low = keep.astype(BF)
        cols = columns(pair, 128)
        k_cols = pl.ds(pl.multiple_of(width + pair * 128, 128), 128)
        v_cols = pl.ds(pl.multiple_of(2 * width + pair * 128, 128), 128)
        for i in range(n_cuts):
            reach = (i + 1) * tokens
            here = pl.ds(i * tokens, tokens)
            query = joined[here, cols] * keep_low
            d_out = dh[i, :, cols] * keep_low
            keys = joined[pl.ds(0, reach), k_cols]
            scores = mm_nt(keys, query) * scaling - lse[head, :, here]
            key_at = lax.broadcasted_iota(jnp.int32, scores.shape, 0)
            query_at = lax.broadcasted_iota(jnp.int32, scores.shape, 1) + i * tokens
            soft = jnp.exp(jnp.where(key_at <= query_at, scores, -1e30))
            d_soft = mm_nt(joined[pl.ds(0, reach), v_cols], d_out)
            delta = jnp.sum(soft * d_soft, axis=0, keepdims=True)
            d_scores = (soft * (d_soft - delta)).astype(BF)
            acc_v[pl.ds(0, reach), cols] += mm(soft.astype(BF), d_out)
            acc_k[pl.ds(0, reach), cols] += mm(d_scores, query)
            acc_q[here, cols] += mm_tn(d_scores, keys) * keep

    dj[:, pl.ds(0, width)] = (acc_q[...] * scaling).astype(BF)
    dj[:, pl.ds(width, width)] = (acc_k[...] * scaling).astype(BF)
    dj[:, pl.ds(2 * width, width)] = acc_v[...].astype(BF)
    for copy in later:
        copy.wait()
    part = tokens // 2
    first, last = pl.ds(0, part), pl.ds(part, part)
    at_x, at_y = (me, jnp.bitwise_xor(cut, 1)), (me, jnp.bitwise_xor(cut, 2))

    def partial_sum(k):
        peer = jnp.bitwise_xor(cut, k)
        dn[k] = mm_nt(dj[columns(peer, tokens), :], qkv_v[...]).astype(BF)

    partial_sum(3)
    passing = [
        send(dn.at[3, first], dn_in.at[2, first], cut_sem, 6, at_x),
        send(dn.at[3, last], dn_in.at[2, last], cut_sem, 7, at_y),
    ]
    partial_sum(1)
    dn_moved = [send(dn.at[1, first], dn_in.at[0, first], cut_sem, 8, at_x)]
    partial_sum(2)
    dn_moved.append(send(dn.at[2, last], dn_in.at[1, last], cut_sem, 12, at_y))

    @pl.loop(0, levels)
    def _(step):
        part = mm_tn(norm_v[:, columns(step, 256)], dj[...]).astype(BF)
        gq[step] = part.reshape(2, 128, part.shape[1])

    twins.append(send(gq.at[:, other], core_q, core_sem, 1, twin))
    d_normed = mm_nt(dj[columns(cut, tokens), :], qkv_v[...])

    for n, rows, k, index, peer in ((0, first, 2, 13, at_y), (1, last, 1, 14, at_x)):
        passing[n].wait_recv()
        dn[k, rows] = (dn[k, rows].astype(F32) + dn_in[2, rows].astype(F32)).astype(BF)
        dn_moved.append(send(dn.at[k, rows], dn_in.at[k - 1, rows], cut_sem, index, peer))
    sent.extend(passing + dn_moved)

    for copy in attn_moved:
        copy.wait_recv()
    total = own[:, columns(cut, piece)].astype(F32)
    for k in range(1, n_cuts):
        total = total + a_in[k - 1].astype(F32)
    a_mine[...] = total.astype(BF)
    attn_z = to_levels(lambda peer: a_mine.at[peer], lambda k: a_z.at[k - 1], 0)

    twins[1].wait_recv()

    @pl.loop(0, levels)
    def _(step):
        own_q[step] = (gq[step, core].astype(F32) + core_q[step].astype(F32)).astype(BF)

    qkv_z = to_levels(lambda peer: own_q.at[peer], lambda k: z_q.at[k - 1], levels - 1)

    for copy in tiny_moved:
        copy.wait_recv()
    small = tiny[:, columns(me, 128)]
    for k in range(1, n_expert):
        small = small + tiny_e[k]
    tiny_m[...] = small

    def tiny_cuts(src, dst, base):
        copies = []
        for k in range(1, n_cuts):
            copies.append(send(src, dst.at[k], tc_sem, base + k - 1, (me, jnp.bitwise_xor(cut, k))))
        sent.extend(copies)
        return copies

    tiny_last = tiny_cuts(tiny_m, tiny_c, 0)

    for copy in dn_moved:
        copy.wait_recv()
    d_normed = d_normed + dn_in[0].astype(F32) + dn_in[1].astype(F32)
    xhat, inv = norm_parts(source[...].astype(F32))
    q = d_normed * gain[...]
    mean_q = jnp.mean(q, axis=-1, keepdims=True)
    mean_qx = jnp.mean(q * xhat, axis=-1, keepdims=True)
    d_source[...] = d_hidden[...] + (q - mean_q - xhat * mean_qx) * inv
    late[...] = jnp.broadcast_to(jnp.sum(d_normed * xhat, axis=0, keepdims=True), late.shape)
    late_moved = to_experts(late, late_e, n_expert - 1)

    for copy in tiny_last:
        copy.wait_recv()
    for k in range(1, n_cuts):
        small = small + tiny_c[k]
    o_tiny[...] = small

    for copy in late_moved:
        copy.wait_recv()
    small = late[:, columns(me, 128)]
    for k in range(1, n_expert):
        small = small + late_e[k]
    late_m[...] = small
    late_last = tiny_cuts(late_m, late_c, n_cuts - 1)

    for copy in attn_z:
        copy.wait_recv()
    total = a_mine[level].astype(F32)
    for k in range(1, levels):
        total = total + a_z[k - 1].astype(F32)
    o_attn[...] = total

    for copy in qkv_z:
        copy.wait_recv()
    total = own_q[level].astype(F32)
    for k in range(1, levels):
        total = total + z_q[k - 1].astype(F32)
    fin_q[...] = total.astype(BF).reshape(fin_q.shape)
    qkv_last = to_cuts(lambda peer: fin_q.at[peer], lambda k: o_qkv.at[cut], 9)
    o_qkv[cut] = fin_q[cut]

    for copy in late_last:
        copy.wait_recv()
    for k in range(1, n_cuts):
        small = small + late_c[k]
    o_gain[...] = small
    for copy in qkv_last:
        copy.wait_recv()
    for copy in sent + twins:
        copy.wait_send()


def tail(g_attn, d_heads, joined, lse, normed, qkv, source, gain, d_hidden, tiny, n_expert, n_cuts):
    tokens, features = d_heads.shape
    heads, seq_len = lse.shape
    levels, own = n_expert // 2, features // n_cuts
    deep = features // n_expert
    piece, wide = deep // n_cuts, 3 * own
    any_spec, vmem_spec = pl.BlockSpec(memory_space=pl.ANY), pl.BlockSpec(memory_space=pltpu.VMEM)
    shape, vmem, dma = jax.ShapeDtypeStruct, pltpu.VMEM, pltpu.SemaphoreType.DMA
    rows = tiny.shape[0]
    grid = (levels, 2, deep, features)
    return pl.pallas_call(
        functools.partial(tail_kernel, heads, HD ** (-0.5)),
        name="tail",
        out_shape=(
            shape((tokens, features), F32), shape((n_cuts, piece, wide), BF), shape((piece, features), F32), shape((rows, 128), F32), shape((8, 128), F32),
        ),
        in_specs=[any_spec] + [vmem_spec] * 3 + [any_spec] * 2 + [vmem_spec] * 4,
        out_specs=(vmem_spec,) * 5,
        scratch_shapes=[
            vmem((levels, deep, features), BF), vmem((levels, deep, features), BF),
            vmem((n_cuts - 1, levels, piece, features), BF),
            vmem((levels - 1, piece, features), BF), vmem((levels, piece, features), BF),
            vmem((levels, 2, deep, wide), BF), vmem((levels, deep, wide), BF), vmem((levels, deep, wide), BF),
            vmem((levels - 1, deep, wide), BF), vmem((n_cuts, piece, wide), BF),
            vmem((n_cuts, tokens, own), BF), vmem((seq_len, wide), BF),
            vmem((seq_len, own), F32), vmem((seq_len, own), F32), vmem((seq_len, own), F32),
            vmem((n_cuts, tokens, features), BF), vmem((n_cuts - 1, tokens, features), BF),
            vmem((seq_len, features), BF), vmem((features, wide), BF),
            vmem((n_expert, rows, 128), F32), vmem((rows, 128), F32), vmem((n_cuts, rows, 128), F32),
            vmem((8, features), F32), vmem((n_expert, 8, 128), F32), vmem((8, 128), F32), vmem((n_cuts, 8, 128), F32),
            dma((3,)), dma((2, 2)), dma((2, 2 * (levels - 1))), dma((2, 15)),
            dma((2, 2 * (n_expert - 1))), dma((2, 2 * (n_cuts - 1))),
        ],
        compiler_params=pltpu.CompilerParams(
            collective_id=2, has_side_effects=True, vmem_limit_bytes=48 << 20
        ),
        cost_estimate=pl.CostEstimate(flops=20_000_000_000, bytes_accessed=24 << 20, transcendentals=0),
    )(
        g_attn.reshape(grid), d_heads, joined, lse.reshape(heads, 1, seq_len),
        normed, qkv, source, gain, d_hidden, tiny,
    )


def head_kernel(
    sizes, source, gains, small, info, sort, w_qkv, w_attn, w_in, cotangent,
    normed, qkv, joined, lse, head_out, attn_full, in_here, small_full, grad_all, grad_rows, placer, gains_all,
    src_v, qkv_v, norm_v, join_v, acc, heads_low, attn_v, in_v, cot_v, slots, zbuf, row_v,
    load_sem, store_sem, cut_sem, twin_sem, z_sem, level_sem,
):
    heads, scaling, groups, here, slab = sizes
    me, cut = lax.axis_index("expert"), lax.axis_index("cuts")
    core = lax.rem(me, 2)
    twin = (jnp.bitwise_xor(me, 1), cut)
    at = [jnp.bitwise_xor(cut, k) for k in range(4)]
    n_cuts, tokens, width = src_v.shape
    n_expert, block = zbuf.shape[1], zbuf.shape[2]
    own, half, levels = width // n_cuts, tokens // 2, n_expert // 2
    level, quarter = lax.div(me, 2), tokens // n_expert

    def span(start, size, step):
        return pl.ds(pl.multiple_of(start, step), size)

    def remote(src, dst, sems, index, peer):
        return pltpu.make_async_remote_copy(
            src_ref=src, dst_ref=dst, send_sem=sems.at[0, index], recv_sem=sems.at[1, index],
            device_id=peer, device_id_type=MESH,
        )

    def local(src, dst, sems, index):
        copy = pltpu.make_async_copy(src, dst, sems.at[index])
        copy.start()
        return copy

    loads = [
        local(cotangent, cot_v, load_sem, 0),
        local(w_attn, attn_v, load_sem, 1),
        local(w_in.at[:, span(cut * width, width, width)], in_v, load_sem, 2),
    ]
    own_qkv = [
        local(
            w_qkv.at[:, span(n * width + cut * own, own, own)],
            qkv_v.at[span(cut * tokens, tokens, tokens), pl.ds(n * own, own)], load_sem, 3 + n,
        )
        for n in range(3)
    ]
    barrier = pltpu.get_barrier_semaphore()
    for k in range(1, n_expert):
        pl.semaphore_signal(barrier, inc=1, device_id=(jnp.bitwise_xor(me, k), cut), device_id_type=MESH)
    for k in range(1, n_cuts):
        pl.semaphore_signal(barrier, inc=1, device_id=(me, at[k]), device_id_type=MESH)
    pl.semaphore_wait(barrier, n_expert + n_cuts - 2)

    def gather(view, first, base):
        return [
            remote(first, view(cut), cut_sem, base, (me, at[1])),
            remote(first, view(cut), cut_sem, base + 1, (me, at[2])),
            remote(view(at[1], 0), view(at[1], 0), cut_sem, base + 2, (me, at[2])),
            remote(view(at[2], 1), view(at[2], 1), cut_sem, base + 3, (me, at[1])),
        ]

    def relay(copies):
        copies[0].wait_recv()
        copies[2].start()
        copies[1].wait_recv()
        copies[3].start()

    def whole(ref):
        def view(owner, piece=None):
            return ref.at[owner] if piece is None else ref.at[owner, pl.ds(piece * half, half)]

        return view

    def weight_rows(owner):
        return span(owner * tokens + core * half + level * quarter, quarter, quarter)

    def pass_levels(ref, base):
        copies = []
        for k in range(1, n_cuts):
            view = ref.at[weight_rows(at[k])]
            for n in range(1, levels):
                peer = (2 * jnp.bitwise_xor(level, n) + core, cut)
                copies.append(remote(view, view, level_sem, base + (k - 1) * (levels - 1) + n - 1, peer))
                copies[-1].start()
        return copies

    def slab_view(owner, piece=None):
        if piece is None:
            return grad_rows.at[:, span(owner * slab, slab, slab // 2)]
        return grad_rows.at[:, span(owner * slab + piece * (slab // 2), slab // 2, slab // 2)]

    def to_cuts(src_of, dst_of, base):
        return [remote(src_of(at[k]), dst_of(k), cut_sem, base + k - 1, (me, at[k])) for k in (3, 1, 2)]

    tokens_moved = gather(whole(src_v), source, 0)
    gains_moved = to_cuts(lambda peer: gains, lambda k: gains_all.at[cut], 16)
    small_moved = to_cuts(lambda peer: small, lambda k: small_full.at[cut], 19)
    qkv_moved = []
    for n in range(3):
        qkv_moved += to_cuts(
            lambda peer: w_qkv.at[weight_rows(0), span(n * width + peer * own, own, own)],
            lambda k: qkv_v.at[weight_rows(cut), pl.ds(n * own, own)],
            22 + 3 * n,
        )
    grad_moved = gather(whole(grad_all), cot_v, 4)
    attn_moved = to_cuts(lambda peer: w_attn.at[weight_rows(0)], lambda k: attn_full.at[weight_rows(cut)], 8)
    slab_moved = gather(slab_view, row_v, 12)
    in_moved = to_cuts(
        lambda peer: w_in.at[weight_rows(0), span(peer * width, width, width)],
        lambda k: in_here.at[weight_rows(cut)], 31,
    )
    for copy in gains_moved + tokens_moved[:2] + qkv_moved + attn_moved + in_moved + small_moved:
        copy.start()
    head_moved = to_cuts(
        lambda peer: heads_low.at[span(peer * tokens, tokens, tokens)],
        lambda k: head_out.at[:, span(cut * own, own, own)], 34,
    )

    loads[0].wait()
    lane = lax.broadcasted_iota(jnp.int32, (tokens, 128), 1).astype(F32)
    picked = jnp.where(lane == info[:, 0:1], info[:, 1:2], 0.0)
    down = lax.broadcasted_iota(jnp.int32, (tokens, tokens), 0)
    right = lax.broadcasted_iota(jnp.int32, (tokens, tokens), 1)
    running = mm((down >= right).astype(F32).astype(BF), picked.astype(BF))
    target = info[:, 2:3] + jnp.sum(picked * running, axis=1, keepdims=True) - 1.0
    column = lax.broadcasted_iota(jnp.int32, placer.shape, 1).astype(F32)
    placer[...] = jnp.where(column == target, info[:, 1:2], 0.0).astype(BF)
    slots[...] = mm_tn(placer[...], cot_v[...]).astype(BF).reshape(slots.shape)
    z_moved = []
    for g in range(groups):
        for k in range(1, n_expert):
            peer = jnp.bitwise_xor(me, k)
            z_moved.append(remote(slots.at[g, peer], zbuf.at[g, me], z_sem, g * n_expert + k, (peer, cut)))
            z_moved[-1].start()
        zbuf[g, me] = slots[g, me]
    src_v[cut] = source[...]
    gains_all[cut] = gains[...]
    small_full[cut] = small[...]
    relay(tokens_moved)
    for copy in grad_moved[:2]:
        copy.start()
    for copy in qkv_moved:
        copy.wait_recv()
    qkv_levels = pass_levels(qkv_v, 0)
    for copy in loads[1:] + own_qkv:
        copy.wait()
    stores = [
        local(cot_v, grad_all.at[cut], store_sem, 0),
        local(attn_v, attn_full.at[span(cut * tokens, tokens, tokens)], store_sem, 1),
        local(in_v, in_here.at[span(cut * tokens, tokens, tokens)], store_sem, 2),
    ]
    for copy in gains_moved:
        copy.wait_recv()

    def normalize(index):
        xhat, _ = norm_parts(src_v[index].astype(F32))
        for n in range(n_cuts):
            cols = slice(n * own, (n + 1) * own)
            norm_v[index, :, cols] = (xhat[:, cols] * gains_all[n, 0:1, :]).astype(BF)

    normalize(cut)
    normalize(at[1])
    normalize(at[2])
    for copy in attn_moved + in_moved:
        copy.wait_recv()
    attn_levels = pass_levels(attn_full, 3 * (levels - 1))
    in_levels = pass_levels(in_here, 6 * (levels - 1))
    for copy in qkv_levels:
        copy.wait_recv()

    def share(ref, base):
        copies = []
        for k in range(1, n_cuts):
            view = ref.at[span(at[k] * tokens + core * half, half, half)]
            copies.append(remote(view, view, twin_sem, base + k - 1, twin))
            copies[-1].start()
        return copies

    shared = share(qkv_v, 0)
    for copy in tokens_moved[2:]:
        copy.wait_recv()
    normalize(at[3])
    for copy in shared:
        copy.wait_recv()

    @pl.loop(0, n_cuts)
    def _(step):
        join_v[step] = mm(norm_v[step], qkv_v[...]).astype(BF)

    stores += [
        local(norm_v, normed, store_sem, 3), local(qkv_v, qkv, store_sem, 4), local(join_v, joined, store_sem, 5),
    ]
    acc[...] = jnp.zeros_like(acc)
    per_group = here // groups
    for copy in z_moved:
        copy.wait_recv()
    for g in range(groups):
        flat = zbuf[g].reshape(n_expert * block, width)
        for j in range(per_group):
            row_v[g * per_group + j] = mm(sort[pl.ds(j * slab, slab), :], flat).astype(BF)
    for copy in slab_moved[:2]:
        copy.start()
    stores.append(local(row_v, slab_view(cut), store_sem, 6))

    @pl.loop(0, heads)
    def _(head):
        @pl.when(head == 2)
        def _():
            relay(grad_moved)

        pair = lax.div(head, 2)
        lane = lax.broadcasted_iota(jnp.int32, (1, 128), 1)
        keep = (lax.div(lane, HD) == lax.rem(head, 2)).astype(F32)
        keep_low = keep.astype(BF)
        cols = span(pair * 128, 128, 128)
        k_cols = span(own + pair * 128, 128, 128)
        v_cols = span(2 * own + pair * 128, 128, 128)
        for i in range(n_cuts):
            reach = (i + 1) * tokens
            query = join_v[i, :, cols] * keep_low
            keys = join_v[pl.ds(0, i + 1), :, k_cols].reshape(reach, 128)
            values = join_v[pl.ds(0, i + 1), :, v_cols].reshape(reach, 128)
            scores = mm_nt(keys, query) * scaling
            key_at = lax.broadcasted_iota(jnp.int32, scores.shape, 0)
            query_at = lax.broadcasted_iota(jnp.int32, scores.shape, 1) + i * tokens
            scores = jnp.where(key_at <= query_at, scores, -1e30)
            peak = jnp.max(scores, axis=0, keepdims=True)
            powers = jnp.exp(scores - peak)
            total = jnp.sum(powers, axis=0, keepdims=True)
            lse[head, :, pl.ds(i * tokens, tokens)] = peak + jnp.log(total)
            soft = (powers / total).astype(BF)
            acc[pl.ds(i * tokens, tokens), cols] += mm_tn(soft, values) * keep

    heads_low[...] = acc[...].astype(BF)
    for copy in head_moved:
        copy.start()
    head_out[:, span(cut * own, own, own)] = heads_low[span(cut * tokens, tokens, tokens), :]
    relay(slab_moved)
    for copy in attn_levels + in_levels:
        copy.wait_recv()
    shared += share(attn_full, 3)
    shared += share(in_here, 6)
    for copy in shared[3:] + grad_moved[2:] + slab_moved[2:] + head_moved + small_moved:
        copy.wait_recv()
    for copy in stores:
        copy.wait()
    everything = tokens_moved + gains_moved + small_moved + qkv_moved + grad_moved + attn_moved + slab_moved
    everything += qkv_levels + attn_levels + in_levels
    for copy in everything + in_moved + head_moved + z_moved + shared:
        copy.wait_send()


def head(source, gains, small, info, sort, w_qkv, w_attn, w_in, cotangent, here, groups, capacity, n_expert, n_cuts):
    tokens, features = source.shape
    seq_len, own = tokens * n_cuts, features // n_cuts
    heads, slab = own // HD, n_expert * capacity
    block = here // groups * capacity
    any_spec, vmem_spec = pl.BlockSpec(memory_space=pl.ANY), pl.BlockSpec(memory_space=pltpu.VMEM)
    shape, vmem, dma = jax.ShapeDtypeStruct, pltpu.VMEM, pltpu.SemaphoreType.DMA
    slots = n_expert * groups * block
    return pl.pallas_call(
        functools.partial(head_kernel, (heads, HD ** (-0.5), groups, here, slab)),
        name="head",
        out_shape=(
            shape((n_cuts, tokens, features), BF), shape((features, 3 * own), BF), shape((n_cuts, tokens, 3 * own), BF),
            shape((heads, 1, seq_len), F32), shape((tokens, features), BF), shape((features, features), BF),
            shape((features, w_in.shape[1] // n_cuts), BF), shape((n_cuts,) + small.shape, BF),
            shape((n_cuts, tokens, features), BF), shape((here, n_cuts * slab, features), BF),
            shape((tokens, slots), BF), shape((n_cuts,) + gains.shape, F32),
        ),
        in_specs=[vmem_spec] * 5 + [any_spec] * 4,
        out_specs=(any_spec,) * 3 + (vmem_spec,) * 2 + (any_spec,) * 2 + (vmem_spec,) + (any_spec,) * 2 + (vmem_spec,) * 2,
        scratch_shapes=[
            vmem((n_cuts, tokens, features), BF), vmem((features, 3 * own), BF), vmem((n_cuts, tokens, features), BF),
            vmem((n_cuts, tokens, 3 * own), BF), vmem((seq_len, own), F32), vmem((seq_len, own), BF),
            vmem((tokens, features), BF), vmem((tokens, features), BF), vmem((tokens, features), BF),
            vmem((groups, n_expert, block, features), BF), vmem((groups, n_expert, block, features), BF),
            vmem((here, slab, features), BF),
            dma((6,)), dma((7,)), dma((2, 37)), dma((2, 9)), dma((2, groups * n_expert)), dma((2, 9 * (n_expert // 2 - 1))),
        ],
        compiler_params=pltpu.CompilerParams(
            collective_id=3, has_side_effects=True, vmem_limit_bytes=48 << 20
        ),
        cost_estimate=pl.CostEstimate(flops=8_000_000_000, bytes_accessed=24 << 20, transcendentals=0),
    )(source, gains, small, info, sort, w_qkv, w_attn, w_in, cotangent)


def expert_grads_kernel(rows, d_first, act, d_rows, grad_in, grad_out, rows_v, first_v, act_v, d_rows_v, sems):
    expert, tile = pl.program_id(0), pl.program_id(1)
    pairs = ((rows, rows_v), (d_first, first_v), (act, act_v), (d_rows, d_rows_v))

    def copies(index):
        return [pltpu.make_async_copy(src.at[index], dst.at[index], sems.at[n, index]) for n, (src, dst) in enumerate(pairs)]

    @pl.when(jnp.logical_and(expert == 0, tile == 0))
    def _():
        for index in range(rows.shape[0]):
            for copy in copies(index):
                copy.start()

    @pl.when(tile == 0)
    def _():
        for copy in copies(expert):
            copy.wait()

    span = tile_of(tile, 512)
    grad_in[0] = mm_tn(rows_v[expert, :, span], first_v[expert])
    grad_out[0] = mm_tn(act_v[expert, :, span], d_rows_v[expert])


def expert_grads(rows, d_first, act, d_rows):
    here, count, width = rows.shape
    hidden = act.shape[2]
    any_spec = pl.BlockSpec(memory_space=pl.ANY)
    return pl.pallas_call(
        expert_grads_kernel,
        name="expert_grads",
        grid=(here, width // 512),
        out_shape=(jax.ShapeDtypeStruct((here, width, hidden), F32), jax.ShapeDtypeStruct((here, hidden, width), F32)),
        in_specs=[any_spec] * 4,
        out_specs=(
            pl.BlockSpec((1, 512, hidden), lambda e, t: (e, t, 0)), pl.BlockSpec((1, 512, width), lambda e, t: (e, t, 0)),
        ),
        scratch_shapes=[
            pltpu.VMEM(rows.shape, BF), pltpu.VMEM(d_first.shape, BF), pltpu.VMEM(act.shape, BF), pltpu.VMEM(d_rows.shape, BF),
            pltpu.SemaphoreType.DMA((4, here)),
        ],
        compiler_params=pltpu.CompilerParams(vmem_limit_bytes=66_000_000),
        cost_estimate=pl.CostEstimate(flops=4 * here * count * width * hidden, bytes_accessed=46 << 20, transcendentals=0),
    )(rows, d_first, act, d_rows)


def shards(
    block_input,
    routes,
    kept_mask,
    w_qkv,
    w_attn_out,
    w_in,
    w_out,
    w_router,
    w_mix,
    gain_attn,
    gain_ffn,
    expert_in,
    expert_out,
    cotangent,
):
    tokens, features = block_input.shape
    n_cuts = lax.axis_size("cuts")
    n_expert = lax.axis_size("expert")
    seq_len = tokens * n_cuts
    scaling = HD ** (-0.5)
    own = features // n_cuts
    heads = own // HD
    experts_all = w_router.shape[1]
    experts_here = expert_in.shape[0]
    capacity = 3 * tokens // (2 * experts_all)

    onehot = (routes[:, None] == jnp.arange(experts_all, dtype=jnp.int32)[None, :]).astype(F32)
    fused = n_cuts == 4
    groups = 2 if fused else 1
    per_group = experts_here // groups
    block = per_group * capacity
    owner, local = routes // experts_here, routes % experts_here
    start = (local // per_group) * (n_expert * block) + owner * block + local % per_group * capacity
    if not fused:
        onehot_kept = onehot * kept_mask.astype(F32)[:, None]
        lower_tri = (jnp.arange(tokens)[:, None] >= jnp.arange(tokens)[None, :]).astype(BF)
        running = mm(lower_tri, onehot_kept.astype(BF))
        slot_num = jnp.sum(onehot_kept * running, axis=1) - 1.0
        target = start.astype(F32) + slot_num
        columns = jnp.arange(experts_all * capacity, dtype=jnp.int32).astype(F32)
        placer = ((columns[None, :] == target[:, None]) & (kept_mask[:, None] > 0)).astype(BF)

    def to_owners(rows):
        grid = mm_tn(placer, rows).astype(BF).reshape(groups, n_expert, block, features)
        grid = grid.swapaxes(0, 1).reshape(n_expert, experts_here, capacity, features)
        moved = lax.all_to_all(grid, "expert", split_axis=0, concat_axis=2, tiled=True)
        return lax.all_gather(moved, "cuts", axis=2, tiled=True)[0]

    def to_sources(rows):
        summed = lax.psum_scatter(rows[None].astype(BF), "cuts", scatter_dimension=2, tiled=True)
        moved = lax.all_to_all(summed, "expert", split_axis=2, concat_axis=0, tiled=True)
        return mm(placer, moved.reshape(-1, features))

    inputs = block_input.astype(F32)
    if fused:
        pair = jnp.stack([gain_attn, gain_ffn], axis=0).astype(F32)
        small_here = jnp.concatenate([w_router, w_mix], axis=1)
        small_cols = small_here.shape[1]
        at = np.arange(n_expert * block)
        slab = n_expert * capacity
        goal = at % slab // capacity * block + at // slab * capacity + at % capacity
        sort = np.asarray(goal[:, None] == at[None, :], dtype=BF)
        info = jnp.stack([routes, kept_mask, start], axis=1).astype(F32)
        normed, qkv_here, joined, log_norm, head_out, attn_full, in_here, small_wide, grad_all, grad_rows, placer, gains = head(
            block_input, jnp.pad(pair, ((0, 6), (0, 0))), jnp.pad(small_here, ((0, 0), (0, -small_cols % 128))),
            info, jnp.asarray(sort), w_qkv, w_attn_out, w_in, cotangent,
            experts_here, groups, capacity, n_expert, n_cuts,
        )
        normed, joined = normed.reshape(seq_len, features), joined.reshape(seq_len, 3 * own)
        small_wide = small_wide.reshape(features, -1)
        small_full = small_wide[:, :small_cols]
        gain_one, gain_two = gains[:, 0].reshape(features), gains[:, 1].reshape(features)
    else:
        gains = gather_cuts(jnp.stack([gain_attn, gain_ffn], axis=1)).astype(F32)
        gain_one, gain_two = gains[:, 0], gains[:, 1]
        xhat_one, inv_one = norm_parts(inputs)
        normed = gather_cuts((xhat_one * gain_one).astype(BF))
        qkv_here = lax.all_to_all(
            w_qkv.reshape(own, 3, n_cuts, own), "cuts", split_axis=2, concat_axis=0, tiled=True
        ).reshape(features, 3 * own)
        joined = mm(normed, qkv_here).astype(BF)
        split = joined.reshape(seq_len, 3, heads, HD)
        q_heads, k_heads, v_heads = split[:, 0], split[:, 1], split[:, 2]
        spots = jnp.arange(seq_len, dtype=jnp.int32)
        visible = (spots[None, :] <= spots[:, None])[None]

        def masked_scores():
            scores = jnp.einsum("qhd,khd->hqk", q_heads, k_heads, preferred_element_type=F32) * scaling
            return jnp.where(visible, scores, -1e30)

        scores = masked_scores()
        peak = jnp.max(scores, axis=-1, keepdims=True)
        row_exp = jnp.exp(scores - peak)
        total = jnp.sum(row_exp, axis=-1, keepdims=True)
        weights_p = (row_exp / total).astype(BF)
        heads_here = jnp.einsum("hqk,khd->qhd", weights_p, v_heads, preferred_element_type=F32)
        log_norm = peak + jnp.log(total)
        head_out = rows_to_cuts(heads_here.reshape(seq_len, own).astype(BF))
        attn_full = gather_cuts(w_attn_out)
        small_full = gather_cuts(jnp.concatenate([w_router, w_mix], axis=1))
        grad_all = gather_cuts(cotangent)
        grad_rows = to_owners(cotangent)
        in_here = columns_to_cuts(w_in)
    hidden = inputs + mm(head_out, attn_full)
    xhat_two, inv_two = norm_parts(hidden)
    second = (xhat_two * gain_two).astype(BF)

    logits = mm(second, small_full)
    router_p = softmax_rows(logits[:, :experts_all])
    mixing = softmax_rows(logits[:, experts_all:])
    gate = jnp.sum(router_p * onehot, axis=1)
    grad = cotangent.astype(F32)
    d_moe = grad * mixing[:, 1:2]

    if fused:
        slots = mm_tn(placer, second).astype(BF).reshape(groups, n_expert, block, features)
        sums, ret_a, ret_b, s_in, s_out, rows_in, d_rows, expert_low, d_first = middle(
            slots, second, grad_all, grad_rows, in_here, w_out, small_wide, jnp.asarray(sort),
            expert_in, expert_out, n_expert, n_cuts,
        )
        dense, d_second_ffn = sums[0], sums[1]
        g_expert_in, g_expert_out = expert_grads(rows_in, d_first, expert_low, d_rows)
        picked = mm(placer, ret_a.reshape(-1, features))
        d_picked_in = mm(placer, ret_b.reshape(-1, features))
    else:
        rows_in = to_owners(second)
        row_logits = jnp.einsum("erd,dk->erk", rows_in, small_full, preferred_element_type=F32)
        ids = lax.axis_index("expert") * experts_here + jnp.arange(experts_here, dtype=jnp.int32)
        is_here = (jnp.arange(experts_all, dtype=jnp.int32)[None, :] == ids[:, None]).astype(F32)
        row_gate = jnp.sum(
            softmax_rows(row_logits[:, :, :experts_all]) * is_here[:, None, :], axis=2, keepdims=True
        )
        row_mixing = softmax_rows(row_logits[:, :, experts_all:])[:, :, 1:2]
        d_rows = (grad_rows.astype(F32) * row_mixing * row_gate).astype(BF)

        first = jnp.einsum("erd,edh->erh", rows_in, expert_in, preferred_element_type=F32)
        expert_act, expert_pull = jax.vjp(jax.nn.gelu, first)
        expert_low = expert_act.astype(BF)
        partial_out = jnp.einsum("erh,ehd->erd", expert_low, expert_out, preferred_element_type=F32)
        picked = to_sources(partial_out)

        second_all = gather_cuts(second)
        mixing_all = softmax_rows(mm(second_all, small_full[:, experts_all:]))
        d_dense_all = (grad_all.astype(F32) * mixing_all[:, 0:1]).astype(BF)
        up_proj = mm(second_all, in_here)
        activ, gelu_pull = jax.vjp(jax.nn.gelu, up_proj)
        activ_low = activ.astype(BF)
        dense = scatter_cuts(mm(activ_low, w_out)).astype(F32)
        d_activ = mm_nt(d_dense_all, w_out)
        g_out = mm_tn(activ_low, d_dense_all)
        d_up = gelu_pull(d_activ)[0].astype(BF)
        g_in = mm_tn(second_all, d_up)
        d_second_ffn = scatter_cuts(mm_nt(d_up, in_here)).astype(F32)

        d_expert_act = jnp.einsum("erd,ehd->erh", d_rows, expert_out, preferred_element_type=F32)
        d_first = expert_pull(d_expert_act)[0].astype(BF)
        d_rows_in = jnp.einsum("erh,edh->erd", d_first, expert_in, preferred_element_type=F32)
        g_expert_out = jnp.einsum("erh,erd->ehd", expert_low, d_rows, preferred_element_type=F32)
        g_expert_in = jnp.einsum("erd,erh->edh", rows_in, d_first, preferred_element_type=F32)
        d_picked_in = to_sources(d_rows_in)

    moe_val = gate[:, None] * picked
    block_out = (hidden + mixing[:, 0:1] * dense + mixing[:, 1:2] * moe_val).astype(BF)
    d_mixing = jnp.stack([jnp.sum(grad * dense, axis=1), jnp.sum(grad * moe_val, axis=1)], axis=1)
    d_gate = jnp.sum(d_moe * picked, axis=1)
    d_router = router_p * (onehot - gate[:, None]) * d_gate[:, None]
    d_mix = mixing * (d_mixing - jnp.sum(mixing * d_mixing, axis=1, keepdims=True))
    d_small = jnp.concatenate([d_router, d_mix], axis=1).astype(BF)
    g_small = mm_tn(d_small, second)
    d_second = d_second_ffn + mm_nt(d_small, small_full) + d_picked_in
    d_hidden_norm, g_gain_two = norm_back(d_second, xhat_two, inv_two, gain_two)
    d_hidden = grad + d_hidden_norm
    d_attn = d_hidden.astype(BF)
    g_attn_out = mm_tn(head_out, d_attn)
    d_head_rows = mm_nt(d_attn, attn_full).astype(BF)
    if fused:
        tiny = jnp.concatenate([g_small, g_gain_two[None, :]], axis=0)
        tiny = jnp.pad(tiny, ((0, -tiny.shape[0] % 8), (0, 0)))
        d_block_input, s_qkv, s_attn_out, tiny, late = tail(
            g_attn_out.astype(BF), d_head_rows, joined, log_norm[:, 0], normed,
            qkv_here, block_input, gain_one[None, :], d_hidden, tiny, n_expert, n_cuts,
        )
        swap = [
            ((flat % n_expert) * n_cuts + flat // n_expert, flat) for flat in range(n_expert * n_cuts)
        ]
        s_out, late = lax.optimization_barrier((s_out, late))
        s_out = lax.ppermute(s_out, ("expert", "cuts"), swap).astype(F32)
        s_in = s_in.swapaxes(0, 1).reshape(-1, w_in.shape[1]).astype(F32)
        s_qkv = s_qkv.reshape(n_cuts, -1, 3, own).transpose(1, 2, 0, 3).reshape(-1, 3 * features).astype(F32)
        width = features // (n_expert * n_cuts)
        spot = lax.axis_index("cuts") * width
        s_tiny = lax.dynamic_slice_in_dim(tiny, spot, width, axis=1)
        s_late = lax.dynamic_slice_in_dim(late, spot, width, axis=1)
        return (
            block_out,
            d_block_input,
            s_qkv,
            s_attn_out,
            s_in,
            s_out,
            s_tiny[:experts_all].T,
            s_tiny[experts_all : experts_all + 2].T,
            s_late[0],
            s_tiny[experts_all + 2],
            g_expert_in,
            g_expert_out,
        )
    d_heads = columns_to_cuts(d_head_rows).reshape(seq_len, heads, HD)

    soft_p = jnp.exp(masked_scores() - log_norm)
    d_soft = jnp.einsum("qhd,khd->hqk", d_heads, v_heads, preferred_element_type=F32)
    delta = jnp.sum(soft_p * d_soft, axis=-1, keepdims=True)
    d_scores = (soft_p * (d_soft - delta)).astype(BF)
    d_query = jnp.einsum("hqk,khd->qhd", d_scores, k_heads, preferred_element_type=F32) * scaling
    d_keys = jnp.einsum("hqk,qhd->khd", d_scores, q_heads, preferred_element_type=F32) * scaling
    d_values = jnp.einsum("hqk,qhd->khd", soft_p.astype(BF), d_heads, preferred_element_type=F32)
    d_joined = jnp.stack([d_query, d_keys, d_values], axis=1).reshape(seq_len, 3 * own).astype(BF)
    g_qkv = mm_tn(normed, d_joined)
    d_normed = scatter_cuts(mm_nt(d_joined, qkv_here)).astype(F32)
    d_input_norm, g_gain_one = norm_back(d_normed, xhat_one, inv_one, gain_one)
    d_block_input = d_hidden + d_input_norm

    def over_experts(part):
        return lax.psum_scatter(part.astype(BF), "expert", scatter_dimension=0, tiled=True)

    s_in = rows_to_cuts(over_experts(g_in)).astype(F32)
    s_out = over_experts(g_out)
    swap = [
        ((flat % n_expert) * n_cuts + flat // n_expert, flat) for flat in range(n_expert * n_cuts)
    ]
    s_out = lax.ppermute(s_out, ("expert", "cuts"), swap).astype(F32)
    s_qkv = over_experts(g_qkv)
    deep = s_qkv.shape[0]
    s_qkv = lax.all_to_all(
        s_qkv.reshape(deep, 3, 1, own), "cuts", split_axis=0, concat_axis=2, tiled=True
    )
    s_qkv = s_qkv.reshape(-1, 3 * features).astype(F32)
    s_attn_out = scatter_cuts(over_experts(g_attn_out)).astype(F32)
    tiny = jnp.concatenate([g_small, g_gain_one[None, :], g_gain_two[None, :]], axis=0)
    tiny = jnp.pad(tiny, ((0, -tiny.shape[0] % 8), (0, 0)))
    tiny = sum_small(tiny, n_expert, n_cuts)
    width = features // (n_expert * n_cuts)
    s_tiny = lax.dynamic_slice_in_dim(tiny, lax.axis_index("cuts") * width, width, axis=1)
    return (
        block_out,
        d_block_input,
        s_qkv,
        s_attn_out,
        s_in,
        s_out,
        s_tiny[:experts_all].T,
        s_tiny[experts_all : experts_all + 2].T,
        s_tiny[experts_all + 2],
        s_tiny[experts_all + 3],
        g_expert_in,
        g_expert_out,
    )


def solution(mesh):
    both = ("expert", "cuts")
    placed = (
        P(both, None),
        P(both),
        P(both),
        P("cuts", None),
        P("cuts", None),
        P("cuts", None),
        P("cuts", None),
        P("cuts", None),
        P("cuts", None),
        P("cuts"),
        P("cuts"),
        P("expert", None, "cuts"),
        P("expert", "cuts", None),
        P(both, None),
    )
    results = (
        P(both, None),
        P(both, None),
        P(both, None),
        P(both, None),
        P(both, None),
        P(both, None),
        P(both, None),
        P(both, None),
        P(both),
        P(both),
        P("expert", None, "cuts"),
        P("expert", "cuts", None),
    )
    return jax.shard_map(
        shards, mesh=mesh, in_specs=placed, out_specs=results, check_vma=False
    )
```

```python
import functools
import math

import jax
import jax.numpy as jnp
import numpy as np
from jax import lax
from jax.experimental import pallas as pl
from jax.experimental.pallas import tpu as pltpu
from jax.sharding import PartitionSpec as P

HD = 64
BF = jnp.bfloat16
F32 = jnp.float32
MESH = pl.DeviceIdType.MESH


def norm_parts(values):
    center = values - jnp.mean(values, axis=-1, keepdims=True)
    spread = jnp.mean(center * center, axis=-1, keepdims=True)
    inv = lax.rsqrt(spread + 1e-05)
    return center * inv, inv


def norm_back(grad, xhat, inv, gain):
    q = grad * gain
    mean_q = jnp.mean(q, axis=-1, keepdims=True)
    mean_qx = jnp.mean(q * xhat, axis=-1, keepdims=True)
    return (q - mean_q - xhat * mean_qx) * inv, jnp.sum(grad * xhat, axis=0)


def mm(left, right):
    return jnp.dot(left, right, preferred_element_type=F32)


def mm_nt(left, right):
    return lax.dot_general(left, right, (((1,), (1,)), ((), ())), preferred_element_type=F32)


def mm_tn(left, right):
    return lax.dot_general(left, right, (((0,), (0,)), ((), ())), preferred_element_type=F32)


def softmax_rows(logits):
    shifted = logits - jnp.max(logits, axis=-1, keepdims=True)
    row_exp = jnp.exp(shifted)
    return row_exp / jnp.sum(row_exp, axis=-1, keepdims=True)


def gather_cuts(rows):
    return lax.all_gather(rows, "cuts", axis=0, tiled=True)


def scatter_cuts(rows):
    return lax.psum_scatter(rows.astype(BF), "cuts", scatter_dimension=0, tiled=True)


def columns_to_cuts(rows):
    return lax.all_to_all(rows, "cuts", split_axis=1, concat_axis=0, tiled=True)


def rows_to_cuts(rows):
    return lax.all_to_all(rows, "cuts", split_axis=0, concat_axis=1, tiled=True)


def ring_mod(index, count):
    return lax.rem(index, count)


def small_kernel(n_expert, n_cuts, src, out, by_expert, mine, by_cuts, send_a, recv_a, send_b, recv_b):
    me, cut = lax.axis_index("expert"), lax.axis_index("cuts")
    width = out.shape[1]
    barrier = pltpu.get_barrier_semaphore()
    for step in range(1, n_expert):
        peer = ring_mod(me + step, n_expert)
        pl.semaphore_signal(barrier, inc=1, device_id=(peer, cut), device_id_type=MESH)
    for step in range(1, n_cuts):
        peer = ring_mod(cut + step, n_cuts)
        pl.semaphore_signal(barrier, inc=1, device_id=(me, peer), device_id_type=MESH)
    pl.semaphore_wait(barrier, n_expert + n_cuts - 2)

    def part(owner):
        return src.at[:, pl.ds(pl.multiple_of(owner * width, 128), width)]

    copies = []
    for step in range(1, n_expert):
        peer = ring_mod(me + step, n_expert)
        copies.append(
            pltpu.make_async_remote_copy(
                src_ref=part(peer),
                dst_ref=by_expert.at[step],
                send_sem=send_a.at[step],
                recv_sem=recv_a.at[step],
                device_id=(peer, cut),
                device_id_type=MESH,
            )
        )
        copies[-1].start()
    total = src[:, pl.ds(pl.multiple_of(me * width, 128), width)]
    for step in range(1, n_expert):
        copies[step - 1].wait()
        total = total + by_expert[step]
    mine[...] = total
    copies = []
    for step in range(1, n_cuts):
        peer = ring_mod(cut + step, n_cuts)
        copies.append(
            pltpu.make_async_remote_copy(
                src_ref=mine,
                dst_ref=by_cuts.at[step],
                send_sem=send_b.at[step],
                recv_sem=recv_b.at[step],
                device_id=(me, peer),
                device_id_type=MESH,
            )
        )
        copies[-1].start()
    for step in range(1, n_cuts):
        copies[step - 1].wait()
        total = total + by_cuts[step]
    out[...] = total


def sum_small(values, n_expert, n_cuts):
    rows, features = values.shape
    width = features // n_expert
    pad = -width % 128
    if pad:
        values = jnp.pad(values.reshape(rows, n_expert, width), ((0, 0), (0, 0), (0, pad)))
        values = values.reshape(rows, n_expert * (width + pad))
    wide = width + pad
    summed = pl.pallas_call(
        functools.partial(small_kernel, n_expert, n_cuts),
        name="sum_small",
        out_shape=jax.ShapeDtypeStruct((rows, wide), F32),
        in_specs=[pl.BlockSpec(memory_space=pltpu.VMEM)],
        out_specs=pl.BlockSpec(memory_space=pltpu.VMEM),
        scratch_shapes=[
            pltpu.VMEM((n_expert, rows, wide), F32),
            pltpu.VMEM((rows, wide), F32),
            pltpu.VMEM((n_cuts, rows, wide), F32),
            pltpu.SemaphoreType.DMA((n_expert,)),
            pltpu.SemaphoreType.DMA((n_expert,)),
            pltpu.SemaphoreType.DMA((n_cuts,)),
            pltpu.SemaphoreType.DMA((n_cuts,)),
        ],
        compiler_params=pltpu.CompilerParams(collective_id=0, has_side_effects=True),
    )(values)
    return summed[:, :width]


def dot_nt(left, right):
    return lax.dot_general(left, right, (((1,), (1,)), ((), ())), preferred_element_type=F32)


def tile_of(step, size):
    return pl.ds(pl.multiple_of(step * size, size), size)


def lane_softmax(logits, low, high):
    lane = lax.broadcasted_iota(jnp.int32, logits.shape, 1)
    inside = (lane >= low) & (lane < high)
    kept = jnp.where(inside, logits, -1e30)
    powers = jnp.exp(kept - jnp.max(kept, axis=1, keepdims=True))
    powers = jnp.where(inside, powers, 0.0)
    return powers / jnp.sum(powers, axis=1, keepdims=True), lane


def mlp_both(rows, d_rows, w_up, w_down, act, d_up, write):
    root, cubic = math.sqrt(2.0 / math.pi), 0.044715

    @pl.loop(0, act.shape[1] // 256)
    def _(step):
        span = tile_of(step, 256)
        up = mm(rows[...], w_up[:, span])
        d_act = dot_nt(d_rows[...], w_down[span, :])
        square = up * up
        bent = jnp.tanh(root * up * (1.0 + cubic * square))
        half = 0.5 * (1.0 + bent)
        act[:, span] = (up * half).astype(BF)
        slope = half + 0.5 * up * (1.0 - bent * bent) * (root + 3.0 * root * cubic * square)
        d_up[:, span] = (d_act * slope).astype(BF)

    @pl.loop(0, w_up.shape[0] // 256)
    def _(step):
        span = tile_of(step, 256)
        write(span, mm(act[...], w_down[:, span]), dot_nt(d_up[...], w_up[span, :]))


def middle_kernel(
    sizes, slots, second, grad_all, grad_rows, w_in, w_out, small, sort, e_in, e_out,
    sums, ret_a, ret_b, o_in, o_out, rows_in, d_rows_all, act_e_all, d_first_all,
    sec, grd, win, wout, act, d_up, part_a, part_b, ffn_x, ffn_y, ffn_qa, ffn_qb,
    zbuf, rows, g_rows, d_rows, act_e, d_first, wi_e, wo_e, out_a, out_b, row_x, row_y, row_qa, row_qb, sorted_back, send_back,
    twin_in, level_in, fin_in,
    load_sem, weight_sem, store_sem, store_e_sem, z_sem, ag_sem, eag_sem, frs_sem, ers_sem, zr_sem,
    twin_sem, level_sem, fin_sem,
):
    n_expert, groups, here, slab = sizes
    me, cut = lax.axis_index("expert"), lax.axis_index("cuts")
    at_x, at_y, at_d = (jnp.bitwise_xor(cut, k) for k in (1, 2, 3))
    block = zbuf.shape[2]
    per_group = here // groups
    experts_all = n_expert * here

    def load(src, dst, index):
        copy = pltpu.make_async_copy(src, dst, load_sem.at[index])
        copy.start()
        return copy

    def remote(src, dst, sems, index, peer):
        return pltpu.make_async_remote_copy(
            src_ref=src, dst_ref=dst, send_sem=sems.at[0, index], recv_sem=sems.at[1, index],
            device_id=peer, device_id_type=MESH,
        )

    def send(src, dst, sems, index, peer):
        copy = remote(src, dst, sems, index, peer)
        copy.start()
        return copy

    loads = [
        load(second, sec.at[cut], 0), load(w_in, win, 1), load(w_out, wout, 2), load(grad_all, grd, 3),
    ]

    def fetch_expert(i):
        slot = i % 2
        copies = [
            pltpu.make_async_copy(e_in.at[i], wi_e.at[slot], weight_sem.at[0, slot]),
            pltpu.make_async_copy(e_out.at[i], wo_e.at[slot], weight_sem.at[1, slot]),
            pltpu.make_async_copy(grad_rows.at[i], g_rows.at[slot], weight_sem.at[2, slot]),
        ]
        for copy in copies:
            copy.start()
        return copies

    fetched = [fetch_expert(0), fetch_expert(1)]
    barrier = pltpu.get_barrier_semaphore()
    for k in range(1, n_expert):
        pl.semaphore_signal(barrier, inc=1, device_id=(jnp.bitwise_xor(me, k), cut), device_id_type=MESH)
    for peer in (at_x, at_y):
        pl.semaphore_signal(barrier, inc=1, device_id=(me, peer), device_id_type=MESH)
    pl.semaphore_signal(barrier, inc=1, device_id=(me, at_d), device_id_type=MESH)
    pl.semaphore_wait(barrier, n_expert + 2)
    core, level = lax.rem(me, 2), lax.div(me, 2)
    levels = n_expert // 2

    z_copies = []
    for g in range(groups):
        for k in range(1, n_expert):
            peer = jnp.bitwise_xor(me, k)
            z_copies.append(send(slots.at[g, peer], zbuf.at[g, me], z_sem, g * n_expert + k, (peer, cut)))
    loads[0].wait()
    ag = [
        send(sec.at[cut], sec.at[cut], ag_sem, 0, (me, at_x)),
        send(sec.at[cut], sec.at[cut], ag_sem, 1, (me, at_y)),
    ]
    half = sec.shape[1] // 2
    ag += [
        remote(sec.at[at_x, pl.ds(0, half)], sec.at[at_x, pl.ds(0, half)], ag_sem, 2, (me, at_y)),
        remote(sec.at[at_y, pl.ds(half, half)], sec.at[at_y, pl.ds(half, half)], ag_sem, 3, (me, at_x)),
    ]
    for g in range(groups):
        zbuf[g, me] = slots[g, me]
    def ffn_block(which, owner):
        mixing, lane = lane_softmax(mm(sec[owner], small[...]), experts_all, experts_all + 2)
        first_mix = jnp.sum(jnp.where(lane == experts_all, mixing, 0.0), axis=1, keepdims=True)
        grd[owner] = (grd[owner].astype(F32) * first_mix).astype(BF)

        def write(span, out, d_row):
            @pl.when(which == 0)
            def _():
                sums[0, :, span] = out
                sums[1, :, span] = d_row

            part_a[which, :, span] = out.astype(BF)
            part_b[which, :, span] = d_row.astype(BF)

        mlp_both(sec.at[owner], grd.at[owner], win, wout, act.at[owner], d_up.at[owner], write)

    def level_rows(index, half):
        return pl.ds(pl.multiple_of(index * 256 + half * 128, 128), 128)

    def weight_grad(m, left, right, held):
        @pl.loop(0, levels)
        def _(step):
            span = tile_of(step, 256)
            lhs = left[:, :, span].reshape(-1, 256)
            held[span, :] = mm_tn(lhs, right[...].reshape(-1, right.shape[2])).astype(BF)

        return [
            send(held.at[level_rows(n, 1 - core)], twin_in.at[m, n], twin_sem, m * levels + n, (jnp.bitwise_xor(me, 1), cut))
            for n in range(levels)
        ]

    def weight_sum(m, held, twins):
        for copy in twins:
            copy.wait_recv()

        @pl.loop(0, levels)
        def _(step):
            here_rows = level_rows(step, core)
            held[here_rows, :] = (held[here_rows, :].astype(F32) + twin_in[m, step].astype(F32)).astype(BF)

        copies = []
        for k in range(1, levels):
            peer = jnp.bitwise_xor(level, k)
            copies.append(
                send(
                    held.at[level_rows(peer, core)], level_in.at[m, k - 1], level_sem, m * (levels - 1) + k - 1,
                    (2 * peer + core, cut),
                )
            )
        return copies

    def weight_total(m, held, copies):
        for copy in copies:
            copy.wait_recv()
        total = held[level_rows(level, core), :].astype(F32)
        for k in range(1, levels):
            total = total + level_in[m, k - 1].astype(F32)
        return total.astype(BF)

    for copy in loads[1:]:
        copy.wait()
    def slab_of(owner):
        return pl.ds(pl.multiple_of(owner * slab, slab), slab)

    eag = {}
    cut_half = slab // 2
    for i in range(here):
        mine = rows.at[i, slab_of(cut)]
        from_x = rows.at[i, pl.ds(pl.multiple_of(at_x * slab, slab), cut_half)]
        from_y = rows.at[i, pl.ds(pl.multiple_of(at_y * slab + cut_half, cut_half), cut_half)]
        eag[i] = [
            remote(mine, mine, eag_sem, 4 * i, (me, at_x)),
            remote(mine, mine, eag_sem, 4 * i + 1, (me, at_y)),
            remote(from_x, from_x, eag_sem, 4 * i + 2, (me, at_y)),
            remote(from_y, from_y, eag_sem, 4 * i + 3, (me, at_x)),
        ]

    def relay(copies):
        copies[0].wait_recv()
        copies[2].start()
        copies[1].wait_recv()
        copies[3].start()

    @pl.loop(0, sec.shape[0])
    def _(which):
        @pl.when(which == 1)
        def _():
            relay(ag)

        @pl.when(which == 2)
        def _():
            for g in range(groups):
                for k in range(1, n_expert):
                    z_copies[g * (n_expert - 1) + k - 1].wait_recv()
                flat = zbuf[g].reshape(n_expert * block, zbuf.shape[3])
                for j in range(per_group):
                    i = g * per_group + j
                    rows[i, slab_of(cut)] = mm(sort[pl.ds(j * slab, slab), :], flat).astype(BF)
                    eag[i][0].start()
                    eag[i][1].start()

        @pl.when(which == 3)
        def _():
            ag[2].wait_recv()
            ag[3].wait_recv()
            relay(eag[0])

        ffn_block(which, jnp.bitwise_xor(cut, which))

    twins_in = weight_grad(0, sec, d_up, win)
    expert_stores = {}
    ers = {}

    def expert(i):
        slot = i % 2
        if i >= 2:
            for copy in expert_stores[i - 2]:
                copy.wait()
        for copy in fetched[i]:
            copy.wait()
        logits = mm(rows[i], small[...])
        router, lane = lane_softmax(logits, 0, experts_all)
        gate = jnp.sum(jnp.where(lane == me * here + i, router, 0.0), axis=1, keepdims=True)
        mixing, lane = lane_softmax(logits, experts_all, experts_all + 2)
        mixing = jnp.sum(jnp.where(lane == experts_all + 1, mixing, 0.0), axis=1, keepdims=True)
        d_rows[slot] = (g_rows[slot].astype(F32) * mixing * gate).astype(BF)

        def write(span, out, d_row):
            out_a[i, :, span] = out.astype(BF)
            out_b[i, :, span] = d_row.astype(BF)

        mlp_both(rows.at[i], d_rows.at[slot], wi_e.at[slot], wo_e.at[slot], act_e.at[slot], d_first.at[slot], write)
        expert_stores[i] = []
        for n, (src, dst) in enumerate(((d_rows, d_rows_all), (act_e, act_e_all), (d_first, d_first_all))):
            copy = pltpu.make_async_copy(src.at[slot], dst.at[i], store_e_sem.at[n, slot])
            copy.start()
            expert_stores[i].append(copy)
        ers[i] = [
            send(out_a.at[i, slab_of(at_x)], row_x.at[i, 0], ers_sem, 6 * i, (me, at_x)),
            send(out_a.at[i, slab_of(at_d)], row_x.at[i, 1], ers_sem, 6 * i + 1, (me, at_x)),
            send(out_b.at[i, slab_of(at_y)], row_y.at[i, 0], ers_sem, 6 * i + 2, (me, at_y)),
            send(out_b.at[i, slab_of(at_d)], row_y.at[i, 1], ers_sem, 6 * i + 3, (me, at_y)),
        ]

    def add_into(ref, *others):
        total = ref[...].astype(F32)
        for other in others:
            total = total + other[...].astype(F32)
        ref[...] = total.astype(BF)

    def pass_on(i):
        for copy in ers[i][:4]:
            copy.wait_recv()
        add_into(out_a.at[i, slab_of(at_y)], row_x.at[i, 1])
        add_into(out_b.at[i, slab_of(at_x)], row_y.at[i, 1])
        ers[i] += [
            send(out_a.at[i, slab_of(at_y)], row_qa.at[i], ers_sem, 6 * i + 4, (me, at_y)),
            send(out_b.at[i, slab_of(at_x)], row_qb.at[i], ers_sem, 6 * i + 5, (me, at_x)),
        ]

    back_copies = []

    def finish(i):
        ers[i][4].wait_recv()
        ers[i][5].wait_recv()
        for n, (out, near, far) in enumerate(((out_a, row_x, row_qa), (out_b, row_y, row_qb))):
            total = out[i, slab_of(cut)].astype(F32) + near[i, 0].astype(F32) + far[i].astype(F32)
            sorted_back[n, i] = total.astype(BF)
        if (i + 1) % per_group == 0:
            g = i // per_group
            for n in range(2):
                flat = sorted_back[n, pl.ds(g * per_group, per_group)].reshape(per_group * slab, -1)
                placed = mm_tn(sort[...], flat).astype(BF)
                send_back[n, g] = placed.reshape(n_expert, block, -1)
                (ret_a, ret_b)[n][g, me] = send_back[n, g, me]
                for k in range(1, n_expert):
                    peer = jnp.bitwise_xor(me, k)
                    back_copies.append(
                        send(
                            send_back.at[n, g, peer], (ret_a, ret_b)[n].at[g, me], zr_sem,
                            (n * groups + g) * n_expert + k, (peer, cut),
                        )
                    )

    for i in range(here):
        if i + 1 < here:
            relay(eag[i + 1])
        eag[i][2].wait_recv()
        eag[i][3].wait_recv()
        expert(i)
        if i + 2 < here:
            fetched.append(fetch_expert(i + 2))
        if i == 0:
            levels_in = weight_sum(0, win, twins_in)
            twins_out = weight_grad(1, act, grd, wout)
        if i == here - 1:
            frs = [
                send(part_a.at[1], ffn_x.at[0], frs_sem, 0, (me, at_x)),
                send(part_a.at[3], ffn_x.at[1], frs_sem, 1, (me, at_x)),
                send(part_b.at[2], ffn_y.at[0], frs_sem, 2, (me, at_y)),
                send(part_b.at[3], ffn_y.at[1], frs_sem, 3, (me, at_y)),
            ]
        if i == 1:
            levels_out = weight_sum(1, wout, twins_out)
        if i >= 1:
            pass_on(i - 1)
        if i >= 2:
            finish(i - 2)
    rows_store = pltpu.make_async_copy(rows, rows_in, store_sem.at[0])
    rows_store.start()
    pass_on(here - 1)
    finish(here - 2)
    finish(here - 1)
    for copy in frs[:4]:
        copy.wait_recv()
    add_into(part_a.at[2], ffn_x.at[1])
    add_into(part_b.at[1], ffn_y.at[1])
    frs += [
        send(part_a.at[2], ffn_qa, frs_sem, 4, (me, at_y)),
        send(part_b.at[1], ffn_qb, frs_sem, 5, (me, at_x)),
    ]
    fin_in[...] = weight_total(0, win, levels_in).reshape(fin_in.shape)
    fin_copies = []
    for k, peer in ((1, at_x), (2, at_y), (3, at_d)):
        fin_copies.append(send(fin_in.at[peer], o_in.at[cut], fin_sem, k - 1, (me, peer)))
    o_in[cut] = fin_in[cut]
    o_out[...] = weight_total(1, wout, levels_out)
    frs[4].wait_recv()
    frs[5].wait_recv()
    sums[0] = sums[0] + ffn_x[0].astype(F32) + ffn_qa[...].astype(F32)
    sums[1] = sums[1] + ffn_y[0].astype(F32) + ffn_qb[...].astype(F32)
    for copy in back_copies + fin_copies:
        copy.wait_recv()
    for copy in z_copies + ag + frs + back_copies + fin_copies + twins_in + twins_out + levels_in + levels_out:
        copy.wait_send()
    for i in range(here):
        for copy in eag[i] + ers[i]:
            copy.wait_send()
    for i in (here - 2, here - 1):
        for copy in expert_stores[i]:
            copy.wait()
    rows_store.wait()


def middle(slots, second, grad_all, grad_rows, w_in, w_out, small, sort, e_in, e_out, n_expert, n_cuts):
    groups, _, block, width = slots.shape
    tokens = second.shape[0]
    here, _, hidden = e_in.shape
    ffn = w_in.shape[1]
    slab = n_expert * block * groups // here
    rows = n_cuts * slab
    levels, deep = n_expert // 2, width // n_expert
    any_spec, vmem_spec = pl.BlockSpec(memory_space=pl.ANY), pl.BlockSpec(memory_space=pltpu.VMEM)
    shape = jax.ShapeDtypeStruct
    dma = pltpu.SemaphoreType.DMA
    flops = 8 * (n_cuts * tokens * ffn + here * rows * hidden) * width
    return pl.pallas_call(
        functools.partial(middle_kernel, (n_expert, groups, here, slab)),
        name="middle",
        out_shape=(
            shape((2, tokens, width), F32), shape((groups, n_expert, block, width), BF),
            shape((groups, n_expert, block, width), BF), shape((n_cuts, deep // n_cuts, ffn), BF), shape((deep, width), BF),
            shape((here, rows, width), BF), shape((here, rows, width), BF),
            shape((here, rows, hidden), BF), shape((here, rows, hidden), BF),
        ),
        in_specs=[vmem_spec] + [any_spec] * 5 + [vmem_spec] * 2 + [any_spec] * 2,
        out_specs=(vmem_spec,) * 5 + (any_spec,) * 4,
        scratch_shapes=[
            pltpu.VMEM((n_cuts, tokens, width), BF), pltpu.VMEM((n_cuts, tokens, width), BF),
            pltpu.VMEM((width, ffn), BF), pltpu.VMEM((ffn, width), BF),
            pltpu.VMEM((n_cuts, tokens, ffn), BF), pltpu.VMEM((n_cuts, tokens, ffn), BF),
            pltpu.VMEM((n_cuts, tokens, width), BF), pltpu.VMEM((n_cuts, tokens, width), BF),
            pltpu.VMEM((2, tokens, width), BF), pltpu.VMEM((2, tokens, width), BF),
            pltpu.VMEM((tokens, width), BF), pltpu.VMEM((tokens, width), BF),
            pltpu.VMEM((groups, n_expert, block, width), BF), pltpu.VMEM((here, rows, width), BF),
            pltpu.VMEM((2, rows, width), BF), pltpu.VMEM((2, rows, width), BF),
            pltpu.VMEM((2, rows, hidden), BF), pltpu.VMEM((2, rows, hidden), BF),
            pltpu.VMEM((2, width, hidden), BF), pltpu.VMEM((2, hidden, width), BF),
            pltpu.VMEM((here, rows, width), BF), pltpu.VMEM((here, rows, width), BF),
            pltpu.VMEM((here, 2, slab, width), BF), pltpu.VMEM((here, 2, slab, width), BF),
            pltpu.VMEM((here, slab, width), BF), pltpu.VMEM((here, slab, width), BF),
            pltpu.VMEM((2, here, slab, width), BF), pltpu.VMEM((2, groups, n_expert, block, width), BF),
            pltpu.VMEM((2, levels, deep, width), BF), pltpu.VMEM((2, levels - 1, deep, width), BF),
            pltpu.VMEM((n_cuts, deep // n_cuts, ffn), BF),
            dma((4,)), dma((3, 2)), dma((1,)), dma((3, 2)),
            dma((2, groups * n_expert)), dma((2, 4)), dma((2, 4 * here)), dma((2, 6)), dma((2, 6 * here)),
            dma((2, 2 * groups * n_expert)),
            dma((2, 2 * levels)), dma((2, 2 * (levels - 1))), dma((2, 3)),
        ],
        compiler_params=pltpu.CompilerParams(
            collective_id=1, has_side_effects=True, vmem_limit_bytes=67_000_000
        ),
        cost_estimate=pl.CostEstimate(flops=flops, bytes_accessed=48 << 20, transcendentals=0),
    )(slots, second, grad_all, grad_rows, w_in, w_out, small, sort, e_in, e_out)


def tail_kernel(
    heads, scaling, g_attn, d_heads, joined, lse, normed, qkv, source, gain, d_hidden, tiny,
    d_source, o_qkv, o_attn, o_tiny, o_gain,
    core_in, own, a_in, a_z, a_mine, gq, core_q, own_q, z_q, fin_q,
    dh, dj, acc_q, acc_k, acc_v, dn, dn_in, norm_v, qkv_v, tiny_e, tiny_m, tiny_c, late, late_e, late_m, late_c,
    load_sem, core_sem, z_sem, cut_sem, te_sem, tc_sem,
):
    me, cut = lax.axis_index("expert"), lax.axis_index("cuts")
    core, level = lax.rem(me, 2), lax.div(me, 2)
    other = 1 - core
    n_cuts, tokens, width = dh.shape
    n_expert = tiny_e.shape[0]
    levels = n_expert // 2
    twin = (jnp.bitwise_xor(me, 1), cut)

    def send(src, dst, sems, index, peer):
        copy = pltpu.make_async_remote_copy(
            src_ref=src, dst_ref=dst, send_sem=sems.at[0, index], recv_sem=sems.at[1, index],
            device_id=peer, device_id_type=MESH,
        )
        copy.start()
        return copy

    def load(src, dst, index):
        copy = pltpu.make_async_copy(src, dst, load_sem.at[index])
        copy.start()
        return copy

    mine = load(g_attn.at[:, core], own, 0)
    later = [load(normed, norm_v, 1), load(qkv, qkv_v, 2)]
    barrier = pltpu.get_barrier_semaphore()
    for k in range(1, n_expert):
        pl.semaphore_signal(barrier, inc=1, device_id=(jnp.bitwise_xor(me, k), cut), device_id_type=MESH)
    for k in range(1, n_cuts):
        pl.semaphore_signal(barrier, inc=1, device_id=(me, jnp.bitwise_xor(cut, k)), device_id_type=MESH)
    pl.semaphore_wait(barrier, n_expert + n_cuts - 2)

    def columns(index, size):
        return pl.ds(pl.multiple_of(index * size, size), size)

    sent = []

    def to_cuts(src_of, dst_of, base):
        copies = []
        for k in range(1, n_cuts):
            peer = jnp.bitwise_xor(cut, k)
            copies.append(send(src_of(peer), dst_of(k), cut_sem, base + k - 1, (me, peer)))
        sent.extend(copies)
        return copies

    def to_levels(src_of, dst_of, base):
        copies = []
        for k in range(1, levels):
            peer = jnp.bitwise_xor(level, k)
            copies.append(send(src_of(peer), dst_of(k), z_sem, base + k - 1, (2 * peer + core, cut)))
        sent.extend(copies)
        return copies

    def to_experts(src, dst, base):
        copies = []
        for k in range(1, n_expert):
            peer = jnp.bitwise_xor(me, k)
            copies.append(send(src.at[:, columns(peer, 128)], dst.at[k], te_sem, base + k - 1, (peer, cut)))
        sent.extend(copies)
        return copies

    heads_moved = to_cuts(lambda peer: d_heads.at[:, columns(peer, width)], lambda k: dh.at[cut], 0)
    twins = [send(g_attn.at[:, other], core_in, core_sem, 0, twin)]
    tiny_moved = to_experts(tiny, tiny_e, 0)
    dh[cut] = d_heads[:, columns(cut, width)]
    mine.wait()
    twins[0].wait_recv()

    @pl.loop(0, levels)
    def _(step):
        own[step] = (own[step].astype(F32) + core_in[step].astype(F32)).astype(BF)

    piece = own.shape[1] // n_cuts
    attn_moved = to_cuts(lambda peer: own.at[:, columns(peer, piece)], lambda k: a_in.at[k - 1], 3)

    acc_q[...] = jnp.zeros_like(acc_q)
    acc_k[...] = jnp.zeros_like(acc_k)
    acc_v[...] = jnp.zeros_like(acc_v)
    for copy in heads_moved:
        copy.wait_recv()

    @pl.loop(0, heads)
    def _(head):
        pair, half = lax.div(head, 2), lax.rem(head, 2)
        lane = lax.broadcasted_iota(jnp.int32, (1, 128), 1)
        keep = (lax.div(lane, HD) == half).astype(F32)
        keep_low = keep.astype(BF)
        cols = columns(pair, 128)
        k_cols = pl.ds(pl.multiple_of(width + pair * 128, 128), 128)
        v_cols = pl.ds(pl.multiple_of(2 * width + pair * 128, 128), 128)
        for i in range(n_cuts):
            reach = (i + 1) * tokens
            here = pl.ds(i * tokens, tokens)
            query = joined[here, cols] * keep_low
            d_out = dh[i, :, cols] * keep_low
            keys = joined[pl.ds(0, reach), k_cols]
            scores = mm_nt(keys, query) * scaling - lse[head, :, here]
            key_at = lax.broadcasted_iota(jnp.int32, scores.shape, 0)
            query_at = lax.broadcasted_iota(jnp.int32, scores.shape, 1) + i * tokens
            soft = jnp.exp(jnp.where(key_at <= query_at, scores, -1e30))
            d_soft = mm_nt(joined[pl.ds(0, reach), v_cols], d_out)
            delta = jnp.sum(soft * d_soft, axis=0, keepdims=True)
            d_scores = (soft * (d_soft - delta)).astype(BF)
            acc_v[pl.ds(0, reach), cols] += mm(soft.astype(BF), d_out)
            acc_k[pl.ds(0, reach), cols] += mm(d_scores, query)
            acc_q[here, cols] += mm_tn(d_scores, keys) * keep

    dj[:, pl.ds(0, width)] = (acc_q[...] * scaling).astype(BF)
    dj[:, pl.ds(width, width)] = (acc_k[...] * scaling).astype(BF)
    dj[:, pl.ds(2 * width, width)] = acc_v[...].astype(BF)
    for copy in later:
        copy.wait()
    part = tokens // 2
    first, last = pl.ds(0, part), pl.ds(part, part)
    at_x, at_y = (me, jnp.bitwise_xor(cut, 1)), (me, jnp.bitwise_xor(cut, 2))

    def partial_sum(k):
        peer = jnp.bitwise_xor(cut, k)
        dn[k] = mm_nt(dj[columns(peer, tokens), :], qkv_v[...]).astype(BF)

    partial_sum(3)
    passing = [
        send(dn.at[3, first], dn_in.at[2, first], cut_sem, 6, at_x),
        send(dn.at[3, last], dn_in.at[2, last], cut_sem, 7, at_y),
    ]
    partial_sum(1)
    dn_moved = [send(dn.at[1, first], dn_in.at[0, first], cut_sem, 8, at_x)]
    partial_sum(2)
    dn_moved.append(send(dn.at[2, last], dn_in.at[1, last], cut_sem, 12, at_y))

    @pl.loop(0, levels)
    def _(step):
        part = mm_tn(norm_v[:, columns(step, 256)], dj[...]).astype(BF)
        gq[step] = part.reshape(2, 128, part.shape[1])

    twins.append(send(gq.at[:, other], core_q, core_sem, 1, twin))
    d_normed = mm_nt(dj[columns(cut, tokens), :], qkv_v[...])

    for n, rows, k, index, peer in ((0, first, 2, 13, at_y), (1, last, 1, 14, at_x)):
        passing[n].wait_recv()
        dn[k, rows] = (dn[k, rows].astype(F32) + dn_in[2, rows].astype(F32)).astype(BF)
        dn_moved.append(send(dn.at[k, rows], dn_in.at[k - 1, rows], cut_sem, index, peer))
    sent.extend(passing + dn_moved)

    for copy in attn_moved:
        copy.wait_recv()
    total = own[:, columns(cut, piece)].astype(F32)
    for k in range(1, n_cuts):
        total = total + a_in[k - 1].astype(F32)
    a_mine[...] = total.astype(BF)
    attn_z = to_levels(lambda peer: a_mine.at[peer], lambda k: a_z.at[k - 1], 0)

    twins[1].wait_recv()

    @pl.loop(0, levels)
    def _(step):
        own_q[step] = (gq[step, core].astype(F32) + core_q[step].astype(F32)).astype(BF)

    qkv_z = to_levels(lambda peer: own_q.at[peer], lambda k: z_q.at[k - 1], levels - 1)

    for copy in tiny_moved:
        copy.wait_recv()
    small = tiny[:, columns(me, 128)]
    for k in range(1, n_expert):
        small = small + tiny_e[k]
    tiny_m[...] = small

    def tiny_cuts(src, dst, base):
        copies = []
        for k in range(1, n_cuts):
            copies.append(send(src, dst.at[k], tc_sem, base + k - 1, (me, jnp.bitwise_xor(cut, k))))
        sent.extend(copies)
        return copies

    tiny_last = tiny_cuts(tiny_m, tiny_c, 0)

    for copy in dn_moved:
        copy.wait_recv()
    d_normed = d_normed + dn_in[0].astype(F32) + dn_in[1].astype(F32)
    xhat, inv = norm_parts(source[...].astype(F32))
    q = d_normed * gain[...]
    mean_q = jnp.mean(q, axis=-1, keepdims=True)
    mean_qx = jnp.mean(q * xhat, axis=-1, keepdims=True)
    d_source[...] = d_hidden[...] + (q - mean_q - xhat * mean_qx) * inv
    late[...] = jnp.broadcast_to(jnp.sum(d_normed * xhat, axis=0, keepdims=True), late.shape)
    late_moved = to_experts(late, late_e, n_expert - 1)

    for copy in tiny_last:
        copy.wait_recv()
    for k in range(1, n_cuts):
        small = small + tiny_c[k]
    o_tiny[...] = small

    for copy in late_moved:
        copy.wait_recv()
    small = late[:, columns(me, 128)]
    for k in range(1, n_expert):
        small = small + late_e[k]
    late_m[...] = small
    late_last = tiny_cuts(late_m, late_c, n_cuts - 1)

    for copy in attn_z:
        copy.wait_recv()
    total = a_mine[level].astype(F32)
    for k in range(1, levels):
        total = total + a_z[k - 1].astype(F32)
    o_attn[...] = total

    for copy in qkv_z:
        copy.wait_recv()
    total = own_q[level].astype(F32)
    for k in range(1, levels):
        total = total + z_q[k - 1].astype(F32)
    fin_q[...] = total.astype(BF).reshape(fin_q.shape)
    qkv_last = to_cuts(lambda peer: fin_q.at[peer], lambda k: o_qkv.at[cut], 9)
    o_qkv[cut] = fin_q[cut]

    for copy in late_last:
        copy.wait_recv()
    for k in range(1, n_cuts):
        small = small + late_c[k]
    o_gain[...] = small
    for copy in qkv_last:
        copy.wait_recv()
    for copy in sent + twins:
        copy.wait_send()


def tail(g_attn, d_heads, joined, lse, normed, qkv, source, gain, d_hidden, tiny, n_expert, n_cuts):
    tokens, features = d_heads.shape
    heads, seq_len = lse.shape
    levels, own = n_expert // 2, features // n_cuts
    deep = features // n_expert
    piece, wide = deep // n_cuts, 3 * own
    any_spec, vmem_spec = pl.BlockSpec(memory_space=pl.ANY), pl.BlockSpec(memory_space=pltpu.VMEM)
    shape, vmem, dma = jax.ShapeDtypeStruct, pltpu.VMEM, pltpu.SemaphoreType.DMA
    rows = tiny.shape[0]
    grid = (levels, 2, deep, features)
    return pl.pallas_call(
        functools.partial(tail_kernel, heads, HD ** (-0.5)),
        name="tail",
        out_shape=(
            shape((tokens, features), F32), shape((n_cuts, piece, wide), BF), shape((piece, features), F32), shape((rows, 128), F32), shape((8, 128), F32),
        ),
        in_specs=[any_spec] + [vmem_spec] * 3 + [any_spec] * 2 + [vmem_spec] * 4,
        out_specs=(vmem_spec,) * 5,
        scratch_shapes=[
            vmem((levels, deep, features), BF), vmem((levels, deep, features), BF),
            vmem((n_cuts - 1, levels, piece, features), BF),
            vmem((levels - 1, piece, features), BF), vmem((levels, piece, features), BF),
            vmem((levels, 2, deep, wide), BF), vmem((levels, deep, wide), BF), vmem((levels, deep, wide), BF),
            vmem((levels - 1, deep, wide), BF), vmem((n_cuts, piece, wide), BF),
            vmem((n_cuts, tokens, own), BF), vmem((seq_len, wide), BF),
            vmem((seq_len, own), F32), vmem((seq_len, own), F32), vmem((seq_len, own), F32),
            vmem((n_cuts, tokens, features), BF), vmem((n_cuts - 1, tokens, features), BF),
            vmem((seq_len, features), BF), vmem((features, wide), BF),
            vmem((n_expert, rows, 128), F32), vmem((rows, 128), F32), vmem((n_cuts, rows, 128), F32),
            vmem((8, features), F32), vmem((n_expert, 8, 128), F32), vmem((8, 128), F32), vmem((n_cuts, 8, 128), F32),
            dma((3,)), dma((2, 2)), dma((2, 2 * (levels - 1))), dma((2, 15)),
            dma((2, 2 * (n_expert - 1))), dma((2, 2 * (n_cuts - 1))),
        ],
        compiler_params=pltpu.CompilerParams(
            collective_id=2, has_side_effects=True, vmem_limit_bytes=48 << 20
        ),
        cost_estimate=pl.CostEstimate(flops=20_000_000_000, bytes_accessed=24 << 20, transcendentals=0),
    )(
        g_attn.reshape(grid), d_heads, joined, lse.reshape(heads, 1, seq_len),
        normed, qkv, source, gain, d_hidden, tiny,
    )


def head_kernel(
    sizes, source, gains, small, info, sort, w_qkv, w_attn, w_in, cotangent,
    normed, qkv, joined, lse, head_out, attn_full, in_here, small_full, grad_all, grad_rows, placer, gains_all,
    src_v, qkv_v, norm_v, join_v, acc, heads_low, attn_v, in_v, cot_v, slots, zbuf, row_v,
    load_sem, store_sem, cut_sem, twin_sem, z_sem, level_sem,
):
    heads, scaling, groups, here, slab = sizes
    me, cut = lax.axis_index("expert"), lax.axis_index("cuts")
    core = lax.rem(me, 2)
    twin = (jnp.bitwise_xor(me, 1), cut)
    at = [jnp.bitwise_xor(cut, k) for k in range(4)]
    n_cuts, tokens, width = src_v.shape
    n_expert, block = zbuf.shape[1], zbuf.shape[2]
    own, half, levels = width // n_cuts, tokens // 2, n_expert // 2
    level, quarter = lax.div(me, 2), tokens // n_expert

    def span(start, size, step):
        return pl.ds(pl.multiple_of(start, step), size)

    def remote(src, dst, sems, index, peer):
        return pltpu.make_async_remote_copy(
            src_ref=src, dst_ref=dst, send_sem=sems.at[0, index], recv_sem=sems.at[1, index],
            device_id=peer, device_id_type=MESH,
        )

    def local(src, dst, sems, index):
        copy = pltpu.make_async_copy(src, dst, sems.at[index])
        copy.start()
        return copy

    loads = [
        local(cotangent, cot_v, load_sem, 0),
        local(w_attn, attn_v, load_sem, 1),
        local(w_in.at[:, span(cut * width, width, width)], in_v, load_sem, 2),
    ]
    own_qkv = [
        local(
            w_qkv.at[:, span(n * width + cut * own, own, own)],
            qkv_v.at[span(cut * tokens, tokens, tokens), pl.ds(n * own, own)], load_sem, 3 + n,
        )
        for n in range(3)
    ]
    barrier = pltpu.get_barrier_semaphore()
    for k in range(1, n_expert):
        pl.semaphore_signal(barrier, inc=1, device_id=(jnp.bitwise_xor(me, k), cut), device_id_type=MESH)
    for k in range(1, n_cuts):
        pl.semaphore_signal(barrier, inc=1, device_id=(me, at[k]), device_id_type=MESH)
    pl.semaphore_wait(barrier, n_expert + n_cuts - 2)

    def gather(view, first, base):
        return [
            remote(first, view(cut), cut_sem, base, (me, at[1])),
            remote(first, view(cut), cut_sem, base + 1, (me, at[2])),
            remote(view(at[1], 0), view(at[1], 0), cut_sem, base + 2, (me, at[2])),
            remote(view(at[2], 1), view(at[2], 1), cut_sem, base + 3, (me, at[1])),
        ]

    def relay(copies):
        copies[0].wait_recv()
        copies[2].start()
        copies[1].wait_recv()
        copies[3].start()

    def whole(ref):
        def view(owner, piece=None):
            return ref.at[owner] if piece is None else ref.at[owner, pl.ds(piece * half, half)]

        return view

    def weight_rows(owner):
        return span(owner * tokens + core * half + level * quarter, quarter, quarter)

    def pass_levels(ref, base):
        copies = []
        for k in range(1, n_cuts):
            view = ref.at[weight_rows(at[k])]
            for n in range(1, levels):
                peer = (2 * jnp.bitwise_xor(level, n) + core, cut)
                copies.append(remote(view, view, level_sem, base + (k - 1) * (levels - 1) + n - 1, peer))
                copies[-1].start()
        return copies

    def slab_view(owner, piece=None):
        if piece is None:
            return grad_rows.at[:, span(owner * slab, slab, slab // 2)]
        return grad_rows.at[:, span(owner * slab + piece * (slab // 2), slab // 2, slab // 2)]

    def to_cuts(src_of, dst_of, base):
        return [remote(src_of(at[k]), dst_of(k), cut_sem, base + k - 1, (me, at[k])) for k in (3, 1, 2)]

    tokens_moved = gather(whole(src_v), source, 0)
    gains_moved = to_cuts(lambda peer: gains, lambda k: gains_all.at[cut], 16)
    small_moved = to_cuts(lambda peer: small, lambda k: small_full.at[cut], 19)
    qkv_moved = []
    for n in range(3):
        qkv_moved += to_cuts(
            lambda peer: w_qkv.at[weight_rows(0), span(n * width + peer * own, own, own)],
            lambda k: qkv_v.at[weight_rows(cut), pl.ds(n * own, own)],
            22 + 3 * n,
        )
    grad_moved = gather(whole(grad_all), cot_v, 4)
    attn_moved = to_cuts(lambda peer: w_attn.at[weight_rows(0)], lambda k: attn_full.at[weight_rows(cut)], 8)
    slab_moved = gather(slab_view, row_v, 12)
    in_moved = to_cuts(
        lambda peer: w_in.at[weight_rows(0), span(peer * width, width, width)],
        lambda k: in_here.at[weight_rows(cut)], 31,
    )
    for copy in gains_moved + tokens_moved[:2] + qkv_moved + attn_moved + in_moved + small_moved:
        copy.start()
    head_moved = to_cuts(
        lambda peer: heads_low.at[span(peer * tokens, tokens, tokens)],
        lambda k: head_out.at[:, span(cut * own, own, own)], 34,
    )

    loads[0].wait()
    lane = lax.broadcasted_iota(jnp.int32, (tokens, 128), 1).astype(F32)
    picked = jnp.where(lane == info[:, 0:1], info[:, 1:2], 0.0)
    down = lax.broadcasted_iota(jnp.int32, (tokens, tokens), 0)
    right = lax.broadcasted_iota(jnp.int32, (tokens, tokens), 1)
    running = mm((down >= right).astype(F32).astype(BF), picked.astype(BF))
    target = info[:, 2:3] + jnp.sum(picked * running, axis=1, keepdims=True) - 1.0
    column = lax.broadcasted_iota(jnp.int32, placer.shape, 1).astype(F32)
    placer[...] = jnp.where(column == target, info[:, 1:2], 0.0).astype(BF)
    slots[...] = mm_tn(placer[...], cot_v[...]).astype(BF).reshape(slots.shape)
    z_moved = []
    for g in range(groups):
        for k in range(1, n_expert):
            peer = jnp.bitwise_xor(me, k)
            z_moved.append(remote(slots.at[g, peer], zbuf.at[g, me], z_sem, g * n_expert + k, (peer, cut)))
            z_moved[-1].start()
        zbuf[g, me] = slots[g, me]
    src_v[cut] = source[...]
    gains_all[cut] = gains[...]
    small_full[cut] = small[...]
    relay(tokens_moved)
    for copy in grad_moved[:2]:
        copy.start()
    for copy in qkv_moved:
        copy.wait_recv()
    qkv_levels = pass_levels(qkv_v, 0)
    for copy in loads[1:] + own_qkv:
        copy.wait()
    stores = [
        local(cot_v, grad_all.at[cut], store_sem, 0),
        local(attn_v, attn_full.at[span(cut * tokens, tokens, tokens)], store_sem, 1),
        local(in_v, in_here.at[span(cut * tokens, tokens, tokens)], store_sem, 2),
    ]
    for copy in gains_moved:
        copy.wait_recv()

    def normalize(index):
        xhat, _ = norm_parts(src_v[index].astype(F32))
        for n in range(n_cuts):
            cols = slice(n * own, (n + 1) * own)
            norm_v[index, :, cols] = (xhat[:, cols] * gains_all[n, 0:1, :]).astype(BF)

    normalize(cut)
    normalize(at[1])
    normalize(at[2])
    for copy in attn_moved + in_moved:
        copy.wait_recv()
    attn_levels = pass_levels(attn_full, 3 * (levels - 1))
    in_levels = pass_levels(in_here, 6 * (levels - 1))
    for copy in qkv_levels:
        copy.wait_recv()

    def share(ref, base):
        copies = []
        for k in range(1, n_cuts):
            view = ref.at[span(at[k] * tokens + core * half, half, half)]
            copies.append(remote(view, view, twin_sem, base + k - 1, twin))
            copies[-1].start()
        return copies

    shared = share(qkv_v, 0)
    for copy in tokens_moved[2:]:
        copy.wait_recv()
    normalize(at[3])
    for copy in shared:
        copy.wait_recv()

    @pl.loop(0, n_cuts)
    def _(step):
        join_v[step] = mm(norm_v[step], qkv_v[...]).astype(BF)

    stores += [
        local(norm_v, normed, store_sem, 3), local(qkv_v, qkv, store_sem, 4), local(join_v, joined, store_sem, 5),
    ]
    acc[...] = jnp.zeros_like(acc)
    per_group = here // groups
    for copy in z_moved:
        copy.wait_recv()
    for g in range(groups):
        flat = zbuf[g].reshape(n_expert * block, width)
        for j in range(per_group):
            row_v[g * per_group + j] = mm(sort[pl.ds(j * slab, slab), :], flat).astype(BF)
    for copy in slab_moved[:2]:
        copy.start()
    stores.append(local(row_v, slab_view(cut), store_sem, 6))

    @pl.loop(0, heads)
    def _(head):
        @pl.when(head == 2)
        def _():
            relay(grad_moved)

        pair = lax.div(head, 2)
        lane = lax.broadcasted_iota(jnp.int32, (1, 128), 1)
        keep = (lax.div(lane, HD) == lax.rem(head, 2)).astype(F32)
        keep_low = keep.astype(BF)
        cols = span(pair * 128, 128, 128)
        k_cols = span(own + pair * 128, 128, 128)
        v_cols = span(2 * own + pair * 128, 128, 128)
        for i in range(n_cuts):
            reach = (i + 1) * tokens
            query = join_v[i, :, cols] * keep_low
            keys = join_v[pl.ds(0, i + 1), :, k_cols].reshape(reach, 128)
            values = join_v[pl.ds(0, i + 1), :, v_cols].reshape(reach, 128)
            scores = mm_nt(keys, query) * scaling
            key_at = lax.broadcasted_iota(jnp.int32, scores.shape, 0)
            query_at = lax.broadcasted_iota(jnp.int32, scores.shape, 1) + i * tokens
            scores = jnp.where(key_at <= query_at, scores, -1e30)
            peak = jnp.max(scores, axis=0, keepdims=True)
            powers = jnp.exp(scores - peak)
            total = jnp.sum(powers, axis=0, keepdims=True)
            lse[head, :, pl.ds(i * tokens, tokens)] = peak + jnp.log(total)
            soft = (powers / total).astype(BF)
            acc[pl.ds(i * tokens, tokens), cols] += mm_tn(soft, values) * keep

    heads_low[...] = acc[...].astype(BF)
    for copy in head_moved:
        copy.start()
    head_out[:, span(cut * own, own, own)] = heads_low[span(cut * tokens, tokens, tokens), :]
    relay(slab_moved)
    for copy in attn_levels + in_levels:
        copy.wait_recv()
    shared += share(attn_full, 3)
    shared += share(in_here, 6)
    for copy in shared[3:] + grad_moved[2:] + slab_moved[2:] + head_moved + small_moved:
        copy.wait_recv()
    for copy in stores:
        copy.wait()
    everything = tokens_moved + gains_moved + small_moved + qkv_moved + grad_moved + attn_moved + slab_moved
    everything += qkv_levels + attn_levels + in_levels
    for copy in everything + in_moved + head_moved + z_moved + shared:
        copy.wait_send()


def head(source, gains, small, info, sort, w_qkv, w_attn, w_in, cotangent, here, groups, capacity, n_expert, n_cuts):
    tokens, features = source.shape
    seq_len, own = tokens * n_cuts, features // n_cuts
    heads, slab = own // HD, n_expert * capacity
    block = here // groups * capacity
    any_spec, vmem_spec = pl.BlockSpec(memory_space=pl.ANY), pl.BlockSpec(memory_space=pltpu.VMEM)
    shape, vmem, dma = jax.ShapeDtypeStruct, pltpu.VMEM, pltpu.SemaphoreType.DMA
    slots = n_expert * groups * block
    return pl.pallas_call(
        functools.partial(head_kernel, (heads, HD ** (-0.5), groups, here, slab)),
        name="head",
        out_shape=(
            shape((n_cuts, tokens, features), BF), shape((features, 3 * own), BF), shape((n_cuts, tokens, 3 * own), BF),
            shape((heads, 1, seq_len), F32), shape((tokens, features), BF), shape((features, features), BF),
            shape((features, w_in.shape[1] // n_cuts), BF), shape((n_cuts,) + small.shape, BF),
            shape((n_cuts, tokens, features), BF), shape((here, n_cuts * slab, features), BF),
            shape((tokens, slots), BF), shape((n_cuts,) + gains.shape, F32),
        ),
        in_specs=[vmem_spec] * 5 + [any_spec] * 4,
        out_specs=(any_spec,) * 3 + (vmem_spec,) * 2 + (any_spec,) * 2 + (vmem_spec,) + (any_spec,) * 2 + (vmem_spec,) * 2,
        scratch_shapes=[
            vmem((n_cuts, tokens, features), BF), vmem((features, 3 * own), BF), vmem((n_cuts, tokens, features), BF),
            vmem((n_cuts, tokens, 3 * own), BF), vmem((seq_len, own), F32), vmem((seq_len, own), BF),
            vmem((tokens, features), BF), vmem((tokens, features), BF), vmem((tokens, features), BF),
            vmem((groups, n_expert, block, features), BF), vmem((groups, n_expert, block, features), BF),
            vmem((here, slab, features), BF),
            dma((6,)), dma((7,)), dma((2, 37)), dma((2, 9)), dma((2, groups * n_expert)), dma((2, 9 * (n_expert // 2 - 1))),
        ],
        compiler_params=pltpu.CompilerParams(
            collective_id=3, has_side_effects=True, vmem_limit_bytes=66_000_000
        ),
        cost_estimate=pl.CostEstimate(flops=8_000_000_000, bytes_accessed=24 << 20, transcendentals=0),
    )(source, gains, small, info, sort, w_qkv, w_attn, w_in, cotangent)


def expert_grads_kernel(rows, d_first, act, d_rows, grad_in, grad_out, rows_v, first_v, act_v, d_rows_v, sems):
    expert, tile = pl.program_id(0), pl.program_id(1)
    pairs = ((rows, rows_v), (d_first, first_v), (act, act_v), (d_rows, d_rows_v))

    def copies(index):
        return [pltpu.make_async_copy(src.at[index], dst.at[index], sems.at[n, index]) for n, (src, dst) in enumerate(pairs)]

    @pl.when(jnp.logical_and(expert == 0, tile == 0))
    def _():
        for index in range(rows.shape[0]):
            for copy in copies(index):
                copy.start()

    @pl.when(tile == 0)
    def _():
        for copy in copies(expert):
            copy.wait()

    span = tile_of(tile, 512)
    grad_in[0] = mm_tn(rows_v[expert, :, span], first_v[expert])
    grad_out[0] = mm_tn(act_v[expert, :, span], d_rows_v[expert])


def expert_grads(rows, d_first, act, d_rows):
    here, count, width = rows.shape
    hidden = act.shape[2]
    any_spec = pl.BlockSpec(memory_space=pl.ANY)
    return pl.pallas_call(
        expert_grads_kernel,
        name="expert_grads",
        grid=(here, width // 512),
        out_shape=(jax.ShapeDtypeStruct((here, width, hidden), F32), jax.ShapeDtypeStruct((here, hidden, width), F32)),
        in_specs=[any_spec] * 4,
        out_specs=(
            pl.BlockSpec((1, 512, hidden), lambda e, t: (e, t, 0)), pl.BlockSpec((1, 512, width), lambda e, t: (e, t, 0)),
        ),
        scratch_shapes=[
            pltpu.VMEM(rows.shape, BF), pltpu.VMEM(d_first.shape, BF), pltpu.VMEM(act.shape, BF), pltpu.VMEM(d_rows.shape, BF),
            pltpu.SemaphoreType.DMA((4, here)),
        ],
        compiler_params=pltpu.CompilerParams(vmem_limit_bytes=66_000_000),
        cost_estimate=pl.CostEstimate(flops=4 * here * count * width * hidden, bytes_accessed=46 << 20, transcendentals=0),
    )(rows, d_first, act, d_rows)


def shards(
    block_input,
    routes,
    kept_mask,
    w_qkv,
    w_attn_out,
    w_in,
    w_out,
    w_router,
    w_mix,
    gain_attn,
    gain_ffn,
    expert_in,
    expert_out,
    cotangent,
):
    tokens, features = block_input.shape
    n_cuts = lax.axis_size("cuts")
    n_expert = lax.axis_size("expert")
    seq_len = tokens * n_cuts
    scaling = HD ** (-0.5)
    own = features // n_cuts
    heads = own // HD
    experts_all = w_router.shape[1]
    experts_here = expert_in.shape[0]
    capacity = 3 * tokens // (2 * experts_all)

    onehot = (routes[:, None] == jnp.arange(experts_all, dtype=jnp.int32)[None, :]).astype(F32)
    fused = n_cuts == 4
    groups = 2 if fused else 1
    per_group = experts_here // groups
    block = per_group * capacity
    owner, local = routes // experts_here, routes % experts_here
    start = (local // per_group) * (n_expert * block) + owner * block + local % per_group * capacity
    if not fused:
        onehot_kept = onehot * kept_mask.astype(F32)[:, None]
        lower_tri = (jnp.arange(tokens)[:, None] >= jnp.arange(tokens)[None, :]).astype(BF)
        running = mm(lower_tri, onehot_kept.astype(BF))
        slot_num = jnp.sum(onehot_kept * running, axis=1) - 1.0
        target = start.astype(F32) + slot_num
        columns = jnp.arange(experts_all * capacity, dtype=jnp.int32).astype(F32)
        placer = ((columns[None, :] == target[:, None]) & (kept_mask[:, None] > 0)).astype(BF)

    def to_owners(rows):
        grid = mm_tn(placer, rows).astype(BF).reshape(groups, n_expert, block, features)
        grid = grid.swapaxes(0, 1).reshape(n_expert, experts_here, capacity, features)
        moved = lax.all_to_all(grid, "expert", split_axis=0, concat_axis=2, tiled=True)
        return lax.all_gather(moved, "cuts", axis=2, tiled=True)[0]

    def to_sources(rows):
        summed = lax.psum_scatter(rows[None].astype(BF), "cuts", scatter_dimension=2, tiled=True)
        moved = lax.all_to_all(summed, "expert", split_axis=2, concat_axis=0, tiled=True)
        return mm(placer, moved.reshape(-1, features))

    inputs = block_input.astype(F32)
    if fused:
        pair = jnp.stack([gain_attn, gain_ffn], axis=0).astype(F32)
        small_here = jnp.concatenate([w_router, w_mix], axis=1)
        small_cols = small_here.shape[1]
        at = np.arange(n_expert * block)
        slab = n_expert * capacity
        goal = at % slab // capacity * block + at // slab * capacity + at % capacity
        sort = np.asarray(goal[:, None] == at[None, :], dtype=BF)
        info = jnp.stack([routes, kept_mask, start], axis=1).astype(F32)
        normed, qkv_here, joined, log_norm, head_out, attn_full, in_here, small_wide, grad_all, grad_rows, placer, gains = head(
            block_input, jnp.pad(pair, ((0, 6), (0, 0))), jnp.pad(small_here, ((0, 0), (0, -small_cols % 128))),
            info, jnp.asarray(sort), w_qkv, w_attn_out, w_in, cotangent,
            experts_here, groups, capacity, n_expert, n_cuts,
        )
        normed, joined = normed.reshape(seq_len, features), joined.reshape(seq_len, 3 * own)
        small_wide = small_wide.reshape(features, -1)
        small_full = small_wide[:, :small_cols]
        gain_one, gain_two = gains[:, 0].reshape(features), gains[:, 1].reshape(features)
    else:
        gains = gather_cuts(jnp.stack([gain_attn, gain_ffn], axis=1)).astype(F32)
        gain_one, gain_two = gains[:, 0], gains[:, 1]
        xhat_one, inv_one = norm_parts(inputs)
        normed = gather_cuts((xhat_one * gain_one).astype(BF))
        qkv_here = lax.all_to_all(
            w_qkv.reshape(own, 3, n_cuts, own), "cuts", split_axis=2, concat_axis=0, tiled=True
        ).reshape(features, 3 * own)
        joined = mm(normed, qkv_here).astype(BF)
        split = joined.reshape(seq_len, 3, heads, HD)
        q_heads, k_heads, v_heads = split[:, 0], split[:, 1], split[:, 2]
        spots = jnp.arange(seq_len, dtype=jnp.int32)
        visible = (spots[None, :] <= spots[:, None])[None]

        def masked_scores():
            scores = jnp.einsum("qhd,khd->hqk", q_heads, k_heads, preferred_element_type=F32) * scaling
            return jnp.where(visible, scores, -1e30)

        scores = masked_scores()
        peak = jnp.max(scores, axis=-1, keepdims=True)
        row_exp = jnp.exp(scores - peak)
        total = jnp.sum(row_exp, axis=-1, keepdims=True)
        weights_p = (row_exp / total).astype(BF)
        heads_here = jnp.einsum("hqk,khd->qhd", weights_p, v_heads, preferred_element_type=F32)
        log_norm = peak + jnp.log(total)
        head_out = rows_to_cuts(heads_here.reshape(seq_len, own).astype(BF))
        attn_full = gather_cuts(w_attn_out)
        small_full = gather_cuts(jnp.concatenate([w_router, w_mix], axis=1))
        grad_all = gather_cuts(cotangent)
        grad_rows = to_owners(cotangent)
        in_here = columns_to_cuts(w_in)
    hidden = inputs + mm(head_out, attn_full)
    xhat_two, inv_two = norm_parts(hidden)
    second = (xhat_two * gain_two).astype(BF)

    logits = mm(second, small_full)
    router_p = softmax_rows(logits[:, :experts_all])
    mixing = softmax_rows(logits[:, experts_all:])
    gate = jnp.sum(router_p * onehot, axis=1)
    grad = cotangent.astype(F32)
    d_moe = grad * mixing[:, 1:2]

    if fused:
        slots = mm_tn(placer, second).astype(BF).reshape(groups, n_expert, block, features)
        sums, ret_a, ret_b, s_in, s_out, rows_in, d_rows, expert_low, d_first = middle(
            slots, second, grad_all, grad_rows, in_here, w_out, small_wide, jnp.asarray(sort),
            expert_in, expert_out, n_expert, n_cuts,
        )
        dense, d_second_ffn = sums[0], sums[1]
        g_expert_in, g_expert_out = expert_grads(rows_in, d_first, expert_low, d_rows)
        picked = mm(placer, ret_a.reshape(-1, features))
        d_picked_in = mm(placer, ret_b.reshape(-1, features))
    else:
        rows_in = to_owners(second)
        row_logits = jnp.einsum("erd,dk->erk", rows_in, small_full, preferred_element_type=F32)
        ids = lax.axis_index("expert") * experts_here + jnp.arange(experts_here, dtype=jnp.int32)
        is_here = (jnp.arange(experts_all, dtype=jnp.int32)[None, :] == ids[:, None]).astype(F32)
        row_gate = jnp.sum(
            softmax_rows(row_logits[:, :, :experts_all]) * is_here[:, None, :], axis=2, keepdims=True
        )
        row_mixing = softmax_rows(row_logits[:, :, experts_all:])[:, :, 1:2]
        d_rows = (grad_rows.astype(F32) * row_mixing * row_gate).astype(BF)

        first = jnp.einsum("erd,edh->erh", rows_in, expert_in, preferred_element_type=F32)
        expert_act, expert_pull = jax.vjp(jax.nn.gelu, first)
        expert_low = expert_act.astype(BF)
        partial_out = jnp.einsum("erh,ehd->erd", expert_low, expert_out, preferred_element_type=F32)
        picked = to_sources(partial_out)

        second_all = gather_cuts(second)
        mixing_all = softmax_rows(mm(second_all, small_full[:, experts_all:]))
        d_dense_all = (grad_all.astype(F32) * mixing_all[:, 0:1]).astype(BF)
        up_proj = mm(second_all, in_here)
        activ, gelu_pull = jax.vjp(jax.nn.gelu, up_proj)
        activ_low = activ.astype(BF)
        dense = scatter_cuts(mm(activ_low, w_out)).astype(F32)
        d_activ = mm_nt(d_dense_all, w_out)
        g_out = mm_tn(activ_low, d_dense_all)
        d_up = gelu_pull(d_activ)[0].astype(BF)
        g_in = mm_tn(second_all, d_up)
        d_second_ffn = scatter_cuts(mm_nt(d_up, in_here)).astype(F32)

        d_expert_act = jnp.einsum("erd,ehd->erh", d_rows, expert_out, preferred_element_type=F32)
        d_first = expert_pull(d_expert_act)[0].astype(BF)
        d_rows_in = jnp.einsum("erh,edh->erd", d_first, expert_in, preferred_element_type=F32)
        g_expert_out = jnp.einsum("erh,erd->ehd", expert_low, d_rows, preferred_element_type=F32)
        g_expert_in = jnp.einsum("erd,erh->edh", rows_in, d_first, preferred_element_type=F32)
        d_picked_in = to_sources(d_rows_in)

    moe_val = gate[:, None] * picked
    block_out = (hidden + mixing[:, 0:1] * dense + mixing[:, 1:2] * moe_val).astype(BF)
    d_mixing = jnp.stack([jnp.sum(grad * dense, axis=1), jnp.sum(grad * moe_val, axis=1)], axis=1)
    d_gate = jnp.sum(d_moe * picked, axis=1)
    d_router = router_p * (onehot - gate[:, None]) * d_gate[:, None]
    d_mix = mixing * (d_mixing - jnp.sum(mixing * d_mixing, axis=1, keepdims=True))
    d_small = jnp.concatenate([d_router, d_mix], axis=1).astype(BF)
    g_small = mm_tn(d_small, second)
    d_second = d_second_ffn + mm_nt(d_small, small_full) + d_picked_in
    d_hidden_norm, g_gain_two = norm_back(d_second, xhat_two, inv_two, gain_two)
    d_hidden = grad + d_hidden_norm
    d_attn = d_hidden.astype(BF)
    g_attn_out = mm_tn(head_out, d_attn)
    d_head_rows = mm_nt(d_attn, attn_full).astype(BF)
    if fused:
        tiny = jnp.concatenate([g_small, g_gain_two[None, :]], axis=0)
        tiny = jnp.pad(tiny, ((0, -tiny.shape[0] % 8), (0, 0)))
        d_block_input, s_qkv, s_attn_out, tiny, late = tail(
            g_attn_out.astype(BF), d_head_rows, joined, log_norm[:, 0], normed,
            qkv_here, block_input, gain_one[None, :], d_hidden, tiny, n_expert, n_cuts,
        )
        swap = [
            ((flat % n_expert) * n_cuts + flat // n_expert, flat) for flat in range(n_expert * n_cuts)
        ]
        s_out, late = lax.optimization_barrier((s_out, late))
        s_out = lax.ppermute(s_out, ("expert", "cuts"), swap).astype(F32)
        s_in = s_in.swapaxes(0, 1).reshape(-1, w_in.shape[1]).astype(F32)
        s_qkv = s_qkv.reshape(n_cuts, -1, 3, own).transpose(1, 2, 0, 3).reshape(-1, 3 * features).astype(F32)
        width = features // (n_expert * n_cuts)
        spot = lax.axis_index("cuts") * width
        s_tiny = lax.dynamic_slice_in_dim(tiny, spot, width, axis=1)
        s_late = lax.dynamic_slice_in_dim(late, spot, width, axis=1)
        return (
            block_out,
            d_block_input,
            s_qkv,
            s_attn_out,
            s_in,
            s_out,
            s_tiny[:experts_all].T,
            s_tiny[experts_all : experts_all + 2].T,
            s_late[0],
            s_tiny[experts_all + 2],
            g_expert_in,
            g_expert_out,
        )
    d_heads = columns_to_cuts(d_head_rows).reshape(seq_len, heads, HD)

    soft_p = jnp.exp(masked_scores() - log_norm)
    d_soft = jnp.einsum("qhd,khd->hqk", d_heads, v_heads, preferred_element_type=F32)
    delta = jnp.sum(soft_p * d_soft, axis=-1, keepdims=True)
    d_scores = (soft_p * (d_soft - delta)).astype(BF)
    d_query = jnp.einsum("hqk,khd->qhd", d_scores, k_heads, preferred_element_type=F32) * scaling
    d_keys = jnp.einsum("hqk,qhd->khd", d_scores, q_heads, preferred_element_type=F32) * scaling
    d_values = jnp.einsum("hqk,qhd->khd", soft_p.astype(BF), d_heads, preferred_element_type=F32)
    d_joined = jnp.stack([d_query, d_keys, d_values], axis=1).reshape(seq_len, 3 * own).astype(BF)
    g_qkv = mm_tn(normed, d_joined)
    d_normed = scatter_cuts(mm_nt(d_joined, qkv_here)).astype(F32)
    d_input_norm, g_gain_one = norm_back(d_normed, xhat_one, inv_one, gain_one)
    d_block_input = d_hidden + d_input_norm

    def over_experts(part):
        return lax.psum_scatter(part.astype(BF), "expert", scatter_dimension=0, tiled=True)

    s_in = rows_to_cuts(over_experts(g_in)).astype(F32)
    s_out = over_experts(g_out)
    swap = [
        ((flat % n_expert) * n_cuts + flat // n_expert, flat) for flat in range(n_expert * n_cuts)
    ]
    s_out = lax.ppermute(s_out, ("expert", "cuts"), swap).astype(F32)
    s_qkv = over_experts(g_qkv)
    deep = s_qkv.shape[0]
    s_qkv = lax.all_to_all(
        s_qkv.reshape(deep, 3, 1, own), "cuts", split_axis=0, concat_axis=2, tiled=True
    )
    s_qkv = s_qkv.reshape(-1, 3 * features).astype(F32)
    s_attn_out = scatter_cuts(over_experts(g_attn_out)).astype(F32)
    tiny = jnp.concatenate([g_small, g_gain_one[None, :], g_gain_two[None, :]], axis=0)
    tiny = jnp.pad(tiny, ((0, -tiny.shape[0] % 8), (0, 0)))
    tiny = sum_small(tiny, n_expert, n_cuts)
    width = features // (n_expert * n_cuts)
    s_tiny = lax.dynamic_slice_in_dim(tiny, lax.axis_index("cuts") * width, width, axis=1)
    return (
        block_out,
        d_block_input,
        s_qkv,
        s_attn_out,
        s_in,
        s_out,
        s_tiny[:experts_all].T,
        s_tiny[experts_all : experts_all + 2].T,
        s_tiny[experts_all + 2],
        s_tiny[experts_all + 3],
        g_expert_in,
        g_expert_out,
    )


def solution(mesh):
    both = ("expert", "cuts")
    placed = (
        P(both, None),
        P(both),
        P(both),
        P("cuts", None),
        P("cuts", None),
        P("cuts", None),
        P("cuts", None),
        P("cuts", None),
        P("cuts", None),
        P("cuts"),
        P("cuts"),
        P("expert", None, "cuts"),
        P("expert", "cuts", None),
        P(both, None),
    )
    results = (
        P(both, None),
        P(both, None),
        P(both, None),
        P(both, None),
        P(both, None),
        P(both, None),
        P(both, None),
        P(both, None),
        P(both),
        P(both),
        P("expert", None, "cuts"),
        P("expert", "cuts", None),
    )
    return jax.shard_map(
        shards, mesh=mesh, in_specs=placed, out_specs=results, check_vma=False
    )
```
